32 devices in a mesh: rows: 8 (over z, x), seq: 4 (over y, core).
Axes of the slice: x: 2, y: 2, z: 4, core: 2. Of those that a mesh axis runs over, the one named last changes fastest.
Arguments:
- tokens: bfloat16 [24, 512, 1024], P('rows', 'seq'), may hold values from -6 to 6
- doc_lengths: int32 [24, 8], P('rows'), may hold values from 1 to 256, 512 in all within a row
- qkv_weight: bfloat16 [1024, 3072], P(('rows', 'seq')), may hold values from -0.25 to 0.25
- out_weight: bfloat16 [1024, 1024], P(('rows', 'seq')), may hold values from -0.5 to 0.5
- up_weight: bfloat16 [1024, 4096], P(('rows', 'seq')), may hold values from -0.1875 to 0.1875
- down_weight: bfloat16 [4096, 1024], P(('rows', 'seq')), may hold values from -0.09375 to 0.09375
- proj_weight: bfloat16 [1024, 128], P(('rows', 'seq')), may hold values from -0.375 to 0.375
- biases: bfloat16 [7, 1024], P(None, ('rows', 'seq')), may hold values from -2 to 2
- gains: bfloat16 [2, 1024], P(None, ('rows', 'seq')), may hold values from 0.5 to 1.5
- up_bias: bfloat16 [4096], P(('rows', 'seq')), may hold values from -2 to 2
- cotangent: float32 [24, 512, 128], P('rows', 'seq'), may hold values from -6 to 6
Outputs:
- output: bfloat16 [24, 512, 128], P('rows', 'seq')
- input_grad: float32 [24, 512, 1024], P('rows', 'seq')
- qkv_grad: float32 [1024, 3072], P(('rows', 'seq'))
- out_grad: float32 [1024, 1024], P(('rows', 'seq'))
- up_grad: float32 [1024, 4096], P(('rows', 'seq'))
- down_grad: float32 [4096, 1024], P(('rows', 'seq'))
- proj_grad: float32 [1024, 128], P(('rows', 'seq'))
- biases_grad: float32 [7, 1024], P(None, ('rows', 'seq'))
- gains_grad: float32 [2, 1024], P(None, ('rows', 'seq'))
- up_bias_grad: float32 [4096], P(('rows', 'seq'))
The draws below stay inside these ranges and needn't reach their ends.
Inputs may be any that keep to these rules, and one draw needn't show every extreme that they name: `doc_lengths`: each stream's 8 document lengths add up to 512, and in every stream the longest is exactly 256.
All inputs are finite; a program needn't handle non-finite values.
Results may differ from the reference program's by a relative error of at most 0.014.
The reference program's roundings to bfloat16 on the way count: a program that leaves them out, or rounds other values in their place, can miss the bound.
Values may be sent and summed in bfloat16 or wider, within the bound.
A program may use at most 192 MiB of HBM per device.

```python
import math
import jax
import jax.numpy as jnp
import numpy as np
from jax import lax

D = 1024
HEADS = 16
HEAD_DIM = 64
FF = 4096
PROJ = 128
DOCS = 8
STREAM = 512
STREAMS = 24
DOC_MAX = 256


def strengthened(array, key, source, target, shards_of, factor):
    def block_of(dim):
        return (jnp.arange(array.shape[dim]) // (array.shape[dim] // shards_of)).reshape((-1,) + (1,) * (array.ndim - 1 - dim))

    first = jax.random.permutation(key, shards_of)[block_of(target)]
    other_side = (block_of(target) + shards_of // 2) % shards_of
    return jnp.where((block_of(source) == first) | (block_of(source) == other_side), factor * array, array)


def levels(own_key, dims, split, smallest, top_value):
    gain = 1.0
    for dim, parts in split:
        heights = jax.random.uniform(jax.random.fold_in(jax.random.fold_in(own_key, 6), dim), (parts,), jnp.float32, smallest / len(split), top_value / len(split))
        gain = gain * jnp.repeat(jnp.exp(heights), dims[dim] // parts).reshape((-1,) + (1,) * (len(dims) - 1 - dim))
    return gain


def length_profile(count, total, most, slope):
    portions = [(1 << 20) // math.isqrt(standing ** slope) + 1 for standing in range(2, count + 1)]
    spare, given = total - most - (count - 1), [1] * (count - 1)
    while spare > 0:
        movable = [i for i in range(count - 1) if given[i] < most]
        mass, budget = sum([portions[i] for i in movable]), spare
        for i in movable:
            addition = min(most - given[i], max(1, budget * portions[i] // mass), spare)
            given[i] = given[i] + addition
            spare = spare - addition
    return np.array([most] + given)


def ragged(stream_key, amount, total, limit, lean):
    if amount == 2:
        one = jax.random.randint(stream_key, (), max(1, total - limit), min(limit, total - 1) + 1)
        return jnp.stack([one, total - one])
    sizes = jnp.asarray(length_profile(amount, total, limit, lean), jnp.int32)
    couples = (amount - 1) // 2
    donor, taker = sizes[1:1 + 2 * couples:2], sizes[2:2 + 2 * couples:2]
    slack = jnp.minimum(donor - 1, limit - taker)
    moved = jax.random.randint(jax.random.fold_in(stream_key, 1), (couples,), 0, 1 << 20) % (slack + 1)
    sizes = sizes.at[1:1 + 2 * couples:2].set(donor - moved).at[2:2 + 2 * couples:2].set(taker + moved)
    return sizes[jax.random.permutation(jax.random.fold_in(stream_key, 2), amount)]


def bell_draw(key, dims, scale, bound, pieces=(), kind=jnp.bfloat16):
    gain = levels(key, dims, pieces, -0.22, 0.18) if pieces else 1.0
    array = jax.random.normal(key, dims, jnp.float32) * scale * gain
    return jnp.minimum(jnp.maximum(array, -bound), bound).astype(kind)


def heavy_noise(key, extent, width, most, shards, heavy, held_as=jnp.bfloat16):
    array = width * jax.random.normal(key, extent, jnp.float32)
    if shards:
        array = array * levels(key, extent, shards, -0.22, 0.18)
    return jnp.clip(strengthened(array, jax.random.fold_in(key, 3), *heavy), -most, most).astype(held_as)


def setup_inputs(seed: int = 0) -> dict:
    keys = jax.random.split(jax.random.key(seed), 12)
    tokens = heavy_noise(keys[0], (STREAMS, STREAM, D), 1.0, 6.0, ((0, 8), (1, 4)), (1, 2, 4, 2.0))
    doc_lengths = jax.vmap(lambda own: ragged(own, DOCS, STREAM, DOC_MAX, 1))(jax.random.split(keys[1], STREAMS)).reshape((STREAMS, DOCS)).astype(jnp.int32)
    qkv_weight = bell_draw(keys[2], (D, 3 * D), (D // 2) ** -0.5, 0.25, ((0, 32),))
    out_weight = bell_draw(keys[3], (D, D), (D // 8) ** -0.5, 0.5, ((0, 32),))
    up_weight = bell_draw(keys[4], (D, FF), D ** -0.5, 0.1875, ((0, 32),))
    down_weight = bell_draw(keys[5], (FF, D), FF ** -0.5, 0.09375, ((0, 32),))
    proj_weight = bell_draw(keys[6], (D, PROJ), (D // 4) ** -0.5, 0.375, ((0, 32),))
    biases = bell_draw(keys[7], (7, D), 0.3, 2.0, ((1, 32),))
    gains = jnp.clip(1.0 + 0.1 * jax.random.normal(keys[8], (2, D), jnp.float32), 0.5, 1.5).astype(jnp.bfloat16)
    up_bias = bell_draw(keys[9], (FF,), 0.3, 2.0, ((0, 32),))
    cotangent = bell_draw(keys[10], (STREAMS, STREAM, PROJ), 1.0, 6.0, ((0, 8), (1, 4)), jnp.float32)
    return dict(tokens=tokens, doc_lengths=doc_lengths, qkv_weight=qkv_weight, out_weight=out_weight, up_weight=up_weight, down_weight=down_weight, proj_weight=proj_weight, biases=biases, gains=gains, up_bias=up_bias, cotangent=cotangent)


epsilon = 1e-05
rope_base = 10000.0
neg_fill = -1e+30
highest = lax.Precision.HIGHEST

@jax.custom_vjp
def low(v):
    return lax.optimization_barrier(v.astype(jnp.bfloat16)).astype(jnp.float32)

@jax.custom_vjp
def low_back(v):
    return v

def low_keep(v):
    return (low(v), None)

def low_pass(kept, grad):
    return (grad,)

def back_keep(v):
    return (v, None)

def back_low(kept, grad):
    return (low(grad),)
low.defvjp(low_keep, low_pass)
low_back.defvjp(back_keep, back_low)

def layer_norm(field, gain_row, shift_row):
    average = lax.optimization_barrier(jnp.mean(field, axis=-1, keepdims=True))
    centred = field - average
    variance = lax.optimization_barrier(jnp.mean(centred * centred, axis=-1, keepdims=True))
    return centred * lax.rsqrt(variance + epsilon) * gain_row + shift_row

def doc_layout(doc_sizes, places):
    doc_ends = jnp.cumsum(doc_sizes).astype(jnp.int32)
    passed = places[:, None] >= doc_ends[None, :]
    segment = lax.optimization_barrier(jnp.sum(passed.astype(jnp.int32), axis=1)).astype(jnp.int32)
    starts = lax.optimization_barrier(jnp.sum(jnp.where(passed, doc_sizes[None, :], 0), axis=1)).astype(jnp.int32)
    return (segment, places - starts)

def rope_tables(position, half_dim):
    steps_f = jnp.arange(half_dim, dtype=jnp.float32)
    inverse = jnp.exp(steps_f * (-math.log(rope_base) / half_dim))
    angle = position.astype(jnp.float32)[:, None] * inverse[None, :]
    return (jnp.cos(angle), jnp.sin(angle))

def rotate(field, cosine, sine_tab, head_count):
    length = field.shape[0]
    halves = field.reshape(length, head_count, 2, -1)
    first_half = halves[:, :, 0]
    second_half = halves[:, :, 1]
    cos_b = cosine[:, None, :]
    sin_b = sine_tab[:, None, :]
    turned = jnp.stack([first_half * cos_b - second_half * sin_b, second_half * cos_b + first_half * sin_b], axis=2)
    return turned.reshape(length, -1)

def head_attention(queries, keys_all, values_all, segment):
    length = queries.shape[0]
    block_rows = math.gcd(length, 512)
    block_count = length // block_rows
    score_scale = HEAD_DIM ** (-0.5)

    def one_block(element):
        query_blk, seg_blk = element
        raw_scores = low_back(jnp.dot(query_blk, keys_all.T, precision=highest))
        scores = jnp.where(seg_blk[:, None] == segment[None, :], raw_scores * score_scale, neg_fill)
        probs_f = jax.nn.softmax(scores, axis=-1)
        return jnp.dot(low(probs_f), values_all, precision=highest)
    blocks = lax.map(jax.checkpoint(one_block), (queries.reshape(block_count, block_rows, -1), segment.reshape(block_count, block_rows)))
    return blocks.reshape(length, -1)

def by_head(field):
    return field.reshape(field.shape[0], HEADS, HEAD_DIM).transpose(1, 0, 2)

def attention(queries, keys_all, values_all, segment):
    length = queries.shape[0]

    def per_head(element):
        return head_attention(element[0], element[1], element[2], segment)
    heads_out = lax.map(per_head, (by_head(queries), by_head(keys_all), by_head(values_all)))
    return heads_out.transpose(1, 0, 2).reshape(length, HEADS * HEAD_DIM)

def layer_forward(tokens_in, w_qkv, w_out, w_up, w_down, w_proj, bias_rows, gain_rows, bias_up, segment, position):
    model_width = tokens_in.shape[1]
    projected = low_back(jnp.dot(tokens_in, w_qkv, precision=highest) + bias_rows[0:3].reshape(-1))
    cosine, sine_tab = rope_tables(position, HEAD_DIM // 2)
    queries = low_back(low(rotate(projected[:, :model_width], cosine, sine_tab, HEADS)))
    keys_all = low_back(low(rotate(projected[:, model_width:2 * model_width], cosine, sine_tab, HEADS)))
    values_all = low_back(low(projected[:, 2 * model_width:]))
    attended = low_back(low(attention(queries, keys_all, values_all, segment)))
    branch = low_back(jnp.dot(attended, w_out, precision=highest) + bias_rows[3])
    h_one = layer_norm(tokens_in + branch, gain_rows[0], bias_rows[4])
    u_pre = low_back(jnp.dot(low(h_one), w_up, precision=highest) + bias_up)
    hidden = low(jax.nn.gelu(u_pre, approximate=False))
    ffn_out = low_back(jnp.dot(hidden, w_down, precision=highest) + bias_rows[5])
    normed = layer_norm(h_one + ffn_out, gain_rows[1], bias_rows[6])
    return low_back(jnp.dot(low(normed), w_proj, precision=highest))

def reference(tokens, doc_lengths, qkv_weight, out_weight, up_weight, down_weight, proj_weight, biases, gains, up_bias, cotangent):
    weights = (qkv_weight.astype(jnp.float32), out_weight.astype(jnp.float32), up_weight.astype(jnp.float32), down_weight.astype(jnp.float32), proj_weight.astype(jnp.float32), biases.astype(jnp.float32), gains.astype(jnp.float32), up_bias.astype(jnp.float32))
    streams_x = tokens.astype(jnp.float32)
    streams_c = cotangent.astype(jnp.float32)
    places = jnp.arange(STREAM, dtype=jnp.int32)

    def one_stream(totals, element):
        stream_x, stream_len, stream_c = element
        segment, position = doc_layout(stream_len, places)

        def forward(tokens_in, w_qkv, w_out, w_up, w_down, w_proj, bias_rows, gain_rows, bias_up):
            return layer_forward(tokens_in, w_qkv, w_out, w_up, w_down, w_proj, bias_rows, gain_rows, bias_up, segment, position)
        result, pullback = jax.vjp(forward, stream_x, weights[0], weights[1], weights[2], weights[3], weights[4], weights[5], weights[6], weights[7])
        gradients = pullback(stream_c)
        totals = tuple((running + addend for running, addend in zip(totals, gradients[1:])))
        return (totals, (result, gradients[0]))
    initial = tuple((jnp.zeros_like(weight) for weight in weights))
    totals, (outputs, input_grads) = lax.scan(one_stream, initial, (streams_x, doc_lengths, streams_c))
    return (outputs.astype(jnp.bfloat16), input_grads, totals[0], totals[1], totals[2], totals[3], totals[4], totals[5], totals[6], totals[7])
```

```python
import functools
import math

import jax
import jax.numpy as jnp
from jax import lax
from jax.experimental import pallas as pl
from jax.experimental.pallas import tpu as pltpu
from jax.sharding import PartitionSpec as P

MESH = pl.DeviceIdType.MESH
Z, X, Y, C = 4, 2, 2, 2
LA, LB = 1, 1
RA, RB, RC = 2, 1, 1
WIDE = 1024


def place():
    r, s = lax.axis_index("rows"), lax.axis_index("seq")
    return r // X, r % X, s // C, s % C


def device(z, x, y, c):
    return (z * X + x, y * C + c)


def peers_of(z, x, y, c):
    others = [device((z + d) % Z, x, y, c) for d in range(1, Z)]
    return others + [device(z, 1 - x, y, c), device(z, x, 1 - y, c), device(z, x, y, 1 - c)]


def greet(z, x, y, c):
    barrier = pltpu.get_barrier_semaphore()
    peers = peers_of(z, x, y, c)
    for peer in peers:
        pl.semaphore_signal(barrier, inc=1, device_id=peer, device_id_type=MESH)
    pl.semaphore_wait(barrier, len(peers))


def pieces(shapes, wide):
    found = []
    for index, (rows, cols) in enumerate(shapes):
        if cols > wide:
            found += [(index, 0, rows, col, wide) for col in range(0, cols, wide)]
        elif rows > 32:
            found += [(index, row, 32, 0, cols) for row in range(0, rows, 32)]
        else:
            found.append((index, 0, rows, 0, cols))
    return found


def gather_kernel(chunks, count, *refs):
    ins, outs, (send, recv, local) = refs[:count], refs[count : 2 * count], refs[2 * count :]
    z, x, y, c = place()
    greet(z, x, y, c)

    def view(chunk, zs, xs, ys, cs):
        index, row, rows, col, cols = chunk
        return outs[index].at[zs, xs, ys, cs, pl.ds(row, rows), pl.ds(col, cols)]

    def push(k, slot, src, dst, peer):
        return pltpu.make_async_remote_copy(
            src_ref=src,
            dst_ref=dst,
            send_sem=send.at[k, slot],
            recv_sem=recv.at[k, slot],
            device_id=peer,
            device_id_type=MESH,
        )

    def along_z(k, d):
        index, row, rows, col, cols = chunks[k]
        src = ins[index].at[pl.ds(row, rows), pl.ds(col, cols)]
        return push(k, d - 1, src, view(chunks[k], z, x, y, c), device((z + d) % Z, x, y, c))

    def first(k):
        slab = view(chunks[k], slice(None), x, y, c)
        peer = device(z, 1 - x, y, c) if k % 2 == 0 else device(z, x, 1 - y, c)
        return push(k, 3, slab, slab, peer)

    def second(k):
        if k % 2 == 0:
            slab, peer = view(chunks[k], slice(None), slice(None), y, c), device(z, x, 1 - y, c)
        else:
            slab, peer = view(chunks[k], slice(None), x, slice(None), c), device(z, 1 - x, y, c)
        return push(k, 4, slab, slab, peer)

    def third(k):
        slab = view(chunks[k], slice(None), slice(None), slice(None), c)
        return push(k, 5, slab, slab, device(z, x, y, 1 - c))

    def own(i):
        return pltpu.make_async_copy(ins[i], outs[i].at[z, x, y, c], local.at[i])

    total = len(chunks)
    for k in range(total):
        for d in range(1, Z):
            along_z(k, d).start()
    for i in range(count):
        own(i).start()
    for i in range(count):
        own(i).wait()
    for step in range(total + LA + LB):
        if step < total:
            for d in range(1, Z):
                along_z(step, d).wait_recv()
            first(step).start()
        if 0 <= step - LA < total:
            first(step - LA).wait_recv()
            second(step - LA).start()
        if 0 <= step - LA - LB < total:
            second(step - LA - LB).wait_recv()
            third(step - LA - LB).start()
    for k in range(total):
        for d in range(1, Z):
            along_z(k, d).wait_send()
        first(k).wait_send()
        second(k).wait_send()
        third(k).wait()


def gather_all(shards, collective_id):
    shapes = [a.shape for a in shards]
    chunks = pieces(shapes, WIDE)
    count = len(shards)
    outs = pl.pallas_call(
        functools.partial(gather_kernel, chunks, count),
        out_shape=[jax.ShapeDtypeStruct((Z, X, Y, C) + a.shape, a.dtype) for a in shards],
        in_specs=[pl.BlockSpec(memory_space=pltpu.VMEM)] * count,
        out_specs=[pl.BlockSpec(memory_space=pl.ANY)] * count,
        scratch_shapes=[
            pltpu.SemaphoreType.DMA((len(chunks), 6)),
            pltpu.SemaphoreType.DMA((len(chunks), 6)),
            pltpu.SemaphoreType.DMA((count,)),
        ],
        compiler_params=pltpu.CompilerParams(collective_id=collective_id, has_side_effects=True),
    )(*shards)
    return [o.reshape(Z * X * Y * C * o.shape[4], o.shape[5]) for o in outs]


def scatter_kernel(chunks, count, *refs):
    ins, outs = refs[:count], refs[count : 2 * count]
    total = len(chunks)
    scratch = refs[2 * count :]
    send, recv, local = scratch[0], scratch[1], scratch[2]
    own, from_core, from_one, from_two, from_z = (
        scratch[3 : 3 + total],
        scratch[3 + total : 3 + 2 * total],
        scratch[3 + 2 * total : 3 + 3 * total],
        scratch[3 + 3 * total : 3 + 4 * total],
        scratch[3 + 4 * total : 3 + 5 * total],
    )
    z, x, y, c = place()
    greet(z, x, y, c)

    def push(k, slot, src, dst, peer):
        return pltpu.make_async_remote_copy(
            src_ref=src,
            dst_ref=dst,
            send_sem=send.at[k, slot],
            recv_sem=recv.at[k, slot],
            device_id=peer,
            device_id_type=MESH,
        )

    def part(chunk, core):
        index, row, rows, col, cols = chunk
        every = slice(None)
        return ins[index].at[every, every, every, core, pl.ds(row, rows), pl.ds(col, cols)]

    def to_core(k):
        return push(k, 5, part(chunks[k], 1 - c), from_core[k], device(z, x, y, 1 - c))

    def load(k):
        return pltpu.make_async_copy(part(chunks[k], c), own[k], local.at[k])

    def first(k):
        if k % 2 == 0:
            return push(k, 4, own[k].at[:, 1 - x], from_one[k], device(z, 1 - x, y, c))
        return push(k, 4, own[k].at[:, :, 1 - y], from_one[k], device(z, x, 1 - y, c))

    def second(k):
        if k % 2 == 0:
            return push(k, 3, own[k].at[:, x, 1 - y], from_two[k], device(z, x, 1 - y, c))
        return push(k, 3, own[k].at[:, 1 - x, y], from_two[k], device(z, 1 - x, y, c))

    def along_z(k, d):
        to = (z + d) % Z
        return push(k, d - 1, own[k].at[to, x, y], from_z[k].at[d - 1], device(to, x, y, c))

    f32, b16 = jnp.float32, jnp.bfloat16

    def add_core(k):
        @pl.loop(0, Z * X * Y)
        def _(i):
            a, b, e = i // (X * Y), (i // Y) % X, i % Y
            own[k][a, b, e] = (own[k][a, b, e].astype(f32) + from_core[k][a, b, e].astype(f32)).astype(b16)

    def add_one(k):
        @pl.loop(0, Z * 2)
        def _(i):
            a, b = i // 2, i % 2
            if k % 2 == 0:
                own[k][a, x, b] = (own[k][a, x, b].astype(f32) + from_one[k][a, b].astype(f32)).astype(b16)
            else:
                own[k][a, b, y] = (own[k][a, b, y].astype(f32) + from_one[k][a, b].astype(f32)).astype(b16)

    def add_two(k):
        @pl.loop(0, Z)
        def _(a):
            own[k][a, x, y] = (own[k][a, x, y].astype(f32) + from_two[k][a].astype(f32)).astype(b16)

    def finish(k):
        index, row, rows, col, cols = chunks[k]
        value = own[k][z, x, y].astype(f32)
        for d in range(Z - 1):
            value = value + from_z[k][d].astype(f32)
        outs[index][pl.ds(row, rows), pl.ds(col, cols)] = value

    for k in range(total):
        load(k).start()
        to_core(k).start()
    for step in range(total + RA + RB + RC):
        if step < total:
            load(step).wait()
            to_core(step).wait_recv()
            add_core(step)
            first(step).start()
        k = step - RA
        if 0 <= k < total:
            first(k).wait()
            add_one(k)
            second(k).start()
        k = step - RA - RB
        if 0 <= k < total:
            second(k).wait()
            add_two(k)
            for d in range(1, Z):
                along_z(k, d).start()
        k = step - RA - RB - RC
        if 0 <= k < total:
            for d in range(1, Z):
                along_z(k, d).wait()
            finish(k)
    for k in range(total):
        to_core(k).wait_send()


def scatter_all(partials, collective_id):
    shapes = [(a.shape[0] // 32, a.shape[1]) for a in partials]
    chunks = pieces(shapes, WIDE)
    count = len(partials)
    b16 = jnp.bfloat16
    tails = [(rows, cols) for _, _, rows, _, cols in chunks]
    scratch = (
        [pltpu.SemaphoreType.DMA((len(chunks), 6)), pltpu.SemaphoreType.DMA((len(chunks), 6)), pltpu.SemaphoreType.DMA((len(chunks),))]
        + [pltpu.VMEM((Z, X, Y) + t, b16) for t in tails]
        + [pltpu.VMEM((Z, X, Y) + t, b16) for t in tails]
        + [pltpu.VMEM((Z, 2) + t, b16) for t in tails]
        + [pltpu.VMEM((Z,) + t, b16) for t in tails]
        + [pltpu.VMEM((Z - 1,) + t, b16) for t in tails]
    )
    return pl.pallas_call(
        functools.partial(scatter_kernel, chunks, count),
        out_shape=[jax.ShapeDtypeStruct(s, jnp.float32) for s in shapes],
        in_specs=[pl.BlockSpec(memory_space=pl.ANY)] * count,
        out_specs=[pl.BlockSpec(memory_space=pltpu.VMEM)] * count,
        scratch_shapes=scratch,
        compiler_params=pltpu.CompilerParams(
            collective_id=collective_id, has_side_effects=True, vmem_limit_bytes=56 << 20
        ),
    )(*[a.reshape((Z, X, Y, C) + s) for a, s in zip(partials, shapes)])


HEAD_DIM = 64


epsilon = 1e-05
rope_base = 10000.0
neg_fill = -1e30


def layer_norm(field, gain_row, shift_row):
    average = jnp.mean(field, axis=-1, keepdims=True)
    centred = field - average
    variance = jnp.mean(centred * centred, axis=-1, keepdims=True)
    return centred * lax.rsqrt(variance + epsilon) * gain_row + shift_row


def doc_layout(doc_sizes, places):
    doc_ends = jnp.cumsum(doc_sizes)
    passed = places[:, None] >= doc_ends[None, :]
    segment = jnp.sum(passed.astype(jnp.int32), axis=1)
    starts = jnp.sum(jnp.where(passed, doc_sizes[None, :], 0), axis=1)
    return (segment, places - starts)


def rope_tables(position, half_dim):
    steps_f = jnp.arange(half_dim, dtype=jnp.float32)
    inverse = jnp.exp(steps_f * (-math.log(rope_base) / half_dim))
    angle = position.astype(jnp.float32)[:, None] * inverse[None, :]
    return (jnp.cos(angle), jnp.sin(angle))


def rotate(field, cosine, sine_tab, head_count):
    length = field.shape[0]
    halves = field.reshape(length, head_count, 2, -1)
    first_half = halves[:, :, 0]
    second_half = halves[:, :, 1]
    cos_b = cosine[:, None, :]
    sin_b = sine_tab[:, None, :]
    turned = jnp.stack(
        [first_half * cos_b - second_half * sin_b, second_half * cos_b + first_half * sin_b], axis=2
    )
    return turned.reshape(length, -1)


def gelu_exact(field):
    return jax.nn.gelu(field, approximate=False)


def scores_of(query_blk, seg_blk, keys_all, stream_seg, score_scale):
    raw_scores = (
        jnp.einsum("qhd,khd->hqk", query_blk, keys_all, preferred_element_type=jnp.float32)
        * score_scale
    )
    same_doc = (seg_blk[:, None] == stream_seg[None, :])[None]
    return jnp.where(same_doc, raw_scores, neg_fill)


def direct_links():
    return lax.axis_size("rows") == Z * X and lax.axis_size("seq") == Y * C


def pack_rows(arrays, width=1024, height=8):
    flat = jnp.concatenate([a.reshape(a.shape[0], -1) for a in arrays], axis=1)
    return jnp.pad(flat, ((0, 0), (0, width * height - flat.shape[1]))).reshape(-1, width)


def unpack_rows(packed, sizes):
    flat = packed.reshape(-1, 8 * 1024)
    ends = [sum(sizes[: i + 1]) for i in range(len(sizes))]
    return [flat[:, end - size : end] for end, size in zip(ends, sizes)]


def gather_parameters(qkv, out, up, down, proj, biases, gains, up_bias):
    axes = ("rows", "seq")
    f32 = jnp.float32
    if not direct_links():
        full = [lax.all_gather(a, axes, axis=0, tiled=True) for a in (qkv, out, up, down, proj)]
        side = [lax.all_gather(a, axes, axis=1, tiled=True).astype(f32) for a in (biases, gains)]
        return (*full, *side, lax.all_gather(up_bias, axes, axis=0, tiled=True).astype(f32))
    small = [a.reshape(1, -1) for a in (proj, biases, gains, up_bias)]
    packed, w_qkv, w_out, w_up, w_down = gather_all([pack_rows(small), qkv, out, up, down], 1)
    owners = Z * X * Y * C
    proj_f, bias_f, gain_f, up_f = unpack_rows(packed, [a.shape[1] for a in small])
    w_proj = proj_f.reshape(owners * proj.shape[0], proj.shape[1])
    bias_rows, gain_rows = (
        f.reshape((owners,) + a.shape).transpose(1, 0, 2).reshape(a.shape[0], -1).astype(f32)
        for f, a in ((bias_f, biases), (gain_f, gains))
    )
    return w_qkv, w_out, w_up, w_down, w_proj, bias_rows, gain_rows, up_f.reshape(-1).astype(f32)


def scatter_gradients(qkv, out, up, down, proj, bias, gain, up_bias):
    axes = ("rows", "seq")
    if not direct_links():
        return tuple(
            lax.psum_scatter(a, axes, scatter_dimension=d, tiled=True)
            for a, d in ((qkv, 0), (out, 0), (up, 0), (down, 0), (proj, 0), (bias, 1), (gain, 1), (up_bias, 0))
        )
    owners = Z * X * Y * C
    by_owner = [
        proj.reshape(owners, -1),
        bias.reshape(bias.shape[0], owners, -1).transpose(1, 0, 2).reshape(owners, -1),
        gain.reshape(gain.shape[0], owners, -1).transpose(1, 0, 2).reshape(owners, -1),
        up_bias.reshape(owners, -1),
    ]
    low = [a.astype(jnp.bfloat16) for a in (pack_rows(by_owner), down, up, out, qkv)]
    packed, down_s, up_s, out_s, qkv_s = scatter_all(low, 2)
    proj_s, bias_s, gain_s, bias_up_s = unpack_rows(packed, [a.shape[1] for a in by_owner])
    return (
        qkv_s,
        out_s,
        up_s,
        down_s,
        proj_s.reshape(-1, proj.shape[1]),
        bias_s.reshape(bias.shape[0], -1),
        gain_s.reshape(gain.shape[0], -1),
        bias_up_s.reshape(-1),
    )


def per_device(
    tokens,
    doc_lengths,
    qkv_weight,
    out_weight,
    up_weight,
    down_weight,
    proj_weight,
    biases,
    gains,
    up_bias,
    cotangent,
):
    stream_count = tokens.shape[0]
    seg_rows = tokens.shape[1]
    model_width = tokens.shape[2]
    seq_parts = lax.axis_size("seq")
    stream = seg_rows * seq_parts
    head_count = model_width // HEAD_DIM
    local_heads = head_count // seq_parts
    flat_width = local_heads * HEAD_DIM
    score_scale = HEAD_DIM ** (-0.5)
    tok_flat = tokens.reshape(stream_count * seg_rows, model_width)
    w_qkv, w_out, w_up, w_down, w_proj, bias_rows, gain_rows, bias_up = gather_parameters(
        qkv_weight, out_weight, up_weight, down_weight, proj_weight, biases, gains, up_bias
    )
    token_places = lax.axis_index("seq") * seg_rows + jnp.arange(seg_rows, dtype=jnp.int32)
    layout_rows = jax.vmap(doc_layout, in_axes=(0, None))
    token_seg, position = layout_rows(doc_lengths, token_places)
    cosine, sine_tab = rope_tables(position.reshape(-1), HEAD_DIM // 2)
    projected = jnp.dot(tok_flat, w_qkv, preferred_element_type=jnp.float32) + bias_rows[
        0:3
    ].reshape(-1)
    queries = (
        rotate(projected[:, :model_width], cosine, sine_tab, head_count)
        .astype(jnp.bfloat16)
        .reshape(stream_count, seg_rows, model_width)
    )
    keys_tok = (
        rotate(projected[:, model_width : 2 * model_width], cosine, sine_tab, head_count)
        .astype(jnp.bfloat16)
        .reshape(stream_count, seg_rows, model_width)
    )
    values_tok = (
        projected[:, 2 * model_width :]
        .astype(jnp.bfloat16)
        .reshape(stream_count, seg_rows, model_width)
    )
    queries_h, keys_h, values_h = (
        lax.all_to_all(queries, "seq", split_axis=2, concat_axis=1, tiled=True),
        lax.all_to_all(keys_tok, "seq", split_axis=2, concat_axis=1, tiled=True),
        lax.all_to_all(values_tok, "seq", split_axis=2, concat_axis=1, tiled=True),
    )
    stream_seg, stream_pos = layout_rows(doc_lengths, jnp.arange(stream, dtype=jnp.int32))
    block_rows = math.gcd(stream, 512)
    block_count = stream // block_rows

    def forward_stream(element):
        query_s, key_s, value_s, seg_s = element
        query_blocks = query_s.reshape(block_count, block_rows, local_heads, HEAD_DIM)
        keys_all = key_s.reshape(stream, local_heads, HEAD_DIM)
        values_all = value_s.reshape(stream, local_heads, HEAD_DIM)
        seg_blocks = seg_s.reshape(block_count, block_rows)

        def forward_block(inner):
            query_blk, seg_blk = inner
            scores = scores_of(query_blk, seg_blk, keys_all, seg_s, score_scale)
            row_max = jnp.max(scores, axis=-1, keepdims=True)
            row_total = jnp.sum(jnp.exp(scores - row_max), axis=-1, keepdims=True)
            log_total = row_max + jnp.log(row_total)
            probs_low = jnp.exp(scores - log_total).astype(jnp.bfloat16)
            attn_blk = jnp.einsum(
                "hqk,khd->qhd", probs_low, values_all, preferred_element_type=jnp.float32
            )
            return (attn_blk.astype(jnp.bfloat16), log_total[:, :, 0])

        attn_blocks, log_blocks = lax.map(forward_block, (query_blocks, seg_blocks))
        return (attn_blocks.reshape(stream, flat_width), log_blocks)

    attn_heads, log_totals = lax.map(forward_stream, (queries_h, keys_h, values_h, stream_seg))
    attended = lax.all_to_all(attn_heads, "seq", split_axis=1, concat_axis=2, tiled=True).reshape(
        stream_count * seg_rows, model_width
    )
    branch = jnp.dot(attended, w_out, preferred_element_type=jnp.float32) + bias_rows[3]
    h_one, norm_one = jax.vjp(
        layer_norm, tok_flat.astype(jnp.float32) + branch, gain_rows[0], bias_rows[4]
    )
    h_low = h_one.astype(jnp.bfloat16)
    u_pre = jnp.dot(h_low, w_up, preferred_element_type=jnp.float32) + bias_up
    hidden_f, gelu_back = jax.vjp(gelu_exact, u_pre)
    hidden = hidden_f.astype(jnp.bfloat16)
    ffn_out = jnp.dot(hidden, w_down, preferred_element_type=jnp.float32) + bias_rows[5]
    normed, norm_two = jax.vjp(layer_norm, h_one + ffn_out, gain_rows[1], bias_rows[6])
    normed_low = normed.astype(jnp.bfloat16)
    result = jnp.dot(normed_low, w_proj, preferred_element_type=jnp.float32).astype(jnp.bfloat16)
    cot_low = cotangent.reshape(stream_count * seg_rows, -1).astype(jnp.bfloat16)
    proj_part = jnp.dot(normed_low.T, cot_low, preferred_element_type=jnp.float32)
    grad_normed = jnp.dot(cot_low, w_proj.T, preferred_element_type=jnp.float32)
    grad_z2, grad_g2, grad_b2 = norm_two(grad_normed)
    grad_ffn = grad_z2.astype(jnp.bfloat16)
    grad_c2 = jnp.sum(grad_ffn, axis=0, dtype=jnp.float32)
    down_part = jnp.dot(hidden.T, grad_ffn, preferred_element_type=jnp.float32)
    grad_hidden = jnp.dot(grad_ffn, w_down.T, preferred_element_type=jnp.float32)
    grad_u = gelu_back(grad_hidden)[0].astype(jnp.bfloat16)
    grad_c1 = jnp.sum(grad_u, axis=0, dtype=jnp.float32)
    up_part = jnp.dot(h_low.T, grad_u, preferred_element_type=jnp.float32)
    ffn_sums = (up_part, down_part, proj_part, grad_c1)
    grad_h1 = grad_z2 + jnp.dot(grad_u, w_up.T, preferred_element_type=jnp.float32)
    grad_z1, grad_g1, grad_b1 = norm_one(grad_h1)
    grad_branch = grad_z1.astype(jnp.bfloat16)
    grad_bo = jnp.sum(grad_branch, axis=0, dtype=jnp.float32)
    out_part = jnp.dot(attended.T, grad_branch, preferred_element_type=jnp.float32)
    grad_attn = jnp.dot(grad_branch, w_out.T, preferred_element_type=jnp.float32).astype(
        jnp.bfloat16
    )
    grad_heads = lax.all_to_all(
        grad_attn.reshape(stream_count, seg_rows, model_width),
        "seq",
        split_axis=2,
        concat_axis=1,
        tiled=True,
    )

    def backward_stream(element):
        query_s, key_s, value_s, seg_s, log_s, grad_s = element
        query_blocks = query_s.reshape(block_count, block_rows, local_heads, HEAD_DIM)
        keys_all = key_s.reshape(stream, local_heads, HEAD_DIM)
        values_all = value_s.reshape(stream, local_heads, HEAD_DIM)
        seg_blocks = seg_s.reshape(block_count, block_rows)
        grad_blocks = grad_s.reshape(block_count, block_rows, local_heads, HEAD_DIM)

        def backward_block(carried, inner):
            grad_keys, grad_values = carried
            query_blk, seg_blk, log_total, grad_blk = inner
            probs_f = jnp.exp(
                scores_of(query_blk, seg_blk, keys_all, seg_s, score_scale) - log_total[:, :, None]
            )
            grad_values = grad_values + jnp.einsum(
                "hqk,qhd->khd",
                probs_f.astype(jnp.bfloat16),
                grad_blk,
                preferred_element_type=jnp.float32,
            )
            grad_probs = jnp.einsum(
                "qhd,khd->hqk", grad_blk, values_all, preferred_element_type=jnp.float32
            )
            row_dot = jnp.sum(probs_f * grad_probs, axis=-1, keepdims=True)
            grad_scores = (probs_f * (grad_probs - row_dot) * score_scale).astype(jnp.bfloat16)
            grad_query = jnp.einsum(
                "hqk,khd->qhd", grad_scores, keys_all, preferred_element_type=jnp.float32
            )
            grad_keys = grad_keys + jnp.einsum(
                "hqk,qhd->khd", grad_scores, query_blk, preferred_element_type=jnp.float32
            )
            return ((grad_keys, grad_values), grad_query.astype(jnp.bfloat16))

        zero_acc = jnp.zeros((stream, local_heads, HEAD_DIM), jnp.float32)
        (grad_keys, grad_values), grad_queries = lax.scan(
            backward_block, (zero_acc, zero_acc), (query_blocks, seg_blocks, log_s, grad_blocks)
        )
        return (
            grad_queries.reshape(stream, flat_width),
            grad_keys.astype(jnp.bfloat16).reshape(stream, flat_width),
            grad_values.astype(jnp.bfloat16).reshape(stream, flat_width),
        )

    head_q, head_k, head_v = lax.map(
        backward_stream, (queries_h, keys_h, values_h, stream_seg, log_totals, grad_heads)
    )
    back_q, back_k, back_v = (
        lax.all_to_all(head_q, "seq", split_axis=1, concat_axis=2, tiled=True),
        lax.all_to_all(head_k, "seq", split_axis=1, concat_axis=2, tiled=True),
        lax.all_to_all(head_v, "seq", split_axis=1, concat_axis=2, tiled=True),
    )
    flat_rows = stream_count * seg_rows
    turned_q = rotate(
        back_q.reshape(flat_rows, model_width).astype(jnp.float32), cosine, -sine_tab, head_count
    )
    turned_k = rotate(
        back_k.reshape(flat_rows, model_width).astype(jnp.float32), cosine, -sine_tab, head_count
    )
    grad_project = jnp.concatenate(
        [turned_q, turned_k, back_v.reshape(flat_rows, model_width).astype(jnp.float32)], axis=1
    ).astype(jnp.bfloat16)
    grad_bqkv = jnp.sum(grad_project, axis=0, dtype=jnp.float32).reshape(3, model_width)
    qkv_part = jnp.dot(tok_flat.T, grad_project, preferred_element_type=jnp.float32)
    input_grad = grad_z1 + jnp.dot(grad_project, w_qkv.T, preferred_element_type=jnp.float32)
    bias_part = jnp.concatenate(
        [grad_bqkv, jnp.stack([grad_bo, grad_b1, grad_c2, grad_b2])], axis=0
    )
    gain_part = jnp.stack([grad_g1, grad_g2])
    qkv_sum, out_sum, up_sum, down_sum, proj_sum, bias_sum, gain_sum, c1_sum = scatter_gradients(
        qkv_part, out_part, ffn_sums[0], ffn_sums[1], ffn_sums[2], bias_part, gain_part, ffn_sums[3]
    )
    output = result.reshape(stream_count, seg_rows, -1)
    return (
        output,
        input_grad.reshape(stream_count, seg_rows, model_width),
        qkv_sum,
        out_sum,
        up_sum,
        down_sum,
        proj_sum,
        bias_sum,
        gain_sum,
        c1_sum,
    )


def solution(mesh):
    in_specs = (
        P("rows", "seq", None),
        P("rows", None),
        P(("rows", "seq"), None),
        P(("rows", "seq"), None),
        P(("rows", "seq"), None),
        P(("rows", "seq"), None),
        P(("rows", "seq"), None),
        P(None, ("rows", "seq")),
        P(None, ("rows", "seq")),
        P(("rows", "seq")),
        P("rows", "seq", None),
    )
    out_specs = (
        P("rows", "seq", None),
        P("rows", "seq", None),
        P(("rows", "seq"), None),
        P(("rows", "seq"), None),
        P(("rows", "seq"), None),
        P(("rows", "seq"), None),
        P(("rows", "seq"), None),
        P(None, ("rows", "seq")),
        P(None, ("rows", "seq")),
        P(("rows", "seq")),
    )
    return jax.shard_map(
        per_device, mesh=mesh, in_specs=in_specs, out_specs=out_specs, check_vma=False
    )
```

```python
import functools
import math

import jax
import jax.numpy as jnp
from jax import lax
from jax.experimental import pallas as pl
from jax.experimental.pallas import tpu as pltpu
from jax.sharding import PartitionSpec as P

epsilon = 1e-05
rope_base = 10000.0
neg_fill = -1e30

HEAD_DIM = 64
PAIR = 2 * HEAD_DIM
MESH = pl.DeviceIdType.MESH
Z, X, Y, C = 4, 2, 2, 2
OWNERS = Z * X * Y * C
f32, b16 = jnp.float32, jnp.bfloat16
FAR = -1e30


def place():
    r, s = lax.axis_index("rows"), lax.axis_index("seq")
    return r // X, r % X, s // C, s % C


def device(z, x, y, c):
    return (z * X + x, y * C + c)


def greet(peers):
    barrier = pltpu.get_barrier_semaphore()
    for peer in peers:
        pl.semaphore_signal(barrier, inc=1, device_id=peer, device_id_type=MESH)
    pl.semaphore_wait(barrier, len(peers))


def send_to(src, dst, send, recv, peer):
    return pltpu.make_async_remote_copy(
        src_ref=src, dst_ref=dst, send_sem=send, recv_sem=recv, device_id=peer, device_id_type=MESH
    )


def normal_rows(field):
    average = jnp.mean(field, axis=-1, keepdims=True)
    centred = field - average
    inverse = lax.rsqrt(jnp.mean(centred * centred, axis=-1, keepdims=True) + epsilon)
    return centred * inverse, inverse


def at_index(index, plan):
    for spot, calls in plan.items():
        if calls:

            @pl.when(index == spot)
            def _(calls=calls):
                for call in calls:
                    call()


def forward_kernel(
    tok, wqkv, wout, wup, wdown, wproj, side, cos4, sin4, seg_col, seg_row,
    o_out, o_up, o_down, o_proj, o_cols, o_rows, o_tok, o_qkv, o_lse, o_att, o_n1, o_r1, o_hlow, o_hid, o_dgelu, o_n2, o_r2, o_nlow, o_res,
    g_out, g_up, g_down, g_proj, g_side, g_cols, g_tok, qkv, head_out, far, att, z_one, h_low, hid, dgelu, n_two, bias_up,
    c_send, c_recv, a_send, a_recv, wz_send, wz_recv, wx_send, wx_recv, y_send, y_recv, k_send, k_recv, t_send, t_recv, save,
):
    streams, part, width = tok.shape
    rows = streams * part
    z, x, y, c = place()
    s = y * C + c
    seq_peer = [(y, 1 - c), (1 - y, c), (1 - y, 1 - c)]
    others = [(z + d) % Z for d in range(1, Z)]
    greet(
        [device(zz, x, y, c) for zz in others]
        + [device(z, 1 - x, y, c)]
        + [device(z, x, yy, cc) for yy, cc in seq_peer]
    )

    every = slice(None)
    sources, targets = [side, wproj, wout], [g_side, g_proj, g_out]
    quarter = width
    for j in range(4):
        sources.append(wup.at[:, pl.ds(j * quarter, quarter)])
        targets.append(g_up.at[j])
    down_cols = width // 4
    for j in range(4):
        sources.append(wdown.at[:, pl.ds(j * down_cols, down_cols)])
        targets.append(g_down.at[j])
    total = len(sources)

    def along_z(k, d):
        return send_to(sources[k], targets[k].at[z, x, y, c], c_send.at[k, d], c_recv.at[k, d], device(others[d], x, y, c))

    def first(k):
        slab = targets[k].at[:, x, y, c]
        peer = device(z, 1 - x, y, c) if k % 2 else device(z, x, 1 - y, c)
        return send_to(slab, slab, c_send.at[k, 3], c_recv.at[k, 3], peer)

    def second(k):
        if k % 2:
            slab, peer = targets[k].at[:, :, y, c], device(z, x, 1 - y, c)
        else:
            slab, peer = targets[k].at[:, x, :, c], device(z, 1 - x, y, c)
        return send_to(slab, slab, c_send.at[k, 4], c_recv.at[k, 4], peer)

    def third(k):
        slab = targets[k].at[:, :, :, c]
        return send_to(slab, slab, c_send.at[k, 5], c_recv.at[k, 5], device(z, x, y, 1 - c))

    def step_one(k):
        for d in range(Z - 1):
            along_z(k, d).wait_recv()
        first(k).start()

    def step_two(k):
        first(k).wait_recv()
        second(k).start()

    def step_three(k):
        second(k).wait_recv()
        third(k).start()

    cols = wqkv.shape[2] // (Y * C)

    def cols_seq(p):
        yy, cc = seq_peer[p]
        src = wqkv.at[:, :, pl.ds(pl.multiple_of((yy * C + cc) * cols, 128), cols)]
        return send_to(src, g_cols.at[:, z, x, y, c], a_send.at[p], a_recv.at[p], device(z, x, yy, cc))

    def cols_z(j, d):
        slab = g_cols.at[j, z, x]
        return send_to(slab, slab, wz_send.at[j, d], wz_recv.at[j, d], device(others[d], x, y, c))

    def cols_x(j):
        slab = g_cols.at[j, :, x]
        return send_to(slab, slab, wx_send.at[j], wx_recv.at[j], device(z, 1 - x, y, c))

    def tok_y(b):
        return send_to(tok.at[b], g_tok.at[b, y, c], y_send.at[b], y_recv.at[b], device(z, x, 1 - y, c))

    def tok_c(b):
        return send_to(tok.at[b], g_tok.at[b, y, c], k_send.at[b, 0], k_recv.at[b, 0], device(z, x, y, 1 - c))

    def tok_yc(b):
        slab = g_tok.at[b, 1 - y, c]
        return send_to(slab, slab, k_send.at[b, 1], k_recv.at[b, 1], device(z, x, y, 1 - c))

    def att_seq(i, p):
        b, half = i // 2, i % 2
        yy, cc = seq_peer[p]
        src = head_out.at[b, half, yy, cc]
        lane = pl.multiple_of((s * 2 + half) * PAIR, PAIR)
        return send_to(src, att.at[b, :, pl.ds(lane, PAIR)], t_send.at[i, p], t_recv.at[i, p], device(z, x, yy, cc))

    for p in range(3):
        cols_seq(p).start()
    for b in range(streams):
        tok_y(b).start()
    for k in range(4):
        for d in range(Z - 1):
            along_z(k, d).start()
    for b in range(streams):
        tok_c(b).start()
    g_cols[:, z, x, y, c] = wqkv[:, :, pl.ds(pl.multiple_of(s * cols, 128), cols)]
    for b in range(streams):
        g_tok[b, y, c] = tok[b]
    for k in range(total):
        targets[k][z, x, y, c] = sources[k][...]
    for p in range(3):
        cols_seq(p).wait_recv()
    for j in range(3):
        for d in range(Z - 1):
            cols_z(j, d).start()
    for k in range(4, total):
        for d in range(Z - 1):
            along_z(k, d).start()

    step_one(0)
    step_one(1)
    step_one(2)
    step_two(0)
    tok_y(0).wait_recv()
    tok_yc(0).start()
    step_two(1)
    step_three(0)
    step_one(3)
    tok_y(1).wait_recv()
    tok_yc(1).start()
    for j in range(3):
        for d in range(Z - 1):
            cols_z(j, d).wait_recv()
        cols_x(j).start()
    step_two(2)
    tok_y(2).wait_recv()
    tok_yc(2).start()
    step_one(4)
    step_three(1)
    third(0).wait_recv()

    lanes = lax.broadcasted_iota(jnp.int32, (16, 128), 1)
    share = 128 // (Y * C)
    for zx in range(Z * X):
        tile = jnp.zeros((16, 128), f32)
        for yc in range(Y * C):
            block = g_side[zx // X, zx % X, yc // C, yc % C].astype(f32)
            bias_up[:, pl.ds((zx * Y * C + yc) * 128, 128)] = block[9:10]
            tile = tile + pltpu.roll(jnp.where(lanes < share, block, 0.0), yc * share, 1)
        o_rows[:, pl.ds(zx * 128, 128)] = tile

    lane = lax.broadcasted_iota(jnp.int32, (1, 128), 1)
    low_half = (lane % HEAD_DIM) < HEAD_DIM // 2
    for j in range(3):
        cols_x(j).wait_recv()
    for b in range(streams):
        tok_c(b).wait_recv()
        tok_yc(b).wait_recv()
    stream = part * Y * C

    def project(b):
        rows_b = g_tok[b].reshape(stream, width)
        for j in range(3):
            bias_row = o_rows[pl.ds(j, 1), pl.ds(pl.multiple_of(s * cols, 128), cols)]
            got = jnp.dot(rows_b, g_cols[j].reshape(width, cols), preferred_element_type=f32) + bias_row
            for half in range(2):
                t = got[:, half * PAIR : (half + 1) * PAIR]
                if j < 2:
                    swapped = jnp.where(low_half, pltpu.roll(t, PAIR - HEAD_DIM // 2, 1), pltpu.roll(t, HEAD_DIM // 2, 1))
                    t = t * cos4[b] + swapped * sin4[b]
                qkv[j, b, half] = t.astype(b16)

    plan = {0: [lambda: step_two(3)], 1: [lambda: step_three(2)], 2: [lambda: step_one(5)]}

    @pl.loop(0, streams)
    def _(b):
        at_index(b, plan)
        project(b)

    q_block = stream // 2
    first_head = lane < HEAD_DIM
    top = lax.broadcasted_iota(jnp.int32, (PAIR, 1), 0) < HEAD_DIM
    score_scale = HEAD_DIM**-0.5

    def attend(i):
        b, half = i // 2, i % 2

        @pl.when(half == 0)
        def _():
            far[...] = jnp.where(seg_col[b] == seg_row[b], 0.0, FAR)

        queries, keys = qkv[0, b, half], qkv[1, b, half]
        values_t = qkv[2, b, half].T
        for block in range(2):
            at = slice(block * q_block, (block + 1) * q_block)
            turned = []
            for head in range(2):
                mine = first_head if head == 0 else jnp.logical_not(first_head)
                q = queries[at] * jnp.where(mine, score_scale, 0.0).astype(b16)
                scores = lax.dot_general(keys, q, (((1,), (1,)), ((), ())), preferred_element_type=f32)
                scores = scores + far[:, pl.ds(block * q_block, q_block)]
                most = jnp.max(scores, axis=0, keepdims=True)
                e = jnp.exp(scores - most)
                mass = jnp.sum(e, axis=0, keepdims=True)
                o_lse[i, pl.ds(head, 1), pl.ds(block * q_block, q_block)] = most + jnp.log(mass)
                probs = (e * (1.0 / mass)).astype(b16)
                turned.append(jnp.dot(values_t, probs, preferred_element_type=f32))
            both = jnp.where(top, turned[0], turned[1]).T.astype(b16)
            for cc in range(C):
                head_out[b, half, block, cc] = both[cc * part : (cc + 1) * part]
        for p in range(3):
            att_seq(i, p).start()
        lane_at = pl.multiple_of((s * 2 + half) * PAIR, PAIR)
        att[b, :, pl.ds(lane_at, PAIR)] = head_out[b, half, y, c]

    plan = {
        0: [lambda: step_two(4), lambda: step_three(3)],
        1: [lambda: step_one(6)],
        2: [lambda: step_two(5), lambda: step_three(4)],
        3: [lambda: step_one(7)],
        4: [lambda: step_two(6), lambda: step_three(5)],
        5: [lambda: step_one(8)],
    }

    @pl.loop(0, streams * 2)
    def _(i):
        at_index(i, plan)
        attend(i)

    @pl.loop(0, streams * 2)
    def _(i):
        for p in range(3):
            att_seq(i, p).wait_recv()

    step_two(7)
    step_three(6)
    third(2).wait_recv()
    n_block = 256

    @pl.loop(0, width // n_block)
    def _(n):
        at = pl.ds(pl.multiple_of(n * n_block, n_block), n_block)
        w = g_out[:, :, :, :, :, at].reshape(width, n_block)
        got = jnp.dot(att[...].reshape(rows, width), w, preferred_element_type=f32)
        z_one[:, at] = tok[:, :, at].reshape(rows, n_block).astype(f32) + (got + o_rows[3:4, at])

    step_one(9)
    r_block = 128

    @pl.loop(0, rows // r_block)
    def _(r):
        at = pl.ds(pl.multiple_of(r * r_block, r_block), r_block)
        n, inverse = normal_rows(z_one[at])
        o_n1[at] = n
        o_r1[at] = jnp.broadcast_to(inverse, (r_block, 128))
        h = n * o_rows[7:8] + o_rows[4:5]
        z_one[at] = h
        h_low[at] = h.astype(b16)

    steps = [[lambda: step_two(8), lambda: step_three(7), lambda: step_one(10)], [lambda: step_two(9)], [lambda: step_three(8)], [lambda: step_two(10), lambda: step_three(9)]]
    for j in range(4):
        third(3 + j).wait_recv()

        @pl.loop(0, quarter // n_block)
        def _(n):
            at = pl.ds(pl.multiple_of(n * n_block, n_block), n_block)
            col = pl.ds(pl.multiple_of(j * quarter + n * n_block, n_block), n_block)
            w = g_up[j, :, :, :, :, :, at].reshape(width, n_block)
            u = jnp.dot(h_low[...], w, preferred_element_type=f32) + bias_up[:, col]
            cdf = 0.5 * (1.0 + lax.erf(u * (2.0**-0.5)))
            hid[:, col] = (u * cdf).astype(b16)
            dgelu[:, col] = (cdf + u * (jnp.exp(-0.5 * u * u) * ((2.0 * math.pi) ** -0.5))).astype(b16)

        for call in steps[j]:
            call()
    for j in range(4):
        if j == 0:
            step_three(10)
        third(7 + j).wait_recv()
        at = pl.ds(j * down_cols, down_cols)
        w = g_down[j].reshape(4 * width, down_cols)
        got = jnp.dot(hid[...], w, preferred_element_type=f32) + o_rows[5:6, j * down_cols : (j + 1) * down_cols]
        n_two[:, at] = z_one[:, at] + got

    third(1).wait_recv()

    @pl.loop(0, rows // r_block)
    def _(r):
        at = pl.ds(pl.multiple_of(r * r_block, r_block), r_block)
        n, inverse = normal_rows(n_two[at])
        o_n2[at] = n
        o_r2[at] = jnp.broadcast_to(inverse, (r_block, 128))
        low = (n * o_rows[8:9] + o_rows[6:7]).astype(b16)
        o_nlow[at] = low
        o_res[at] = jnp.dot(low, g_proj[...].reshape(width, wproj.shape[1]), preferred_element_type=f32).astype(b16)

    kept = [(g_out, o_out), (g_up, o_up), (g_down, o_down), (g_proj, o_proj), (g_cols, o_cols), (g_tok, o_tok), (qkv, o_qkv), (att, o_att), (h_low, o_hlow), (hid, o_hid), (dgelu, o_dgelu)]
    copies = [pltpu.make_async_copy(a, b, save.at[i]) for i, (a, b) in enumerate(kept)]
    for copy in copies:
        copy.start()
    for k in range(total):
        for d in range(Z - 1):
            along_z(k, d).wait_send()
        first(k).wait_send()
        second(k).wait_send()
        third(k).wait_send()
    for p in range(3):
        cols_seq(p).wait_send()
    for j in range(3):
        for d in range(Z - 1):
            cols_z(j, d).wait_send()
        cols_x(j).wait_send()
    for b in range(streams):
        tok_y(b).wait_send()
        tok_c(b).wait_send()
        tok_yc(b).wait_send()

    @pl.loop(0, streams * 2)
    def _(i):
        for p in range(3):
            att_seq(i, p).wait_send()

    for copy in copies:
        copy.wait()


def run_forward(tokens, wqkv, wout, wup, wdown, wproj, side, cos4, sin4, seg_col, seg_row):
    streams, part, width = tokens.shape
    rows, stream, ff = streams * part, part * Y * C, wup.shape[1]
    proj = wproj.shape[1]
    cols = width // (Y * C)
    grid = (Z, X, Y, C)
    shape = jax.ShapeDtypeStruct
    vmem, hbm = pl.BlockSpec(memory_space=pltpu.VMEM), pl.BlockSpec(memory_space=pl.ANY)
    kept = [
        (grid + wout.shape, b16),
        ((4,) + grid + (wup.shape[0], ff // 4), b16),
        ((4,) + grid + (wdown.shape[0], width // 4), b16),
        (grid + wproj.shape, b16),
        ((3,) + grid + (wqkv.shape[1], cols), b16),
        ((streams, Y, C, part, width), b16),
        ((3, streams, 2, stream, PAIR), b16),
        ((streams, part, width), b16),
        ((rows, width), b16),
        ((rows, ff), b16),
        ((rows, ff), b16),
    ]
    outs = [
        (kept[0], hbm), (kept[1], hbm), (kept[2], hbm), (kept[3], hbm), (kept[4], hbm),
        (((16, width), f32), vmem),
        (kept[5], hbm), (kept[6], hbm),
        (((streams * 2, 8, stream), f32), vmem),
        (kept[7], hbm),
        (((rows, width), f32), vmem), (((rows, 128), f32), vmem),
        (kept[8], hbm), (kept[9], hbm), (kept[10], hbm),
        (((rows, width), f32), vmem), (((rows, 128), f32), vmem),
        (((rows, width), b16), vmem), (((rows, proj), b16), vmem),
    ]
    v = [pltpu.VMEM(*k) for k in kept]
    dma = pltpu.SemaphoreType.DMA
    scratch = [
        v[0], v[1], v[2], v[3], pltpu.VMEM(grid + side.shape, b16), v[4], v[5], v[6],
        pltpu.VMEM((streams, 2, Y, C, part, PAIR), b16),
        pltpu.VMEM((stream, stream), f32),
        v[7],
        pltpu.VMEM((rows, width), f32),
        v[8], v[9], v[10],
        pltpu.VMEM((rows, width), f32),
        pltpu.VMEM((1, ff), f32),
        dma((11, 6)), dma((11, 6)), dma((3,)), dma((3,)), dma((3, 3)), dma((3, 3)), dma((3,)), dma((3,)),
        dma((streams,)), dma((streams,)), dma((streams, 2)), dma((streams, 2)), dma((streams * 2, 3)), dma((streams * 2, 3)), dma((len(kept),)),
    ]
    return pl.pallas_call(
        forward_kernel,
        out_shape=[shape(*o[0]) for o in outs],
        in_specs=[vmem] * 11,
        out_specs=[o[1] for o in outs],
        scratch_shapes=scratch,
        compiler_params=pltpu.CompilerParams(collective_id=3, has_side_effects=True, vmem_limit_bytes=62 << 20),
    )(tokens, wqkv, wout, wup, wdown, wproj, side, cos4, sin4, seg_col, seg_row)


def pieces(shapes, wide):
    found = []
    for index, (rows, cols) in enumerate(shapes):
        if cols > wide:
            found += [(index, 0, rows, col, wide) for col in range(0, cols, wide)]
        elif rows > 32:
            found += [(index, row, 32, 0, cols) for row in range(0, rows, 32)]
        else:
            found.append((index, 0, rows, 0, cols))
    return found


def scatter_kernel(chunks, count, *refs):
    ins, outs = refs[:count], refs[count : 2 * count]
    total = len(chunks)
    scratch = refs[2 * count :]
    send, recv, local = scratch[0], scratch[1], scratch[2]
    own, from_core, from_one, from_two, from_z = (
        scratch[3 : 3 + total],
        scratch[3 + total : 3 + 2 * total],
        scratch[3 + 2 * total : 3 + 3 * total],
        scratch[3 + 3 * total : 3 + 4 * total],
        scratch[3 + 4 * total : 3 + 5 * total],
    )
    z, x, y, c = place()
    greet([device((z + d) % Z, x, y, c) for d in range(1, Z)] + [device(z, 1 - x, y, c), device(z, x, 1 - y, c), device(z, x, y, 1 - c)])

    def push(k, slot, src, dst, peer):
        return pltpu.make_async_remote_copy(
            src_ref=src,
            dst_ref=dst,
            send_sem=send.at[k, slot],
            recv_sem=recv.at[k, slot],
            device_id=peer,
            device_id_type=MESH,
        )

    def part(chunk, core):
        index, row, rows, col, cols = chunk
        every = slice(None)
        return ins[index].at[every, every, every, core, pl.ds(row, rows), pl.ds(col, cols)]

    def to_core(k):
        return push(k, 5, part(chunks[k], 1 - c), from_core[k], device(z, x, y, 1 - c))

    def load(k):
        return pltpu.make_async_copy(part(chunks[k], c), own[k], local.at[k])

    def first(k):
        if k % 2 == 0:
            return push(k, 4, own[k].at[:, 1 - x], from_one[k], device(z, 1 - x, y, c))
        return push(k, 4, own[k].at[:, :, 1 - y], from_one[k], device(z, x, 1 - y, c))

    def second(k):
        if k % 2 == 0:
            return push(k, 3, own[k].at[:, x, 1 - y], from_two[k], device(z, x, 1 - y, c))
        return push(k, 3, own[k].at[:, 1 - x, y], from_two[k], device(z, 1 - x, y, c))

    def along_z(k, d):
        to = (z + d) % Z
        return push(k, d - 1, own[k].at[to, x, y], from_z[k].at[d - 1], device(to, x, y, c))


    def add_core(k):
        @pl.loop(0, Z * X * Y)
        def _(i):
            a, b, e = i // (X * Y), (i // Y) % X, i % Y
            own[k][a, b, e] = (own[k][a, b, e].astype(f32) + from_core[k][a, b, e].astype(f32)).astype(b16)

    def add_one(k):
        @pl.loop(0, Z * 2)
        def _(i):
            a, b = i // 2, i % 2
            if k % 2 == 0:
                own[k][a, x, b] = (own[k][a, x, b].astype(f32) + from_one[k][a, b].astype(f32)).astype(b16)
            else:
                own[k][a, b, y] = (own[k][a, b, y].astype(f32) + from_one[k][a, b].astype(f32)).astype(b16)

    def add_two(k):
        @pl.loop(0, Z)
        def _(a):
            own[k][a, x, y] = (own[k][a, x, y].astype(f32) + from_two[k][a].astype(f32)).astype(b16)

    def finish(k):
        index, row, rows, col, cols = chunks[k]
        value = own[k][z, x, y].astype(f32)
        for d in range(Z - 1):
            value = value + from_z[k][d].astype(f32)
        outs[index][pl.ds(row, rows), pl.ds(col, cols)] = value

    for k in range(total):
        load(k).start()
        to_core(k).start()
    for step in range(total + 4):
        if step < total:
            load(step).wait()
            to_core(step).wait_recv()
            add_core(step)
            first(step).start()
        k = step - 2
        if 0 <= k < total:
            first(k).wait()
            add_one(k)
            second(k).start()
        k = step - 3
        if 0 <= k < total:
            second(k).wait()
            add_two(k)
            for d in range(1, Z):
                along_z(k, d).start()
        k = step - 4
        if 0 <= k < total:
            for d in range(1, Z):
                along_z(k, d).wait()
            finish(k)
    for k in range(total):
        to_core(k).wait_send()


def scatter_all(partials, collective_id):
    shapes = [(a.shape[0] // 32, a.shape[1]) for a in partials]
    chunks = pieces(shapes, 1024)
    count = len(partials)
    tails = [(rows, cols) for _, _, rows, _, cols in chunks]
    scratch = (
        [pltpu.SemaphoreType.DMA((len(chunks), 6)), pltpu.SemaphoreType.DMA((len(chunks), 6)), pltpu.SemaphoreType.DMA((len(chunks),))]
        + [pltpu.VMEM((Z, X, Y) + t, b16) for t in tails]
        + [pltpu.VMEM((Z, X, Y) + t, b16) for t in tails]
        + [pltpu.VMEM((Z, 2) + t, b16) for t in tails]
        + [pltpu.VMEM((Z,) + t, b16) for t in tails]
        + [pltpu.VMEM((Z - 1,) + t, b16) for t in tails]
    )
    return pl.pallas_call(
        functools.partial(scatter_kernel, chunks, count),
        out_shape=[jax.ShapeDtypeStruct(s, jnp.float32) for s in shapes],
        in_specs=[pl.BlockSpec(memory_space=pl.ANY)] * count,
        out_specs=[pl.BlockSpec(memory_space=pltpu.VMEM)] * count,
        scratch_shapes=scratch,
        compiler_params=pltpu.CompilerParams(
            collective_id=collective_id, has_side_effects=True, vmem_limit_bytes=56 << 20
        ),
    )(*[a.reshape((Z, X, Y, C) + s) for a, s in zip(partials, shapes)])


def layer_norm(field, gain_row, shift_row):
    average = jnp.mean(field, axis=-1, keepdims=True)
    centred = field - average
    variance = jnp.mean(centred * centred, axis=-1, keepdims=True)
    return centred * lax.rsqrt(variance + epsilon) * gain_row + shift_row


def doc_layout(doc_sizes, places):
    doc_ends = jnp.cumsum(doc_sizes)
    passed = places[:, None] >= doc_ends[None, :]
    segment = jnp.sum(passed.astype(jnp.int32), axis=1)
    starts = jnp.sum(jnp.where(passed, doc_sizes[None, :], 0), axis=1)
    return (segment, places - starts)


def rope_tables(position, half_dim):
    steps_f = jnp.arange(half_dim, dtype=jnp.float32)
    inverse = jnp.exp(steps_f * (-math.log(rope_base) / half_dim))
    angle = position.astype(jnp.float32)[:, None] * inverse[None, :]
    return (jnp.cos(angle), jnp.sin(angle))


def rotate(field, cosine, sine_tab, head_count):
    length = field.shape[0]
    halves = field.reshape(length, head_count, 2, -1)
    first_half = halves[:, :, 0]
    second_half = halves[:, :, 1]
    cos_b = cosine[:, None, :]
    sin_b = sine_tab[:, None, :]
    turned = jnp.stack(
        [first_half * cos_b - second_half * sin_b, second_half * cos_b + first_half * sin_b], axis=2
    )
    return turned.reshape(length, -1)


def gelu_exact(field):
    return jax.nn.gelu(field, approximate=False)


def scores_of(query_blk, seg_blk, keys_all, stream_seg, score_scale):
    raw_scores = (
        jnp.einsum("qhd,khd->hqk", query_blk, keys_all, preferred_element_type=jnp.float32)
        * score_scale
    )
    same_doc = (seg_blk[:, None] == stream_seg[None, :])[None]
    return jnp.where(same_doc, raw_scores, neg_fill)


def per_device_any(
    tokens,
    doc_lengths,
    qkv_weight,
    out_weight,
    up_weight,
    down_weight,
    proj_weight,
    biases,
    gains,
    up_bias,
    cotangent,
):
    stream_count = tokens.shape[0]
    seg_rows = tokens.shape[1]
    model_width = tokens.shape[2]
    seq_parts = lax.axis_size("seq")
    stream = seg_rows * seq_parts
    head_count = model_width // HEAD_DIM
    local_heads = head_count // seq_parts
    flat_width = local_heads * HEAD_DIM
    score_scale = HEAD_DIM ** (-0.5)
    tok_flat = tokens.reshape(stream_count * seg_rows, model_width)
    gathered = (
        lax.all_gather(qkv_weight, ("rows", "seq"), axis=0, tiled=True),
        lax.all_gather(out_weight, ("rows", "seq"), axis=0, tiled=True),
        lax.all_gather(up_weight, ("rows", "seq"), axis=0, tiled=True),
        lax.all_gather(down_weight, ("rows", "seq"), axis=0, tiled=True),
        lax.all_gather(proj_weight, ("rows", "seq"), axis=0, tiled=True),
        lax.all_gather(biases, ("rows", "seq"), axis=1, tiled=True),
        lax.all_gather(gains, ("rows", "seq"), axis=1, tiled=True),
        lax.all_gather(up_bias, ("rows", "seq"), axis=0, tiled=True),
    )
    w_qkv, w_out, w_up, w_down, w_proj = (
        gathered[0],
        gathered[1],
        gathered[2],
        gathered[3],
        gathered[4],
    )
    bias_rows = gathered[5].astype(jnp.float32)
    gain_rows = gathered[6].astype(jnp.float32)
    bias_up = gathered[7].astype(jnp.float32)
    token_places = lax.axis_index("seq") * seg_rows + jnp.arange(seg_rows, dtype=jnp.int32)
    layout_rows = jax.vmap(doc_layout, in_axes=(0, None))
    token_seg, position = layout_rows(doc_lengths, token_places)
    cosine, sine_tab = rope_tables(position.reshape(-1), HEAD_DIM // 2)
    projected = jnp.dot(tok_flat, w_qkv, preferred_element_type=jnp.float32) + bias_rows[
        0:3
    ].reshape(-1)
    queries = (
        rotate(projected[:, :model_width], cosine, sine_tab, head_count)
        .astype(jnp.bfloat16)
        .reshape(stream_count, seg_rows, model_width)
    )
    keys_tok = (
        rotate(projected[:, model_width : 2 * model_width], cosine, sine_tab, head_count)
        .astype(jnp.bfloat16)
        .reshape(stream_count, seg_rows, model_width)
    )
    values_tok = (
        projected[:, 2 * model_width :]
        .astype(jnp.bfloat16)
        .reshape(stream_count, seg_rows, model_width)
    )
    queries_h, keys_h, values_h = (
        lax.all_to_all(queries, "seq", split_axis=2, concat_axis=1, tiled=True),
        lax.all_to_all(keys_tok, "seq", split_axis=2, concat_axis=1, tiled=True),
        lax.all_to_all(values_tok, "seq", split_axis=2, concat_axis=1, tiled=True),
    )
    stream_seg, stream_pos = layout_rows(doc_lengths, jnp.arange(stream, dtype=jnp.int32))
    block_rows = math.gcd(stream, 512)
    block_count = stream // block_rows

    def forward_stream(element):
        query_s, key_s, value_s, seg_s = element
        query_blocks = query_s.reshape(block_count, block_rows, local_heads, HEAD_DIM)
        keys_all = key_s.reshape(stream, local_heads, HEAD_DIM)
        values_all = value_s.reshape(stream, local_heads, HEAD_DIM)
        seg_blocks = seg_s.reshape(block_count, block_rows)

        def forward_block(inner):
            query_blk, seg_blk = inner
            scores = scores_of(query_blk, seg_blk, keys_all, seg_s, score_scale)
            row_max = jnp.max(scores, axis=-1, keepdims=True)
            row_total = jnp.sum(jnp.exp(scores - row_max), axis=-1, keepdims=True)
            log_total = row_max + jnp.log(row_total)
            probs_low = jnp.exp(scores - log_total).astype(jnp.bfloat16)
            attn_blk = jnp.einsum(
                "hqk,khd->qhd", probs_low, values_all, preferred_element_type=jnp.float32
            )
            return (attn_blk.astype(jnp.bfloat16), log_total[:, :, 0])

        attn_blocks, log_blocks = lax.map(forward_block, (query_blocks, seg_blocks))
        return (attn_blocks.reshape(stream, flat_width), log_blocks)

    attn_heads, log_totals = lax.map(forward_stream, (queries_h, keys_h, values_h, stream_seg))
    attended = lax.all_to_all(attn_heads, "seq", split_axis=1, concat_axis=2, tiled=True).reshape(
        stream_count * seg_rows, model_width
    )
    branch = jnp.dot(attended, w_out, preferred_element_type=jnp.float32) + bias_rows[3]
    h_one, norm_one = jax.vjp(
        layer_norm, tok_flat.astype(jnp.float32) + branch, gain_rows[0], bias_rows[4]
    )
    h_low = h_one.astype(jnp.bfloat16)
    u_pre = jnp.dot(h_low, w_up, preferred_element_type=jnp.float32) + bias_up
    hidden_f, gelu_back = jax.vjp(gelu_exact, u_pre)
    hidden = hidden_f.astype(jnp.bfloat16)
    ffn_out = jnp.dot(hidden, w_down, preferred_element_type=jnp.float32) + bias_rows[5]
    normed, norm_two = jax.vjp(layer_norm, h_one + ffn_out, gain_rows[1], bias_rows[6])
    normed_low = normed.astype(jnp.bfloat16)
    result = jnp.dot(normed_low, w_proj, preferred_element_type=jnp.float32).astype(jnp.bfloat16)
    w_qkv, w_out, w_up, w_down, w_proj = (
        lax.all_gather(qkv_weight, ("rows", "seq"), axis=0, tiled=True),
        lax.all_gather(out_weight, ("rows", "seq"), axis=0, tiled=True),
        lax.all_gather(up_weight, ("rows", "seq"), axis=0, tiled=True),
        lax.all_gather(down_weight, ("rows", "seq"), axis=0, tiled=True),
        lax.all_gather(proj_weight, ("rows", "seq"), axis=0, tiled=True),
    )
    cot_low = cotangent.reshape(stream_count * seg_rows, -1).astype(jnp.bfloat16)
    proj_part = jnp.dot(normed_low.T, cot_low, preferred_element_type=jnp.float32)
    grad_normed = jnp.dot(cot_low, w_proj.T, preferred_element_type=jnp.float32)
    grad_z2, grad_g2, grad_b2 = norm_two(grad_normed)
    grad_ffn = grad_z2.astype(jnp.bfloat16)
    grad_c2 = jnp.sum(grad_ffn, axis=0, dtype=jnp.float32)
    down_part = jnp.dot(hidden.T, grad_ffn, preferred_element_type=jnp.float32)
    grad_hidden = jnp.dot(grad_ffn, w_down.T, preferred_element_type=jnp.float32)
    grad_u = gelu_back(grad_hidden)[0].astype(jnp.bfloat16)
    grad_c1 = jnp.sum(grad_u, axis=0, dtype=jnp.float32)
    up_part = jnp.dot(h_low.T, grad_u, preferred_element_type=jnp.float32)
    ffn_sums = (up_part, down_part, proj_part, grad_c1)
    grad_h1 = grad_z2 + jnp.dot(grad_u, w_up.T, preferred_element_type=jnp.float32)
    grad_z1, grad_g1, grad_b1 = norm_one(grad_h1)
    grad_branch = grad_z1.astype(jnp.bfloat16)
    grad_bo = jnp.sum(grad_branch, axis=0, dtype=jnp.float32)
    out_part = jnp.dot(attended.T, grad_branch, preferred_element_type=jnp.float32)
    grad_attn = jnp.dot(grad_branch, w_out.T, preferred_element_type=jnp.float32).astype(
        jnp.bfloat16
    )
    grad_heads = lax.all_to_all(
        grad_attn.reshape(stream_count, seg_rows, model_width),
        "seq",
        split_axis=2,
        concat_axis=1,
        tiled=True,
    )

    def backward_stream(element):
        query_s, key_s, value_s, seg_s, log_s, grad_s = element
        query_blocks = query_s.reshape(block_count, block_rows, local_heads, HEAD_DIM)
        keys_all = key_s.reshape(stream, local_heads, HEAD_DIM)
        values_all = value_s.reshape(stream, local_heads, HEAD_DIM)
        seg_blocks = seg_s.reshape(block_count, block_rows)
        grad_blocks = grad_s.reshape(block_count, block_rows, local_heads, HEAD_DIM)

        def backward_block(carried, inner):
            grad_keys, grad_values = carried
            query_blk, seg_blk, log_total, grad_blk = inner
            probs_f = jnp.exp(
                scores_of(query_blk, seg_blk, keys_all, seg_s, score_scale) - log_total[:, :, None]
            )
            grad_values = grad_values + jnp.einsum(
                "hqk,qhd->khd",
                probs_f.astype(jnp.bfloat16),
                grad_blk,
                preferred_element_type=jnp.float32,
            )
            grad_probs = jnp.einsum(
                "qhd,khd->hqk", grad_blk, values_all, preferred_element_type=jnp.float32
            )
            row_dot = jnp.sum(probs_f * grad_probs, axis=-1, keepdims=True)
            grad_scores = (probs_f * (grad_probs - row_dot) * score_scale).astype(jnp.bfloat16)
            grad_query = jnp.einsum(
                "hqk,khd->qhd", grad_scores, keys_all, preferred_element_type=jnp.float32
            )
            grad_keys = grad_keys + jnp.einsum(
                "hqk,qhd->khd", grad_scores, query_blk, preferred_element_type=jnp.float32
            )
            return ((grad_keys, grad_values), grad_query.astype(jnp.bfloat16))

        zero_acc = jnp.zeros((stream, local_heads, HEAD_DIM), jnp.float32)
        (grad_keys, grad_values), grad_queries = lax.scan(
            backward_block, (zero_acc, zero_acc), (query_blocks, seg_blocks, log_s, grad_blocks)
        )
        return (
            grad_queries.reshape(stream, flat_width),
            grad_keys.astype(jnp.bfloat16).reshape(stream, flat_width),
            grad_values.astype(jnp.bfloat16).reshape(stream, flat_width),
        )

    head_q, head_k, head_v = lax.map(
        backward_stream, (queries_h, keys_h, values_h, stream_seg, log_totals, grad_heads)
    )
    back_q, back_k, back_v = (
        lax.all_to_all(head_q, "seq", split_axis=1, concat_axis=2, tiled=True),
        lax.all_to_all(head_k, "seq", split_axis=1, concat_axis=2, tiled=True),
        lax.all_to_all(head_v, "seq", split_axis=1, concat_axis=2, tiled=True),
    )
    flat_rows = stream_count * seg_rows
    turned_q = rotate(
        back_q.reshape(flat_rows, model_width).astype(jnp.float32), cosine, -sine_tab, head_count
    )
    turned_k = rotate(
        back_k.reshape(flat_rows, model_width).astype(jnp.float32), cosine, -sine_tab, head_count
    )
    grad_project = jnp.concatenate(
        [turned_q, turned_k, back_v.reshape(flat_rows, model_width).astype(jnp.float32)], axis=1
    ).astype(jnp.bfloat16)
    grad_bqkv = jnp.sum(grad_project, axis=0, dtype=jnp.float32).reshape(3, model_width)
    qkv_part = jnp.dot(tok_flat.T, grad_project, preferred_element_type=jnp.float32)
    input_grad = grad_z1 + jnp.dot(grad_project, w_qkv.T, preferred_element_type=jnp.float32)
    bias_part = jnp.concatenate(
        [grad_bqkv, jnp.stack([grad_bo, grad_b1, grad_c2, grad_b2])], axis=0
    )
    gain_part = jnp.stack([grad_g1, grad_g2])
    qkv_sum, out_sum, up_sum, down_sum, proj_sum, bias_sum, gain_sum, c1_sum = (
        lax.psum_scatter(qkv_part, ("rows", "seq"), scatter_dimension=0, tiled=True),
        lax.psum_scatter(out_part, ("rows", "seq"), scatter_dimension=0, tiled=True),
        lax.psum_scatter(ffn_sums[0], ("rows", "seq"), scatter_dimension=0, tiled=True),
        lax.psum_scatter(ffn_sums[1], ("rows", "seq"), scatter_dimension=0, tiled=True),
        lax.psum_scatter(ffn_sums[2], ("rows", "seq"), scatter_dimension=0, tiled=True),
        lax.psum_scatter(bias_part, ("rows", "seq"), scatter_dimension=1, tiled=True),
        lax.psum_scatter(gain_part, ("rows", "seq"), scatter_dimension=1, tiled=True),
        lax.psum_scatter(ffn_sums[3], ("rows", "seq"), scatter_dimension=0, tiled=True),
    )
    output = result.reshape(stream_count, seg_rows, -1)
    return (
        output,
        input_grad.reshape(stream_count, seg_rows, model_width),
        qkv_sum,
        out_sum,
        up_sum,
        down_sum,
        proj_sum,
        bias_sum,
        gain_sum,
        c1_sum,
    )


def direct_links():
    return lax.axis_size("rows") == Z * X and lax.axis_size("seq") == Y * C


def norm_back(e, gain, n, inverse):
    ge = e * gain
    mean = jnp.mean(ge, axis=-1, keepdims=True)
    along = jnp.mean(ge * n, axis=-1, keepdims=True)
    return inverse * (ge - mean - n * along), jnp.sum(e * n, axis=0), jnp.sum(e, axis=0)


def turn_tables(doc_lengths, stream):
    stream_seg, stream_pos = jax.vmap(doc_layout, in_axes=(0, None))(doc_lengths, jnp.arange(stream, dtype=jnp.int32))
    cosine, sine = rope_tables(stream_pos.reshape(-1), HEAD_DIM // 2)
    shape = stream_seg.shape + (PAIR,)
    cos4 = jnp.concatenate([cosine] * 4, axis=1).reshape(shape)
    sin4 = jnp.concatenate([-sine, sine, -sine, sine], axis=1).reshape(shape)
    return stream_seg, cos4, sin4


def per_device_direct(
    tokens, doc_lengths, qkv_weight, out_weight, up_weight, down_weight, proj_weight, biases, gains, up_bias, cotangent
):
    streams, part, width = tokens.shape
    rows, stream = streams * part, part * Y * C
    cols = width // (Y * C)
    s = lax.axis_index("seq")
    seg, cos4, sin4 = turn_tables(doc_lengths, stream)
    side = jnp.zeros((16, 128), b16).at[:7, : biases.shape[1]].set(biases).at[7:9, : gains.shape[1]].set(gains).at[9].set(up_bias)
    wqkv = qkv_weight.reshape(-1, 3, width).transpose(1, 0, 2)
    (
        w_out, w_up, w_down, w_proj, w_cols, side_rows, tok_all, qkv, lse, att, n_one, r_one, h_low, hid, dgelu, n_two, r_two, normed_low, result,
    ) = run_forward(
        tokens, wqkv, out_weight, up_weight, down_weight, proj_weight, side, cos4, sin4, seg[:, :, None], seg[:, None, :]
    )
    w_out, w_proj = w_out.reshape(width, width), w_proj.reshape(width, -1)
    w_up, w_down = w_up.reshape(4, width, -1), w_down.reshape(4, -1, width // 4)
    w_cols = w_cols.reshape(3, width, cols)
    cot_low = cotangent.reshape(rows, -1).astype(b16)
    dot = functools.partial(jnp.dot, preferred_element_type=f32)
    proj_part = dot(normed_low.T, cot_low)
    grad_normed = dot(cot_low, w_proj.T)
    grad_z2, grad_g2, grad_b2 = norm_back(grad_normed, side_rows[8], n_two, r_two[:, :1])
    grad_ffn = grad_z2.astype(b16)
    grad_c2 = jnp.sum(grad_ffn, axis=0, dtype=f32)
    down_part = dot(hid.T, grad_ffn)
    grad_hidden = sum(dot(grad_ffn[:, j * cols : (j + 1) * cols], w_down[j].T) for j in range(4))
    grad_u = (grad_hidden * dgelu.astype(f32)).astype(b16)
    grad_c1 = jnp.sum(grad_u, axis=0, dtype=f32)
    up_part = dot(h_low.T, grad_u)
    grad_h1 = grad_z2 + sum(dot(grad_u[:, j * width : (j + 1) * width], w_up[j].T) for j in range(4))
    grad_z1, grad_g1, grad_b1 = norm_back(grad_h1, side_rows[7], n_one, r_one[:, :1])
    grad_branch = grad_z1.astype(b16)
    grad_bo = jnp.sum(grad_branch, axis=0, dtype=f32)
    out_part = dot(att.reshape(rows, width).T, grad_branch)
    grad_attn = dot(grad_branch, w_out.T).astype(b16)
    grad_heads = lax.all_to_all(grad_attn.reshape(streams, part, width), "seq", split_axis=2, concat_axis=1, tiled=True)
    local = cols // HEAD_DIM
    q, k, v = (t.reshape(streams, 2, stream, 2, HEAD_DIM).transpose(0, 2, 1, 3, 4).reshape(streams, stream, local, HEAD_DIM) for t in qkv)
    g = grad_heads.reshape(streams, stream, local, HEAD_DIM)
    logs = lse.reshape(streams, 2, 8, stream)[:, :, :2].reshape(streams, local, stream)
    scale = HEAD_DIM**-0.5
    ein = functools.partial(jnp.einsum, preferred_element_type=f32)
    same = (seg[:, None, :, None] == seg[:, None, None, :])
    scores = jnp.where(same, ein("bqhd,bkhd->bhqk", q, k) * scale, neg_fill)
    probs = jnp.exp(scores - logs[..., None])
    grad_v = ein("bhqk,bqhd->bkhd", probs.astype(b16), g)
    grad_p = ein("bqhd,bkhd->bhqk", g, v)
    row_dot = jnp.sum(probs * grad_p, axis=-1, keepdims=True)
    grad_s = (probs * (grad_p - row_dot) * scale).astype(b16)
    grad_q = ein("bhqk,bkhd->bqhd", grad_s, k)
    grad_k = ein("bhqk,bqhd->bkhd", grad_s, q)

    def back(t):
        t = t.astype(b16).astype(f32).reshape(streams * stream, local, HEAD_DIM)
        return rotate(t.reshape(streams * stream, -1), cos4.reshape(-1, PAIR)[:, :32], -sin4.reshape(-1, PAIR)[:, 32:64], local)

    grad_project = jnp.concatenate([back(grad_q), back(grad_k), grad_v.astype(b16).astype(f32).reshape(streams * stream, -1)], axis=1).astype(b16)
    own_bias = jnp.sum(grad_project, axis=0, dtype=f32).reshape(3, cols)
    grad_bqkv = lax.dynamic_update_slice(jnp.zeros((3, width), f32), own_bias, (0, s * cols))
    qkv_part = dot(tok_all.reshape(streams * stream, width).T, grad_project)
    qkv_rows = lax.psum_scatter(qkv_part, "rows", scatter_dimension=0, tiled=True)
    qkv_sum = lax.all_to_all(qkv_rows.reshape(-1, 3, cols), "seq", split_axis=0, concat_axis=2, tiled=True).reshape(-1, 3 * width)
    back_rows = sum(dot(grad_project[:, j * cols : (j + 1) * cols], w_cols[j].T) for j in range(3))
    input_grad = grad_z1.reshape(streams, part, width) + lax.psum_scatter(
        back_rows.reshape(streams, stream, width), "seq", scatter_dimension=1, tiled=True
    )
    bias_part = jnp.concatenate([grad_bqkv, jnp.stack([grad_bo, grad_b1, grad_c2, grad_b2])], axis=0)
    gain_part = jnp.stack([grad_g1, grad_g2])
    lanes = width // OWNERS
    side_part = jnp.concatenate([bias_part, gain_part], axis=0).reshape(9, OWNERS, lanes).transpose(1, 0, 2)
    side_part = jnp.zeros((OWNERS, 16, 128), f32).at[:, :9, :lanes].set(side_part).at[:, 9].set(grad_c1.reshape(OWNERS, 128)).reshape(OWNERS * 16, 128)
    side_sum, proj_sum, down_sum, up_sum, out_sum = scatter_all([a.astype(b16) for a in (side_part, proj_part, down_part, up_part, out_part)], 2)
    return (
        result.reshape(streams, part, -1),
        input_grad,
        qkv_sum,
        out_sum,
        up_sum,
        down_sum,
        proj_sum,
        side_sum[:7, :lanes],
        side_sum[7:9, :lanes],
        side_sum[9],
    )


def per_device(*args):
    return per_device_direct(*args) if direct_links() else per_device_any(*args)


def solution(mesh):
    in_specs = (
        P("rows", "seq", None),
        P("rows", None),
        P(("rows", "seq"), None),
        P(("rows", "seq"), None),
        P(("rows", "seq"), None),
        P(("rows", "seq"), None),
        P(("rows", "seq"), None),
        P(None, ("rows", "seq")),
        P(None, ("rows", "seq")),
        P(("rows", "seq")),
        P("rows", "seq", None),
    )
    out_specs = (
        P("rows", "seq", None),
        P("rows", "seq", None),
        P(("rows", "seq"), None),
        P(("rows", "seq"), None),
        P(("rows", "seq"), None),
        P(("rows", "seq"), None),
        P(("rows", "seq"), None),
        P(None, ("rows", "seq")),
        P(None, ("rows", "seq")),
        P(("rows", "seq")),
    )
    return jax.shard_map(
        per_device, mesh=mesh, in_specs=in_specs, out_specs=out_specs, check_vma=False
    )
```

```python
import math

import jax
import jax.numpy as jnp
from jax import lax
from jax.experimental import pallas as pl
from jax.experimental.pallas import tpu as pltpu
from jax.sharding import PartitionSpec as P

epsilon = 1e-05
rope_base = 10000.0
neg_fill = -1e30

HEAD_DIM = 64
PAIR = 2 * HEAD_DIM
MESH = pl.DeviceIdType.MESH
Z, X, Y, C = 4, 2, 2, 2
OWNERS = Z * X * Y * C
f32, b16 = jnp.float32, jnp.bfloat16
FAR = -1e30


def place():
    r, s = lax.axis_index("rows"), lax.axis_index("seq")
    return r // X, r % X, s // C, s % C


def device(z, x, y, c):
    return (z * X + x, y * C + c)


def greet(peers):
    barrier = pltpu.get_barrier_semaphore()
    for peer in peers:
        pl.semaphore_signal(barrier, inc=1, device_id=peer, device_id_type=MESH)
    pl.semaphore_wait(barrier, len(peers))


def send_to(src, dst, send, recv, peer):
    return pltpu.make_async_remote_copy(
        src_ref=src, dst_ref=dst, send_sem=send, recv_sem=recv, device_id=peer, device_id_type=MESH
    )


def normal_rows(field):
    average = jnp.mean(field, axis=-1, keepdims=True)
    centred = field - average
    inverse = lax.rsqrt(jnp.mean(centred * centred, axis=-1, keepdims=True) + epsilon)
    return centred * inverse, inverse


def at_index(index, plan):
    for spot, calls in plan.items():
        if calls:

            @pl.when(index == spot)
            def _(calls=calls):
                for call in calls:
                    call()


def forward_kernel(
    tok, wqkv, wout, wup, wdown, wproj, side, cos4, sin4, seg_col, seg_row,
    o_out, o_up, o_down, o_proj, o_cols, o_rows, o_tok_t, o_qkv, o_lse, o_att_t, o_n1, o_r1, o_hlow_t, o_hid_t, o_dgelu, o_n2, o_r2, o_nlow_t, o_res,
    g_out, g_up, g_down, g_proj, g_side, g_cols, g_tok, tok_t, qkv, head_out, far, att, att_t, z_one, n_one, h_low, h_low_t, hid, hid_t, dgelu, n_two, bias_up,
    c_send, c_recv, a_send, a_recv, wz_send, wz_recv, wx_send, wx_recv, y_send, y_recv, k_send, k_recv, t_send, t_recv, save,
):
    streams, part, width = tok.shape
    rows = streams * part
    z, x, y, c = place()
    s = y * C + c
    seq_peer = [(y, 1 - c), (1 - y, c), (1 - y, 1 - c)]
    others = [(z + d) % Z for d in range(1, Z)]
    greet(
        [device(zz, x, y, c) for zz in others]
        + [device(z, 1 - x, y, c)]
        + [device(z, x, yy, cc) for yy, cc in seq_peer]
    )

    every = slice(None)
    sources, targets = [side, wproj, wout], [g_side, g_proj, g_out]
    quarter = width
    for j in range(4):
        sources.append(wup.at[:, pl.ds(j * quarter, quarter)])
        targets.append(g_up.at[j])
    down_cols = width // 4
    for j in range(4):
        sources.append(wdown.at[:, pl.ds(j * down_cols, down_cols)])
        targets.append(g_down.at[j])
    total = len(sources)

    def along_z(k, d):
        return send_to(sources[k], targets[k].at[z, x, y, c], c_send.at[k, d], c_recv.at[k, d], device(others[d], x, y, c))

    def first(k):
        slab = targets[k].at[:, x, y, c]
        peer = device(z, 1 - x, y, c) if k % 2 else device(z, x, 1 - y, c)
        return send_to(slab, slab, c_send.at[k, 3], c_recv.at[k, 3], peer)

    def second(k):
        if k % 2:
            slab, peer = targets[k].at[:, :, y, c], device(z, x, 1 - y, c)
        else:
            slab, peer = targets[k].at[:, x, :, c], device(z, 1 - x, y, c)
        return send_to(slab, slab, c_send.at[k, 4], c_recv.at[k, 4], peer)

    def third(k):
        slab = targets[k].at[:, :, :, c]
        return send_to(slab, slab, c_send.at[k, 5], c_recv.at[k, 5], device(z, x, y, 1 - c))

    def step_one(k):
        for d in range(Z - 1):
            along_z(k, d).wait_recv()
        first(k).start()

    def step_two(k):
        first(k).wait_recv()
        second(k).start()

    def step_three(k):
        second(k).wait_recv()
        third(k).start()

    cols = wqkv.shape[2] // (Y * C)

    def cols_seq(p):
        yy, cc = seq_peer[p]
        src = wqkv.at[:, :, pl.ds(pl.multiple_of((yy * C + cc) * cols, 128), cols)]
        return send_to(src, g_cols.at[:, z, x, y, c], a_send.at[p], a_recv.at[p], device(z, x, yy, cc))

    def cols_z(j, d):
        slab = g_cols.at[j, z, x]
        return send_to(slab, slab, wz_send.at[j, d], wz_recv.at[j, d], device(others[d], x, y, c))

    def cols_x(j):
        slab = g_cols.at[j, :, x]
        return send_to(slab, slab, wx_send.at[j], wx_recv.at[j], device(z, 1 - x, y, c))

    def tok_y(b):
        return send_to(tok.at[b], g_tok.at[b, y, c], y_send.at[b], y_recv.at[b], device(z, x, 1 - y, c))

    def tok_c(b):
        return send_to(tok.at[b], g_tok.at[b, y, c], k_send.at[b, 0], k_recv.at[b, 0], device(z, x, y, 1 - c))

    def tok_yc(b):
        slab = g_tok.at[b, 1 - y, c]
        return send_to(slab, slab, k_send.at[b, 1], k_recv.at[b, 1], device(z, x, y, 1 - c))

    def att_seq(i, p):
        b, half = i // 2, i % 2
        yy, cc = seq_peer[p]
        src = head_out.at[b, half, yy, cc]
        lane = pl.multiple_of((s * 2 + half) * PAIR, PAIR)
        return send_to(src, att.at[b, :, pl.ds(lane, PAIR)], t_send.at[i, p], t_recv.at[i, p], device(z, x, yy, cc))

    for p in range(3):
        cols_seq(p).start()
    for b in range(streams):
        tok_y(b).start()
    for k in range(4):
        for d in range(Z - 1):
            along_z(k, d).start()
    for b in range(streams):
        tok_c(b).start()
    g_cols[:, z, x, y, c] = wqkv[:, :, pl.ds(pl.multiple_of(s * cols, 128), cols)]
    for b in range(streams):
        g_tok[b, y, c] = tok[b]
    for k in range(total):
        targets[k][z, x, y, c] = sources[k][...]
    for p in range(3):
        cols_seq(p).wait_recv()
    for j in range(3):
        for d in range(Z - 1):
            cols_z(j, d).start()
    for k in range(4, total):
        for d in range(Z - 1):
            along_z(k, d).start()

    step_one(0)
    step_one(1)
    step_one(2)
    step_two(0)
    tok_y(0).wait_recv()
    tok_yc(0).start()
    step_two(1)
    step_three(0)
    step_one(3)
    tok_y(1).wait_recv()
    tok_yc(1).start()
    for j in range(3):
        for d in range(Z - 1):
            cols_z(j, d).wait_recv()
        cols_x(j).start()
    step_two(2)
    tok_y(2).wait_recv()
    tok_yc(2).start()
    step_one(4)
    step_three(1)
    third(0).wait_recv()

    lanes = lax.broadcasted_iota(jnp.int32, (16, 128), 1)
    share = 128 // (Y * C)
    for zx in range(Z * X):
        tile = jnp.zeros((16, 128), f32)
        for yc in range(Y * C):
            block = g_side[zx // X, zx % X, yc // C, yc % C].astype(f32)
            bias_up[:, pl.ds((zx * Y * C + yc) * 128, 128)] = block[9:10]
            tile = tile + pltpu.roll(jnp.where(lanes < share, block, 0.0), yc * share, 1)
        o_rows[:, pl.ds(zx * 128, 128)] = tile

    lane = lax.broadcasted_iota(jnp.int32, (1, 128), 1)
    low_half = (lane % HEAD_DIM) < HEAD_DIM // 2
    for j in range(3):
        cols_x(j).wait_recv()
    for b in range(streams):
        tok_c(b).wait_recv()
        tok_yc(b).wait_recv()
    stream = part * Y * C

    def project(b):
        rows_b = g_tok[b].reshape(stream, width)
        tok_t[b] = rows_b.T
        for j in range(3):
            bias_row = o_rows[pl.ds(j, 1), pl.ds(pl.multiple_of(s * cols, 128), cols)]
            got = jnp.dot(rows_b, g_cols[j].reshape(width, cols), preferred_element_type=f32) + bias_row
            for half in range(2):
                t = got[:, half * PAIR : (half + 1) * PAIR]
                if j < 2:
                    swapped = jnp.where(low_half, pltpu.roll(t, PAIR - HEAD_DIM // 2, 1), pltpu.roll(t, HEAD_DIM // 2, 1))
                    t = t * cos4[b] + swapped * sin4[b]
                qkv[j, b, half] = t.astype(b16)

    plan = {0: [lambda: step_two(3)], 1: [lambda: step_three(2)], 2: [lambda: step_one(5)]}

    @pl.loop(0, streams)
    def _(b):
        at_index(b, plan)
        project(b)

    q_block = stream // 2
    first_head = lane < HEAD_DIM
    top = lax.broadcasted_iota(jnp.int32, (PAIR, 1), 0) < HEAD_DIM
    score_scale = HEAD_DIM**-0.5

    def attend(i):
        b, half = i // 2, i % 2

        @pl.when(half == 0)
        def _():
            far[...] = jnp.where(seg_col[b] == seg_row[b], 0.0, FAR)

        queries, keys = qkv[0, b, half], qkv[1, b, half]
        values_t = qkv[2, b, half].T
        for block in range(2):
            at = slice(block * q_block, (block + 1) * q_block)
            turned = []
            for head in range(2):
                mine = first_head if head == 0 else jnp.logical_not(first_head)
                q = queries[at] * jnp.where(mine, score_scale, 0.0).astype(b16)
                scores = lax.dot_general(keys, q, (((1,), (1,)), ((), ())), preferred_element_type=f32)
                scores = scores + far[:, pl.ds(block * q_block, q_block)]
                most = jnp.max(scores, axis=0, keepdims=True)
                e = jnp.exp(scores - most)
                mass = jnp.sum(e, axis=0, keepdims=True)
                o_lse[i, pl.ds(head, 1), pl.ds(block * q_block, q_block)] = most + jnp.log(mass)
                probs = (e * (1.0 / mass)).astype(b16)
                turned.append(jnp.dot(values_t, probs, preferred_element_type=f32))
            both = jnp.where(top, turned[0], turned[1]).T.astype(b16)
            for cc in range(C):
                head_out[b, half, block, cc] = both[cc * part : (cc + 1) * part]
        for p in range(3):
            att_seq(i, p).start()
        lane_at = pl.multiple_of((s * 2 + half) * PAIR, PAIR)
        att[b, :, pl.ds(lane_at, PAIR)] = head_out[b, half, y, c]

    plan = {
        0: [lambda: step_two(4), lambda: step_three(3)],
        1: [lambda: step_one(6)],
        2: [lambda: step_two(5), lambda: step_three(4)],
        3: [lambda: step_one(7)],
        4: [lambda: step_two(6), lambda: step_three(5)],
        5: [lambda: step_one(8)],
    }

    @pl.loop(0, streams * 2)
    def _(i):
        at_index(i, plan)
        attend(i)

    @pl.loop(0, streams * 2)
    def _(i):
        for p in range(3):
            att_seq(i, p).wait_recv()

    step_two(7)
    step_three(6)
    third(2).wait_recv()
    n_block = 256

    @pl.loop(0, width // n_block)
    def _(n):
        at = pl.ds(pl.multiple_of(n * n_block, n_block), n_block)
        w = g_out[:, :, :, :, :, at].reshape(width, n_block)
        got = jnp.dot(att[...].reshape(rows, width), w, preferred_element_type=f32)
        z_one[:, at] = tok[:, :, at].reshape(rows, n_block).astype(f32) + (got + o_rows[3:4, at])

    step_one(9)
    r_block = 128

    @pl.loop(0, rows // r_block)
    def _(r):
        at = pl.ds(pl.multiple_of(r * r_block, r_block), r_block)
        n, inverse = normal_rows(z_one[at])
        n_one[at] = n
        o_r1[at] = jnp.broadcast_to(inverse, (r_block, 128))
        h = n * o_rows[7:8] + o_rows[4:5]
        z_one[at] = h
        h_low[at] = h.astype(b16)
        h_low_t[:, at] = h.astype(b16).T
        att_t[:, at] = att[r].T

    steps = [[lambda: step_two(8), lambda: step_three(7), lambda: step_one(10)], [lambda: step_two(9)], [lambda: step_three(8)], [lambda: step_two(10), lambda: step_three(9)]]
    for j in range(4):
        third(3 + j).wait_recv()

        @pl.loop(0, quarter // n_block)
        def _(n):
            at = pl.ds(pl.multiple_of(n * n_block, n_block), n_block)
            col = pl.ds(pl.multiple_of(j * quarter + n * n_block, n_block), n_block)
            w = g_up[j, :, :, :, :, :, at].reshape(width, n_block)
            u = jnp.dot(h_low[...], w, preferred_element_type=f32) + bias_up[:, col]
            cdf = 0.5 * (1.0 + lax.erf(u * (2.0**-0.5)))
            low = (u * cdf).astype(b16)
            hid[:, col] = low
            hid_t[col, :] = low.T
            dgelu[:, col] = (cdf + u * (jnp.exp(-0.5 * u * u) * ((2.0 * math.pi) ** -0.5))).astype(b16)

        for call in steps[j]:
            call()
    for j in range(4):
        if j == 0:
            step_three(10)
        third(7 + j).wait_recv()
        at = pl.ds(j * down_cols, down_cols)
        w = g_down[j].reshape(4 * width, down_cols)
        got = jnp.dot(hid[...], w, preferred_element_type=f32) + o_rows[5:6, j * down_cols : (j + 1) * down_cols]
        n_two[:, at] = z_one[:, at] + got

    third(1).wait_recv()

    @pl.loop(0, rows // r_block)
    def _(r):
        at = pl.ds(pl.multiple_of(r * r_block, r_block), r_block)
        n, inverse = normal_rows(n_two[at])
        n_two[at] = n
        o_r2[at] = jnp.broadcast_to(inverse, (r_block, 128))
        low = (n * o_rows[8:9] + o_rows[6:7]).astype(b16)
        o_nlow_t[:, at] = low.T
        o_res[at] = jnp.dot(low, g_proj[...].reshape(width, wproj.shape[1]), preferred_element_type=f32).astype(b16)

    kept = [(g_out, o_out), (g_up, o_up), (g_proj, o_proj), (tok_t, o_tok_t), (qkv, o_qkv), (att_t, o_att_t), (n_one, o_n1), (h_low_t, o_hlow_t), (hid_t, o_hid_t), (dgelu, o_dgelu), (n_two, o_n2)]
    kept += [(g_down.at[j], o_down.at[:, :, :, :, :, pl.ds(j * down_cols, down_cols)]) for j in range(4)]
    kept += [
        (g_cols.at[j, :, :, :, :, :, pl.ds(half * PAIR, PAIR)], o_cols.at[half, :, :, :, :, :, pl.ds(j * PAIR, PAIR)])
        for j in range(3)
        for half in range(2)
    ]
    copies = [pltpu.make_async_copy(a, b, save.at[i]) for i, (a, b) in enumerate(kept)]
    for copy in copies:
        copy.start()
    for k in range(total):
        for d in range(Z - 1):
            along_z(k, d).wait_send()
        first(k).wait_send()
        second(k).wait_send()
        third(k).wait_send()
    for p in range(3):
        cols_seq(p).wait_send()
    for j in range(3):
        for d in range(Z - 1):
            cols_z(j, d).wait_send()
        cols_x(j).wait_send()
    for b in range(streams):
        tok_y(b).wait_send()
        tok_c(b).wait_send()
        tok_yc(b).wait_send()

    @pl.loop(0, streams * 2)
    def _(i):
        for p in range(3):
            att_seq(i, p).wait_send()

    for copy in copies:
        copy.wait()


def run_forward(tokens, wqkv, wout, wup, wdown, wproj, side, cos4, sin4, seg_col, seg_row):
    streams, part, width = tokens.shape
    rows, stream, ff = streams * part, part * Y * C, wup.shape[1]
    proj = wproj.shape[1]
    cols = width // (Y * C)
    grid = (Z, X, Y, C)
    shape = jax.ShapeDtypeStruct
    vmem, hbm = pl.BlockSpec(memory_space=pltpu.VMEM), pl.BlockSpec(memory_space=pl.ANY)
    vm = pltpu.VMEM
    outs = [
        ((grid + wout.shape, b16), hbm),
        (((4,) + grid + (wup.shape[0], ff // 4), b16), hbm),
        ((grid + wdown.shape, b16), hbm),
        ((grid + wproj.shape, b16), hbm),
        (((2,) + grid + (wqkv.shape[1], 3 * PAIR), b16), hbm),
        (((16, width), f32), vmem),
        (((streams, width, stream), b16), hbm),
        (((3, streams, 2, stream, PAIR), b16), hbm),
        (((streams * 2, 8, stream), f32), vmem),
        (((width, rows), b16), hbm),
        (((rows, width), f32), hbm),
        (((rows, 128), f32), vmem),
        (((width, rows), b16), hbm),
        (((ff, rows), b16), hbm),
        (((rows, ff), b16), hbm),
        (((rows, width), f32), hbm),
        (((rows, 128), f32), vmem),
        (((width, rows), b16), vmem),
        (((rows, proj), b16), vmem),
    ]
    dma = pltpu.SemaphoreType.DMA
    scratch = [
        vm(grid + wout.shape, b16),
        vm((4,) + grid + (wup.shape[0], ff // 4), b16),
        vm((4,) + grid + (wdown.shape[0], width // 4), b16),
        vm(grid + wproj.shape, b16),
        vm(grid + side.shape, b16),
        vm((3,) + grid + (wqkv.shape[1], cols), b16),
        vm((streams, Y, C, part, width), b16),
        vm((streams, width, stream), b16),
        vm((3, streams, 2, stream, PAIR), b16),
        vm((streams, 2, Y, C, part, PAIR), b16),
        vm((stream, stream), f32),
        vm((streams, part, width), b16),
        vm((width, rows), b16),
        vm((rows, width), f32),
        vm((rows, width), f32),
        vm((rows, width), b16),
        vm((width, rows), b16),
        vm((rows, ff), b16),
        vm((ff, rows), b16),
        vm((rows, ff), b16),
        vm((rows, width), f32),
        vm((1, ff), f32),
        dma((11, 6)), dma((11, 6)), dma((3,)), dma((3,)), dma((3, 3)), dma((3, 3)), dma((3,)), dma((3,)),
        dma((streams,)), dma((streams,)), dma((streams, 2)), dma((streams, 2)), dma((streams * 2, 3)), dma((streams * 2, 3)), dma((21,)),
    ]
    return pl.pallas_call(
        forward_kernel,
        out_shape=[shape(*o[0]) for o in outs],
        in_specs=[vmem] * 11,
        out_specs=[o[1] for o in outs],
        scratch_shapes=scratch,
        compiler_params=pltpu.CompilerParams(collective_id=3, has_side_effects=True, vmem_limit_bytes=62 << 20),
    )(tokens, wqkv, wout, wup, wdown, wproj, side, cos4, sin4, seg_col, seg_row)


def turned_back(t, cosine, sine, low_half):
    swapped = jnp.where(low_half, pltpu.roll(t, PAIR - HEAD_DIM // 2, 1), pltpu.roll(t, HEAD_DIM // 2, 1))
    return t * cosine - swapped * sine


def backward_kernel(
    w_out, w_up, w_down, w_proj, w_cols, side_rows, i_tok_t, i_qkv, lse, i_att_t, i_n1, r_one, i_hlow_t, i_hid_t, i_dgelu, i_n2, r_two, nlow_t,
    cot, cos4, sin4, seg_col, seg_row,
    o_in, o_qkv, o_out, o_up, o_down, o_proj, o_side,
    ring, gelu_ring, norm, att_t, h_low_t, hid_t, qkv, cols_one, sums, sum_up, grad_ffn, grad_u, grad_branch, grad_att, heads, far, turned,
    send_d, send_u, send_o, send_p, send_s, in_d, in_u, in_o, in_p, in_s,
    one_d, one_u, one_o, one_p, one_s, two_d, two_u, two_o, two_p, two_s, z_d, z_u, z_o, z_p, z_s,
    q_send, q_x, q_z, q_seq, q_in, i_send, i_c, i_y_send, i_y,
    c_send, c_recv, a_send, a_recv, qx_send, qx_recv, qz_send, qz_recv, qs_send, qs_recv, ic_send, ic_recv, iy_send, iy_recv,
    load, ring_sem, gelu_sem,
):
    rows, width = o_in.shape
    streams = qkv.shape[1]
    part, stream = rows // streams, qkv.shape[3]
    ff = grad_u.shape[1]
    quarter, down_cols = ff // 4, width // 4
    cols = width // (Y * C)
    block = 256
    r_block = 128
    z, x, y, c = place()
    s = y * C + c
    seq_peer = [(y, 1 - c), (1 - y, c), (1 - y, 1 - c)]
    others = [(z + d) % Z for d in range(1, Z)]
    nt = (((1,), (1,)), ((), ()))

    def fetch(src, dst, i):
        return pltpu.make_async_copy(src, dst, load.at[i])

    first_loads = [fetch(i_n2, norm, 0), fetch(i_hid_t, hid_t, 1), fetch(i_hlow_t, h_low_t, 2), fetch(i_att_t, att_t, 3), fetch(i_qkv, qkv, 4)]
    second_norm = fetch(i_n1, norm, 5)
    tok_loads = [fetch(i_tok_t.at[b], ring.at[b // 2, :, pl.ds((b % 2) * stream, stream)], 6 + b) for b in range(streams)]
    col_loads = [fetch(w_cols.at[0], ring.at[1, :, pl.ds(stream, 3 * PAIR)], 6 + streams), fetch(w_cols.at[1], cols_one, 7 + streams)]
    blocks = []
    for j in range(4):
        blocks += [w_down.at[pl.ds(j * quarter, quarter)], w_up.at[j]]
    blocks.append(w_out)

    def stream_in(i):
        return pltpu.make_async_copy(blocks[i], ring.at[i % 2], ring_sem.at[i])

    def gelu_in(j):
        return pltpu.make_async_copy(i_dgelu.at[:, pl.ds(j * quarter, quarter)], gelu_ring.at[j % 2], gelu_sem.at[j])

    first_loads[0].start()
    stream_in(0).start()
    gelu_in(0).start()
    stream_in(1).start()
    gelu_in(1).start()
    for copy in first_loads[1:]:
        copy.start()
    greet(
        [device(zz, x, y, c) for zz in others]
        + [device(z, 1 - x, y, c)]
        + [device(z, x, yy, cc) for yy, cc in seq_peer]
    )

    outgoing = [send_d.at[j % 2] for j in range(4)] + [send_u.at[j % 2] for j in range(4)] + [send_o, send_p, send_s.at[:, :, :, 1 - c]]
    held = [in_d.at[j] for j in range(4)] + [in_u.at[j] for j in range(4)] + [in_o, in_p, in_s]
    from_one = [one_d.at[j] for j in range(4)] + [one_u.at[j] for j in range(4)] + [one_o, one_p, one_s]
    from_two = [two_d.at[j] for j in range(4)] + [two_u.at[j] for j in range(4)] + [two_o, two_p, two_s]
    from_z = [z_d.at[j] for j in range(4)] + [z_u.at[j] for j in range(4)] + [z_o, z_p, z_s]
    total = len(held)

    def to_core(k):
        return send_to(outgoing[k], held[k], c_send.at[k, 5], c_recv.at[k, 5], device(z, x, y, 1 - c))

    def first(k):
        if k % 2 == 0:
            return send_to(held[k].at[:, 1 - x], from_one[k], c_send.at[k, 4], c_recv.at[k, 4], device(z, 1 - x, y, c))
        return send_to(held[k].at[:, :, 1 - y], from_one[k], c_send.at[k, 4], c_recv.at[k, 4], device(z, x, 1 - y, c))

    def second(k):
        if k % 2 == 0:
            return send_to(held[k].at[:, x, 1 - y], from_two[k], c_send.at[k, 3], c_recv.at[k, 3], device(z, x, 1 - y, c))
        return send_to(held[k].at[:, 1 - x, y], from_two[k], c_send.at[k, 3], c_recv.at[k, 3], device(z, 1 - x, y, c))

    def along_z(k, d):
        src, dst = held[k].at[others[d], x, y], from_z[k].at[d]
        return send_to(src, dst, c_send.at[k, d], c_recv.at[k, d], device(others[d], x, y, c))

    def half_down(j, core, zz):
        a = hid_t[zz, :, :, core].reshape(-1, rows)
        return jnp.dot(a, grad_ffn[:, j * down_cols : (j + 1) * down_cols], preferred_element_type=f32)

    def half_rows(a_t, core, b, at):
        return jnp.dot(a_t[:, :, :, core].reshape(-1, rows), b[:, at], preferred_element_type=f32)

    def make_send(k):
        if k < 4:

            @pl.loop(0, Z)
            def _(zz):
                send_d[k % 2, zz] = half_down(k, 1 - c, zz).astype(b16).reshape(X, Y, -1, down_cols)

        elif k < 9:
            a_t, b = (h_low_t, grad_u) if k < 8 else (att_t, grad_branch)

            @pl.loop(0, width // block)
            def _(n):
                at = pl.ds(pl.multiple_of(n * block, block), block)
                col = pl.ds(pl.multiple_of(((k - 4) * quarter if k < 8 else 0) + n * block, block), block)
                got = half_rows(a_t, 1 - c, b, col).astype(b16).reshape(Z, X, Y, -1, block)
                if k < 8:
                    send_u[k % 2, :, :, :, :, at] = got
                else:
                    send_o[:, :, :, :, at] = got

        elif k == 9:
            send_p[...] = half_rows(nlow_t, 1 - c, cot, slice(None)).astype(b16).reshape(Z, X, Y, -1, cot.shape[1])
        to_core(k).start()

    def step_one(k):
        to_core(k).wait_recv()
        if k < 4:

            @pl.loop(0, Z)
            def _(zz):
                got = half_down(k, c, zz).reshape(X, Y, -1, down_cols)
                in_d[k, zz] = (in_d[k, zz].astype(f32) + got).astype(b16)

        elif k < 9:
            a_t, b = (h_low_t, grad_u) if k < 8 else (att_t, grad_branch)

            @pl.loop(0, width // block)
            def _(n):
                at = pl.ds(pl.multiple_of(n * block, block), block)
                col = pl.ds(pl.multiple_of(((k - 4) * quarter if k < 8 else 0) + n * block, block), block)
                got = half_rows(a_t, c, b, col).reshape(Z, X, Y, -1, block)
                if k < 8:
                    in_u[k - 4, :, :, :, :, at] = (in_u[k - 4, :, :, :, :, at].astype(f32) + got).astype(b16)
                else:
                    in_o[:, :, :, :, at] = (in_o[:, :, :, :, at].astype(f32) + got).astype(b16)

        elif k == 9:
            got = half_rows(nlow_t, c, cot, slice(None)).reshape(Z, X, Y, -1, cot.shape[1])
            in_p[...] = (in_p[...].astype(f32) + got).astype(b16)
        else:
            in_s[...] = (in_s[...].astype(f32) + send_s[:, :, :, c].astype(f32)).astype(b16)
        first(k).start()

    def step_two(k):
        first(k).wait_recv()

        @pl.loop(0, Z)
        def _(zz):
            for i in range(2):
                spot = (zz, x, i) if k % 2 == 0 else (zz, i, y)
                held[k][spot] = (held[k][spot].astype(f32) + from_one[k][zz, i].astype(f32)).astype(b16)

        second(k).start()

    def step_three(k):
        second(k).wait_recv()

        @pl.loop(0, Z)
        def _(zz):
            held[k][zz, x, y] = (held[k][zz, x, y].astype(f32) + from_two[k][zz].astype(f32)).astype(b16)

        for d in range(Z - 1):
            along_z(k, d).start()

    def step_four(k):
        value = held[k][z, x, y].astype(f32)
        for d in range(Z - 1):
            along_z(k, d).wait_recv()
        for d in range(Z - 1):
            value = value + from_z[k][d].astype(f32)
        if k < 4:
            o_down[:, k * down_cols : (k + 1) * down_cols] = value
        elif k < 8:
            o_up[:, (k - 4) * quarter : (k - 3) * quarter] = value
        else:
            (o_out, o_proj, o_side)[k - 8][...] = value

    sums[...] = jnp.zeros_like(sums)

    def norm_back(e, gain_row, n, inverse, at, low_ref, spots):
        ge = e * side_rows[gain_row : gain_row + 1]
        mean = jnp.mean(ge, axis=-1, keepdims=True)
        along = jnp.mean(ge * n, axis=-1, keepdims=True)
        grad = inverse * (ge - mean - n * along)
        low = grad.astype(b16)
        o_in[at] = grad
        low_ref[at] = low
        for spot, value in zip(spots, (e * n, e, low.astype(f32))):
            sums[spot : spot + 1] += jnp.sum(value, axis=0, keepdims=True)

    first_loads[0].wait()

    @pl.loop(0, rows // r_block)
    def _(r):
        at = pl.ds(pl.multiple_of(r * r_block, r_block), r_block)
        e = lax.dot_general(cot[at], w_proj[...], nt, preferred_element_type=f32)
        norm_back(e, 8, norm[at], r_two[at, :1], at, grad_ffn, (8, 6, 5))

    second_norm.start()
    first_loads[1].wait()
    make_send(0)
    make_send(1)
    for j in range(4):
        stream_in(2 * j).wait()
        gelu_in(j).wait()

        @pl.loop(0, quarter // block)
        def _(n):
            at = pl.ds(pl.multiple_of(n * block, block), block)
            col = pl.ds(pl.multiple_of(j * quarter + n * block, block), block)
            got = lax.dot_general(grad_ffn[...], ring[0, at], nt, preferred_element_type=f32)
            low = (got * gelu_ring[j % 2, :, at].astype(f32)).astype(b16)
            grad_u[:, col] = low
            sum_up[:, col] = jnp.sum(low.astype(f32), axis=0, keepdims=True)

        stream_in(2 * j + 2).start()
        if j < 2:
            gelu_in(j + 2).start()
        stream_in(2 * j + 1).wait()

        @pl.loop(0, width // block)
        def _(n):
            at = pl.ds(pl.multiple_of(n * block, block), block)
            o_in[:, at] += lax.dot_general(
                grad_u[:, j * quarter : (j + 1) * quarter], ring[1, at], nt, preferred_element_type=f32
            )

        if j < 3:
            stream_in(2 * j + 3).start()
        if j == 0:
            step_one(0)
        if j == 1:
            step_one(1)
            to_core(0).wait_send()
            make_send(2)
            to_core(1).wait_send()
            make_send(3)
        if j == 2:
            step_one(2)
        if j == 3:
            step_one(3)

    second_norm.wait()

    @pl.loop(0, rows // r_block)
    def _(r):
        at = pl.ds(pl.multiple_of(r * r_block, r_block), r_block)
        norm_back(o_in[at], 7, norm[at], r_one[at, :1], at, grad_branch, (7, 4, 3))

    def att_seq(p):
        yy, cc = seq_peer[p]
        src = grad_att.at[:, :, pl.ds(pl.multiple_of((yy * C + cc) * cols, cols), cols)]
        return send_to(src, heads.at[:, y, c], a_send.at[p], a_recv.at[p], device(z, x, yy, cc))

    stream_in(8).wait()

    def grad_heads(to):
        at = pl.ds(pl.multiple_of(to * cols, cols), cols)
        got = lax.dot_general(grad_branch[...], ring[0, at], nt, preferred_element_type=f32)
        grad_att[:, :, at] = got.astype(b16).reshape(streams, part, cols)

    for p in (1, 2, 0):
        yy, cc = seq_peer[p]
        grad_heads(yy * C + cc)
        att_seq(p).start()
    grad_heads(s)
    heads[:, y, c] = grad_att[:, :, pl.ds(pl.multiple_of(s * cols, cols), cols)]
    for copy in tok_loads + col_loads:
        copy.start()
    for copy in first_loads[2:]:
        copy.wait()
    make_send(4)
    make_send(5)
    step_one(4)
    step_two(0)
    step_one(5)
    step_two(1)
    for p in range(3):
        att_seq(p).wait_recv()
    for copy in tok_loads + col_loads:
        copy.wait()

    lane = lax.broadcasted_iota(jnp.int32, (1, PAIR), 1)
    low_half = (lane % HEAD_DIM) < HEAD_DIM // 2
    top = lax.broadcasted_iota(jnp.int32, (PAIR, 1), 0) < HEAD_DIM
    masks = [(lane < HEAD_DIM).astype(f32).astype(b16), (lane >= HEAD_DIM).astype(f32).astype(b16)]
    score_scale = HEAD_DIM**-0.5
    q_block = stream // 2

    def attend_back(i):
        half, b = i // streams, i % streams
        far[...] = jnp.where(seg_col[b] == seg_row[b], 0.0, FAR)
        queries, keys, values = qkv[0, b, half], qkv[1, b, half], qkv[2, b, half]
        given = heads[b, :, :, :, pl.ds(pl.multiple_of(half * PAIR, PAIR), PAIR)].reshape(stream, PAIR)
        keys_t = keys.T
        grad_k, grad_v = jnp.zeros((stream, PAIR), f32), jnp.zeros((stream, PAIR), f32)
        grad_q = []
        for part_q in range(2):
            at = slice(part_q * q_block, (part_q + 1) * q_block)
            q_t = []
            for head in range(2):
                q = queries[at] * (masks[head] * b16(score_scale))
                g = given[at] * masks[head]
                scores = lax.dot_general(keys, q, nt, preferred_element_type=f32) + far[:, at]
                probs = jnp.exp(scores - lse[b * 2 + half, head : head + 1, at])
                grad_p = lax.dot_general(values, g, nt, preferred_element_type=f32)
                row_dot = jnp.sum(probs * grad_p, axis=0, keepdims=True)
                grad_s = (probs * (grad_p - row_dot)).astype(b16)
                grad_v = grad_v + jnp.dot(probs.astype(b16), g, preferred_element_type=f32)
                grad_k = grad_k + jnp.dot(grad_s, q, preferred_element_type=f32)
                q_t.append(jnp.dot(keys_t, grad_s, preferred_element_type=f32))
            grad_q.append(jnp.where(top, q_t[0], q_t[1]).T * score_scale)
        grad_q = jnp.concatenate(grad_q, axis=0)
        lane_at = pl.multiple_of(s * cols + half * PAIR, PAIR)
        done = []
        for t in (grad_q, grad_k):
            done.append(turned_back(t.astype(b16).astype(f32), cos4[b], sin4[b], low_half).astype(b16))
        done.append(grad_v.astype(b16))
        for j in range(3):
            turned[half, b, :, j * PAIR : (j + 1) * PAIR] = done[j]
            sums[j : j + 1, pl.ds(lane_at, PAIR)] += jnp.sum(done[j].astype(f32), axis=0, keepdims=True)

    def qkv_rows(half, zz, xx):
        at = pl.ds(pl.multiple_of((zz * X + xx) * 128, 128), 128)
        got = jnp.zeros((128, 3 * PAIR), f32)
        for b in range(streams):
            got = got + jnp.dot(
                ring[b // 2, at, (b % 2) * stream : (b % 2 + 1) * stream], turned[half, b], preferred_element_type=f32
            )
        return got

    def qkv_x(half):
        return send_to(q_send.at[half], q_x.at[half], qx_send.at[half], qx_recv.at[half], device(z, 1 - x, y, c))

    def qkv_z(half, d):
        return send_to(q_x.at[half, others[d]], q_z.at[half, d], qz_send.at[half, d], qz_recv.at[half, d], device(others[d], x, y, c))

    def qkv_seq(half, p):
        yy, cc = seq_peer[p]
        return send_to(q_seq.at[half, yy, cc], q_in.at[half, y, c], qs_send.at[half, p], qs_recv.at[half, p], device(z, x, yy, cc))

    def qkv_one(half):
        @pl.loop(0, Z)
        def _(zz):
            q_send[half, zz] = qkv_rows(half, zz, 1 - x).astype(b16)

        qkv_x(half).start()

    def qkv_two(half):
        qkv_x(half).wait_recv()

        @pl.loop(0, Z)
        def _(zz):
            q_x[half, zz] = (q_x[half, zz].astype(f32) + qkv_rows(half, zz, x)).astype(b16)

        for d in range(Z - 1):
            qkv_z(half, d).start()

    def qkv_three(half):
        value = q_x[half, z].astype(f32)
        for d in range(Z - 1):
            qkv_z(half, d).wait_recv()
        for d in range(Z - 1):
            value = value + q_z[half, d].astype(f32)
        q_seq[half] = value.reshape(Y, C, -1, 3 * PAIR)
        for p in range(3):
            qkv_seq(half, p).start()
        q_in[half, y, c] = q_seq[half, y, c]

    def qkv_four(half):
        for p in range(3):
            qkv_seq(half, p).wait_recv()
        for owner in range(Y * C):
            for j in range(3):
                lane_at = j * width + owner * cols + half * PAIR
                o_qkv[:, lane_at : lane_at + PAIR] = q_in[half, owner // C, owner % C, :, j * PAIR : (j + 1) * PAIR]

    plan = {
        0: [lambda: to_core(4).wait_send(), lambda: make_send(6), lambda: step_two(2)],
        1: [lambda: step_one(6), lambda: step_three(0)],
        2: [lambda: to_core(5).wait_send(), lambda: make_send(7), lambda: step_two(3), lambda: step_three(1)],
        3: [lambda: qkv_one(0), lambda: step_one(7), lambda: step_four(0)],
        4: [lambda: step_two(4), lambda: make_send(8), lambda: step_three(2), lambda: step_four(1)],
        5: [lambda: step_one(8), lambda: make_send(9), lambda: step_two(5), lambda: step_three(3)],
    }

    @pl.loop(0, streams * 2)
    def _(i):
        at_index(i, plan)
        attend_back(i)

    def in_c(b):
        return send_to(i_send.at[b], i_c.at[b], ic_send.at[b], ic_recv.at[b], device(z, x, y, 1 - c))

    def in_y(b):
        return send_to(i_y_send.at[b], i_y.at[b], iy_send.at[b], iy_recv.at[b], device(z, x, 1 - y, c))

    def input_rows(b, yy, cc):
        at = pl.ds(pl.multiple_of((yy * C + cc) * part, part), part)
        got = lax.dot_general(turned[0, b, at], ring[1, :, stream : stream + 3 * PAIR], nt, preferred_element_type=f32)
        return got + lax.dot_general(turned[1, b, at], cols_one[...], nt, preferred_element_type=f32)

    qkv_one(1)

    @pl.loop(0, streams)
    def _(b):
        for yy in range(Y):
            i_send[b, yy] = input_rows(b, yy, 1 - c).astype(b16)
        in_c(b).start()

    lanes = lax.broadcasted_iota(jnp.int32, (16, 128), 1)
    spots = lax.broadcasted_iota(jnp.int32, (16, 128), 0)
    share = 128 // (Y * C)
    for zx in range(Z * X):
        tile = sums[:, zx * 128 : (zx + 1) * 128]
        for yc in range(Y * C):
            owner = zx * Y * C + yc
            moved = pltpu.roll(tile, (128 - yc * share) % 128, 1) if yc else tile
            value = jnp.where(lanes < share, moved, 0.0)
            value = jnp.where(spots == 9, sum_up[:, owner * 128 : (owner + 1) * 128], value)
            send_s[zx // X, zx % X, yc // C, yc % C] = value.astype(b16)
    to_core(10).start()

    @pl.loop(0, streams)
    def _(b):
        in_c(b).wait_recv()
        i_y_send[b] = (input_rows(b, 1 - y, c) + i_c[b, 1 - y].astype(f32)).astype(b16)
        in_y(b).start()

    step_one(10)
    step_one(9)
    qkv_two(0)
    step_two(6)
    step_two(7)
    step_three(4)
    step_three(5)
    step_four(2)
    step_four(3)

    @pl.loop(0, streams)
    def _(b):
        at = pl.ds(pl.multiple_of(b * part, part), part)
        o_in[at] += input_rows(b, y, c) + i_c[b, y].astype(f32)

    qkv_two(1)
    step_two(10)
    step_two(8)
    step_two(9)
    qkv_three(0)
    step_three(6)
    step_three(7)
    step_four(4)
    step_four(5)
    qkv_four(0)
    step_three(10)
    step_three(8)
    step_three(9)
    qkv_three(1)
    step_four(6)
    step_four(7)

    @pl.loop(0, streams)
    def _(b):
        at = pl.ds(pl.multiple_of(b * part, part), part)
        in_y(b).wait_recv()
        o_in[at] += i_y[b].astype(f32)

    qkv_four(1)
    for k in (8, 9, 10):
        step_four(k)

    for k in range(total):
        if k not in (0, 1, 4, 5):
            to_core(k).wait_send()
        first(k).wait_send()
        second(k).wait_send()
        for d in range(Z - 1):
            along_z(k, d).wait_send()
    for p in range(3):
        att_seq(p).wait_send()
        for half in range(2):
            qkv_seq(half, p).wait_send()
    for half in range(2):
        qkv_x(half).wait_send()
        for d in range(Z - 1):
            qkv_z(half, d).wait_send()

    @pl.loop(0, streams)
    def _(b):
        in_c(b).wait_send()
        in_y(b).wait_send()


def run_backward(kept, cot, cos4, sin4, seg_col, seg_row):
    (w_out, w_up, w_down, w_proj, w_cols, side_rows, tok_t, qkv, lse, att_t, n_one, r_one, h_low_t, hid_t, dgelu, n_two, r_two, nlow_t) = kept
    rows, width = n_one.shape
    ff = dgelu.shape[1]
    streams, _, stream = tok_t.shape
    proj = w_proj.shape[-1]
    cols, quarter, down_cols = width // (Y * C), ff // 4, width // 4
    grid = (Z, X, Y, C)
    part = rows // streams
    vm, dma = pltpu.VMEM, pltpu.SemaphoreType.DMA
    vmem, hbm = pl.BlockSpec(memory_space=pltpu.VMEM), pl.BlockSpec(memory_space=pl.ANY)
    owner = width // OWNERS
    tails = [((4,), (ff // OWNERS, down_cols)), ((4,), (owner, quarter)), ((), (owner, width)), ((), (owner, proj)), ((), (16, 128))]
    inputs = [
        (w_out.reshape(width, width), hbm), (w_up.reshape(4, width, quarter), hbm), (w_down.reshape(ff, width), hbm),
        (w_proj.reshape(width, proj), vmem), (w_cols.reshape(2, width, 3 * PAIR), hbm), (side_rows, vmem), (tok_t, hbm), (qkv, hbm),
        (lse, vmem), (att_t.reshape(grid + (owner, rows)), hbm), (n_one, hbm), (r_one, vmem), (h_low_t.reshape(grid + (owner, rows)), hbm),
        (hid_t.reshape(grid + (ff // OWNERS, rows)), hbm), (dgelu, hbm), (n_two, hbm), (r_two, vmem), (nlow_t.reshape(grid + (owner, rows)), vmem),
        (cot, vmem), (cos4, vmem), (sin4, vmem), (seg_col, vmem), (seg_row, vmem),
    ]
    scratch = [
        vm((2, width, width), b16), vm((2, rows, quarter), b16), vm((rows, width), f32),
        vm(grid + (owner, rows), b16), vm(grid + (owner, rows), b16), vm(grid + (ff // OWNERS, rows), b16),
        vm(qkv.shape, b16), vm((width, 3 * PAIR), b16), vm((16, width), f32), vm((1, ff), f32),
        vm((rows, width), b16), vm((rows, ff), b16), vm((rows, width), b16), vm((streams, part, width), b16),
        vm((streams, Y, C, part, cols), b16), vm((stream, stream), f32), vm((2, streams, stream, 3 * PAIR), b16),
        vm((2, Z, X, Y) + tails[0][1], b16), vm((2, Z, X, Y) + tails[1][1], b16), vm((Z, X, Y) + tails[2][1], b16), vm((Z, X, Y) + tails[3][1], b16),
        vm(grid + tails[4][1], b16),
    ]
    for lead in ((Z, X, Y), (Z, 2), (Z,), (Z - 1,)):
        scratch += [vm(many + lead + tail, b16) for many, tail in tails]
    scratch += [
        vm((2, Z, 128, 3 * PAIR), b16), vm((2, Z, 128, 3 * PAIR), b16), vm((2, Z - 1, 128, 3 * PAIR), b16),
        vm((2, Y, C, 32, 3 * PAIR), f32), vm((2, Y, C, 32, 3 * PAIR), f32),
        vm((streams, Y, part, width), b16), vm((streams, Y, part, width), b16), vm((streams, part, width), b16), vm((streams, part, width), b16),
        dma((11, 6)), dma((11, 6)), dma((3,)), dma((3,)), dma((2,)), dma((2,)), dma((2, 3)), dma((2, 3)), dma((2, 3)), dma((2, 3)),
        dma((streams,)), dma((streams,)), dma((streams,)), dma((streams,)),
        dma((8 + streams,)), dma((9,)), dma((4,)),
    ]
    outs = [(rows, width), (owner, 3 * width), (owner, width), (owner, ff), (ff // OWNERS, width), (owner, proj), (16, 128)]
    return pl.pallas_call(
        backward_kernel,
        out_shape=[jax.ShapeDtypeStruct(o, f32) for o in outs],
        in_specs=[spec for _, spec in inputs],
        out_specs=[vmem] * len(outs),
        scratch_shapes=scratch,
        compiler_params=pltpu.CompilerParams(collective_id=4, has_side_effects=True, vmem_limit_bytes=63 << 20),
    )(*[a for a, _ in inputs])


def layer_norm(field, gain_row, shift_row):
    average = jnp.mean(field, axis=-1, keepdims=True)
    centred = field - average
    variance = jnp.mean(centred * centred, axis=-1, keepdims=True)
    return centred * lax.rsqrt(variance + epsilon) * gain_row + shift_row


def doc_layout(doc_sizes, places):
    doc_ends = jnp.cumsum(doc_sizes)
    passed = places[:, None] >= doc_ends[None, :]
    segment = jnp.sum(passed.astype(jnp.int32), axis=1)
    starts = jnp.sum(jnp.where(passed, doc_sizes[None, :], 0), axis=1)
    return (segment, places - starts)


def rope_tables(position, half_dim):
    steps_f = jnp.arange(half_dim, dtype=jnp.float32)
    inverse = jnp.exp(steps_f * (-math.log(rope_base) / half_dim))
    angle = position.astype(jnp.float32)[:, None] * inverse[None, :]
    return (jnp.cos(angle), jnp.sin(angle))


def rotate(field, cosine, sine_tab, head_count):
    length = field.shape[0]
    halves = field.reshape(length, head_count, 2, -1)
    first_half = halves[:, :, 0]
    second_half = halves[:, :, 1]
    cos_b = cosine[:, None, :]
    sin_b = sine_tab[:, None, :]
    turned = jnp.stack(
        [first_half * cos_b - second_half * sin_b, second_half * cos_b + first_half * sin_b], axis=2
    )
    return turned.reshape(length, -1)


def gelu_exact(field):
    return jax.nn.gelu(field, approximate=False)


def scores_of(query_blk, seg_blk, keys_all, stream_seg, score_scale):
    raw_scores = (
        jnp.einsum("qhd,khd->hqk", query_blk, keys_all, preferred_element_type=jnp.float32)
        * score_scale
    )
    same_doc = (seg_blk[:, None] == stream_seg[None, :])[None]
    return jnp.where(same_doc, raw_scores, neg_fill)


def per_device_any(
    tokens,
    doc_lengths,
    qkv_weight,
    out_weight,
    up_weight,
    down_weight,
    proj_weight,
    biases,
    gains,
    up_bias,
    cotangent,
):
    stream_count = tokens.shape[0]
    seg_rows = tokens.shape[1]
    model_width = tokens.shape[2]
    seq_parts = lax.axis_size("seq")
    stream = seg_rows * seq_parts
    head_count = model_width // HEAD_DIM
    local_heads = head_count // seq_parts
    flat_width = local_heads * HEAD_DIM
    score_scale = HEAD_DIM ** (-0.5)
    tok_flat = tokens.reshape(stream_count * seg_rows, model_width)
    gathered = (
        lax.all_gather(qkv_weight, ("rows", "seq"), axis=0, tiled=True),
        lax.all_gather(out_weight, ("rows", "seq"), axis=0, tiled=True),
        lax.all_gather(up_weight, ("rows", "seq"), axis=0, tiled=True),
        lax.all_gather(down_weight, ("rows", "seq"), axis=0, tiled=True),
        lax.all_gather(proj_weight, ("rows", "seq"), axis=0, tiled=True),
        lax.all_gather(biases, ("rows", "seq"), axis=1, tiled=True),
        lax.all_gather(gains, ("rows", "seq"), axis=1, tiled=True),
        lax.all_gather(up_bias, ("rows", "seq"), axis=0, tiled=True),
    )
    w_qkv, w_out, w_up, w_down, w_proj = (
        gathered[0],
        gathered[1],
        gathered[2],
        gathered[3],
        gathered[4],
    )
    bias_rows = gathered[5].astype(jnp.float32)
    gain_rows = gathered[6].astype(jnp.float32)
    bias_up = gathered[7].astype(jnp.float32)
    token_places = lax.axis_index("seq") * seg_rows + jnp.arange(seg_rows, dtype=jnp.int32)
    layout_rows = jax.vmap(doc_layout, in_axes=(0, None))
    token_seg, position = layout_rows(doc_lengths, token_places)
    cosine, sine_tab = rope_tables(position.reshape(-1), HEAD_DIM // 2)
    projected = jnp.dot(tok_flat, w_qkv, preferred_element_type=jnp.float32) + bias_rows[
        0:3
    ].reshape(-1)
    queries = (
        rotate(projected[:, :model_width], cosine, sine_tab, head_count)
        .astype(jnp.bfloat16)
        .reshape(stream_count, seg_rows, model_width)
    )
    keys_tok = (
        rotate(projected[:, model_width : 2 * model_width], cosine, sine_tab, head_count)
        .astype(jnp.bfloat16)
        .reshape(stream_count, seg_rows, model_width)
    )
    values_tok = (
        projected[:, 2 * model_width :]
        .astype(jnp.bfloat16)
        .reshape(stream_count, seg_rows, model_width)
    )
    queries_h, keys_h, values_h = (
        lax.all_to_all(queries, "seq", split_axis=2, concat_axis=1, tiled=True),
        lax.all_to_all(keys_tok, "seq", split_axis=2, concat_axis=1, tiled=True),
        lax.all_to_all(values_tok, "seq", split_axis=2, concat_axis=1, tiled=True),
    )
    stream_seg, stream_pos = layout_rows(doc_lengths, jnp.arange(stream, dtype=jnp.int32))
    block_rows = math.gcd(stream, 512)
    block_count = stream // block_rows

    def forward_stream(element):
        query_s, key_s, value_s, seg_s = element
        query_blocks = query_s.reshape(block_count, block_rows, local_heads, HEAD_DIM)
        keys_all = key_s.reshape(stream, local_heads, HEAD_DIM)
        values_all = value_s.reshape(stream, local_heads, HEAD_DIM)
        seg_blocks = seg_s.reshape(block_count, block_rows)

        def forward_block(inner):
            query_blk, seg_blk = inner
            scores = scores_of(query_blk, seg_blk, keys_all, seg_s, score_scale)
            row_max = jnp.max(scores, axis=-1, keepdims=True)
            row_total = jnp.sum(jnp.exp(scores - row_max), axis=-1, keepdims=True)
            log_total = row_max + jnp.log(row_total)
            probs_low = jnp.exp(scores - log_total).astype(jnp.bfloat16)
            attn_blk = jnp.einsum(
                "hqk,khd->qhd", probs_low, values_all, preferred_element_type=jnp.float32
            )
            return (attn_blk.astype(jnp.bfloat16), log_total[:, :, 0])

        attn_blocks, log_blocks = lax.map(forward_block, (query_blocks, seg_blocks))
        return (attn_blocks.reshape(stream, flat_width), log_blocks)

    attn_heads, log_totals = lax.map(forward_stream, (queries_h, keys_h, values_h, stream_seg))
    attended = lax.all_to_all(attn_heads, "seq", split_axis=1, concat_axis=2, tiled=True).reshape(
        stream_count * seg_rows, model_width
    )
    branch = jnp.dot(attended, w_out, preferred_element_type=jnp.float32) + bias_rows[3]
    h_one, norm_one = jax.vjp(
        layer_norm, tok_flat.astype(jnp.float32) + branch, gain_rows[0], bias_rows[4]
    )
    h_low = h_one.astype(jnp.bfloat16)
    u_pre = jnp.dot(h_low, w_up, preferred_element_type=jnp.float32) + bias_up
    hidden_f, gelu_back = jax.vjp(gelu_exact, u_pre)
    hidden = hidden_f.astype(jnp.bfloat16)
    ffn_out = jnp.dot(hidden, w_down, preferred_element_type=jnp.float32) + bias_rows[5]
    normed, norm_two = jax.vjp(layer_norm, h_one + ffn_out, gain_rows[1], bias_rows[6])
    normed_low = normed.astype(jnp.bfloat16)
    result = jnp.dot(normed_low, w_proj, preferred_element_type=jnp.float32).astype(jnp.bfloat16)
    w_qkv, w_out, w_up, w_down, w_proj = (
        lax.all_gather(qkv_weight, ("rows", "seq"), axis=0, tiled=True),
        lax.all_gather(out_weight, ("rows", "seq"), axis=0, tiled=True),
        lax.all_gather(up_weight, ("rows", "seq"), axis=0, tiled=True),
        lax.all_gather(down_weight, ("rows", "seq"), axis=0, tiled=True),
        lax.all_gather(proj_weight, ("rows", "seq"), axis=0, tiled=True),
    )
    cot_low = cotangent.reshape(stream_count * seg_rows, -1).astype(jnp.bfloat16)
    proj_part = jnp.dot(normed_low.T, cot_low, preferred_element_type=jnp.float32)
    grad_normed = jnp.dot(cot_low, w_proj.T, preferred_element_type=jnp.float32)
    grad_z2, grad_g2, grad_b2 = norm_two(grad_normed)
    grad_ffn = grad_z2.astype(jnp.bfloat16)
    grad_c2 = jnp.sum(grad_ffn, axis=0, dtype=jnp.float32)
    down_part = jnp.dot(hidden.T, grad_ffn, preferred_element_type=jnp.float32)
    grad_hidden = jnp.dot(grad_ffn, w_down.T, preferred_element_type=jnp.float32)
    grad_u = gelu_back(grad_hidden)[0].astype(jnp.bfloat16)
    grad_c1 = jnp.sum(grad_u, axis=0, dtype=jnp.float32)
    up_part = jnp.dot(h_low.T, grad_u, preferred_element_type=jnp.float32)
    ffn_sums = (up_part, down_part, proj_part, grad_c1)
    grad_h1 = grad_z2 + jnp.dot(grad_u, w_up.T, preferred_element_type=jnp.float32)
    grad_z1, grad_g1, grad_b1 = norm_one(grad_h1)
    grad_branch = grad_z1.astype(jnp.bfloat16)
    grad_bo = jnp.sum(grad_branch, axis=0, dtype=jnp.float32)
    out_part = jnp.dot(attended.T, grad_branch, preferred_element_type=jnp.float32)
    grad_attn = jnp.dot(grad_branch, w_out.T, preferred_element_type=jnp.float32).astype(
        jnp.bfloat16
    )
    grad_heads = lax.all_to_all(
        grad_attn.reshape(stream_count, seg_rows, model_width),
        "seq",
        split_axis=2,
        concat_axis=1,
        tiled=True,
    )

    def backward_stream(element):
        query_s, key_s, value_s, seg_s, log_s, grad_s = element
        query_blocks = query_s.reshape(block_count, block_rows, local_heads, HEAD_DIM)
        keys_all = key_s.reshape(stream, local_heads, HEAD_DIM)
        values_all = value_s.reshape(stream, local_heads, HEAD_DIM)
        seg_blocks = seg_s.reshape(block_count, block_rows)
        grad_blocks = grad_s.reshape(block_count, block_rows, local_heads, HEAD_DIM)

        def backward_block(carried, inner):
            grad_keys, grad_values = carried
            query_blk, seg_blk, log_total, grad_blk = inner
            probs_f = jnp.exp(
                scores_of(query_blk, seg_blk, keys_all, seg_s, score_scale) - log_total[:, :, None]
            )
            grad_values = grad_values + jnp.einsum(
                "hqk,qhd->khd",
                probs_f.astype(jnp.bfloat16),
                grad_blk,
                preferred_element_type=jnp.float32,
            )
            grad_probs = jnp.einsum(
                "qhd,khd->hqk", grad_blk, values_all, preferred_element_type=jnp.float32
            )
            row_dot = jnp.sum(probs_f * grad_probs, axis=-1, keepdims=True)
            grad_scores = (probs_f * (grad_probs - row_dot) * score_scale).astype(jnp.bfloat16)
            grad_query = jnp.einsum(
                "hqk,khd->qhd", grad_scores, keys_all, preferred_element_type=jnp.float32
            )
            grad_keys = grad_keys + jnp.einsum(
                "hqk,qhd->khd", grad_scores, query_blk, preferred_element_type=jnp.float32
            )
            return ((grad_keys, grad_values), grad_query.astype(jnp.bfloat16))

        zero_acc = jnp.zeros((stream, local_heads, HEAD_DIM), jnp.float32)
        (grad_keys, grad_values), grad_queries = lax.scan(
            backward_block, (zero_acc, zero_acc), (query_blocks, seg_blocks, log_s, grad_blocks)
        )
        return (
            grad_queries.reshape(stream, flat_width),
            grad_keys.astype(jnp.bfloat16).reshape(stream, flat_width),
            grad_values.astype(jnp.bfloat16).reshape(stream, flat_width),
        )

    head_q, head_k, head_v = lax.map(
        backward_stream, (queries_h, keys_h, values_h, stream_seg, log_totals, grad_heads)
    )
    back_q, back_k, back_v = (
        lax.all_to_all(head_q, "seq", split_axis=1, concat_axis=2, tiled=True),
        lax.all_to_all(head_k, "seq", split_axis=1, concat_axis=2, tiled=True),
        lax.all_to_all(head_v, "seq", split_axis=1, concat_axis=2, tiled=True),
    )
    flat_rows = stream_count * seg_rows
    turned_q = rotate(
        back_q.reshape(flat_rows, model_width).astype(jnp.float32), cosine, -sine_tab, head_count
    )
    turned_k = rotate(
        back_k.reshape(flat_rows, model_width).astype(jnp.float32), cosine, -sine_tab, head_count
    )
    grad_project = jnp.concatenate(
        [turned_q, turned_k, back_v.reshape(flat_rows, model_width).astype(jnp.float32)], axis=1
    ).astype(jnp.bfloat16)
    grad_bqkv = jnp.sum(grad_project, axis=0, dtype=jnp.float32).reshape(3, model_width)
    qkv_part = jnp.dot(tok_flat.T, grad_project, preferred_element_type=jnp.float32)
    input_grad = grad_z1 + jnp.dot(grad_project, w_qkv.T, preferred_element_type=jnp.float32)
    bias_part = jnp.concatenate(
        [grad_bqkv, jnp.stack([grad_bo, grad_b1, grad_c2, grad_b2])], axis=0
    )
    gain_part = jnp.stack([grad_g1, grad_g2])
    qkv_sum, out_sum, up_sum, down_sum, proj_sum, bias_sum, gain_sum, c1_sum = (
        lax.psum_scatter(qkv_part, ("rows", "seq"), scatter_dimension=0, tiled=True),
        lax.psum_scatter(out_part, ("rows", "seq"), scatter_dimension=0, tiled=True),
        lax.psum_scatter(ffn_sums[0], ("rows", "seq"), scatter_dimension=0, tiled=True),
        lax.psum_scatter(ffn_sums[1], ("rows", "seq"), scatter_dimension=0, tiled=True),
        lax.psum_scatter(ffn_sums[2], ("rows", "seq"), scatter_dimension=0, tiled=True),
        lax.psum_scatter(bias_part, ("rows", "seq"), scatter_dimension=1, tiled=True),
        lax.psum_scatter(gain_part, ("rows", "seq"), scatter_dimension=1, tiled=True),
        lax.psum_scatter(ffn_sums[3], ("rows", "seq"), scatter_dimension=0, tiled=True),
    )
    output = result.reshape(stream_count, seg_rows, -1)
    return (
        output,
        input_grad.reshape(stream_count, seg_rows, model_width),
        qkv_sum,
        out_sum,
        up_sum,
        down_sum,
        proj_sum,
        bias_sum,
        gain_sum,
        c1_sum,
    )


def direct_links():
    return lax.axis_size("rows") == Z * X and lax.axis_size("seq") == Y * C


def turn_tables(doc_lengths, stream):
    stream_seg, stream_pos = jax.vmap(doc_layout, in_axes=(0, None))(doc_lengths, jnp.arange(stream, dtype=jnp.int32))
    cosine, sine = rope_tables(stream_pos.reshape(-1), HEAD_DIM // 2)
    shape = stream_seg.shape + (PAIR,)
    cos4 = jnp.concatenate([cosine] * 4, axis=1).reshape(shape)
    sin4 = jnp.concatenate([-sine, sine, -sine, sine], axis=1).reshape(shape)
    return stream_seg, cos4, sin4


def per_device_direct(
    tokens, doc_lengths, qkv_weight, out_weight, up_weight, down_weight, proj_weight, biases, gains, up_bias, cotangent
):
    streams, part, width = tokens.shape
    lanes = biases.shape[1]
    seg, cos4, sin4 = turn_tables(doc_lengths, part * Y * C)
    seg_col, seg_row = seg[:, :, None], seg[:, None, :]
    side = jnp.zeros((16, 128), b16).at[:7, :lanes].set(biases).at[7:9, :lanes].set(gains).at[9].set(up_bias)
    wqkv = qkv_weight.reshape(-1, 3, width).transpose(1, 0, 2)
    *kept, result = run_forward(
        tokens, wqkv, out_weight, up_weight, down_weight, proj_weight, side, cos4, sin4, seg_col, seg_row
    )
    cot = cotangent.reshape(streams * part, -1).astype(b16)
    input_grad, qkv, out, up, down, proj, side_sum = run_backward(kept, cot, cos4, sin4, seg_col, seg_row)
    return (
        result.reshape(streams, part, -1),
        input_grad.reshape(streams, part, width),
        qkv,
        out,
        up,
        down,
        proj,
        side_sum[:7, :lanes],
        side_sum[7:9, :lanes],
        side_sum[9],
    )


def per_device(*args):
    return per_device_direct(*args) if direct_links() else per_device_any(*args)


def solution(mesh):
    in_specs = (
        P("rows", "seq", None),
        P("rows", None),
        P(("rows", "seq"), None),
        P(("rows", "seq"), None),
        P(("rows", "seq"), None),
        P(("rows", "seq"), None),
        P(("rows", "seq"), None),
        P(None, ("rows", "seq")),
        P(None, ("rows", "seq")),
        P(("rows", "seq")),
        P("rows", "seq", None),
    )
    out_specs = (
        P("rows", "seq", None),
        P("rows", "seq", None),
        P(("rows", "seq"), None),
        P(("rows", "seq"), None),
        P(("rows", "seq"), None),
        P(("rows", "seq"), None),
        P(("rows", "seq"), None),
        P(None, ("rows", "seq")),
        P(None, ("rows", "seq")),
        P(("rows", "seq")),
    )
    return jax.shard_map(
        per_device, mesh=mesh, in_specs=in_specs, out_specs=out_specs, check_vma=False
    )
```

```python
import functools
import math

import jax
import jax.numpy as jnp
from jax import lax
from jax.experimental import pallas as pl
from jax.experimental.pallas import tpu as pltpu
from jax.sharding import PartitionSpec as P

epsilon = 1e-05
rope_base = 10000.0
neg_fill = -1e30

HEAD_DIM = 64
PAIR = 2 * HEAD_DIM
MESH = pl.DeviceIdType.MESH
Z, X, Y, C = 4, 2, 2, 2
OWNERS = Z * X * Y * C
f32, b16 = jnp.float32, jnp.bfloat16
FAR = -1e30


def place():
    r, s = lax.axis_index("rows"), lax.axis_index("seq")
    return r // X, r % X, s // C, s % C


def device(z, x, y, c):
    return (z * X + x, y * C + c)


def greet(peers):
    barrier = pltpu.get_barrier_semaphore()
    for peer in peers:
        pl.semaphore_signal(barrier, inc=1, device_id=peer, device_id_type=MESH)
    pl.semaphore_wait(barrier, len(peers))


def send_to(src, dst, send, recv, peer):
    return pltpu.make_async_remote_copy(
        src_ref=src, dst_ref=dst, send_sem=send, recv_sem=recv, device_id=peer, device_id_type=MESH
    )


def normal_rows(field):
    average = jnp.mean(field, axis=-1, keepdims=True)
    centred = field - average
    inverse = lax.rsqrt(jnp.mean(centred * centred, axis=-1, keepdims=True) + epsilon)
    return centred * inverse, inverse


def doc_marks(sizes, b, places):
    segment, start, end = jnp.zeros_like(places), jnp.zeros_like(places), jnp.int32(0)
    for d in range(sizes.shape[1]):
        end = end + sizes[b, d]
        passed = places >= end
        segment = segment + jnp.where(passed, 1, 0)
        start = start + jnp.where(passed, sizes[b, d], 0)
    return segment, places - start


def far_keys(sizes, b, stream):
    down, _ = doc_marks(sizes, b, lax.broadcasted_iota(jnp.int32, (stream, 1), 0))
    across, _ = doc_marks(sizes, b, lax.broadcasted_iota(jnp.int32, (1, stream), 1))
    return jnp.where(down == across, 0.0, FAR)


class Steps:
    def __init__(self, copies, needs):
        self.copies, self.needs, self.seen = copies, needs, set()

    def arrive(self, names):
        for name in names:
            if name not in self.seen:
                self.seen.add(name)
                self.copies(name).wait_recv()

    def start(self, name):
        self.arrive(self.needs(name))
        self.copies(name).start()

    def run(self, names):
        for name in names:
            self.start(name)


def at_index(index, plan):
    for spot, call in plan.items():

        @pl.when(index == spot)
        def _(call=call):
            call()


FORWARD_ROUTES = ("zyx", "zxy", "yzx", "yzx", "zxy", "yzx", "zxy", "zxy", "zxy", "zxy", "yzx")
FORWARD_ORDER = {
    ("tb", 0): (("y", 0), ("y", 2), ("k0", 2), ("a", 0, 0), ("a", 0, 1), ("a", 0, 2), ("a", 1, 0), ("a", 1, 1), ("a", 1, 2), ("a", 2, 0), ("a", 2, 1), ("a", 2, 2), ("y", 1), ("k0", 0), (0, 1, 1), (0, 1, 3), (0, 3), ("k0", 1), (0, 4, 2), (0, 4, 1), (0, 6, 1), (0, 2), (0, 7, 3), (0, 6, 3), (0, 6, 2), (0, 0, 2), (0, 0, 3), (0, 1, 2), (0, 0, 1), (0, 4, 3), (0, 9, 1), (0, 8, 3), (0, 7, 1), (0, 8, 1), (0, 5), (0, 9, 3), (0, 8, 2), (0, 7, 2), (0, 10), (0, 9, 2),),
    ("bias",): (("k1", 0), ("k1", 2), (1, 6), ("wz", 0, 3), ("wz", 0, 2), ("wz", 0, 1), ("wz", 1, 1), ("wz", 1, 3), ("wz", 1, 2), ("wz", 2, 1), ("wz", 2, 2), ("wz", 2, 3), (1, 1), (1, 0), (1, 4), ("k1", 1), (2, 6), (2, 1), (1, 3, 2), (1, 3, 3), (1, 3, 1), (1, 2, 1), (1, 2, 3), (1, 2, 2), (1, 5, 3), (1, 5, 2), (1, 5, 1), (1, 8), (1, 10, 3), (1, 10, 1), (1, 10, 2), (2, 0), (2, 4), (1, 7), (1, 9), (2, 8), (3, 0),),
    ("at", 0): (("wx", 0), (3, 6), (2, 7), (3, 1), ("wx", 1), (2, 9), ("wx", 2), (3, 4), (2, 3),),
    ("at", 1): ((3, 8),),
    ("at", 2): ((2, 2),),
    ("at", 3): ((3, 3), (3, 7),),
    ("out",): ((2, 5), (3, 9), (3, 2),),
    ("ln",): ((2, 10),),
    ("u", 1): ((3, 5),),
    ("d", 1): ((3, 10),),
}


def forward_kernel(
    tok, sizes, wqkv, wout, wup, wdown, wproj, biases, gains, up_bias,
    o_out, o_up, o_down, o_proj, o_cols, o_rows, o_tok_t, o_qkv, o_lse, o_att_t, o_n1, o_r1, o_hlow_t, o_hid_t, o_dgelu,
    o_n2, o_r2, o_nlow_t, o_cos, o_sin, o_res,
    g_out, g_up, g_down, g_proj, g_side, g_cols, g_tok, tok_t, qkv, head_out, far, att, att_t, z_one, n_one, h_low, h_low_t,
    hid, hid_t, dgelu, n_two, bias_up, mix, cos4, sin4,
    c_send, c_recv, a_send, a_recv, wz_send, wz_recv, wx_send, wx_recv, y_send, y_recv, k_send, k_recv, t_send, t_recv, save,
):
    streams, part, width = tok.shape
    rows, stream = streams * part, part * Y * C
    z, x, y, c = place()
    s = y * C + c
    seq_peer = [(y, 1 - c), (1 - y, c), (1 - y, 1 - c)]
    others = [(z + d) % Z for d in range(1, Z)]
    quarter, down_cols = width, width // 4
    cols = wqkv.shape[1] // (3 * Y * C)

    targets = [g_side, g_proj, g_out] + [g_up.at[j] for j in range(4)] + [g_down.at[j] for j in range(4)]
    total = len(targets)
    axis_peer = {"x": device(z, 1 - x, y, c), "y": device(z, x, 1 - y, c)}

    def piece(name):
        stage, k = name[0], name[1]
        route, held = FORWARD_ROUTES[k], targets[k]
        every = slice(None)
        along = {"x": x, "y": y, "z": z}
        spot = {axis: every if axis in route[:stage] else along[axis] for axis in "zxy"}
        if stage == 3:
            slab, slot, peer = held.at[:, :, :, c], 5, device(z, x, y, 1 - c)
        else:
            slab = held.at[spot["z"], spot["x"], spot["y"], c]
            if route[stage] == "z":
                slot, peer = name[2] - 1, device(others[name[2] - 1], x, y, c)
            else:
                slot, peer = 3 + "xy".index(route[stage]), axis_peer[route[stage]]
        return send_to(slab, slab, c_send.at[k, slot], c_recv.at[k, slot], peer)

    def piece_names(stage, k):
        if stage < 3 and FORWARD_ROUTES[k][stage] == "z":
            return [(stage, k, d) for d in range(1, Z)]
        return [(stage, k)]

    def transfer(name):
        kind = name[0]
        if not isinstance(kind, str):
            return piece(name)
        if kind == "a":
            j, p = name[1:]
            yy, cc = seq_peer[p]
            src = wqkv.at[:, pl.ds(pl.multiple_of(j * width + (yy * C + cc) * cols, 128), cols)]
            return send_to(src, g_cols.at[j, z, x, y, c], a_send.at[j, p], a_recv.at[j, p], device(z, x, yy, cc))
        if kind == "wz":
            j, d = name[1:]
            slab = g_cols.at[j, z, x]
            return send_to(slab, slab, wz_send.at[j, d - 1], wz_recv.at[j, d - 1], device(others[d - 1], x, y, c))
        if kind == "wx":
            j = name[1]
            slab = g_cols.at[j, :, x]
            return send_to(slab, slab, wx_send.at[j], wx_recv.at[j], device(z, 1 - x, y, c))
        b = name[1]
        if kind == "y":
            return send_to(tok.at[b], g_tok.at[b, y, c], y_send.at[b], y_recv.at[b], device(z, x, 1 - y, c))
        if kind == "k0":
            return send_to(tok.at[b], g_tok.at[b, y, c], k_send.at[b, 0], k_recv.at[b, 0], device(z, x, y, 1 - c))
        slab = g_tok.at[b, 1 - y, c]
        return send_to(slab, slab, k_send.at[b, 1], k_recv.at[b, 1], device(z, x, y, 1 - c))

    def needs(name):
        kind = name[0]
        if not isinstance(kind, str):
            return piece_names(kind - 1, name[1]) if kind else []
        if kind == "wz":
            return [("a", name[1], p) for p in range(3)]
        if kind == "wx":
            return [("wz", name[1], d) for d in range(1, Z)]
        return [("y", name[1])] if kind == "k1" else []

    steps = Steps(transfer, needs)

    def run(*spot):
        steps.run(FORWARD_ORDER.get(spot, ()))

    def att_seq(i, p):
        b, half = i // 2, i % 2
        yy, cc = seq_peer[p]
        lane = pl.multiple_of((s * 2 + half) * PAIR, PAIR)
        dst = att.at[b, :, pl.ds(lane, PAIR)]
        return send_to(head_out.at[b, half, yy, cc], dst, t_send.at[i, p], t_recv.at[i, p], device(z, x, yy, cc))

    mix[...] = jnp.zeros_like(mix)
    lanes_own = biases.shape[1]
    mix[0:7, 0:lanes_own] = biases[...].astype(f32)
    mix[7:9, 0:lanes_own] = gains[...].astype(f32)
    mix[9:10] = up_bias[...].astype(f32)
    g_side[z, x, y, c] = mix[...].astype(b16)
    g_proj[z, x, y, c] = wproj[...]
    g_out[z, x, y, c] = wout[...]
    for j in range(4):
        g_up[j, z, x, y, c] = wup[:, j * quarter : (j + 1) * quarter]
        g_down[j, z, x, y, c] = wdown[:, j * down_cols : (j + 1) * down_cols]
    for j in range(3):
        g_cols[j, z, x, y, c] = wqkv[:, pl.ds(pl.multiple_of(j * width + s * cols, 128), cols)]
    for b in range(streams):
        g_tok[b, y, c] = tok[b]
    greet(
        [device(zz, x, y, c) for zz in others]
        + [device(z, 1 - x, y, c)]
        + [device(z, x, yy, cc) for yy, cc in seq_peer]
    )
    run("own")

    lane = lax.broadcasted_iota(jnp.int32, (1, PAIR), 1)
    low_half = (lane % HEAD_DIM) < HEAD_DIM // 2
    inverse_f = jnp.exp((lane % (HEAD_DIM // 2)).astype(f32) * (-math.log(rope_base) / (HEAD_DIM // 2)))

    def tables(b):
        _, position = doc_marks(sizes, b, lax.broadcasted_iota(jnp.int32, (stream, PAIR), 0))
        angle = position.astype(f32) * inverse_f
        cos4[b] = jnp.cos(angle)
        sin4[b] = jnp.sin(angle) * jnp.where(low_half, -1.0, 1.0)

    @pl.loop(0, streams)
    def _(b):
        at_index(b, {spot: functools.partial(run, "tb", spot) for spot in range(streams)})
        tables(b)

    run("bias")
    steps.arrive(piece_names(3, 0))
    lanes = lax.broadcasted_iota(jnp.int32, (16, 128), 1)
    share = 128 // (Y * C)
    for zx in range(Z * X):
        tile = jnp.zeros((16, 128), f32)
        for yc in range(Y * C):
            block = g_side[zx // X, zx % X, yc // C, yc % C].astype(f32)
            bias_up[:, pl.ds((zx * Y * C + yc) * 128, 128)] = block[9:10]
            tile = tile + pltpu.roll(jnp.where(lanes < share, block, 0.0), yc * share, 1)
        o_rows[:, pl.ds(zx * 128, 128)] = tile

    def project(b):
        rows_b = g_tok[b].reshape(stream, width)
        tok_t[b] = rows_b.T
        for j in range(3):
            bias_row = o_rows[pl.ds(j, 1), pl.ds(pl.multiple_of(s * cols, 128), cols)]
            got = jnp.dot(rows_b, g_cols[j].reshape(width, cols), preferred_element_type=f32) + bias_row
            for half in range(2):
                t = got[:, half * PAIR : (half + 1) * PAIR]
                if j < 2:
                    swapped = jnp.where(
                        low_half, pltpu.roll(t, PAIR - HEAD_DIM // 2, 1), pltpu.roll(t, HEAD_DIM // 2, 1)
                    )
                    t = t * cos4[b] + swapped * sin4[b]
                qkv[j, b, half] = t.astype(b16)
        far[...] = far_keys(sizes, b, stream)

    q_block = stream // 2
    top = lax.broadcasted_iota(jnp.int32, (PAIR, 1), 0) < HEAD_DIM
    score_scale = HEAD_DIM**-0.5
    masks = [jnp.where(lane < HEAD_DIM, score_scale, 0.0).astype(b16), jnp.where(lane < HEAD_DIM, 0.0, score_scale).astype(b16)]

    def attend(i):
        b, half = i // 2, i % 2
        queries, keys = qkv[0, b, half], qkv[1, b, half]
        values_t = qkv[2, b, half].T
        for block in range(2):
            at = slice(block * q_block, (block + 1) * q_block)
            turned = []
            for head in range(2):
                q = queries[at] * masks[head]
                scores = lax.dot_general(keys, q, (((1,), (1,)), ((), ())), preferred_element_type=f32)
                scores = scores + far[:, pl.ds(block * q_block, q_block)]
                most = jnp.max(scores, axis=0, keepdims=True)
                e = jnp.exp(scores - most)
                mass = jnp.sum(e, axis=0, keepdims=True)
                o_lse[i, pl.ds(head, 1), pl.ds(block * q_block, q_block)] = most + jnp.log(mass)
                probs = (e * (1.0 / mass)).astype(b16)
                turned.append(jnp.dot(values_t, probs, preferred_element_type=f32))
            both = jnp.where(top, turned[0], turned[1]).T.astype(b16)
            for cc in range(C):
                head_out[b, half, block, cc] = both[cc * part : (cc + 1) * part]
        for p in range(3):
            att_seq(i, p).start()
        lane_at = pl.multiple_of((s * 2 + half) * PAIR, PAIR)
        att[b, :, pl.ds(lane_at, PAIR)] = head_out[b, half, y, c]

    def before(i):
        run("at", i)
        if i % 2 == 0:
            steps.arrive([("wx", j) for j in range(3)] + [("k0", i // 2), ("k1", i // 2)])

    @pl.loop(0, streams * 2)
    def _(i):
        at_index(i, {spot: functools.partial(before, spot) for spot in range(streams * 2)})

        @pl.when(i % 2 == 0)
        def _():
            project(i // 2)

        attend(i)

    run("out")

    @pl.loop(0, streams * 2)
    def _(i):
        for p in range(3):
            att_seq(i, p).wait_recv()

    steps.arrive(piece_names(3, 2))
    n_block = 256

    @pl.loop(0, width // n_block)
    def _(n):
        at = pl.ds(pl.multiple_of(n * n_block, n_block), n_block)
        w = g_out[:, :, :, :, :, at].reshape(width, n_block)
        got = jnp.dot(att[...].reshape(rows, width), w, preferred_element_type=f32)
        z_one[:, at] = tok[:, :, at].reshape(rows, n_block).astype(f32) + (got + o_rows[3:4, at])

    run("ln")
    r_block = 128

    @pl.loop(0, rows // r_block)
    def _(r):
        at = pl.ds(pl.multiple_of(r * r_block, r_block), r_block)
        n, inverse = normal_rows(z_one[at])
        n_one[at] = n
        o_r1[at] = jnp.broadcast_to(inverse, (r_block, 128))
        h = n * o_rows[7:8] + o_rows[4:5]
        z_one[at] = h
        h_low[at] = h.astype(b16)
        h_low_t[:, at] = h.astype(b16).T
        att_t[:, at] = att[r].T

    kept = [
        (g_out, o_out), (tok_t, o_tok_t), (qkv, o_qkv), (att_t, o_att_t), (n_one, o_n1), (h_low_t, o_hlow_t), (cos4, o_cos), (sin4, o_sin),
    ]
    kept += [
        (g_cols.at[j, :, :, :, :, :, pl.ds(half * PAIR, PAIR)], o_cols.at[half, :, :, :, :, :, pl.ds(j * PAIR, PAIR)])
        for j in range(3)
        for half in range(2)
    ]
    early = len(kept)
    kept += [(g_up.at[j], o_up.at[j]) for j in range(4)]
    kept += [(hid_t, o_hid_t), (dgelu, o_dgelu)]
    kept += [(g_down.at[j], o_down.at[:, :, :, :, :, pl.ds(j * down_cols, down_cols)]) for j in range(4)]
    kept += [(g_proj, o_proj), (n_two, o_n2)]
    copies = [pltpu.make_async_copy(a, b, save.at[i]) for i, (a, b) in enumerate(kept)]
    for copy in copies[:early]:
        copy.start()
    for j in range(4):
        run("u", j)
        steps.arrive(piece_names(3, 3 + j))

        @pl.loop(0, quarter // n_block)
        def _(n):
            at = pl.ds(pl.multiple_of(n * n_block, n_block), n_block)
            col = pl.ds(pl.multiple_of(j * quarter + n * n_block, n_block), n_block)
            w = g_up[j, :, :, :, :, :, at].reshape(width, n_block)
            u = jnp.dot(h_low[...], w, preferred_element_type=f32) + bias_up[:, col]
            cdf = 0.5 * (1.0 + lax.erf(u * (2.0**-0.5)))
            low = (u * cdf).astype(b16)
            hid[:, col] = low
            hid_t[col, :] = low.T
            dgelu[:, col] = (cdf + u * (jnp.exp(-0.5 * u * u) * ((2.0 * math.pi) ** -0.5))).astype(b16)

        copies[early + j].start()

    copies[early + 4].start()
    copies[early + 5].start()
    for j in range(4):
        run("d", j)
        steps.arrive(piece_names(3, 7 + j))
        copies[early + 6 + j].start()
        at = pl.ds(j * down_cols, down_cols)
        w = g_down[j].reshape(4 * width, down_cols)
        got = jnp.dot(hid[...], w, preferred_element_type=f32) + o_rows[5:6, j * down_cols : (j + 1) * down_cols]
        n_two[:, at] = z_one[:, at] + got

    run("ln2")
    steps.arrive(piece_names(3, 1))
    copies[early + 10].start()

    @pl.loop(0, rows // r_block)
    def _(r):
        at = pl.ds(pl.multiple_of(r * r_block, r_block), r_block)
        n, inverse = normal_rows(n_two[at])
        n_two[at] = n
        o_r2[at] = jnp.broadcast_to(inverse, (r_block, 128))
        low = (n * o_rows[8:9] + o_rows[6:7]).astype(b16)
        o_nlow_t[:, at] = low.T
        o_res[at] = jnp.dot(low, g_proj[...].reshape(width, wproj.shape[1]), preferred_element_type=f32).astype(b16)

    copies[early + 11].start()
    for k in range(total):
        for stage in range(4):
            for name in piece_names(stage, k):
                transfer(name).wait_send()
    for j in range(3):
        for p in range(3):
            transfer(("a", j, p)).wait_send()
        for d in range(1, Z):
            transfer(("wz", j, d)).wait_send()
        transfer(("wx", j)).wait_send()
    for b in range(streams):
        for kind in ("y", "k0", "k1"):
            transfer((kind, b)).wait_send()

    @pl.loop(0, streams * 2)
    def _(i):
        for p in range(3):
            att_seq(i, p).wait_send()

    for copy in copies:
        copy.wait()


def run_forward(tokens, sizes, wqkv, wout, wup, wdown, wproj, biases, gains, up_bias):
    streams, part, width = tokens.shape
    rows, stream, ff = streams * part, part * Y * C, wup.shape[1]
    proj = wproj.shape[1]
    cols = width // (Y * C)
    grid = (Z, X, Y, C)
    shape = jax.ShapeDtypeStruct
    vmem, hbm = pl.BlockSpec(memory_space=pltpu.VMEM), pl.BlockSpec(memory_space=pl.ANY)
    vm = pltpu.VMEM
    outs = [
        ((grid + wout.shape, b16), hbm),
        (((4,) + grid + (wup.shape[0], ff // 4), b16), hbm),
        ((grid + wdown.shape, b16), hbm),
        ((grid + wproj.shape, b16), hbm),
        (((2,) + grid + (wqkv.shape[0], 3 * PAIR), b16), hbm),
        (((16, width), f32), vmem),
        (((streams, width, stream), b16), hbm),
        (((3, streams, 2, stream, PAIR), b16), hbm),
        (((streams * 2, 8, stream), f32), vmem),
        (((width, rows), b16), hbm),
        (((rows, width), f32), hbm),
        (((rows, 128), f32), vmem),
        (((width, rows), b16), hbm),
        (((ff, rows), b16), hbm),
        (((rows, ff), b16), hbm),
        (((rows, width), f32), hbm),
        (((rows, 128), f32), vmem),
        (((width, rows), b16), vmem),
        (((streams, stream, PAIR), f32), hbm),
        (((streams, stream, PAIR), f32), hbm),
        (((rows, proj), b16), vmem),
    ]
    dma = pltpu.SemaphoreType.DMA
    scratch = [
        vm(grid + wout.shape, b16),
        vm((4,) + grid + (wup.shape[0], ff // 4), b16),
        vm((4,) + grid + (wdown.shape[0], width // 4), b16),
        vm(grid + wproj.shape, b16),
        vm(grid + (16, 128), b16),
        vm((3,) + grid + (wqkv.shape[0], cols), b16),
        vm((streams, Y, C, part, width), b16),
        vm((streams, width, stream), b16),
        vm((3, streams, 2, stream, PAIR), b16),
        vm((streams, 2, Y, C, part, PAIR), b16),
        vm((stream, stream), f32),
        vm((streams, part, width), b16),
        vm((width, rows), b16),
        vm((rows, width), f32),
        vm((rows, width), f32),
        vm((rows, width), b16),
        vm((width, rows), b16),
        vm((rows, ff), b16),
        vm((ff, rows), b16),
        vm((rows, ff), b16),
        vm((rows, width), f32),
        vm((1, ff), f32),
        vm((16, 128), f32),
        vm((streams, stream, PAIR), f32),
        vm((streams, stream, PAIR), f32),
        dma((11, 6)), dma((11, 6)), dma((3, 3)), dma((3, 3)), dma((3, 3)), dma((3, 3)), dma((3,)), dma((3,)),
        dma((streams,)), dma((streams,)), dma((streams, 2)), dma((streams, 2)), dma((streams * 2, 3)), dma((streams * 2, 3)), dma((26,)),
    ]
    return pl.pallas_call(
        forward_kernel,
        out_shape=[shape(*o[0]) for o in outs],
        in_specs=[vmem, pl.BlockSpec(memory_space=pltpu.SMEM)] + [vmem] * 8,
        out_specs=[o[1] for o in outs],
        scratch_shapes=scratch,
        compiler_params=pltpu.CompilerParams(collective_id=3, has_side_effects=True, vmem_limit_bytes=63 << 20),
    )(tokens, sizes, wqkv, wout, wup, wdown, wproj, biases, gains, up_bias)


def turned_back(t, cosine, sine, low_half):
    swapped = jnp.where(low_half, pltpu.roll(t, PAIR - HEAD_DIM // 2, 1), pltpu.roll(t, HEAD_DIM // 2, 1))
    return t * cosine - swapped * sine


BACKWARD_ROUTES = ("xzy", "xyz", "yxz", "xzy", "yzx", "yxz", "yxz", "xyz", "yxz", "yxz", "xyz")
BACKWARD_ORDER = (
    ("ln2b",),
    ("mk", 0),
    ("mk", 2),
    ("mk", 1),
    ("gh", 0),
    ("own", 0),
    ("g1", 0),
    ("own", 2),
    ("mk", 3),
    ("mk", 4),
    ("own", 1),
    ("gh", 1),
    ("mk", 5),
    ("own", 3),
    ("g1", 1),
    ("own", 4),
    ("gh", 2),
    ("g1", 2),
    ("add", 0, 0),
    ("gh", 3),
    ("add", 2, 0),
    ("g1", 3),
    ("ln1b",),
    ("ga", 1),
    ("ga", 2),
    ("mk", 7),
    ("ga", 0),
    ("mk", 8),
    ("ga", 3),
    ("mk", 6),
    ("own", 5),
    ("add", 1, 0),
    ("add", 4, 0),
    ("own", 7),
    ("add", 0, 1),
    ("mk", 9),
    ("own", 8),
    ("own", 6),
    ("own", 9),
    ("at", 0),
    ("add", 3, 0),
    ("at", 1),
    ("add", 2, 1),
    ("at", 2),
    ("add", 5, 0),
    ("q1", 0),
    ("at", 3),
    ("add", 1, 1),
    ("add", 7, 0),
    ("add", 3, 1),
    ("at", 4),
    ("add", 5, 1),
    ("at", 5),
    ("q1", 1),
    ("i1", 0),
    ("i1", 2),
    ("q2", 0),
    ("mk", 10),
    ("i1", 1),
    ("i2", 0),
    ("own", 10),
    ("i2", 2),
    ("add", 8, 0),
    ("add", 4, 1),
    ("i3", 2),
    ("i2", 1),
    ("fin", 1),
    ("i3", 0),
    ("i3", 1),
    ("fin", 0),
    ("fin", 5),
    ("fin", 2),
    ("q2", 1),
    ("add", 10, 0),
    ("add", 6, 0),
    ("add", 9, 0),
    ("q3", 0),
    ("add", 8, 1),
    ("add", 7, 1),
    ("fin", 4),
    ("fin", 3),
    ("q3", 1),
    ("add", 6, 1),
    ("add", 9, 1),
    ("i4", 0),
    ("fin", 8),
    ("i4", 2),
    ("fin", 7),
    ("i4", 1),
    ("add", 10, 1),
    ("fin", 6),
    ("q4", 0),
    ("fin", 9),
    ("fin", 10),
    ("q4", 1),
)


def backward_kernel(
    w_out, w_up, w_down, w_proj, w_cols, side_rows, i_tok_t, i_qkv, lse, i_att_t, i_n1, r_one, i_hlow_t, i_hid_t, i_dgelu, i_n2, r_two, nlow_t,
    sizes, cot_f, cos4, sin4,
    o_in, o_qkv, o_out, o_up, o_down, o_proj, o_side,
    ring, gelu_ring, norm, att_t, h_low_t, hid_t, qkv, cols_one, sums, sum_up, grad_ffn, grad_u, grad_branch, grad_att, heads, far, turned,
    send_d, send_u, send_o, send_p, send_s, cot,
    q_send, q_x, q_z, q_seq, q_in, i_send, i_c, i_y_send, i_y,
    c_send, c_recv, a_send, a_recv, qx_send, qx_recv, qz_send, qz_recv, qs_send, qs_recv, ic_send, ic_recv, iy_send, iy_recv,
    load, ring_sem, gelu_sem, *pieces,
):
    rows, width = o_in.shape
    streams = qkv.shape[1]
    part, stream = rows // streams, qkv.shape[3]
    ff = grad_u.shape[1]
    quarter, down_cols = ff // 4, width // 4
    cols = width // (Y * C)
    block = 256
    r_block = 128
    z, x, y, c = place()
    s = y * C + c
    seq_peer = [(y, 1 - c), (1 - y, c), (1 - y, 1 - c)]
    others = [(z + d) % Z for d in range(1, Z)]
    nt = (((1,), (1,)), ((), ()))

    def fetch(src, dst, i):
        return pltpu.make_async_copy(src, dst, load.at[i])

    first_loads = [fetch(i_n2, norm, 0), fetch(i_hid_t, hid_t, 1), fetch(i_hlow_t, h_low_t, 2), fetch(i_att_t, att_t, 3), fetch(i_qkv, qkv, 4)]
    second_norm = fetch(i_n1, norm, 5)
    tok_loads = [fetch(i_tok_t.at[b], ring.at[b // 2, :, pl.ds((b % 2) * stream, stream)], 6 + b) for b in range(streams)]
    col_loads = [fetch(w_cols.at[0], ring.at[1, :, pl.ds(stream, 3 * PAIR)], 6 + streams), fetch(w_cols.at[1], cols_one, 7 + streams)]
    blocks = []
    for j in range(4):
        blocks += [w_down.at[pl.ds(j * quarter, quarter)], w_up.at[j]]
    blocks.append(w_out)

    def stream_in(i):
        return pltpu.make_async_copy(blocks[i], ring.at[i % 2], ring_sem.at[i])

    def gelu_in(j):
        return pltpu.make_async_copy(i_dgelu.at[:, pl.ds(j * quarter, quarter)], gelu_ring.at[j % 2], gelu_sem.at[j])

    first_loads[0].start()
    stream_in(0).start()
    gelu_in(0).start()
    stream_in(1).start()
    gelu_in(1).start()
    for copy in first_loads[1:]:
        copy.start()
    greet(
        [device(zz, x, y, c) for zz in others]
        + [device(z, 1 - x, y, c)]
        + [device(z, x, yy, cc) for yy, cc in seq_peer]
    )

    outgoing = [None] * 8 + [send_o, send_p, send_s.at[:, :, :, 1 - c]]
    total = len(outgoing)
    held, landed = pieces[:total], [pieces[total + 3 * k : total + 3 * k + 3] for k in range(total)]
    own_spot = {"z": z, "x": x, "y": y}
    axis_size = {"z": Z, "x": X, "y": Y}

    def to_core(k):
        return send_to(outgoing[k], held[k], c_send.at[k, 8], c_recv.at[k, 8], device(z, x, y, 1 - c))

    def along(k, stage):
        route = BACKWARD_ROUTES[k]
        axis = route[stage]
        if axis == "z":
            peers = [(others[d], device(others[d], x, y, c)) for d in range(Z - 1)]
        else:
            peers = [(1 - x, device(z, 1 - x, y, c))] if axis == "x" else [(1 - y, device(z, x, 1 - y, c))]
        copies = []
        for d, (spot, peer) in enumerate(peers):
            at = {a: own_spot[a] if a in route[:stage] else slice(None) for a in "zxy"} | {axis: spot}
            dst = landed[k][stage].at[d] if axis == "z" else landed[k][stage]
            slot = d if axis == "z" else 3 + stage
            copies.append(send_to(held[k].at[at["z"], at["x"], at["y"]], dst, c_send.at[k, slot], c_recv.at[k, slot], peer))
        return copies

    def begin(k, stage):
        for copy in along(k, stage):
            copy.start()

    def arrived(k, stage):
        for copy in along(k, stage):
            copy.wait_recv()

    def add_landed(k, stage):
        route = BACKWARD_ROUTES[k]
        arrived(k, stage)
        rest = [a for a in "zxy" if a not in route[: stage + 1]]
        count = math.prod(axis_size[a] for a in rest)

        @pl.loop(0, count)
        def _(i):
            at, spot = dict(own_spot), []
            for a in reversed(rest):
                at[a] = i % axis_size[a]
                spot.insert(0, at[a])
                i = i // axis_size[a]
            here = (at["z"], at["x"], at["y"])
            value = held[k][here].astype(f32)
            if route[stage] == "z":
                for d in range(Z - 1):
                    value = value + landed[k][stage][(d, *spot)].astype(f32)
            else:
                value = value + landed[k][stage][tuple(spot)].astype(f32)
            held[k][here] = value.astype(b16)

        begin(k, stage + 1)

    def half_down(j, core, zz):
        a = hid_t[zz, :, :, core].reshape(-1, rows)
        return jnp.dot(a, grad_ffn[:, j * down_cols : (j + 1) * down_cols], preferred_element_type=f32)

    def half_rows(a_t, core, b, at):
        return jnp.dot(a_t[:, :, :, core].reshape(-1, rows), b[:, at], preferred_element_type=f32)

    taken = {}

    def free_slot(kind, k):
        used = taken.setdefault(kind, [])
        if len(used) >= 2:
            to_core(used[-2]).wait_send()
        used.append(k)
        outgoing[k] = (send_d, send_u)[kind].at[(len(used) - 1) % 2]
        return (len(used) - 1) % 2

    def make_send(k):
        if k < 4:
            slot = free_slot(0, k)

            @pl.loop(0, Z)
            def _(zz):
                send_d[slot, zz] = half_down(k, 1 - c, zz).astype(b16).reshape(X, Y, -1, down_cols)

        elif k < 9:
            a_t, b = (h_low_t, grad_u) if k < 8 else (att_t, grad_branch)
            slot = free_slot(1, k) if k < 8 else 0

            @pl.loop(0, width // block)
            def _(n):
                at = pl.ds(pl.multiple_of(n * block, block), block)
                col = pl.ds(pl.multiple_of(((k - 4) * quarter if k < 8 else 0) + n * block, block), block)
                got = half_rows(a_t, 1 - c, b, col).astype(b16).reshape(Z, X, Y, -1, block)
                if k < 8:
                    send_u[slot, :, :, :, :, at] = got
                else:
                    send_o[:, :, :, :, at] = got

        elif k == 9:
            send_p[...] = half_rows(nlow_t, 1 - c, cot, slice(None)).astype(b16).reshape(Z, X, Y, -1, cot.shape[1])
        to_core(k).start()

    def own_half(k):
        to_core(k).wait_recv()
        mine = held[k]
        if k < 4:

            @pl.loop(0, Z)
            def _(zz):
                got = half_down(k, c, zz).reshape(X, Y, -1, down_cols)
                mine[zz] = (mine[zz].astype(f32) + got).astype(b16)

        elif k < 9:
            a_t, b = (h_low_t, grad_u) if k < 8 else (att_t, grad_branch)

            @pl.loop(0, width // block)
            def _(n):
                at = pl.ds(pl.multiple_of(n * block, block), block)
                col = pl.ds(pl.multiple_of(((k - 4) * quarter if k < 8 else 0) + n * block, block), block)
                got = half_rows(a_t, c, b, col).reshape(Z, X, Y, -1, block)
                mine[:, :, :, :, at] = (mine[:, :, :, :, at].astype(f32) + got).astype(b16)

        elif k == 9:
            got = half_rows(nlow_t, c, cot, slice(None)).reshape(Z, X, Y, -1, cot.shape[1])
            mine[...] = (mine[...].astype(f32) + got).astype(b16)
        else:
            mine[...] = (mine[...].astype(f32) + send_s[:, :, :, c].astype(f32)).astype(b16)
        begin(k, 0)

    def finish(k):
        arrived(k, 2)
        value = held[k][z, x, y].astype(f32)
        if BACKWARD_ROUTES[k][2] == "z":
            for d in range(Z - 1):
                value = value + landed[k][2][d].astype(f32)
        else:
            value = value + landed[k][2][...].astype(f32)
        if k < 4:
            o_down[:, k * down_cols : (k + 1) * down_cols] = value
        elif k < 8:
            o_up[:, (k - 4) * quarter : (k - 3) * quarter] = value
        else:
            (o_out, o_proj, o_side)[k - 8][...] = value

    sums[...] = jnp.zeros_like(sums)

    def norm_back(e, gain_row, n, inverse, at, low_ref, spots):
        ge = e * side_rows[gain_row : gain_row + 1]
        mean = jnp.mean(ge, axis=-1, keepdims=True)
        along = jnp.mean(ge * n, axis=-1, keepdims=True)
        grad = inverse * (ge - mean - n * along)
        low = grad.astype(b16)
        o_in[at] = grad
        low_ref[at] = low
        for spot, value in zip(spots, (e * n, e, low.astype(f32))):
            sums[spot : spot + 1] += jnp.sum(value, axis=0, keepdims=True)

    def second_norm_back():
        cot[...] = cot_f[...].astype(b16)
        first_loads[0].wait()

        @pl.loop(0, rows // r_block)
        def _(r):
            at = pl.ds(pl.multiple_of(r * r_block, r_block), r_block)
            e = lax.dot_general(cot[at], w_proj[...], nt, preferred_element_type=f32)
            norm_back(e, 8, norm[at], r_two[at, :1], at, grad_ffn, (8, 6, 5))

        second_norm.start()
        for copy in first_loads[1:]:
            copy.wait()

    def hidden_back(j):
        stream_in(2 * j).wait()
        gelu_in(j).wait()

        @pl.loop(0, quarter // block)
        def _(n):
            at = pl.ds(pl.multiple_of(n * block, block), block)
            col = pl.ds(pl.multiple_of(j * quarter + n * block, block), block)
            got = lax.dot_general(grad_ffn[...], ring[0, at], nt, preferred_element_type=f32)
            low = (got * gelu_ring[j % 2, :, at].astype(f32)).astype(b16)
            grad_u[:, col] = low
            sum_up[:, col] = jnp.sum(low.astype(f32), axis=0, keepdims=True)

        stream_in(2 * j + 2).start()
        if j < 2:
            gelu_in(j + 2).start()

    def inner_back(j):
        stream_in(2 * j + 1).wait()

        @pl.loop(0, width // block)
        def _(n):
            at = pl.ds(pl.multiple_of(n * block, block), block)
            o_in[:, at] += lax.dot_general(
                grad_u[:, j * quarter : (j + 1) * quarter], ring[1, at], nt, preferred_element_type=f32
            )

        if j < 3:
            stream_in(2 * j + 3).start()

    def first_norm_back():
        second_norm.wait()

        @pl.loop(0, rows // r_block)
        def _(r):
            at = pl.ds(pl.multiple_of(r * r_block, r_block), r_block)
            norm_back(o_in[at], 7, norm[at], r_one[at, :1], at, grad_branch, (7, 4, 3))

    def att_seq(p):
        yy, cc = seq_peer[p]
        src = grad_att.at[:, :, pl.ds(pl.multiple_of((yy * C + cc) * cols, cols), cols)]
        return send_to(src, heads.at[:, y, c], a_send.at[p], a_recv.at[p], device(z, x, yy, cc))

    def grad_heads(to):
        at = pl.ds(pl.multiple_of(to * cols, cols), cols)
        got = lax.dot_general(grad_branch[...], ring[0, at], nt, preferred_element_type=f32)
        grad_att[:, :, at] = got.astype(b16).reshape(streams, part, cols)

    sent = []

    def att_back_send(p):
        if not sent:
            stream_in(8).wait()
        sent.append(p)
        if p < 3:
            yy, cc = seq_peer[p]
            grad_heads(yy * C + cc)
            att_seq(p).start()
        else:
            grad_heads(s)
            heads[:, y, c] = grad_att[:, :, pl.ds(pl.multiple_of(s * cols, cols), cols)]
        if len(sent) == 4:
            for copy in tok_loads + col_loads:
                copy.start()

    lane = lax.broadcasted_iota(jnp.int32, (1, PAIR), 1)
    low_half = (lane % HEAD_DIM) < HEAD_DIM // 2
    top = lax.broadcasted_iota(jnp.int32, (PAIR, 1), 0) < HEAD_DIM
    masks = [(lane < HEAD_DIM).astype(f32).astype(b16), (lane >= HEAD_DIM).astype(f32).astype(b16)]
    score_scale = HEAD_DIM**-0.5
    q_block = stream // 2

    def attend_back(i):
        half, b = i // streams, i % streams
        far[...] = far_keys(sizes, b, stream)
        queries, keys, values = qkv[0, b, half], qkv[1, b, half], qkv[2, b, half]
        given = heads[b, :, :, :, pl.ds(pl.multiple_of(half * PAIR, PAIR), PAIR)].reshape(stream, PAIR)
        keys_t = keys.T
        grad_k, grad_v = jnp.zeros((stream, PAIR), f32), jnp.zeros((stream, PAIR), f32)
        grad_q = []
        for part_q in range(2):
            at = slice(part_q * q_block, (part_q + 1) * q_block)
            q_t = []
            for head in range(2):
                q = queries[at] * (masks[head] * b16(score_scale))
                g = given[at] * masks[head]
                scores = lax.dot_general(keys, q, nt, preferred_element_type=f32) + far[:, at]
                probs = jnp.exp(scores - lse[b * 2 + half, head : head + 1, at])
                grad_p = lax.dot_general(values, g, nt, preferred_element_type=f32)
                row_dot = jnp.sum(probs * grad_p, axis=0, keepdims=True)
                grad_s = (probs * (grad_p - row_dot)).astype(b16)
                grad_v = grad_v + jnp.dot(probs.astype(b16), g, preferred_element_type=f32)
                grad_k = grad_k + jnp.dot(grad_s, q, preferred_element_type=f32)
                q_t.append(jnp.dot(keys_t, grad_s, preferred_element_type=f32))
            grad_q.append(jnp.where(top, q_t[0], q_t[1]).T * score_scale)
        grad_q = jnp.concatenate(grad_q, axis=0)
        lane_at = pl.multiple_of(s * cols + half * PAIR, PAIR)
        done = []
        for t in (grad_q, grad_k):
            done.append(turned_back(t.astype(b16).astype(f32), cos4[b], sin4[b], low_half).astype(b16))
        done.append(grad_v.astype(b16))
        for j in range(3):
            turned[half, b, :, j * PAIR : (j + 1) * PAIR] = done[j]
            sums[j : j + 1, pl.ds(lane_at, PAIR)] += jnp.sum(done[j].astype(f32), axis=0, keepdims=True)

    def qkv_rows(half, zz, xx):
        at = pl.ds(pl.multiple_of((zz * X + xx) * 128, 128), 128)
        got = jnp.zeros((128, 3 * PAIR), f32)
        for b in range(streams):
            got = got + jnp.dot(
                ring[b // 2, at, (b % 2) * stream : (b % 2 + 1) * stream], turned[half, b], preferred_element_type=f32
            )
        return got

    def qkv_x(half):
        return send_to(q_send.at[half], q_x.at[half], qx_send.at[half], qx_recv.at[half], device(z, 1 - x, y, c))

    def qkv_z(half, d):
        return send_to(q_x.at[half, others[d]], q_z.at[half, d], qz_send.at[half, d], qz_recv.at[half, d], device(others[d], x, y, c))

    def qkv_seq(half, p):
        yy, cc = seq_peer[p]
        return send_to(q_seq.at[half, yy, cc], q_in.at[half, y, c], qs_send.at[half, p], qs_recv.at[half, p], device(z, x, yy, cc))

    def qkv_one(half):
        @pl.loop(0, Z)
        def _(zz):
            q_send[half, zz] = qkv_rows(half, zz, 1 - x).astype(b16)

        qkv_x(half).start()

    def qkv_two(half):
        qkv_x(half).wait_recv()

        @pl.loop(0, Z)
        def _(zz):
            q_x[half, zz] = (q_x[half, zz].astype(f32) + qkv_rows(half, zz, x)).astype(b16)

        for d in range(Z - 1):
            qkv_z(half, d).start()

    def qkv_three(half):
        value = q_x[half, z].astype(f32)
        for d in range(Z - 1):
            qkv_z(half, d).wait_recv()
        for d in range(Z - 1):
            value = value + q_z[half, d].astype(f32)
        q_seq[half] = value.reshape(Y, C, -1, 3 * PAIR)
        for p in range(3):
            qkv_seq(half, p).start()
        q_in[half, y, c] = q_seq[half, y, c]

    def qkv_four(half):
        for p in range(3):
            qkv_seq(half, p).wait_recv()
        for owner in range(Y * C):
            for j in range(3):
                lane_at = j * width + owner * cols + half * PAIR
                o_qkv[:, lane_at : lane_at + PAIR] = q_in[half, owner // C, owner % C, :, j * PAIR : (j + 1) * PAIR]

    def in_c(b):
        return send_to(i_send.at[b], i_c.at[b], ic_send.at[b], ic_recv.at[b], device(z, x, y, 1 - c))

    def in_y(b):
        return send_to(i_y_send.at[b], i_y.at[b], iy_send.at[b], iy_recv.at[b], device(z, x, 1 - y, c))

    def input_rows(b, yy, cc):
        at = pl.ds(pl.multiple_of((yy * C + cc) * part, part), part)
        got = lax.dot_general(turned[0, b, at], ring[1, :, stream : stream + 3 * PAIR], nt, preferred_element_type=f32)
        return got + lax.dot_general(turned[1, b, at], cols_one[...], nt, preferred_element_type=f32)

    def input_one(b):
        for yy in range(Y):
            i_send[b, yy] = input_rows(b, yy, 1 - c).astype(b16)
        in_c(b).start()

    def input_two(b):
        in_c(b).wait_recv()
        i_y_send[b] = (input_rows(b, 1 - y, c) + i_c[b, 1 - y].astype(f32)).astype(b16)
        in_y(b).start()

    def input_three(b):
        o_in[b * part : (b + 1) * part] += input_rows(b, y, c) + i_c[b, y].astype(f32)

    def input_four(b):
        in_y(b).wait_recv()
        o_in[b * part : (b + 1) * part] += i_y[b].astype(f32)

    def small_sums():
        lanes = lax.broadcasted_iota(jnp.int32, (16, 128), 1)
        spots = lax.broadcasted_iota(jnp.int32, (16, 128), 0)
        share = 128 // (Y * C)
        for zx in range(Z * X):
            tile = sums[:, zx * 128 : (zx + 1) * 128]
            for yc in range(Y * C):
                owner = zx * Y * C + yc
                moved = pltpu.roll(tile, (128 - yc * share) % 128, 1) if yc else tile
                value = jnp.where(lanes < share, moved, 0.0)
                value = jnp.where(spots == 9, sum_up[:, owner * 128 : (owner + 1) * 128], value)
                send_s[zx // X, zx % X, yc // C, yc % C] = value.astype(b16)
        to_core(10).start()

    work = {
        "ln2b": second_norm_back, "gh": hidden_back, "g1": inner_back, "ln1b": first_norm_back, "ga": att_back_send,
        "mk": lambda k: make_send(k) if k < 10 else small_sums(), "own": own_half, "add": add_landed, "fin": finish,
        "q1": qkv_one, "q2": qkv_two, "q3": qkv_three, "q4": qkv_four,
        "i1": input_one, "i2": input_two, "i3": input_three, "i4": input_four,
    }
    spots = [i for i, name in enumerate(BACKWARD_ORDER) if name[0] == "at"]

    def run(first_spot, last_spot):
        for name in BACKWARD_ORDER[first_spot:last_spot]:
            work[name[0]](*name[1:])

    run(0, spots[0])

    def before(i):
        if i == 0:
            for p in range(3):
                att_seq(p).wait_recv()
            for copy in tok_loads + col_loads:
                copy.wait()
        else:
            run(spots[i - 1] + 1, spots[i])

    @pl.loop(0, streams * 2)
    def _(i):
        at_index(i, {spot: functools.partial(before, spot) for spot in range(streams * 2)})
        attend_back(i)

    run(spots[-1] + 1, len(BACKWARD_ORDER))

    for k in range(total):
        if k >= 8 or k in (taken[0][-2:] + taken[1][-2:]):
            to_core(k).wait_send()
        for stage in range(3):
            for copy in along(k, stage):
                copy.wait_send()
    for p in range(3):
        att_seq(p).wait_send()
        for half in range(2):
            qkv_seq(half, p).wait_send()
    for half in range(2):
        qkv_x(half).wait_send()
        for d in range(Z - 1):
            qkv_z(half, d).wait_send()
    for b in range(streams):
        in_c(b).wait_send()
        in_y(b).wait_send()


def run_backward(kept, sizes, cot):
    (
        w_out, w_up, w_down, w_proj, w_cols, side_rows, tok_t, qkv, lse, att_t, n_one, r_one, h_low_t, hid_t, dgelu, n_two, r_two, nlow_t, cos4, sin4,
    ) = kept
    rows, width = n_one.shape
    ff = dgelu.shape[1]
    streams, _, stream = tok_t.shape
    proj = w_proj.shape[-1]
    cols, quarter, down_cols = width // (Y * C), ff // 4, width // 4
    grid = (Z, X, Y, C)
    part = rows // streams
    vm, dma = pltpu.VMEM, pltpu.SemaphoreType.DMA
    vmem, hbm = pl.BlockSpec(memory_space=pltpu.VMEM), pl.BlockSpec(memory_space=pl.ANY)
    owner = width // OWNERS
    tails = [(ff // OWNERS, down_cols)] * 4 + [(owner, quarter)] * 4 + [(owner, width), (owner, proj), (16, 128)]
    inputs = [
        (w_out.reshape(width, width), hbm), (w_up.reshape(4, width, quarter), hbm), (w_down.reshape(ff, width), hbm),
        (w_proj.reshape(width, proj), vmem), (w_cols.reshape(2, width, 3 * PAIR), hbm), (side_rows, vmem), (tok_t, hbm), (qkv, hbm),
        (lse, vmem), (att_t.reshape(grid + (owner, rows)), hbm), (n_one, hbm), (r_one, vmem), (h_low_t.reshape(grid + (owner, rows)), hbm),
        (hid_t.reshape(grid + (ff // OWNERS, rows)), hbm), (dgelu, hbm), (n_two, hbm), (r_two, vmem), (nlow_t.reshape(grid + (owner, rows)), vmem),
        (sizes, pl.BlockSpec(memory_space=pltpu.SMEM)), (cot, vmem), (cos4, vmem), (sin4, vmem),
    ]
    scratch = [
        vm((2, width, width), b16), vm((2, rows, quarter), b16), vm((rows, width), f32),
        vm(grid + (owner, rows), b16), vm(grid + (owner, rows), b16), vm(grid + (ff // OWNERS, rows), b16),
        vm(qkv.shape, b16), vm((width, 3 * PAIR), b16), vm((16, width), f32), vm((1, ff), f32),
        vm((rows, width), b16), vm((rows, ff), b16), vm((rows, width), b16), vm((streams, part, width), b16),
        vm((streams, Y, C, part, cols), b16), vm((stream, stream), f32), vm((2, streams, stream, 3 * PAIR), b16),
        vm((2, Z, X, Y) + tails[0], b16), vm((2, Z, X, Y) + tails[4], b16), vm((Z, X, Y) + tails[8], b16), vm((Z, X, Y) + tails[9], b16),
        vm(grid + tails[10], b16), vm(cot.shape, b16),
    ]
    scratch += [
        vm((2, Z, 128, 3 * PAIR), b16), vm((2, Z, 128, 3 * PAIR), b16), vm((2, Z - 1, 128, 3 * PAIR), b16),
        vm((2, Y, C, 32, 3 * PAIR), f32), vm((2, Y, C, 32, 3 * PAIR), f32),
        vm((streams, Y, part, width), b16), vm((streams, Y, part, width), b16), vm((streams, part, width), b16), vm((streams, part, width), b16),
        dma((11, 9)), dma((11, 9)), dma((3,)), dma((3,)), dma((2,)), dma((2,)), dma((2, 3)), dma((2, 3)), dma((2, 3)), dma((2, 3)),
        dma((streams,)), dma((streams,)), dma((streams,)), dma((streams,)),
        dma((8 + streams,)), dma((9,)), dma((4,)),
    ]
    size = {"z": Z, "x": X, "y": Y}
    scratch += [vm((Z, X, Y) + tail, b16) for tail in tails]
    for route, tail in zip(BACKWARD_ROUTES, tails):
        for stage in range(3):
            rest = tuple(size[a] for a in "zxy" if a not in route[: stage + 1])
            scratch.append(vm(((Z - 1,) if route[stage] == "z" else ()) + rest + tail, b16))
    outs = [(rows, width), (owner, 3 * width), (owner, width), (owner, ff), (ff // OWNERS, width), (owner, proj), (16, 128)]
    return pl.pallas_call(
        backward_kernel,
        out_shape=[jax.ShapeDtypeStruct(o, f32) for o in outs],
        in_specs=[spec for _, spec in inputs],
        out_specs=[vmem] * len(outs),
        scratch_shapes=scratch,
        compiler_params=pltpu.CompilerParams(collective_id=4, has_side_effects=True, vmem_limit_bytes=63 << 20),
    )(*[a for a, _ in inputs])


def layer_norm(field, gain_row, shift_row):
    average = jnp.mean(field, axis=-1, keepdims=True)
    centred = field - average
    variance = jnp.mean(centred * centred, axis=-1, keepdims=True)
    return centred * lax.rsqrt(variance + epsilon) * gain_row + shift_row


def doc_layout(doc_sizes, places):
    doc_ends = jnp.cumsum(doc_sizes)
    passed = places[:, None] >= doc_ends[None, :]
    segment = jnp.sum(passed.astype(jnp.int32), axis=1)
    starts = jnp.sum(jnp.where(passed, doc_sizes[None, :], 0), axis=1)
    return (segment, places - starts)


def rope_tables(position, half_dim):
    steps_f = jnp.arange(half_dim, dtype=jnp.float32)
    inverse = jnp.exp(steps_f * (-math.log(rope_base) / half_dim))
    angle = position.astype(jnp.float32)[:, None] * inverse[None, :]
    return (jnp.cos(angle), jnp.sin(angle))


def rotate(field, cosine, sine_tab, head_count):
    length = field.shape[0]
    halves = field.reshape(length, head_count, 2, -1)
    first_half = halves[:, :, 0]
    second_half = halves[:, :, 1]
    cos_b = cosine[:, None, :]
    sin_b = sine_tab[:, None, :]
    turned = jnp.stack(
        [first_half * cos_b - second_half * sin_b, second_half * cos_b + first_half * sin_b], axis=2
    )
    return turned.reshape(length, -1)


def gelu_exact(field):
    return jax.nn.gelu(field, approximate=False)


def scores_of(query_blk, seg_blk, keys_all, stream_seg, score_scale):
    raw_scores = (
        jnp.einsum("qhd,khd->hqk", query_blk, keys_all, preferred_element_type=jnp.float32)
        * score_scale
    )
    same_doc = (seg_blk[:, None] == stream_seg[None, :])[None]
    return jnp.where(same_doc, raw_scores, neg_fill)


def per_device_any(
    tokens,
    doc_lengths,
    qkv_weight,
    out_weight,
    up_weight,
    down_weight,
    proj_weight,
    biases,
    gains,
    up_bias,
    cotangent,
):
    stream_count = tokens.shape[0]
    seg_rows = tokens.shape[1]
    model_width = tokens.shape[2]
    seq_parts = lax.axis_size("seq")
    stream = seg_rows * seq_parts
    head_count = model_width // HEAD_DIM
    local_heads = head_count // seq_parts
    flat_width = local_heads * HEAD_DIM
    score_scale = HEAD_DIM ** (-0.5)
    tok_flat = tokens.reshape(stream_count * seg_rows, model_width)
    gathered = (
        lax.all_gather(qkv_weight, ("rows", "seq"), axis=0, tiled=True),
        lax.all_gather(out_weight, ("rows", "seq"), axis=0, tiled=True),
        lax.all_gather(up_weight, ("rows", "seq"), axis=0, tiled=True),
        lax.all_gather(down_weight, ("rows", "seq"), axis=0, tiled=True),
        lax.all_gather(proj_weight, ("rows", "seq"), axis=0, tiled=True),
        lax.all_gather(biases, ("rows", "seq"), axis=1, tiled=True),
        lax.all_gather(gains, ("rows", "seq"), axis=1, tiled=True),
        lax.all_gather(up_bias, ("rows", "seq"), axis=0, tiled=True),
    )
    w_qkv, w_out, w_up, w_down, w_proj = (
        gathered[0],
        gathered[1],
        gathered[2],
        gathered[3],
        gathered[4],
    )
    bias_rows = gathered[5].astype(jnp.float32)
    gain_rows = gathered[6].astype(jnp.float32)
    bias_up = gathered[7].astype(jnp.float32)
    token_places = lax.axis_index("seq") * seg_rows + jnp.arange(seg_rows, dtype=jnp.int32)
    layout_rows = jax.vmap(doc_layout, in_axes=(0, None))
    token_seg, position = layout_rows(doc_lengths, token_places)
    cosine, sine_tab = rope_tables(position.reshape(-1), HEAD_DIM // 2)
    projected = jnp.dot(tok_flat, w_qkv, preferred_element_type=jnp.float32) + bias_rows[
        0:3
    ].reshape(-1)
    queries = (
        rotate(projected[:, :model_width], cosine, sine_tab, head_count)
        .astype(jnp.bfloat16)
        .reshape(stream_count, seg_rows, model_width)
    )
    keys_tok = (
        rotate(projected[:, model_width : 2 * model_width], cosine, sine_tab, head_count)
        .astype(jnp.bfloat16)
        .reshape(stream_count, seg_rows, model_width)
    )
    values_tok = (
        projected[:, 2 * model_width :]
        .astype(jnp.bfloat16)
        .reshape(stream_count, seg_rows, model_width)
    )
    queries_h, keys_h, values_h = (
        lax.all_to_all(queries, "seq", split_axis=2, concat_axis=1, tiled=True),
        lax.all_to_all(keys_tok, "seq", split_axis=2, concat_axis=1, tiled=True),
        lax.all_to_all(values_tok, "seq", split_axis=2, concat_axis=1, tiled=True),
    )
    stream_seg, stream_pos = layout_rows(doc_lengths, jnp.arange(stream, dtype=jnp.int32))
    block_rows = math.gcd(stream, 512)
    block_count = stream // block_rows

    def forward_stream(element):
        query_s, key_s, value_s, seg_s = element
        query_blocks = query_s.reshape(block_count, block_rows, local_heads, HEAD_DIM)
        keys_all = key_s.reshape(stream, local_heads, HEAD_DIM)
        values_all = value_s.reshape(stream, local_heads, HEAD_DIM)
        seg_blocks = seg_s.reshape(block_count, block_rows)

        def forward_block(inner):
            query_blk, seg_blk = inner
            scores = scores_of(query_blk, seg_blk, keys_all, seg_s, score_scale)
            row_max = jnp.max(scores, axis=-1, keepdims=True)
            row_total = jnp.sum(jnp.exp(scores - row_max), axis=-1, keepdims=True)
            log_total = row_max + jnp.log(row_total)
            probs_low = jnp.exp(scores - log_total).astype(jnp.bfloat16)
            attn_blk = jnp.einsum(
                "hqk,khd->qhd", probs_low, values_all, preferred_element_type=jnp.float32
            )
            return (attn_blk.astype(jnp.bfloat16), log_total[:, :, 0])

        attn_blocks, log_blocks = lax.map(forward_block, (query_blocks, seg_blocks))
        return (attn_blocks.reshape(stream, flat_width), log_blocks)

    attn_heads, log_totals = lax.map(forward_stream, (queries_h, keys_h, values_h, stream_seg))
    attended = lax.all_to_all(attn_heads, "seq", split_axis=1, concat_axis=2, tiled=True).reshape(
        stream_count * seg_rows, model_width
    )
    branch = jnp.dot(attended, w_out, preferred_element_type=jnp.float32) + bias_rows[3]
    h_one, norm_one = jax.vjp(
        layer_norm, tok_flat.astype(jnp.float32) + branch, gain_rows[0], bias_rows[4]
    )
    h_low = h_one.astype(jnp.bfloat16)
    u_pre = jnp.dot(h_low, w_up, preferred_element_type=jnp.float32) + bias_up
    hidden_f, gelu_back = jax.vjp(gelu_exact, u_pre)
    hidden = hidden_f.astype(jnp.bfloat16)
    ffn_out = jnp.dot(hidden, w_down, preferred_element_type=jnp.float32) + bias_rows[5]
    normed, norm_two = jax.vjp(layer_norm, h_one + ffn_out, gain_rows[1], bias_rows[6])
    normed_low = normed.astype(jnp.bfloat16)
    result = jnp.dot(normed_low, w_proj, preferred_element_type=jnp.float32).astype(jnp.bfloat16)
    w_qkv, w_out, w_up, w_down, w_proj = (
        lax.all_gather(qkv_weight, ("rows", "seq"), axis=0, tiled=True),
        lax.all_gather(out_weight, ("rows", "seq"), axis=0, tiled=True),
        lax.all_gather(up_weight, ("rows", "seq"), axis=0, tiled=True),
        lax.all_gather(down_weight, ("rows", "seq"), axis=0, tiled=True),
        lax.all_gather(proj_weight, ("rows", "seq"), axis=0, tiled=True),
    )
    cot_low = cotangent.reshape(stream_count * seg_rows, -1).astype(jnp.bfloat16)
    proj_part = jnp.dot(normed_low.T, cot_low, preferred_element_type=jnp.float32)
    grad_normed = jnp.dot(cot_low, w_proj.T, preferred_element_type=jnp.float32)
    grad_z2, grad_g2, grad_b2 = norm_two(grad_normed)
    grad_ffn = grad_z2.astype(jnp.bfloat16)
    grad_c2 = jnp.sum(grad_ffn, axis=0, dtype=jnp.float32)
    down_part = jnp.dot(hidden.T, grad_ffn, preferred_element_type=jnp.float32)
    grad_hidden = jnp.dot(grad_ffn, w_down.T, preferred_element_type=jnp.float32)
    grad_u = gelu_back(grad_hidden)[0].astype(jnp.bfloat16)
    grad_c1 = jnp.sum(grad_u, axis=0, dtype=jnp.float32)
    up_part = jnp.dot(h_low.T, grad_u, preferred_element_type=jnp.float32)
    ffn_sums = (up_part, down_part, proj_part, grad_c1)
    grad_h1 = grad_z2 + jnp.dot(grad_u, w_up.T, preferred_element_type=jnp.float32)
    grad_z1, grad_g1, grad_b1 = norm_one(grad_h1)
    grad_branch = grad_z1.astype(jnp.bfloat16)
    grad_bo = jnp.sum(grad_branch, axis=0, dtype=jnp.float32)
    out_part = jnp.dot(attended.T, grad_branch, preferred_element_type=jnp.float32)
    grad_attn = jnp.dot(grad_branch, w_out.T, preferred_element_type=jnp.float32).astype(
        jnp.bfloat16
    )
    grad_heads = lax.all_to_all(
        grad_attn.reshape(stream_count, seg_rows, model_width),
        "seq",
        split_axis=2,
        concat_axis=1,
        tiled=True,
    )

    def backward_stream(element):
        query_s, key_s, value_s, seg_s, log_s, grad_s = element
        query_blocks = query_s.reshape(block_count, block_rows, local_heads, HEAD_DIM)
        keys_all = key_s.reshape(stream, local_heads, HEAD_DIM)
        values_all = value_s.reshape(stream, local_heads, HEAD_DIM)
        seg_blocks = seg_s.reshape(block_count, block_rows)
        grad_blocks = grad_s.reshape(block_count, block_rows, local_heads, HEAD_DIM)

        def backward_block(carried, inner):
            grad_keys, grad_values = carried
            query_blk, seg_blk, log_total, grad_blk = inner
            probs_f = jnp.exp(
                scores_of(query_blk, seg_blk, keys_all, seg_s, score_scale) - log_total[:, :, None]
            )
            grad_values = grad_values + jnp.einsum(
                "hqk,qhd->khd",
                probs_f.astype(jnp.bfloat16),
                grad_blk,
                preferred_element_type=jnp.float32,
            )
            grad_probs = jnp.einsum(
                "qhd,khd->hqk", grad_blk, values_all, preferred_element_type=jnp.float32
            )
            row_dot = jnp.sum(probs_f * grad_probs, axis=-1, keepdims=True)
            grad_scores = (probs_f * (grad_probs - row_dot) * score_scale).astype(jnp.bfloat16)
            grad_query = jnp.einsum(
                "hqk,khd->qhd", grad_scores, keys_all, preferred_element_type=jnp.float32
            )
            grad_keys = grad_keys + jnp.einsum(
                "hqk,qhd->khd", grad_scores, query_blk, preferred_element_type=jnp.float32
            )
            return ((grad_keys, grad_values), grad_query.astype(jnp.bfloat16))

        zero_acc = jnp.zeros((stream, local_heads, HEAD_DIM), jnp.float32)
        (grad_keys, grad_values), grad_queries = lax.scan(
            backward_block, (zero_acc, zero_acc), (query_blocks, seg_blocks, log_s, grad_blocks)
        )
        return (
            grad_queries.reshape(stream, flat_width),
            grad_keys.astype(jnp.bfloat16).reshape(stream, flat_width),
            grad_values.astype(jnp.bfloat16).reshape(stream, flat_width),
        )

    head_q, head_k, head_v = lax.map(
        backward_stream, (queries_h, keys_h, values_h, stream_seg, log_totals, grad_heads)
    )
    back_q, back_k, back_v = (
        lax.all_to_all(head_q, "seq", split_axis=1, concat_axis=2, tiled=True),
        lax.all_to_all(head_k, "seq", split_axis=1, concat_axis=2, tiled=True),
        lax.all_to_all(head_v, "seq", split_axis=1, concat_axis=2, tiled=True),
    )
    flat_rows = stream_count * seg_rows
    turned_q = rotate(
        back_q.reshape(flat_rows, model_width).astype(jnp.float32), cosine, -sine_tab, head_count
    )
    turned_k = rotate(
        back_k.reshape(flat_rows, model_width).astype(jnp.float32), cosine, -sine_tab, head_count
    )
    grad_project = jnp.concatenate(
        [turned_q, turned_k, back_v.reshape(flat_rows, model_width).astype(jnp.float32)], axis=1
    ).astype(jnp.bfloat16)
    grad_bqkv = jnp.sum(grad_project, axis=0, dtype=jnp.float32).reshape(3, model_width)
    qkv_part = jnp.dot(tok_flat.T, grad_project, preferred_element_type=jnp.float32)
    input_grad = grad_z1 + jnp.dot(grad_project, w_qkv.T, preferred_element_type=jnp.float32)
    bias_part = jnp.concatenate(
        [grad_bqkv, jnp.stack([grad_bo, grad_b1, grad_c2, grad_b2])], axis=0
    )
    gain_part = jnp.stack([grad_g1, grad_g2])
    qkv_sum, out_sum, up_sum, down_sum, proj_sum, bias_sum, gain_sum, c1_sum = (
        lax.psum_scatter(qkv_part, ("rows", "seq"), scatter_dimension=0, tiled=True),
        lax.psum_scatter(out_part, ("rows", "seq"), scatter_dimension=0, tiled=True),
        lax.psum_scatter(ffn_sums[0], ("rows", "seq"), scatter_dimension=0, tiled=True),
        lax.psum_scatter(ffn_sums[1], ("rows", "seq"), scatter_dimension=0, tiled=True),
        lax.psum_scatter(ffn_sums[2], ("rows", "seq"), scatter_dimension=0, tiled=True),
        lax.psum_scatter(bias_part, ("rows", "seq"), scatter_dimension=1, tiled=True),
        lax.psum_scatter(gain_part, ("rows", "seq"), scatter_dimension=1, tiled=True),
        lax.psum_scatter(ffn_sums[3], ("rows", "seq"), scatter_dimension=0, tiled=True),
    )
    output = result.reshape(stream_count, seg_rows, -1)
    return (
        output,
        input_grad.reshape(stream_count, seg_rows, model_width),
        qkv_sum,
        out_sum,
        up_sum,
        down_sum,
        proj_sum,
        bias_sum,
        gain_sum,
        c1_sum,
    )


def direct_links():
    return lax.axis_size("rows") == Z * X and lax.axis_size("seq") == Y * C


def copy_out(count, *refs):
    for src, dst in zip(refs[:count], refs[count + 1 :]):
        dst[...] = src[...]
    side, (o_bias, o_gain, o_up) = refs[count], refs[-3:]
    lanes = o_bias.shape[1]
    o_bias[...] = side[:7, :lanes]
    o_gain[...] = side[7:9, :lanes]
    o_up[...] = side[9:10]


def per_device_direct(
    tokens, doc_lengths, qkv_weight, out_weight, up_weight, down_weight, proj_weight, biases, gains, up_bias, cotangent
):
    streams, part, width = tokens.shape
    *kept, result = run_forward(
        tokens, doc_lengths, qkv_weight, out_weight, up_weight, down_weight, proj_weight, biases, gains, up_bias.reshape(1, -1)
    )
    *big, side_sum = run_backward(kept, doc_lengths, cotangent.reshape(streams * part, -1))
    lanes = biases.shape[1]
    shape = jax.ShapeDtypeStruct
    vmem = pl.BlockSpec(memory_space=pltpu.VMEM)
    input_grad, qkv, out, up, down, proj, bias_sum, gain_sum, up_sum = pl.pallas_call(
        functools.partial(copy_out, len(big)),
        out_shape=[shape(a.shape, f32) for a in big] + [shape((7, lanes), f32), shape((2, lanes), f32), shape((1, 128), f32)],
        in_specs=[vmem] * (len(big) + 1),
        out_specs=[vmem] * (len(big) + 3),
    )(*big, side_sum)
    return (
        result.reshape(streams, part, -1),
        input_grad.reshape(streams, part, width),
        qkv,
        out,
        up,
        down,
        proj,
        bias_sum,
        gain_sum,
        up_sum.reshape(-1),
    )


def per_device(*args):
    return per_device_direct(*args) if direct_links() else per_device_any(*args)


def solution(mesh):
    in_specs = (
        P("rows", "seq", None),
        P("rows", None),
        P(("rows", "seq"), None),
        P(("rows", "seq"), None),
        P(("rows", "seq"), None),
        P(("rows", "seq"), None),
        P(("rows", "seq"), None),
        P(None, ("rows", "seq")),
        P(None, ("rows", "seq")),
        P(("rows", "seq")),
        P("rows", "seq", None),
    )
    out_specs = (
        P("rows", "seq", None),
        P("rows", "seq", None),
        P(("rows", "seq"), None),
        P(("rows", "seq"), None),
        P(("rows", "seq"), None),
        P(("rows", "seq"), None),
        P(("rows", "seq"), None),
        P(None, ("rows", "seq")),
        P(None, ("rows", "seq")),
        P(("rows", "seq")),
    )
    return jax.shard_map(
        per_device, mesh=mesh, in_specs=in_specs, out_specs=out_specs, check_vma=False
    )
```

```python
import functools
import math

import jax
import jax.numpy as jnp
from jax import lax
from jax.experimental import pallas as pl
from jax.experimental.pallas import tpu as pltpu
from jax.sharding import PartitionSpec as P

epsilon = 1e-05
rope_base = 10000.0
neg_fill = -1e30

HEAD_DIM = 64
PAIR = 2 * HEAD_DIM
MESH = pl.DeviceIdType.MESH
Z, X, Y, C = 4, 2, 2, 2
OWNERS = Z * X * Y * C
f32, b16 = jnp.float32, jnp.bfloat16
FAR = -1e30


def place():
    r, s = lax.axis_index("rows"), lax.axis_index("seq")
    return r // X, r % X, s // C, s % C


def device(z, x, y, c):
    return (z * X + x, y * C + c)


def greet(peers):
    barrier = pltpu.get_barrier_semaphore()
    for peer in peers:
        pl.semaphore_signal(barrier, inc=1, device_id=peer, device_id_type=MESH)
    pl.semaphore_wait(barrier, len(peers))


def send_to(src, dst, send, recv, peer):
    return pltpu.make_async_remote_copy(
        src_ref=src, dst_ref=dst, send_sem=send, recv_sem=recv, device_id=peer, device_id_type=MESH
    )


def normal_rows(field):
    average = jnp.mean(field, axis=-1, keepdims=True)
    centred = field - average
    inverse = lax.rsqrt(jnp.mean(centred * centred, axis=-1, keepdims=True) + epsilon)
    return centred * inverse, inverse


def doc_marks(sizes, b, places):
    segment, start, end = jnp.zeros_like(places), jnp.zeros_like(places), jnp.int32(0)
    for d in range(sizes.shape[1]):
        end = end + sizes[b, d]
        passed = places >= end
        segment = segment + jnp.where(passed, 1, 0)
        start = start + jnp.where(passed, sizes[b, d], 0)
    return segment, places - start


def far_keys(sizes, b, stream):
    down, _ = doc_marks(sizes, b, lax.broadcasted_iota(jnp.int32, (stream, 1), 0))
    across, _ = doc_marks(sizes, b, lax.broadcasted_iota(jnp.int32, (1, stream), 1))
    return jnp.where(down == across, 0.0, FAR)


class Steps:
    def __init__(self, copies, needs):
        self.copies, self.needs, self.seen = copies, needs, set()

    def arrive(self, names):
        for name in names:
            if name not in self.seen:
                self.seen.add(name)
                self.copies(name).wait_recv()

    def start(self, name):
        self.arrive(self.needs(name))
        self.copies(name).start()

    def run(self, names):
        for name in names:
            self.start(name)


def at_index(index, plan):
    for spot, call in plan.items():

        @pl.when(index == spot)
        def _(call=call):
            call()


FORWARD_ROUTES = ("xzy", "xzy", "zxy")
FORWARD_ORDER = (
    (0, 2, 3), (0, 2, 2), (0, 0), ("ua", 2), (0, 2, 1), ("a", 0, 0), ("a", 0, 1), ("a", 0, 2), ("wz", 0, 3),
    (1, 0, 1), (1, 0, 2), ("wz", 0, 2), ("a", 1, 0), ("a", 1, 1), ("a", 1, 2), ("wz", 1, 1), ("a", 2, 0),
    ("a", 2, 1), ("a", 2, 2), ("wz", 2, 1), ("wz", 0, 1), ("y", 1), ("wz", 1, 2), (0, 1), (1, 0, 3),
    ("wz", 1, 3), ("wz", 2, 2), (1, 2), ("wz", 2, 3), ("wx", 0), ("ua", 0), ("ua", 1), ("uz", 0, 3),
    ("uz", 0, 1), ("k0", 0), (2, 0), ("y", 0), ("y", 2), ("uz", 0, 2), ("wx", 1), (3, 0), ("tb",), ("bias",),
    ("k0", 1), ("uz", 1, 2), ("uz", 1, 1), ("uz", 1, 3), ("k1", 1), ("dz", 1, 1), ("wx", 2), ("k1", 0),
    (2, 2), ("ux", 0), ("dz", 1, 2), ("k1", 2), ("at", 0), ("at", 1), ("at", 2), ("dz", 1, 3), (3, 2),
    ("dz", 0, 3), ("ux", 1), ("at", 3), ("k0", 2), ("at", 4), ("at", 5), ("keep", 0), ("dx", 1), ("dz", 0, 2),
    ("dz", 0, 1), ("out",), ("ln", 0), ("hy", 0), ("hk0", 0), ("ln", 1), ("hk0", 1), ("ln", 2), ("keep", 1),
    ("hk0", 2), ("up", 2, 0), (1, 1, 1), ("hy", 1), ("dx", 0), (1, 1, 2), (1, 1, 3), (2, 1), ("hk1", 0),
    ("up", 0, 1), ("up", 0, 0), ("hk1", 1), ("up", 1, 1), ("hy", 2), ("up", 1, 0), ("dn", 1, 0), ("dn", 1, 1),
    ("fc", 1), ("f2", 1), ("fy", 1), ("dn", 0, 0), ("dn", 0, 1), ("fc", 0), ("f2", 0), ("fy", 0), ("hk1", 2),
    (3, 1), ("dn", 2, 0), ("up", 2, 1), ("dn", 2, 1), ("keep", 2), ("ln2", 1), ("fc", 2), ("f2", 2),
    ("fy", 2), ("ln2", 0), ("ln2", 2), ("keep", 3),
)


def forward_kernel(
    tok, sizes, wqkv, wout, wup, wdown, wproj, biases, gains, up_bias,
    o_out, o_up, o_down, o_proj, o_cols, o_rows, o_tok_t, o_qkv, o_lse, o_att_t, o_n1, o_r1, o_h_t, o_hid_t, o_dgelu,
    o_n2, o_r2, o_nlow_t, o_cos, o_sin, o_res,
    g_out, g_up, g_down, g_proj, g_side, g_cols, g_tok, tok_t, qkv, head_out, far, att, att_t, z_one, n_one, g_h, h_t,
    hid, hid_t, dgelu, n_two, bias_up, mix, cos4, sin4, up_mix, f_send, f_c, f_y_send, f_y,
    c_send, c_recv, a_send, a_recv, wz_send, wz_recv, wx_send, wx_recv, y_send, y_recv, k_send, k_recv, t_send, t_recv,
    ua_send, ua_recv, uz_send, uz_recv, ux_send, ux_recv, fc_send, fc_recv, fy_send, fy_recv, save,
):
    streams, part, width = tok.shape
    rows, stream = streams * part, part * Y * C
    z, x, y, c = place()
    s = y * C + c
    seq_peer = [(y, 1 - c), (1 - y, c), (1 - y, 1 - c)]
    others = [(z + d) % Z for d in range(1, Z)]
    half_width = width // 2
    hidden = g_up.shape[-1]
    cols = wqkv.shape[1] // (3 * Y * C)

    targets = [g_side, g_proj, g_out]
    total = len(targets)
    axis_peer = {"x": device(z, 1 - x, y, c), "y": device(z, x, 1 - y, c)}

    def piece(name):
        stage, k = name[0], name[1]
        route, held = FORWARD_ROUTES[k], targets[k]
        every = slice(None)
        along = {"x": x, "y": y, "z": z}
        spot = {axis: every if axis in route[:stage] else along[axis] for axis in "zxy"}
        if stage == 3:
            slab, slot, peer = held.at[:, :, :, c], 5, device(z, x, y, 1 - c)
        else:
            slab = held.at[spot["z"], spot["x"], spot["y"], c]
            if route[stage] == "z":
                slot, peer = name[2] - 1, device(others[name[2] - 1], x, y, c)
            else:
                slot, peer = 3 + "xy".index(route[stage]), axis_peer[route[stage]]
        return send_to(slab, slab, c_send.at[k, slot], c_recv.at[k, slot], peer)

    def piece_names(stage, k):
        if stage < 3 and FORWARD_ROUTES[k][stage] == "z":
            return [(stage, k, d) for d in range(1, Z)]
        return [(stage, k)]

    def transfer(name):
        kind = name[0]
        if not isinstance(kind, str):
            return piece(name)
        if kind == "a":
            j, p = name[1:]
            yy, cc = seq_peer[p]
            src = wqkv.at[:, pl.ds(pl.multiple_of(j * width + (yy * C + cc) * cols, 128), cols)]
            return send_to(src, g_cols.at[j, z, x, y, c], a_send.at[j, p], a_recv.at[j, p], device(z, x, yy, cc))
        if kind == "wz":
            j, d = name[1:]
            slab = g_cols.at[j, z, x]
            return send_to(slab, slab, wz_send.at[j, d - 1], wz_recv.at[j, d - 1], device(others[d - 1], x, y, c))
        if kind == "wx":
            j = name[1]
            slab = g_cols.at[j, :, x]
            return send_to(slab, slab, wx_send.at[j], wx_recv.at[j], device(z, 1 - x, y, c))
        if kind == "ua":
            p = name[1]
            yy, cc = seq_peer[p]
            return send_to(up_mix.at[yy, cc], g_up.at[z, x, y, c], ua_send.at[p], ua_recv.at[p], device(z, x, yy, cc))
        if kind in ("uz", "dz", "ux", "dx"):
            h, row = name[1], "ud".index(kind[0]) * 2 + name[1]
            lanes = pl.ds(h * half_width, half_width)
            xs = (z, x) if kind[1] == "z" else (slice(None), x)
            slab = g_up.at[*xs, :, :, :, lanes] if kind[0] == "u" else g_down.at[*xs, :, lanes]
            if kind[1] == "z":
                d = name[2]
                return send_to(slab, slab, uz_send.at[row, d - 1], uz_recv.at[row, d - 1], device(others[d - 1], x, y, c))
            return send_to(slab, slab, ux_send.at[row], ux_recv.at[row], device(z, 1 - x, y, c))
        b = name[1]
        if kind == "fc":
            return send_to(f_send.at[b], f_c.at[b], fc_send.at[b], fc_recv.at[b], device(z, x, y, 1 - c))
        if kind == "fy":
            return send_to(f_y_send.at[b], f_y.at[b], fy_send.at[b], fy_recv.at[b], device(z, x, 1 - y, c))
        if kind[0] == "h":
            mine = g_h.at[b, y, c]
            if kind == "hy":
                return send_to(mine, mine, y_send.at[streams + b], y_recv.at[streams + b], device(z, x, 1 - y, c))
            slab = mine if kind == "hk0" else g_h.at[b, 1 - y, c]
            i = int(kind[2])
            return send_to(slab, slab, k_send.at[streams + b, i], k_recv.at[streams + b, i], device(z, x, y, 1 - c))
        if kind == "y":
            return send_to(tok.at[b], g_tok.at[b, y, c], y_send.at[b], y_recv.at[b], device(z, x, 1 - y, c))
        if kind == "k0":
            return send_to(tok.at[b], g_tok.at[b, y, c], k_send.at[b, 0], k_recv.at[b, 0], device(z, x, y, 1 - c))
        slab = g_tok.at[b, 1 - y, c]
        return send_to(slab, slab, k_send.at[b, 1], k_recv.at[b, 1], device(z, x, y, 1 - c))

    def needs(name):
        kind = name[0]
        if not isinstance(kind, str):
            return piece_names(kind - 1, name[1]) if kind else []
        if kind == "wz":
            return [("a", name[1], p) for p in range(3)]
        if kind == "wx":
            return [("wz", name[1], d) for d in range(1, Z)]
        if kind in ("uz", "ux"):
            return [("ua", p) for p in range(3)] if kind == "uz" else [("uz", name[1], d) for d in range(1, Z)]
        if kind == "dx":
            return [("dz", name[1], d) for d in range(1, Z)]
        return {"k1": [("y", name[1])], "hk1": [("hy", name[1])]}.get(kind, [])

    steps = Steps(transfer, needs)

    def att_seq(i, p):
        b, half = i // 2, i % 2
        yy, cc = seq_peer[p]
        lane = pl.multiple_of((s * 2 + half) * PAIR, PAIR)
        dst = att.at[b, :, pl.ds(lane, PAIR)]
        return send_to(head_out.at[b, half, yy, cc], dst, t_send.at[i, p], t_recv.at[i, p], device(z, x, yy, cc))

    mix[...] = jnp.zeros_like(mix)
    lanes_own = biases.shape[1]
    mix[0:7, 0:lanes_own] = biases[...].astype(f32)
    mix[7:9, 0:lanes_own] = gains[...].astype(f32)
    mix[9:10] = up_bias[...].astype(f32)
    g_side[z, x, y, c] = mix[...].astype(b16)
    g_proj[z, x, y, c] = wproj[...]
    g_out[z, x, y, c] = wout[...]
    for yc in range(Y * C):
        for zx in range(Z * X):
            lane_at = (zx * Y * C + yc) * 128
            up_mix[yc // C, yc % C, :, zx * 128 : (zx + 1) * 128] = wup[:, lane_at : lane_at + 128]
    g_up[z, x, y, c] = up_mix[y, c]
    g_down[z, x] = wdown[...]
    for j in range(3):
        g_cols[j, z, x, y, c] = wqkv[:, pl.ds(pl.multiple_of(j * width + s * cols, 128), cols)]
    for b in range(streams):
        g_tok[b, y, c] = tok[b]
    greet(
        [device(zz, x, y, c) for zz in others]
        + [device(z, 1 - x, y, c)]
        + [device(z, x, yy, cc) for yy, cc in seq_peer]
    )

    lane = lax.broadcasted_iota(jnp.int32, (1, PAIR), 1)
    low_half = (lane % HEAD_DIM) < HEAD_DIM // 2
    inverse_f = jnp.exp((lane % (HEAD_DIM // 2)).astype(f32) * (-math.log(rope_base) / (HEAD_DIM // 2)))

    def tables(b):
        _, position = doc_marks(sizes, b, lax.broadcasted_iota(jnp.int32, (stream, PAIR), 0))
        angle = position.astype(f32) * inverse_f
        cos4[b] = jnp.cos(angle)
        sin4[b] = jnp.sin(angle) * jnp.where(low_half, -1.0, 1.0)

    def all_tables():
        pl.loop(0, streams)(tables)

    def whole_rows():
        steps.arrive(piece_names(3, 0))
        lanes = lax.broadcasted_iota(jnp.int32, (16, 128), 1)
        share = 128 // (Y * C)
        for zx in range(Z * X):
            tile = jnp.zeros((16, 128), f32)
            for yc in range(Y * C):
                block = g_side[zx // X, zx % X, yc // C, yc % C].astype(f32)
                tile = tile + pltpu.roll(jnp.where(lanes < share, block, 0.0), yc * share, 1)
            o_rows[:, pl.ds(zx * 128, 128)] = tile
            bias_up[:, pl.ds(zx * 128, 128)] = g_side[zx // X, zx % X, y, c].astype(f32)[9:10]

    def project(b):
        rows_b = g_tok[b].reshape(stream, width)
        tok_t[b] = rows_b.T
        for j in range(3):
            bias_row = o_rows[pl.ds(j, 1), pl.ds(pl.multiple_of(s * cols, 128), cols)]
            got = jnp.dot(rows_b, g_cols[j].reshape(width, cols), preferred_element_type=f32) + bias_row
            for half in range(2):
                t = got[:, half * PAIR : (half + 1) * PAIR]
                if j < 2:
                    swapped = jnp.where(
                        low_half, pltpu.roll(t, PAIR - HEAD_DIM // 2, 1), pltpu.roll(t, HEAD_DIM // 2, 1)
                    )
                    t = t * cos4[b] + swapped * sin4[b]
                qkv[j, b, half] = t.astype(b16)
        far[...] = far_keys(sizes, b, stream)

    q_block = stream // 2
    top = lax.broadcasted_iota(jnp.int32, (PAIR, 1), 0) < HEAD_DIM
    score_scale = HEAD_DIM**-0.5
    masks = [jnp.where(lane < HEAD_DIM, score_scale, 0.0).astype(b16), jnp.where(lane < HEAD_DIM, 0.0, score_scale).astype(b16)]

    def attend(i):
        b, half = i // 2, i % 2
        queries, keys = qkv[0, b, half], qkv[1, b, half]
        values_t = qkv[2, b, half].T
        for block in range(2):
            at = slice(block * q_block, (block + 1) * q_block)
            turned = []
            for head in range(2):
                q = queries[at] * masks[head]
                scores = lax.dot_general(keys, q, (((1,), (1,)), ((), ())), preferred_element_type=f32)
                scores = scores + far[:, pl.ds(block * q_block, q_block)]
                most = jnp.max(scores, axis=0, keepdims=True)
                e = jnp.exp(scores - most)
                mass = jnp.sum(e, axis=0, keepdims=True)
                o_lse[i, pl.ds(head, 1), pl.ds(block * q_block, q_block)] = most + jnp.log(mass)
                probs = (e * (1.0 / mass)).astype(b16)
                turned.append(jnp.dot(values_t, probs, preferred_element_type=f32))
            both = jnp.where(top, turned[0], turned[1]).T.astype(b16)
            for cc in range(C):
                head_out[b, half, block, cc] = both[cc * part : (cc + 1) * part]
        for p in range(3):
            att_seq(i, p).start()
        lane_at = pl.multiple_of((s * 2 + half) * PAIR, PAIR)
        att[b, :, pl.ds(lane_at, PAIR)] = head_out[b, half, y, c]

    n_block = 512
    r_block = part

    def attention_out():
        @pl.loop(0, streams * 2)
        def _(i):
            for p in range(3):
                att_seq(i, p).wait_recv()

        steps.arrive(piece_names(3, 2))

        @pl.loop(0, width // n_block)
        def _(n):
            at = pl.ds(pl.multiple_of(n * n_block, n_block), n_block)
            w = g_out[:, :, :, :, :, at].reshape(width, n_block)
            got = jnp.dot(att[...].reshape(rows, width), w, preferred_element_type=f32)
            z_one[:, at] = tok[:, :, at].reshape(rows, n_block).astype(f32) + (got + o_rows[3:4, at])

    def rows_of(b):
        return slice(b * part, (b + 1) * part)

    def first_norm(b):
        at = rows_of(b)
        n, inverse = normal_rows(z_one[at])
        n_one[at] = n
        o_r1[at] = jnp.broadcast_to(inverse, (part, 128))
        h = n * o_rows[7:8] + o_rows[4:5]
        z_one[at] = h
        g_h[b, y, c] = h.astype(b16)
        att_t[:, at] = att[b].T

    def hidden_rows(b, away):
        yy = 1 - y if away else y
        steps.arrive([("ux", 0), ("ux", 1)] + ([("hy", b), ("hk1", b)] if away else [("hk0", b)]))
        h = g_h[b, yy].reshape(C * part, width)
        col = pl.ds(pl.multiple_of(yy * C * part, C * part), C * part)
        h_t[b, :, col] = h.T

        @pl.loop(0, hidden // n_block)
        def _(n):
            at = pl.ds(pl.multiple_of(n * n_block, n_block), n_block)
            w = g_up[:, :, :, :, :, at].reshape(width, n_block)
            u = jnp.dot(g_h[b, yy].reshape(C * part, width), w, preferred_element_type=f32) + bias_up[:, at]
            cdf = 0.5 * (1.0 + lax.erf(u * (2.0**-0.5)))
            low = (u * cdf).astype(b16)
            hid[b, yy, :, at] = low
            hid_t[b, at, col] = low.T
            dgelu[b, yy, :, at] = (cdf + u * (jnp.exp(-0.5 * u * u) * ((2.0 * math.pi) ** -0.5))).astype(b16)

    def down_rows(b, away):
        yy = 1 - y if away else y
        steps.arrive([("dx", 0), ("dx", 1)])
        at = rows_of(b)

        @pl.loop(0, width // n_block)
        def _(n):
            col = pl.ds(pl.multiple_of(n * n_block, n_block), n_block)
            w = g_down[:, :, :, col].reshape(hidden, n_block)
            f_send[b, yy, :, col] = jnp.dot(hid[b, yy, pl.ds((1 - c) * part, part)], w, preferred_element_type=f32).astype(b16)
            got = jnp.dot(hid[b, yy, pl.ds(c * part, part)], w, preferred_element_type=f32)
            if away:
                n_two[at, col] = got
            else:
                z_one[at, col] += got + o_rows[5:6, col]

    def core_sum(b):
        steps.arrive([("fc", b)])
        at = rows_of(b)
        f_y_send[b] = (n_two[at] + f_c[b, 1 - y].astype(f32)).astype(b16)

    def second_norm(b):
        steps.arrive([("fy", b)] + piece_names(3, 1))
        at = rows_of(b)
        n, inverse = normal_rows(z_one[at] + f_c[b, y].astype(f32) + f_y[b].astype(f32))
        n_two[at] = n
        o_r2[at] = jnp.broadcast_to(inverse, (part, 128))
        low = (n * o_rows[8:9] + o_rows[6:7]).astype(b16)
        o_nlow_t[:, at] = low.T
        o_res[at] = jnp.dot(low, g_proj[...].reshape(width, wproj.shape[1]), preferred_element_type=f32).astype(b16)

    kept = [(cos4, o_cos), (sin4, o_sin), (tok_t, o_tok_t), (qkv, o_qkv)]
    kept += [
        (g_cols.at[j, :, :, :, :, :, pl.ds(half * PAIR, PAIR)], o_cols.at[half, :, :, :, :, :, pl.ds(j * PAIR, PAIR)])
        for j in range(3)
        for half in range(2)
    ]
    early = len(kept)
    kept += [(g_out, o_out), (att_t, o_att_t), (n_one, o_n1)]
    middle = len(kept)
    kept += [(g_up, o_up), (g_down, o_down), (h_t, o_h_t), (hid_t, o_hid_t), (dgelu, o_dgelu)]
    late = len(kept)
    kept += [(n_two, o_n2), (g_proj, o_proj)]
    copies = [pltpu.make_async_copy(a, b, save.at[i]) for i, (a, b) in enumerate(kept)]

    def keep(first_copy, last_copy):
        for copy in copies[first_copy:last_copy]:
            copy.start()

    work = {
        "tb": all_tables, "bias": whole_rows, "out": attention_out, "ln": first_norm, "up": hidden_rows, "dn": down_rows,
        "f2": core_sum, "ln2": second_norm, "keep": lambda i: keep((0, early, middle, late)[i], (early, middle, late, len(kept))[i]),
    }
    spots = [i for i, name in enumerate(FORWARD_ORDER) if name[0] == "at"]

    def run(first_spot, last_spot):
        for name in FORWARD_ORDER[first_spot:last_spot]:
            if name[0] in work:
                work[name[0]](*name[1:])
            else:
                steps.start(name)

    run(0, spots[0])

    def before(i):
        if i:
            run(spots[i - 1] + 1, spots[i])
        if i % 2 == 0:
            steps.arrive([("wx", j) for j in range(3)] + [("k0", i // 2), ("k1", i // 2)])

    @pl.loop(0, streams * 2)
    def _(i):
        at_index(i, {spot: functools.partial(before, spot) for spot in range(streams * 2)})

        @pl.when(i % 2 == 0)
        def _():
            project(i // 2)

        attend(i)

    run(spots[-1] + 1, len(FORWARD_ORDER))
    for k in range(total):
        for stage in range(4):
            for name in piece_names(stage, k):
                transfer(name).wait_send()
    for j in range(3):
        for p in range(3):
            transfer(("a", j, p)).wait_send()
        for d in range(1, Z):
            transfer(("wz", j, d)).wait_send()
        transfer(("wx", j)).wait_send()
    for p in range(3):
        transfer(("ua", p)).wait_send()
    for kind in "ud":
        for h in range(2):
            for d in range(1, Z):
                transfer((kind + "z", h, d)).wait_send()
            transfer((kind + "x", h)).wait_send()
    for b in range(streams):
        for kind in ("y", "k0", "k1", "hy", "hk0", "hk1", "fc", "fy"):
            transfer((kind, b)).wait_send()

    @pl.loop(0, streams * 2)
    def _(i):
        for p in range(3):
            att_seq(i, p).wait_send()

    for copy in copies:
        copy.wait()


def run_forward(tokens, sizes, wqkv, wout, wup, wdown, wproj, biases, gains, up_bias):
    streams, part, width = tokens.shape
    rows, stream, hidden = streams * part, part * Y * C, wup.shape[1] // (Y * C)
    proj = wproj.shape[1]
    cols = width // (Y * C)
    grid = (Z, X, Y, C)
    shape = jax.ShapeDtypeStruct
    vmem, hbm = pl.BlockSpec(memory_space=pltpu.VMEM), pl.BlockSpec(memory_space=pl.ANY)
    vm = pltpu.VMEM
    outs = [
        ((grid + wout.shape, b16), hbm),
        ((grid + (wup.shape[0], hidden), b16), hbm),
        (((Z, X) + wdown.shape, b16), hbm),
        ((grid + wproj.shape, b16), hbm),
        (((2,) + grid + (wqkv.shape[0], 3 * PAIR), b16), hbm),
        (((16, width), f32), vmem),
        (((streams, width, stream), b16), hbm),
        (((3, streams, 2, stream, PAIR), b16), hbm),
        (((streams * 2, 8, stream), f32), vmem),
        (((width, rows), b16), hbm),
        (((rows, width), f32), hbm),
        (((rows, 128), f32), vmem),
        (((streams, width, stream), b16), hbm),
        (((streams, hidden, stream), b16), hbm),
        (((streams, Y, C * part, hidden), b16), hbm),
        (((rows, width), f32), hbm),
        (((rows, 128), f32), vmem),
        (((width, rows), b16), vmem),
        (((streams, stream, PAIR), f32), hbm),
        (((streams, stream, PAIR), f32), hbm),
        (((rows, proj), b16), vmem),
    ]
    dma = pltpu.SemaphoreType.DMA
    scratch = [
        vm(grid + wout.shape, b16),
        vm(grid + (wup.shape[0], hidden), b16),
        vm((Z, X) + wdown.shape, b16),
        vm(grid + wproj.shape, b16),
        vm(grid + (16, 128), b16),
        vm((3,) + grid + (wqkv.shape[0], cols), b16),
        vm((streams, Y, C, part, width), b16),
        vm((streams, width, stream), b16),
        vm((3, streams, 2, stream, PAIR), b16),
        vm((streams, 2, Y, C, part, PAIR), b16),
        vm((stream, stream), f32),
        vm((streams, part, width), b16),
        vm((width, rows), b16),
        vm((rows, width), f32),
        vm((rows, width), f32),
        vm((streams, Y, C, part, width), b16),
        vm((streams, width, stream), b16),
        vm((streams, Y, C * part, hidden), b16),
        vm((streams, hidden, stream), b16),
        vm((streams, Y, C * part, hidden), b16),
        vm((rows, width), f32),
        vm((1, hidden), f32),
        vm((16, 128), f32),
        vm((streams, stream, PAIR), f32),
        vm((streams, stream, PAIR), f32),
        vm((Y, C, wup.shape[0], hidden), b16),
        vm((streams, Y, part, width), b16), vm((streams, Y, part, width), b16), vm((streams, part, width), b16), vm((streams, part, width), b16),
        dma((3, 6)), dma((3, 6)), dma((3, 3)), dma((3, 3)), dma((3, 3)), dma((3, 3)), dma((3,)), dma((3,)),
        dma((2 * streams,)), dma((2 * streams,)), dma((2 * streams, 2)), dma((2 * streams, 2)), dma((streams * 2, 3)), dma((streams * 2, 3)),
        dma((3,)), dma((3,)), dma((4, 3)), dma((4, 3)), dma((4,)), dma((4,)), dma((streams,)), dma((streams,)), dma((streams,)), dma((streams,)),
        dma((26,)),
    ]
    return pl.pallas_call(
        forward_kernel,
        out_shape=[shape(*o[0]) for o in outs],
        in_specs=[vmem, pl.BlockSpec(memory_space=pltpu.SMEM)] + [vmem] * 8,
        out_specs=[o[1] for o in outs],
        scratch_shapes=scratch,
        compiler_params=pltpu.CompilerParams(collective_id=3, has_side_effects=True, vmem_limit_bytes=63 << 20),
    )(tokens, sizes, wqkv, wout, wup, wdown, wproj, biases, gains, up_bias)


def turned_back(t, cosine, sine, low_half):
    swapped = jnp.where(low_half, pltpu.roll(t, PAIR - HEAD_DIM // 2, 1), pltpu.roll(t, HEAD_DIM // 2, 1))
    return t * cosine - swapped * sine


BACKWARD_ROUTES = ("yxz", "xzy", "yxz")
BACKWARD_ORDER = (
    ("ln2b", 2), ("ln2b", 0), ("gh", 0, 0), ("mk", 1), ("own", 1), ("add", 1, 0), ("ln2b", 1), ("gh", 2, 0),
    ("g1", 2, 0), ("gk", 2), ("gh", 2, 1), ("g1", 2, 1), ("f2", 2), ("gk", 0), ("gk", 1), ("w1", 0),
    ("gh", 1, 1), ("g1", 1, 1), ("gh", 1, 0), ("g1", 1, 0), ("f2", 1), ("gh", 0, 1), ("w1", 2), ("g1", 0, 0),
    ("g1", 0, 1), ("f2", 0), ("w2", 0), ("w1", 3), ("ln1b", 0), ("ln1b", 1), ("ln1b", 2), ("mk", 0),
    ("ga", 1), ("w1", 1), ("w2", 2), ("ga", 0), ("ga", 2), ("ga", 3), ("at", 0), ("w2", 3), ("at", 1),
    ("at", 2), ("q1", 0), ("own", 0), ("w3", 2), ("at", 3), ("w2", 1), ("at", 4), ("at", 5), ("q1", 1),
    ("i1", 1), ("add", 1, 1), ("i2", 1), ("i3", 1), ("q2", 0), ("i1", 0), ("i2", 0), ("mk", 2), ("add", 0, 0),
    ("q2", 1), ("w3", 3), ("own", 2), ("i4", 1), ("i3", 0), ("i1", 2), ("i2", 2), ("q3", 0), ("add", 2, 0),
    ("add", 0, 1), ("add", 2, 1), ("fin", 1), ("w4", 1), ("i3", 2), ("i4", 2), ("w3", 1), ("w4", 0),
    ("i4", 0), ("q3", 1), ("q4", 1), ("q4", 0), ("fin", 0), ("w3", 0), ("fin", 2),
)


def backward_kernel(
    w_out, w_up, w_down, w_proj, w_cols, side_rows, i_tok_t, i_qkv, lse, i_att_t, i_n1, r_one, i_h_t, i_hid_t, i_dgelu, i_n2, r_two, nlow_t,
    cos4, sin4, sizes, cot_f,
    o_in, o_qkv, o_out, o_up, o_down, o_proj, o_side,
    wo, wu, wd, norm, att_t, h_t, hid_t, dgelu, tok_t, qkv, cols_all, sums, sum_up, grad_ffn, grad_branch, grad_att, heads, far,
    turned, send_o, send_p, send_s, cot, w_send, w_x, w_z, u_seq, u_in, apart, g_send, g_c, g_y_send, g_y,
    q_send, q_x, q_z, q_seq, q_in,
    c_send, c_recv, a_send, a_recv, qx_send, qx_recv, qz_send, qz_recv, qs_send, qs_recv, ic_send, ic_recv, iy_send, iy_recv,
    wx_send, wx_recv, wz_send, wz_recv, us_send, us_recv, gy_send, gy_recv, gk_send, gk_recv, gc_send, gc_recv, gf_send, gf_recv,
    load, *pieces,
):
    rows, width = o_in.shape
    streams = qkv.shape[1]
    part, stream = rows // streams, qkv.shape[3]
    hidden = sum_up.shape[1]
    half_width = width // 2
    cols = width // (Y * C)
    block = 512
    z, x, y, c = place()
    s = y * C + c
    seq_peer = [(y, 1 - c), (1 - y, c), (1 - y, 1 - c)]
    others = [(z + d) % Z for d in range(1, Z)]
    nt = (((1,), (1,)), ((), ()))
    grad_u = dgelu

    first_loads = [(i_n2, norm), (w_down, wd), (i_dgelu, dgelu), (w_up, wu), (i_hid_t, hid_t), (i_h_t, h_t), (i_n1, norm), (w_out, wo)]
    first_loads += [(i_att_t, att_t), (i_qkv, qkv), (i_tok_t, tok_t), (w_cols, cols_all)]
    loads = [pltpu.make_async_copy(a, b, load.at[i]) for i, (a, b) in enumerate(first_loads)]
    for i, copy in enumerate(loads):
        if i != 6:
            copy.start()
    loaded = set()

    def need(*which):
        for i in which:
            if i not in loaded:
                loaded.add(i)
                loads[i].wait()

    greet(
        [device(zz, x, y, c) for zz in others]
        + [device(z, 1 - x, y, c)]
        + [device(z, x, yy, cc) for yy, cc in seq_peer]
    )

    outgoing = [send_o, send_p, send_s.at[:, :, :, 1 - c]]
    total = len(outgoing)
    held, landed = pieces[:total], [pieces[total + 3 * k : total + 3 * k + 3] for k in range(total)]
    own_spot = {"z": z, "x": x, "y": y}
    axis_size = {"z": Z, "x": X, "y": Y}

    def to_core(k):
        return send_to(outgoing[k], held[k], c_send.at[k, 8], c_recv.at[k, 8], device(z, x, y, 1 - c))

    def along(k, stage):
        route = BACKWARD_ROUTES[k]
        axis = route[stage]
        if axis == "z":
            peers = [(others[d], device(others[d], x, y, c)) for d in range(Z - 1)]
        else:
            peers = [(1 - x, device(z, 1 - x, y, c))] if axis == "x" else [(1 - y, device(z, x, 1 - y, c))]
        copies = []
        for d, (spot, peer) in enumerate(peers):
            at = {a: own_spot[a] if a in route[:stage] else slice(None) for a in "zxy"} | {axis: spot}
            dst = landed[k][stage].at[d] if axis == "z" else landed[k][stage]
            slot = d if axis == "z" else 3 + stage
            copies.append(send_to(held[k].at[at["z"], at["x"], at["y"]], dst, c_send.at[k, slot], c_recv.at[k, slot], peer))
        return copies

    def begin(k, stage):
        for copy in along(k, stage):
            copy.start()

    def arrived(k, stage):
        for copy in along(k, stage):
            copy.wait_recv()

    def add_landed(k, stage):
        route = BACKWARD_ROUTES[k]
        arrived(k, stage)
        rest = [a for a in "zxy" if a not in route[: stage + 1]]
        count = math.prod(axis_size[a] for a in rest)

        @pl.loop(0, count)
        def _(i):
            at, spot = dict(own_spot), []
            for a in reversed(rest):
                at[a] = i % axis_size[a]
                spot.insert(0, at[a])
                i = i // axis_size[a]
            here = (at["z"], at["x"], at["y"])
            value = held[k][here].astype(f32)
            if route[stage] == "z":
                for d in range(Z - 1):
                    value = value + landed[k][stage][(d, *spot)].astype(f32)
            else:
                value = value + landed[k][stage][tuple(spot)].astype(f32)
            held[k][here] = value.astype(b16)

        begin(k, stage + 1)

    def half_rows(a_t, core, b, at):
        return jnp.dot(a_t[:, :, :, core].reshape(-1, rows), b[:, at], preferred_element_type=f32)

    def make_send(k):
        if k == 0:

            @pl.loop(0, width // block)
            def _(n):
                at = pl.ds(pl.multiple_of(n * block, block), block)
                send_o[:, :, :, :, at] = half_rows(att_t, 1 - c, grad_branch, at).astype(b16).reshape(Z, X, Y, -1, block)

        else:
            send_p[...] = half_rows(nlow_t, 1 - c, cot, slice(None)).astype(b16).reshape(Z, X, Y, -1, cot.shape[1])
        to_core(k).start()

    def own_half(k):
        to_core(k).wait_recv()
        mine = held[k]
        if k == 0:

            @pl.loop(0, width // block)
            def _(n):
                at = pl.ds(pl.multiple_of(n * block, block), block)
                got = half_rows(att_t, c, grad_branch, at).reshape(Z, X, Y, -1, block)
                mine[:, :, :, :, at] = (mine[:, :, :, :, at].astype(f32) + got).astype(b16)

        elif k == 1:
            got = half_rows(nlow_t, c, cot, slice(None)).reshape(Z, X, Y, -1, cot.shape[1])
            mine[...] = (mine[...].astype(f32) + got).astype(b16)
        else:
            mine[...] = (mine[...].astype(f32) + send_s[:, :, :, c].astype(f32)).astype(b16)
        begin(k, 0)

    def finish(k):
        arrived(k, 2)
        value = held[k][z, x, y].astype(f32)
        if BACKWARD_ROUTES[k][2] == "z":
            for d in range(Z - 1):
                value = value + landed[k][2][d].astype(f32)
        else:
            value = value + landed[k][2][...].astype(f32)
        (o_out, o_proj, o_side)[k][...] = value

    def ffn_rows(k, xx):
        lanes = slice((k % 2) * half_width, (k % 2 + 1) * half_width)
        got = jnp.zeros((Z * 128, half_width), f32)
        for b in range(streams):
            if k < 2:
                left, right = hid_t[b, :, xx], grad_ffn[b].reshape(stream, width)[:, lanes]
            else:
                left, right = h_t[b, :, xx], grad_u[b].reshape(stream, hidden)[:, lanes]
            got = got + jnp.dot(left.reshape(Z * 128, stream), right, preferred_element_type=f32)
        return got.reshape(Z, 128, half_width)

    def ffn_x(k):
        return send_to(w_send.at[k], w_x.at[k], wx_send.at[k], wx_recv.at[k], device(z, 1 - x, y, c))

    def ffn_z(k, d):
        return send_to(w_x.at[k, others[d]], w_z.at[k, d], wz_send.at[k, d], wz_recv.at[k, d], device(others[d], x, y, c))

    def ffn_seq(h, p):
        yy, cc = seq_peer[p]
        return send_to(u_seq.at[h, yy, cc], u_in.at[h, y, c], us_send.at[h, p], us_recv.at[h, p], device(z, x, yy, cc))

    def ffn_one(k):
        need(4, 5)
        for b in range(streams):
            core_arrived(b, 0)
            core_arrived(b, 1)
        w_send[k] = ffn_rows(k, 1 - x).astype(b16)
        ffn_x(k).start()

    def ffn_two(k):
        ffn_x(k).wait_recv()
        w_x[k] = (w_x[k].astype(f32) + ffn_rows(k, x)).astype(b16)
        for d in range(Z - 1):
            ffn_z(k, d).start()

    def ffn_three(k):
        value = w_x[k, z].astype(f32)
        for d in range(Z - 1):
            ffn_z(k, d).wait_recv()
        for d in range(Z - 1):
            value = value + w_z[k, d].astype(f32)
        if k < 2:
            o_down[:, k * half_width : (k + 1) * half_width] = value
        else:
            u_seq[k - 2] = value.astype(b16).reshape(Y, C, -1, half_width)
            for p in range(3):
                ffn_seq(k - 2, p).start()
            u_in[k - 2, y, c] = u_seq[k - 2, y, c]

    def ffn_four(h):
        for p in range(3):
            ffn_seq(h, p).wait_recv()
        for owner in range(Y * C):
            for q in range(half_width // 128):
                lane_at = ((h * (half_width // 128) + q) * Y * C + owner) * 128
                o_up[:, lane_at : lane_at + 128] = u_in[h, owner // C, owner % C, :, q * 128 : (q + 1) * 128].astype(f32)

    sums[...] = jnp.zeros_like(sums)
    sum_up[...] = jnp.zeros_like(sum_up)
    cot[...] = cot_f[...].astype(b16)

    def rows_of(b):
        return slice(b * part, (b + 1) * part)

    def norm_back(e, gain_row, n, inverse, spots):
        ge = e * side_rows[gain_row : gain_row + 1]
        mean = jnp.mean(ge, axis=-1, keepdims=True)
        along = jnp.mean(ge * n, axis=-1, keepdims=True)
        grad = inverse * (ge - mean - n * along)
        low = grad.astype(b16)
        for spot, value in zip(spots, (e * n, e, low.astype(f32))):
            sums[spot : spot + 1] += jnp.sum(value, axis=0, keepdims=True)
        return grad, low

    def grad_y(b):
        mine = grad_ffn.at[b, y, c]
        return send_to(mine, mine, gy_send.at[b], gy_recv.at[b], device(z, x, 1 - y, c))

    def grad_core(b, i):
        slab = grad_ffn.at[b, 1 - y if i else y, c]
        return send_to(slab, slab, gk_send.at[b, i], gk_recv.at[b, i], device(z, x, y, 1 - c))

    used = []

    def second_norm_back(b):
        need(0)
        at = rows_of(b)
        e = lax.dot_general(cot[at], w_proj[...], nt, preferred_element_type=f32)
        o_in[at], low = norm_back(e, 8, norm[at], r_two[at, :1], (8, 6, 5))
        grad_ffn[b, y, c] = low
        used.append(b)
        if len(used) == streams:
            loads[6].start()
        grad_y(b).start()
        grad_core(b, 0).start()

    def forward_grad(b):
        grad_y(b).wait_recv()
        grad_core(b, 1).start()

    core_here = set()

    def core_arrived(b, i):
        if (b, i) not in core_here:
            core_here.add((b, i))
            grad_core(b, i).wait_recv()

    def hidden_back(b, away):
        need(1, 2)
        yy = 1 - y if away else y
        core_arrived(b, 1 if away else 0)

        @pl.loop(0, hidden // block)
        def _(n):
            at = pl.ds(pl.multiple_of(n * block, block), block)
            got = lax.dot_general(grad_ffn[b, yy].reshape(C * part, width), wd[at], nt, preferred_element_type=f32)
            low = (got * dgelu[b, yy, :, at].astype(f32)).astype(b16)
            grad_u[b, yy, :, at] = low
            sum_up[:, at] += jnp.sum(low.astype(f32), axis=0, keepdims=True)

    def share_core(b):
        return send_to(g_send.at[b], g_c.at[b], gc_send.at[b], gc_recv.at[b], device(z, x, y, 1 - c))

    def share_y(b):
        return send_to(g_y_send.at[b], g_y.at[b], gf_send.at[b], gf_recv.at[b], device(z, x, 1 - y, c))

    ready = set()

    def inner_back(b, away):
        need(3)
        yy = 1 - y if away else y
        at = rows_of(b)

        @pl.loop(0, width // block)
        def _(n):
            col = pl.ds(pl.multiple_of(n * block, block), block)
            got = lax.dot_general(grad_u[b, yy, pl.ds((1 - c) * part, part)], wu[col], nt, preferred_element_type=f32)
            g_send[b, yy, :, col] = got.astype(b16)
            got = lax.dot_general(grad_u[b, yy, pl.ds(c * part, part)], wu[col], nt, preferred_element_type=f32)
            if away:
                apart[at, col] = got
            else:
                o_in[at, col] += got

        ready.add((b, away))
        if len([r for r in ready if r[0] == b]) == 2:
            share_core(b).start()

    def core_sum(b):
        share_core(b).wait_recv()
        g_y_send[b] = (apart[rows_of(b)] + g_c[b, 1 - y].astype(f32)).astype(b16)
        share_y(b).start()

    def first_norm_back(b):
        need(6)
        at = rows_of(b)
        share_y(b).wait_recv()
        e = o_in[at] + g_c[b, y].astype(f32) + g_y[b].astype(f32)
        o_in[at], grad_branch[at] = norm_back(e, 7, norm[at], r_one[at, :1], (7, 4, 3))

    def att_seq(p):
        yy, cc = seq_peer[p]
        src = grad_att.at[:, :, pl.ds(pl.multiple_of((yy * C + cc) * cols, cols), cols)]
        return send_to(src, heads.at[:, y, c], a_send.at[p], a_recv.at[p], device(z, x, yy, cc))

    def grad_heads(to):
        need(7)
        at = pl.ds(pl.multiple_of(to * cols, cols), cols)
        got = lax.dot_general(grad_branch[...], wo[at], nt, preferred_element_type=f32)
        grad_att[:, :, at] = got.astype(b16).reshape(streams, part, cols)

    def att_back_send(p):
        if p < 3:
            yy, cc = seq_peer[p]
            grad_heads(yy * C + cc)
            att_seq(p).start()
        else:
            grad_heads(s)
            heads[:, y, c] = grad_att[:, :, pl.ds(pl.multiple_of(s * cols, cols), cols)]

    lane = lax.broadcasted_iota(jnp.int32, (1, PAIR), 1)
    low_half = (lane % HEAD_DIM) < HEAD_DIM // 2
    top = lax.broadcasted_iota(jnp.int32, (PAIR, 1), 0) < HEAD_DIM
    masks = [(lane < HEAD_DIM).astype(f32).astype(b16), (lane >= HEAD_DIM).astype(f32).astype(b16)]
    score_scale = HEAD_DIM**-0.5
    q_block = stream // 2

    def attend_back(i):
        half, b = i // streams, i % streams
        far[...] = far_keys(sizes, b, stream)
        queries, keys, values = qkv[0, b, half], qkv[1, b, half], qkv[2, b, half]
        given = heads[b, :, :, :, pl.ds(pl.multiple_of(half * PAIR, PAIR), PAIR)].reshape(stream, PAIR)
        keys_t = keys.T
        grad_k, grad_v = jnp.zeros((stream, PAIR), f32), jnp.zeros((stream, PAIR), f32)
        grad_q = []
        for part_q in range(2):
            at = slice(part_q * q_block, (part_q + 1) * q_block)
            q_t = []
            for head in range(2):
                q = queries[at] * (masks[head] * b16(score_scale))
                g = given[at] * masks[head]
                scores = lax.dot_general(keys, q, nt, preferred_element_type=f32) + far[:, at]
                probs = jnp.exp(scores - lse[b * 2 + half, head : head + 1, at])
                grad_p = lax.dot_general(values, g, nt, preferred_element_type=f32)
                row_dot = jnp.sum(probs * grad_p, axis=0, keepdims=True)
                grad_s = (probs * (grad_p - row_dot)).astype(b16)
                grad_v = grad_v + jnp.dot(probs.astype(b16), g, preferred_element_type=f32)
                grad_k = grad_k + jnp.dot(grad_s, q, preferred_element_type=f32)
                q_t.append(jnp.dot(keys_t, grad_s, preferred_element_type=f32))
            grad_q.append(jnp.where(top, q_t[0], q_t[1]).T * score_scale)
        grad_q = jnp.concatenate(grad_q, axis=0)
        lane_at = pl.multiple_of(s * cols + half * PAIR, PAIR)
        done = []
        for t in (grad_q, grad_k):
            done.append(turned_back(t.astype(b16).astype(f32), cos4[b], sin4[b], low_half).astype(b16))
        done.append(grad_v.astype(b16))
        for j in range(3):
            turned[half, b, :, j * PAIR : (j + 1) * PAIR] = done[j]
            sums[j : j + 1, pl.ds(lane_at, PAIR)] += jnp.sum(done[j].astype(f32), axis=0, keepdims=True)

    def qkv_rows(half, xx):
        got = jnp.zeros((Z * 128, 3 * PAIR), f32)
        for b in range(streams):
            got = got + jnp.dot(tok_t[b, :, xx].reshape(Z * 128, stream), turned[half, b], preferred_element_type=f32)
        return got.reshape(Z, 128, 3 * PAIR)

    def qkv_x(half):
        return send_to(q_send.at[half], q_x.at[half], qx_send.at[half], qx_recv.at[half], device(z, 1 - x, y, c))

    def qkv_z(half, d):
        return send_to(q_x.at[half, others[d]], q_z.at[half, d], qz_send.at[half, d], qz_recv.at[half, d], device(others[d], x, y, c))

    def qkv_seq(half, p):
        yy, cc = seq_peer[p]
        return send_to(q_seq.at[half, yy, cc], q_in.at[half, y, c], qs_send.at[half, p], qs_recv.at[half, p], device(z, x, yy, cc))

    def qkv_one(half):
        q_send[half] = qkv_rows(half, 1 - x).astype(b16)

        qkv_x(half).start()

    def qkv_two(half):
        qkv_x(half).wait_recv()
        q_x[half] = (q_x[half].astype(f32) + qkv_rows(half, x)).astype(b16)

        for d in range(Z - 1):
            qkv_z(half, d).start()

    def qkv_three(half):
        value = q_x[half, z].astype(f32)
        for d in range(Z - 1):
            qkv_z(half, d).wait_recv()
        for d in range(Z - 1):
            value = value + q_z[half, d].astype(f32)
        q_seq[half] = value.reshape(Y, C, -1, 3 * PAIR)
        for p in range(3):
            qkv_seq(half, p).start()
        q_in[half, y, c] = q_seq[half, y, c]

    def qkv_four(half):
        for p in range(3):
            qkv_seq(half, p).wait_recv()
        for owner in range(Y * C):
            for j in range(3):
                lane_at = j * width + owner * cols + half * PAIR
                o_qkv[:, lane_at : lane_at + PAIR] = q_in[half, owner // C, owner % C, :, j * PAIR : (j + 1) * PAIR]

    def in_c(b):
        return send_to(g_send.at[b], g_c.at[b], ic_send.at[b], ic_recv.at[b], device(z, x, y, 1 - c))

    def in_y(b):
        return send_to(g_y_send.at[b], g_y.at[b], iy_send.at[b], iy_recv.at[b], device(z, x, 1 - y, c))

    def input_rows(b, yy, cc):
        at = pl.ds(pl.multiple_of((yy * C + cc) * part, part), part)
        got = lax.dot_general(turned[0, b, at], cols_all[0], nt, preferred_element_type=f32)
        return got + lax.dot_general(turned[1, b, at], cols_all[1], nt, preferred_element_type=f32)

    def input_one(b):
        share_core(b).wait_send()
        for yy in range(Y):
            g_send[b, yy] = input_rows(b, yy, 1 - c).astype(b16)
        in_c(b).start()

    def input_two(b):
        in_c(b).wait_recv()
        share_y(b).wait_send()
        g_y_send[b] = (input_rows(b, 1 - y, c) + g_c[b, 1 - y].astype(f32)).astype(b16)
        in_y(b).start()

    def input_three(b):
        o_in[b * part : (b + 1) * part] += input_rows(b, y, c) + g_c[b, y].astype(f32)

    def input_four(b):
        in_y(b).wait_recv()
        o_in[b * part : (b + 1) * part] += g_y[b].astype(f32)

    def small_sums():
        lanes = lax.broadcasted_iota(jnp.int32, (16, 128), 1)
        spots = lax.broadcasted_iota(jnp.int32, (16, 128), 0)
        share = 128 // (Y * C)
        for zx in range(Z * X):
            tile = sums[:, zx * 128 : (zx + 1) * 128]
            for yc in range(Y * C):
                moved = pltpu.roll(tile, (128 - yc * share) % 128, 1) if yc else tile
                value = jnp.where(lanes < share, moved, 0.0)
                value = jnp.where(spots == 9, sum_up[:, zx * 128 : (zx + 1) * 128] * (s == yc).astype(f32), value)
                send_s[zx // X, zx % X, yc // C, yc % C] = value.astype(b16)
        to_core(2).start()

    work = {
        "ln2b": second_norm_back, "gk": forward_grad, "gh": hidden_back, "g1": inner_back, "f2": core_sum, "ln1b": first_norm_back, "ga": att_back_send,
        "w1": ffn_one, "w2": ffn_two, "w3": ffn_three, "w4": ffn_four,
        "mk": lambda k: make_send(k) if k < 2 else small_sums(), "own": own_half, "add": add_landed, "fin": finish,
        "q1": qkv_one, "q2": qkv_two, "q3": qkv_three, "q4": qkv_four,
        "i1": input_one, "i2": input_two, "i3": input_three, "i4": input_four,
    }
    spots = [i for i, name in enumerate(BACKWARD_ORDER) if name[0] == "at"]

    def run(first_spot, last_spot):
        for name in BACKWARD_ORDER[first_spot:last_spot]:
            if name == ("mk", 0):
                need(8)
            work[name[0]](*name[1:])

    run(0, spots[0])
    need(*range(len(loads)))

    def before(i):
        if i == 0:
            for p in range(3):
                att_seq(p).wait_recv()
        else:
            run(spots[i - 1] + 1, spots[i])

    @pl.loop(0, streams * 2)
    def _(i):
        at_index(i, {spot: functools.partial(before, spot) for spot in range(streams * 2)})
        attend_back(i)

    run(spots[-1] + 1, len(BACKWARD_ORDER))

    for k in range(total):
        to_core(k).wait_send()
        for stage in range(3):
            for copy in along(k, stage):
                copy.wait_send()
    for k in range(4):
        ffn_x(k).wait_send()
        for d in range(Z - 1):
            ffn_z(k, d).wait_send()
    for p in range(3):
        att_seq(p).wait_send()
        for half in range(2):
            qkv_seq(half, p).wait_send()
            ffn_seq(half, p).wait_send()
    for half in range(2):
        qkv_x(half).wait_send()
        for d in range(Z - 1):
            qkv_z(half, d).wait_send()
    for b in range(streams):
        for copy in (in_c(b), in_y(b), grad_y(b), grad_core(b, 0), grad_core(b, 1)):
            copy.wait_send()


def run_backward(kept, sizes, cot):
    (
        w_out, w_up, w_down, w_proj, w_cols, side_rows, tok_t, qkv, lse, att_t, n_one, r_one, h_t, hid_t, dgelu, n_two, r_two, nlow_t, cos4, sin4,
    ) = kept
    rows, width = n_one.shape
    streams, _, stream = tok_t.shape
    hidden = dgelu.shape[-1]
    ff = hidden * Y * C
    proj = w_proj.shape[-1]
    cols, half_width = width // (Y * C), width // 2
    grid = (Z, X, Y, C)
    part = rows // streams
    vm, dma = pltpu.VMEM, pltpu.SemaphoreType.DMA
    vmem, hbm = pl.BlockSpec(memory_space=pltpu.VMEM), pl.BlockSpec(memory_space=pl.ANY)
    owner = width // OWNERS
    tails = [(owner, width), (owner, proj), (16, 128)]
    split_rows = (streams, Z, X, width // (Z * X), stream)
    inputs = [
        (w_out.reshape(width, width), hbm), (w_up.reshape(width, hidden), hbm), (w_down.reshape(hidden, width), hbm),
        (w_proj.reshape(width, proj), vmem), (w_cols.reshape(2, width, 3 * PAIR), hbm), (side_rows, vmem), (tok_t.reshape(split_rows), hbm), (qkv, hbm),
        (lse, vmem), (att_t.reshape(grid + (owner, rows)), hbm), (n_one, hbm), (r_one, vmem), (h_t.reshape(split_rows), hbm),
        (hid_t.reshape(split_rows), hbm), (dgelu, hbm), (n_two, hbm), (r_two, vmem), (nlow_t.reshape(grid + (owner, rows)), vmem),
        (cos4, vmem), (sin4, vmem), (sizes, pl.BlockSpec(memory_space=pltpu.SMEM)), (cot, vmem),
    ]
    scratch = [
        vm((width, width), b16), vm((width, hidden), b16), vm((hidden, width), b16), vm((rows, width), f32),
        vm(grid + (owner, rows), b16), vm(split_rows, b16), vm(split_rows, b16), vm(dgelu.shape, b16), vm(split_rows, b16),
        vm(qkv.shape, b16), vm((2, width, 3 * PAIR), b16), vm((16, width), f32), vm((1, hidden), f32),
        vm((streams, Y, C, part, width), b16), vm((rows, width), b16), vm((streams, part, width), b16),
        vm((streams, Y, C, part, cols), b16), vm((stream, stream), f32), vm((2, streams, stream, 3 * PAIR), b16),
        vm((Z, X, Y) + tails[0], b16), vm((Z, X, Y) + tails[1], b16), vm(grid + tails[2], b16), vm(cot.shape, b16),
        vm((4, Z, 128, half_width), b16), vm((4, Z, 128, half_width), b16), vm((4, Z - 1, 128, half_width), b16),
        vm((2, Y, C, owner, half_width), b16), vm((2, Y, C, owner, half_width), b16), vm((rows, width), f32),
        vm((streams, Y, part, width), b16), vm((streams, Y, part, width), b16), vm((streams, part, width), b16), vm((streams, part, width), b16),
        vm((2, Z, 128, 3 * PAIR), b16), vm((2, Z, 128, 3 * PAIR), b16), vm((2, Z - 1, 128, 3 * PAIR), b16),
        vm((2, Y, C, 32, 3 * PAIR), f32), vm((2, Y, C, 32, 3 * PAIR), f32),
        dma((3, 9)), dma((3, 9)), dma((3,)), dma((3,)), dma((2,)), dma((2,)), dma((2, 3)), dma((2, 3)), dma((2, 3)), dma((2, 3)),
        dma((streams,)), dma((streams,)), dma((streams,)), dma((streams,)),
        dma((4,)), dma((4,)), dma((4, 3)), dma((4, 3)), dma((2, 3)), dma((2, 3)), dma((streams,)), dma((streams,)), dma((streams, 2)), dma((streams, 2)),
        dma((streams,)), dma((streams,)), dma((streams,)), dma((streams,)),
        dma((12,)),
    ]
    size = {"z": Z, "x": X, "y": Y}
    scratch += [vm((Z, X, Y) + tail, b16) for tail in tails]
    for route, tail in zip(BACKWARD_ROUTES, tails):
        for stage in range(3):
            rest = tuple(size[a] for a in "zxy" if a not in route[: stage + 1])
            scratch.append(vm(((Z - 1,) if route[stage] == "z" else ()) + rest + tail, b16))
    outs = [(rows, width), (owner, 3 * width), (owner, width), (owner, ff), (ff // OWNERS, width), (owner, proj), (16, 128)]
    return pl.pallas_call(
        backward_kernel,
        out_shape=[jax.ShapeDtypeStruct(o, f32) for o in outs],
        in_specs=[spec for _, spec in inputs],
        out_specs=[vmem] * len(outs),
        scratch_shapes=scratch,
        compiler_params=pltpu.CompilerParams(collective_id=4, has_side_effects=True, vmem_limit_bytes=63 << 20),
    )(*[a for a, _ in inputs])


def layer_norm(field, gain_row, shift_row):
    average = jnp.mean(field, axis=-1, keepdims=True)
    centred = field - average
    variance = jnp.mean(centred * centred, axis=-1, keepdims=True)
    return centred * lax.rsqrt(variance + epsilon) * gain_row + shift_row


def doc_layout(doc_sizes, places):
    doc_ends = jnp.cumsum(doc_sizes)
    passed = places[:, None] >= doc_ends[None, :]
    segment = jnp.sum(passed.astype(jnp.int32), axis=1)
    starts = jnp.sum(jnp.where(passed, doc_sizes[None, :], 0), axis=1)
    return (segment, places - starts)


def rope_tables(position, half_dim):
    steps_f = jnp.arange(half_dim, dtype=jnp.float32)
    inverse = jnp.exp(steps_f * (-math.log(rope_base) / half_dim))
    angle = position.astype(jnp.float32)[:, None] * inverse[None, :]
    return (jnp.cos(angle), jnp.sin(angle))


def rotate(field, cosine, sine_tab, head_count):
    length = field.shape[0]
    halves = field.reshape(length, head_count, 2, -1)
    first_half = halves[:, :, 0]
    second_half = halves[:, :, 1]
    cos_b = cosine[:, None, :]
    sin_b = sine_tab[:, None, :]
    turned = jnp.stack(
        [first_half * cos_b - second_half * sin_b, second_half * cos_b + first_half * sin_b], axis=2
    )
    return turned.reshape(length, -1)


def gelu_exact(field):
    return jax.nn.gelu(field, approximate=False)


def scores_of(query_blk, seg_blk, keys_all, stream_seg, score_scale):
    raw_scores = (
        jnp.einsum("qhd,khd->hqk", query_blk, keys_all, preferred_element_type=jnp.float32)
        * score_scale
    )
    same_doc = (seg_blk[:, None] == stream_seg[None, :])[None]
    return jnp.where(same_doc, raw_scores, neg_fill)


def per_device_any(
    tokens,
    doc_lengths,
    qkv_weight,
    out_weight,
    up_weight,
    down_weight,
    proj_weight,
    biases,
    gains,
    up_bias,
    cotangent,
):
    stream_count = tokens.shape[0]
    seg_rows = tokens.shape[1]
    model_width = tokens.shape[2]
    seq_parts = lax.axis_size("seq")
    stream = seg_rows * seq_parts
    head_count = model_width // HEAD_DIM
    local_heads = head_count // seq_parts
    flat_width = local_heads * HEAD_DIM
    score_scale = HEAD_DIM ** (-0.5)
    tok_flat = tokens.reshape(stream_count * seg_rows, model_width)
    gathered = (
        lax.all_gather(qkv_weight, ("rows", "seq"), axis=0, tiled=True),
        lax.all_gather(out_weight, ("rows", "seq"), axis=0, tiled=True),
        lax.all_gather(up_weight, ("rows", "seq"), axis=0, tiled=True),
        lax.all_gather(down_weight, ("rows", "seq"), axis=0, tiled=True),
        lax.all_gather(proj_weight, ("rows", "seq"), axis=0, tiled=True),
        lax.all_gather(biases, ("rows", "seq"), axis=1, tiled=True),
        lax.all_gather(gains, ("rows", "seq"), axis=1, tiled=True),
        lax.all_gather(up_bias, ("rows", "seq"), axis=0, tiled=True),
    )
    w_qkv, w_out, w_up, w_down, w_proj = (
        gathered[0],
        gathered[1],
        gathered[2],
        gathered[3],
        gathered[4],
    )
    bias_rows = gathered[5].astype(jnp.float32)
    gain_rows = gathered[6].astype(jnp.float32)
    bias_up = gathered[7].astype(jnp.float32)
    token_places = lax.axis_index("seq") * seg_rows + jnp.arange(seg_rows, dtype=jnp.int32)
    layout_rows = jax.vmap(doc_layout, in_axes=(0, None))
    token_seg, position = layout_rows(doc_lengths, token_places)
    cosine, sine_tab = rope_tables(position.reshape(-1), HEAD_DIM // 2)
    projected = jnp.dot(tok_flat, w_qkv, preferred_element_type=jnp.float32) + bias_rows[
        0:3
    ].reshape(-1)
    queries = (
        rotate(projected[:, :model_width], cosine, sine_tab, head_count)
        .astype(jnp.bfloat16)
        .reshape(stream_count, seg_rows, model_width)
    )
    keys_tok = (
        rotate(projected[:, model_width : 2 * model_width], cosine, sine_tab, head_count)
        .astype(jnp.bfloat16)
        .reshape(stream_count, seg_rows, model_width)
    )
    values_tok = (
        projected[:, 2 * model_width :]
        .astype(jnp.bfloat16)
        .reshape(stream_count, seg_rows, model_width)
    )
    queries_h, keys_h, values_h = (
        lax.all_to_all(queries, "seq", split_axis=2, concat_axis=1, tiled=True),
        lax.all_to_all(keys_tok, "seq", split_axis=2, concat_axis=1, tiled=True),
        lax.all_to_all(values_tok, "seq", split_axis=2, concat_axis=1, tiled=True),
    )
    stream_seg, stream_pos = layout_rows(doc_lengths, jnp.arange(stream, dtype=jnp.int32))
    block_rows = math.gcd(stream, 512)
    block_count = stream // block_rows

    def forward_stream(element):
        query_s, key_s, value_s, seg_s = element
        query_blocks = query_s.reshape(block_count, block_rows, local_heads, HEAD_DIM)
        keys_all = key_s.reshape(stream, local_heads, HEAD_DIM)
        values_all = value_s.reshape(stream, local_heads, HEAD_DIM)
        seg_blocks = seg_s.reshape(block_count, block_rows)

        def forward_block(inner):
            query_blk, seg_blk = inner
            scores = scores_of(query_blk, seg_blk, keys_all, seg_s, score_scale)
            row_max = jnp.max(scores, axis=-1, keepdims=True)
            row_total = jnp.sum(jnp.exp(scores - row_max), axis=-1, keepdims=True)
            log_total = row_max + jnp.log(row_total)
            probs_low = jnp.exp(scores - log_total).astype(jnp.bfloat16)
            attn_blk = jnp.einsum(
                "hqk,khd->qhd", probs_low, values_all, preferred_element_type=jnp.float32
            )
            return (attn_blk.astype(jnp.bfloat16), log_total[:, :, 0])

        attn_blocks, log_blocks = lax.map(forward_block, (query_blocks, seg_blocks))
        return (attn_blocks.reshape(stream, flat_width), log_blocks)

    attn_heads, log_totals = lax.map(forward_stream, (queries_h, keys_h, values_h, stream_seg))
    attended = lax.all_to_all(attn_heads, "seq", split_axis=1, concat_axis=2, tiled=True).reshape(
        stream_count * seg_rows, model_width
    )
    branch = jnp.dot(attended, w_out, preferred_element_type=jnp.float32) + bias_rows[3]
    h_one, norm_one = jax.vjp(
        layer_norm, tok_flat.astype(jnp.float32) + branch, gain_rows[0], bias_rows[4]
    )
    h_low = h_one.astype(jnp.bfloat16)
    u_pre = jnp.dot(h_low, w_up, preferred_element_type=jnp.float32) + bias_up
    hidden_f, gelu_back = jax.vjp(gelu_exact, u_pre)
    hidden = hidden_f.astype(jnp.bfloat16)
    ffn_out = jnp.dot(hidden, w_down, preferred_element_type=jnp.float32) + bias_rows[5]
    normed, norm_two = jax.vjp(layer_norm, h_one + ffn_out, gain_rows[1], bias_rows[6])
    normed_low = normed.astype(jnp.bfloat16)
    result = jnp.dot(normed_low, w_proj, preferred_element_type=jnp.float32).astype(jnp.bfloat16)
    w_qkv, w_out, w_up, w_down, w_proj = (
        lax.all_gather(qkv_weight, ("rows", "seq"), axis=0, tiled=True),
        lax.all_gather(out_weight, ("rows", "seq"), axis=0, tiled=True),
        lax.all_gather(up_weight, ("rows", "seq"), axis=0, tiled=True),
        lax.all_gather(down_weight, ("rows", "seq"), axis=0, tiled=True),
        lax.all_gather(proj_weight, ("rows", "seq"), axis=0, tiled=True),
    )
    cot_low = cotangent.reshape(stream_count * seg_rows, -1).astype(jnp.bfloat16)
    proj_part = jnp.dot(normed_low.T, cot_low, preferred_element_type=jnp.float32)
    grad_normed = jnp.dot(cot_low, w_proj.T, preferred_element_type=jnp.float32)
    grad_z2, grad_g2, grad_b2 = norm_two(grad_normed)
    grad_ffn = grad_z2.astype(jnp.bfloat16)
    grad_c2 = jnp.sum(grad_ffn, axis=0, dtype=jnp.float32)
    down_part = jnp.dot(hidden.T, grad_ffn, preferred_element_type=jnp.float32)
    grad_hidden = jnp.dot(grad_ffn, w_down.T, preferred_element_type=jnp.float32)
    grad_u = gelu_back(grad_hidden)[0].astype(jnp.bfloat16)
    grad_c1 = jnp.sum(grad_u, axis=0, dtype=jnp.float32)
    up_part = jnp.dot(h_low.T, grad_u, preferred_element_type=jnp.float32)
    ffn_sums = (up_part, down_part, proj_part, grad_c1)
    grad_h1 = grad_z2 + jnp.dot(grad_u, w_up.T, preferred_element_type=jnp.float32)
    grad_z1, grad_g1, grad_b1 = norm_one(grad_h1)
    grad_branch = grad_z1.astype(jnp.bfloat16)
    grad_bo = jnp.sum(grad_branch, axis=0, dtype=jnp.float32)
    out_part = jnp.dot(attended.T, grad_branch, preferred_element_type=jnp.float32)
    grad_attn = jnp.dot(grad_branch, w_out.T, preferred_element_type=jnp.float32).astype(
        jnp.bfloat16
    )
    grad_heads = lax.all_to_all(
        grad_attn.reshape(stream_count, seg_rows, model_width),
        "seq",
        split_axis=2,
        concat_axis=1,
        tiled=True,
    )

    def backward_stream(element):
        query_s, key_s, value_s, seg_s, log_s, grad_s = element
        query_blocks = query_s.reshape(block_count, block_rows, local_heads, HEAD_DIM)
        keys_all = key_s.reshape(stream, local_heads, HEAD_DIM)
        values_all = value_s.reshape(stream, local_heads, HEAD_DIM)
        seg_blocks = seg_s.reshape(block_count, block_rows)
        grad_blocks = grad_s.reshape(block_count, block_rows, local_heads, HEAD_DIM)

        def backward_block(carried, inner):
            grad_keys, grad_values = carried
            query_blk, seg_blk, log_total, grad_blk = inner
            probs_f = jnp.exp(
                scores_of(query_blk, seg_blk, keys_all, seg_s, score_scale) - log_total[:, :, None]
            )
            grad_values = grad_values + jnp.einsum(
                "hqk,qhd->khd",
                probs_f.astype(jnp.bfloat16),
                grad_blk,
                preferred_element_type=jnp.float32,
            )
            grad_probs = jnp.einsum(
                "qhd,khd->hqk", grad_blk, values_all, preferred_element_type=jnp.float32
            )
            row_dot = jnp.sum(probs_f * grad_probs, axis=-1, keepdims=True)
            grad_scores = (probs_f * (grad_probs - row_dot) * score_scale).astype(jnp.bfloat16)
            grad_query = jnp.einsum(
                "hqk,khd->qhd", grad_scores, keys_all, preferred_element_type=jnp.float32
            )
            grad_keys = grad_keys + jnp.einsum(
                "hqk,qhd->khd", grad_scores, query_blk, preferred_element_type=jnp.float32
            )
            return ((grad_keys, grad_values), grad_query.astype(jnp.bfloat16))

        zero_acc = jnp.zeros((stream, local_heads, HEAD_DIM), jnp.float32)
        (grad_keys, grad_values), grad_queries = lax.scan(
            backward_block, (zero_acc, zero_acc), (query_blocks, seg_blocks, log_s, grad_blocks)
        )
        return (
            grad_queries.reshape(stream, flat_width),
            grad_keys.astype(jnp.bfloat16).reshape(stream, flat_width),
            grad_values.astype(jnp.bfloat16).reshape(stream, flat_width),
        )

    head_q, head_k, head_v = lax.map(
        backward_stream, (queries_h, keys_h, values_h, stream_seg, log_totals, grad_heads)
    )
    back_q, back_k, back_v = (
        lax.all_to_all(head_q, "seq", split_axis=1, concat_axis=2, tiled=True),
        lax.all_to_all(head_k, "seq", split_axis=1, concat_axis=2, tiled=True),
        lax.all_to_all(head_v, "seq", split_axis=1, concat_axis=2, tiled=True),
    )
    flat_rows = stream_count * seg_rows
    turned_q = rotate(
        back_q.reshape(flat_rows, model_width).astype(jnp.float32), cosine, -sine_tab, head_count
    )
    turned_k = rotate(
        back_k.reshape(flat_rows, model_width).astype(jnp.float32), cosine, -sine_tab, head_count
    )
    grad_project = jnp.concatenate(
        [turned_q, turned_k, back_v.reshape(flat_rows, model_width).astype(jnp.float32)], axis=1
    ).astype(jnp.bfloat16)
    grad_bqkv = jnp.sum(grad_project, axis=0, dtype=jnp.float32).reshape(3, model_width)
    qkv_part = jnp.dot(tok_flat.T, grad_project, preferred_element_type=jnp.float32)
    input_grad = grad_z1 + jnp.dot(grad_project, w_qkv.T, preferred_element_type=jnp.float32)
    bias_part = jnp.concatenate(
        [grad_bqkv, jnp.stack([grad_bo, grad_b1, grad_c2, grad_b2])], axis=0
    )
    gain_part = jnp.stack([grad_g1, grad_g2])
    qkv_sum, out_sum, up_sum, down_sum, proj_sum, bias_sum, gain_sum, c1_sum = (
        lax.psum_scatter(qkv_part, ("rows", "seq"), scatter_dimension=0, tiled=True),
        lax.psum_scatter(out_part, ("rows", "seq"), scatter_dimension=0, tiled=True),
        lax.psum_scatter(ffn_sums[0], ("rows", "seq"), scatter_dimension=0, tiled=True),
        lax.psum_scatter(ffn_sums[1], ("rows", "seq"), scatter_dimension=0, tiled=True),
        lax.psum_scatter(ffn_sums[2], ("rows", "seq"), scatter_dimension=0, tiled=True),
        lax.psum_scatter(bias_part, ("rows", "seq"), scatter_dimension=1, tiled=True),
        lax.psum_scatter(gain_part, ("rows", "seq"), scatter_dimension=1, tiled=True),
        lax.psum_scatter(ffn_sums[3], ("rows", "seq"), scatter_dimension=0, tiled=True),
    )
    output = result.reshape(stream_count, seg_rows, -1)
    return (
        output,
        input_grad.reshape(stream_count, seg_rows, model_width),
        qkv_sum,
        out_sum,
        up_sum,
        down_sum,
        proj_sum,
        bias_sum,
        gain_sum,
        c1_sum,
    )


def direct_links():
    return lax.axis_size("rows") == Z * X and lax.axis_size("seq") == Y * C


def copy_out(count, *refs):
    for src, dst in zip(refs[:count], refs[count + 1 :]):
        dst[...] = src[...]
    side, (o_bias, o_gain, o_up) = refs[count], refs[-3:]
    lanes = o_bias.shape[1]
    o_bias[...] = side[:7, :lanes]
    o_gain[...] = side[7:9, :lanes]
    o_up[...] = side[9:10]


def per_device_direct(
    tokens, doc_lengths, qkv_weight, out_weight, up_weight, down_weight, proj_weight, biases, gains, up_bias, cotangent
):
    streams, part, width = tokens.shape
    *kept, result = run_forward(
        tokens, doc_lengths, qkv_weight, out_weight, up_weight, down_weight, proj_weight, biases, gains, up_bias.reshape(1, -1)
    )
    *big, side_sum = run_backward(kept, doc_lengths, cotangent.reshape(streams * part, -1))
    lanes = biases.shape[1]
    shape = jax.ShapeDtypeStruct
    vmem = pl.BlockSpec(memory_space=pltpu.VMEM)
    input_grad, qkv, out, up, down, proj, bias_sum, gain_sum, up_sum = pl.pallas_call(
        functools.partial(copy_out, len(big)),
        out_shape=[shape(a.shape, f32) for a in big] + [shape((7, lanes), f32), shape((2, lanes), f32), shape((1, 128), f32)],
        in_specs=[vmem] * (len(big) + 1),
        out_specs=[vmem] * (len(big) + 3),
    )(*big, side_sum)
    return (
        result.reshape(streams, part, -1),
        input_grad.reshape(streams, part, width),
        qkv,
        out,
        up,
        down,
        proj,
        bias_sum,
        gain_sum,
        up_sum.reshape(-1),
    )


def per_device(*args):
    return per_device_direct(*args) if direct_links() else per_device_any(*args)


def solution(mesh):
    in_specs = (
        P("rows", "seq", None),
        P("rows", None),
        P(("rows", "seq"), None),
        P(("rows", "seq"), None),
        P(("rows", "seq"), None),
        P(("rows", "seq"), None),
        P(("rows", "seq"), None),
        P(None, ("rows", "seq")),
        P(None, ("rows", "seq")),
        P(("rows", "seq")),
        P("rows", "seq", None),
    )
    out_specs = (
        P("rows", "seq", None),
        P("rows", "seq", None),
        P(("rows", "seq"), None),
        P(("rows", "seq"), None),
        P(("rows", "seq"), None),
        P(("rows", "seq"), None),
        P(("rows", "seq"), None),
        P(None, ("rows", "seq")),
        P(None, ("rows", "seq")),
        P(("rows", "seq")),
    )
    return jax.shard_map(
        per_device, mesh=mesh, in_specs=in_specs, out_specs=out_specs, check_vma=False
    )
```

```python
import functools
import math

import jax
import jax.numpy as jnp
from jax import lax
from jax.experimental import pallas as pl
from jax.experimental.pallas import tpu as pltpu
from jax.sharding import PartitionSpec as P

epsilon = 1e-05
rope_base = 10000.0
neg_fill = -1e30

HEAD_DIM = 64
PAIR = 2 * HEAD_DIM
MESH = pl.DeviceIdType.MESH
Z, X, Y, C = 4, 2, 2, 2
OWNERS = Z * X * Y * C
f32, b16 = jnp.float32, jnp.bfloat16
FAR = -1e30


def place():
    r, s = lax.axis_index("rows"), lax.axis_index("seq")
    return r // X, r % X, s // C, s % C


def device(z, x, y, c):
    return (z * X + x, y * C + c)


def greet(peers):
    barrier = pltpu.get_barrier_semaphore()
    for peer in peers:
        pl.semaphore_signal(barrier, inc=1, device_id=peer, device_id_type=MESH)
    pl.semaphore_wait(barrier, len(peers))


def send_to(src, dst, send, recv, peer):
    return pltpu.make_async_remote_copy(
        src_ref=src, dst_ref=dst, send_sem=send, recv_sem=recv, device_id=peer, device_id_type=MESH
    )


def normal_rows(field):
    average = jnp.mean(field, axis=-1, keepdims=True)
    centred = field - average
    inverse = lax.rsqrt(jnp.mean(centred * centred, axis=-1, keepdims=True) + epsilon)
    return centred * inverse, inverse


def doc_marks(sizes, b, places):
    segment, start, end = jnp.zeros_like(places), jnp.zeros_like(places), jnp.int32(0)
    for d in range(sizes.shape[1]):
        end = end + sizes[b, d]
        passed = places >= end
        segment = segment + jnp.where(passed, 1, 0)
        start = start + jnp.where(passed, sizes[b, d], 0)
    return segment, places - start


def far_keys(sizes, b, stream):
    down, _ = doc_marks(sizes, b, lax.broadcasted_iota(jnp.int32, (stream, 1), 0))
    across, _ = doc_marks(sizes, b, lax.broadcasted_iota(jnp.int32, (1, stream), 1))
    return jnp.where(down == across, 0.0, FAR)


class Steps:
    def __init__(self, copies, needs):
        self.copies, self.needs, self.seen = copies, needs, set()

    def arrive(self, names):
        for name in names:
            if name not in self.seen:
                self.seen.add(name)
                self.copies(name).wait_recv()

    def start(self, name):
        self.arrive(self.needs(name))
        self.copies(name).start()

    def run(self, names):
        for name in names:
            self.start(name)


def at_index(index, plan):
    for spot, call in plan.items():

        @pl.when(index == spot)
        def _(call=call):
            call()


FORWARD_ROUTES = ("xzy", "xzy", "zxy")
FORWARD_ORDER = (
    (0, 2, 2), (0, 2, 1), (0, 2, 3), (0, 0), ("a", 0, 1), ("a", 1, 0), ("a", 0, 0), ("a", 0, 2), ("wz", 0, 1),
    (1, 0, 1), ("a", 2, 1), ("wz", 0, 3), ("a", 2, 0), ("a", 2, 2), ("wz", 2, 3), ("a", 1, 1), ("a", 1, 2),
    ("wz", 1, 3), ("ua", 2), ("wz", 0, 2), ("k0", 2), (1, 2), ("y", 2), ("tb",), (0, 1), ("wz", 1, 2),
    ("ua", 1), ("wx", 0), ("wz", 1, 1), (1, 0, 3), ("wz", 2, 2), (1, 0, 2), ("y", 0), ("k0", 0), ("wz", 2, 1),
    ("ua", 0), ("uz", 0, 3), ("uz", 0, 1), ("k0", 1), ("wx", 1), ("uz", 0, 2), ("wx", 2), ("k1", 2),
    ("uz", 1, 1), (2, 0), ("uz", 1, 3), ("k1", 0), ("uz", 1, 2), ("y", 1), ("dz", 1, 3), (2, 2), (3, 0),
    ("bias",), ("ux", 0), ("dz", 1, 2), ("dz", 1, 1), ("k1", 1), ("dz", 0, 3), ("at", 0), ("at", 1),
    ("at", 2), ("ux", 1), ("at", 3), ("at", 4), ("at", 5), ("keep", 0), (3, 2), ("dx", 1), ("dz", 0, 2),
    ("out",), ("ln", 0), ("hy", 0), ("dz", 0, 1), ("ln", 2), ("hk0", 2), ("ln", 1), ("keep", 1), ("hy", 1),
    ("up", 2, 0), ("hk0", 0), ("hk0", 1), ("up", 1, 0), ("dx", 0), ("up", 0, 0), ("hk1", 0), ("up", 0, 1),
    ("hy", 2), ("hk1", 1), ("up", 1, 1), (1, 1, 1), (1, 1, 2), (1, 1, 3), (2, 1), ("dn", 0, 0), ("dn", 0, 1),
    ("fc", 0), ("f2", 0), ("fy", 0), ("dn", 1, 0), ("hk1", 2), ("dn", 1, 1), ("fc", 1), ("f2", 1), ("fy", 1),
    (3, 1), ("dn", 2, 0), ("up", 2, 1), ("dn", 2, 1), ("keep", 2), ("ln2", 0), ("fc", 2), ("f2", 2),
    ("fy", 2), ("ln2", 1), ("ln2", 2), ("keep", 3),
)


def forward_kernel(
    tok, sizes, wqkv, wout, wup, wdown, wproj, biases, gains, up_bias,
    o_out, o_up, o_down, o_proj, o_cols, o_rows, o_tok_t, o_qkv, o_lse, o_att_t, o_n1, o_r1, o_h_t, o_hid_t, o_dgelu,
    o_n2, o_r2, o_nlow_t, o_cos, o_sin, o_res,
    g_out, g_up, g_down, g_proj, g_side, g_cols, g_tok, tok_t, qkv, head_out, far, att, att_t, z_one, n_one, g_h, h_t,
    hid, hid_t, dgelu, n_two, bias_up, mix, cos4, sin4, up_mix, f_send, f_c, f_y_send, f_y,
    c_send, c_recv, a_send, a_recv, wz_send, wz_recv, wx_send, wx_recv, y_send, y_recv, k_send, k_recv, t_send, t_recv,
    ua_send, ua_recv, uz_send, uz_recv, ux_send, ux_recv, fc_send, fc_recv, fy_send, fy_recv, save,
):
    streams, part, width = tok.shape
    rows, stream = streams * part, part * Y * C
    z, x, y, c = place()
    s = y * C + c
    seq_peer = [(y, 1 - c), (1 - y, c), (1 - y, 1 - c)]
    others = [(z + d) % Z for d in range(1, Z)]
    half_width = width // 2
    hidden = g_up.shape[-1]
    cols = wqkv.shape[1] // (3 * Y * C)

    targets = [g_side, g_proj, g_out]
    total = len(targets)
    axis_peer = {"x": device(z, 1 - x, y, c), "y": device(z, x, 1 - y, c)}

    def piece(name):
        stage, k = name[0], name[1]
        route, held = FORWARD_ROUTES[k], targets[k]
        every = slice(None)
        along = {"x": x, "y": y, "z": z}
        spot = {axis: every if axis in route[:stage] else along[axis] for axis in "zxy"}
        if stage == 3:
            slab, slot, peer = held.at[:, :, :, c], 5, device(z, x, y, 1 - c)
        else:
            slab = held.at[spot["z"], spot["x"], spot["y"], c]
            if route[stage] == "z":
                slot, peer = name[2] - 1, device(others[name[2] - 1], x, y, c)
            else:
                slot, peer = 3 + "xy".index(route[stage]), axis_peer[route[stage]]
        return send_to(slab, slab, c_send.at[k, slot], c_recv.at[k, slot], peer)

    def piece_names(stage, k):
        if stage < 3 and FORWARD_ROUTES[k][stage] == "z":
            return [(stage, k, d) for d in range(1, Z)]
        return [(stage, k)]

    def transfer(name):
        kind = name[0]
        if not isinstance(kind, str):
            return piece(name)
        if kind == "a":
            j, p = name[1:]
            yy, cc = seq_peer[p]
            src = wqkv.at[:, pl.ds(pl.multiple_of(j * width + (yy * C + cc) * cols, 128), cols)]
            return send_to(src, g_cols.at[j, z, x, y, c], a_send.at[j, p], a_recv.at[j, p], device(z, x, yy, cc))
        if kind == "wz":
            j, d = name[1:]
            slab = g_cols.at[j, z, x]
            return send_to(slab, slab, wz_send.at[j, d - 1], wz_recv.at[j, d - 1], device(others[d - 1], x, y, c))
        if kind == "wx":
            j = name[1]
            slab = g_cols.at[j, :, x]
            return send_to(slab, slab, wx_send.at[j], wx_recv.at[j], device(z, 1 - x, y, c))
        if kind == "ua":
            p = name[1]
            yy, cc = seq_peer[p]
            return send_to(up_mix.at[yy, cc], g_up.at[z, x, y, c], ua_send.at[p], ua_recv.at[p], device(z, x, yy, cc))
        if kind in ("uz", "dz", "ux", "dx"):
            h, row = name[1], "ud".index(kind[0]) * 2 + name[1]
            lanes = pl.ds(h * half_width, half_width)
            xs = (z, x) if kind[1] == "z" else (slice(None), x)
            slab = g_up.at[*xs, :, :, :, lanes] if kind[0] == "u" else g_down.at[*xs, :, lanes]
            if kind[1] == "z":
                d = name[2]
                return send_to(slab, slab, uz_send.at[row, d - 1], uz_recv.at[row, d - 1], device(others[d - 1], x, y, c))
            return send_to(slab, slab, ux_send.at[row], ux_recv.at[row], device(z, 1 - x, y, c))
        b = name[1]
        if kind == "fc":
            return send_to(f_send.at[b], f_c.at[b], fc_send.at[b], fc_recv.at[b], device(z, x, y, 1 - c))
        if kind == "fy":
            return send_to(f_y_send.at[b], f_y.at[b], fy_send.at[b], fy_recv.at[b], device(z, x, 1 - y, c))
        if kind[0] == "h":
            mine = g_h.at[b, y, c]
            if kind == "hy":
                return send_to(mine, mine, y_send.at[streams + b], y_recv.at[streams + b], device(z, x, 1 - y, c))
            slab = mine if kind == "hk0" else g_h.at[b, 1 - y, c]
            i = int(kind[2])
            return send_to(slab, slab, k_send.at[streams + b, i], k_recv.at[streams + b, i], device(z, x, y, 1 - c))
        if kind == "y":
            return send_to(tok.at[b], g_tok.at[b, y, c], y_send.at[b], y_recv.at[b], device(z, x, 1 - y, c))
        if kind == "k0":
            return send_to(tok.at[b], g_tok.at[b, y, c], k_send.at[b, 0], k_recv.at[b, 0], device(z, x, y, 1 - c))
        slab = g_tok.at[b, 1 - y, c]
        return send_to(slab, slab, k_send.at[b, 1], k_recv.at[b, 1], device(z, x, y, 1 - c))

    def needs(name):
        kind = name[0]
        if not isinstance(kind, str):
            return piece_names(kind - 1, name[1]) if kind else []
        if kind == "wz":
            return [("a", name[1], p) for p in range(3)]
        if kind == "wx":
            return [("wz", name[1], d) for d in range(1, Z)]
        if kind in ("uz", "ux"):
            return [("ua", p) for p in range(3)] if kind == "uz" else [("uz", name[1], d) for d in range(1, Z)]
        if kind == "dx":
            return [("dz", name[1], d) for d in range(1, Z)]
        return {"k1": [("y", name[1])], "hk1": [("hy", name[1])]}.get(kind, [])

    steps = Steps(transfer, needs)

    def att_seq(i, p):
        b, half = i // 2, i % 2
        yy, cc = seq_peer[p]
        lane = pl.multiple_of((s * 2 + half) * PAIR, PAIR)
        dst = att.at[b, :, pl.ds(lane, PAIR)]
        return send_to(head_out.at[b, half, yy, cc], dst, t_send.at[i, p], t_recv.at[i, p], device(z, x, yy, cc))

    mix[...] = jnp.zeros_like(mix)
    lanes_own = biases.shape[1]
    mix[0:7, 0:lanes_own] = biases[...].astype(f32)
    mix[7:9, 0:lanes_own] = gains[...].astype(f32)
    mix[9:10] = up_bias[...].astype(f32)
    g_side[z, x, y, c] = mix[...].astype(b16)
    g_proj[z, x, y, c] = wproj[...]
    g_out[z, x, y, c] = wout[...]
    for yc in range(Y * C):
        for zx in range(Z * X):
            lane_at = (zx * Y * C + yc) * 128
            up_mix[yc // C, yc % C, :, zx * 128 : (zx + 1) * 128] = wup[:, lane_at : lane_at + 128]
    g_up[z, x, y, c] = up_mix[y, c]
    g_down[z, x] = wdown[...]
    for j in range(3):
        g_cols[j, z, x, y, c] = wqkv[:, pl.ds(pl.multiple_of(j * width + s * cols, 128), cols)]
    for b in range(streams):
        g_tok[b, y, c] = tok[b]
    greet(
        [device(zz, x, y, c) for zz in others]
        + [device(z, 1 - x, y, c)]
        + [device(z, x, yy, cc) for yy, cc in seq_peer]
    )

    lane = lax.broadcasted_iota(jnp.int32, (1, PAIR), 1)
    low_half = (lane % HEAD_DIM) < HEAD_DIM // 2
    inverse_f = jnp.exp((lane % (HEAD_DIM // 2)).astype(f32) * (-math.log(rope_base) / (HEAD_DIM // 2)))

    def tables(b):
        _, position = doc_marks(sizes, b, lax.broadcasted_iota(jnp.int32, (stream, PAIR), 0))
        angle = position.astype(f32) * inverse_f
        cos4[b] = jnp.cos(angle)
        sin4[b] = jnp.sin(angle) * jnp.where(low_half, -1.0, 1.0)

    def all_tables():
        pl.loop(0, streams)(tables)

    def whole_rows():
        steps.arrive(piece_names(3, 0))
        lanes = lax.broadcasted_iota(jnp.int32, (16, 128), 1)
        share = 128 // (Y * C)
        for zx in range(Z * X):
            tile = jnp.zeros((16, 128), f32)
            for yc in range(Y * C):
                block = g_side[zx // X, zx % X, yc // C, yc % C].astype(f32)
                tile = tile + pltpu.roll(jnp.where(lanes < share, block, 0.0), yc * share, 1)
            o_rows[:, pl.ds(zx * 128, 128)] = tile
            bias_up[:, pl.ds(zx * 128, 128)] = g_side[zx // X, zx % X, y, c].astype(f32)[9:10]

    def project(b):
        rows_b = g_tok[b].reshape(stream, width)
        tok_t[b] = rows_b.T
        for j in range(3):
            bias_row = o_rows[pl.ds(j, 1), pl.ds(pl.multiple_of(s * cols, 128), cols)]
            got = jnp.dot(rows_b, g_cols[j].reshape(width, cols), preferred_element_type=f32) + bias_row
            for half in range(2):
                t = got[:, half * PAIR : (half + 1) * PAIR]
                if j < 2:
                    swapped = jnp.where(
                        low_half, pltpu.roll(t, PAIR - HEAD_DIM // 2, 1), pltpu.roll(t, HEAD_DIM // 2, 1)
                    )
                    t = t * cos4[b] + swapped * sin4[b]
                qkv[j, b, half] = t.astype(b16)
        far[...] = far_keys(sizes, b, stream)

    q_block = stream // 2
    top = lax.broadcasted_iota(jnp.int32, (PAIR, 1), 0) < HEAD_DIM
    score_scale = HEAD_DIM**-0.5
    masks = [jnp.where(lane < HEAD_DIM, score_scale, 0.0).astype(b16), jnp.where(lane < HEAD_DIM, 0.0, score_scale).astype(b16)]

    def attend(i):
        b, half = i // 2, i % 2
        queries, keys = qkv[0, b, half], qkv[1, b, half]
        values_t = qkv[2, b, half].T
        for block in range(2):
            at = slice(block * q_block, (block + 1) * q_block)
            turned = []
            for head in range(2):
                q = queries[at] * masks[head]
                scores = lax.dot_general(keys, q, (((1,), (1,)), ((), ())), preferred_element_type=f32)
                scores = scores + far[:, pl.ds(block * q_block, q_block)]
                most = jnp.max(scores, axis=0, keepdims=True)
                e = jnp.exp(scores - most)
                mass = jnp.sum(e, axis=0, keepdims=True)
                o_lse[i, pl.ds(head, 1), pl.ds(block * q_block, q_block)] = most + jnp.log(mass)
                probs = (e * (1.0 / mass)).astype(b16)
                turned.append(jnp.dot(values_t, probs, preferred_element_type=f32))
            both = jnp.where(top, turned[0], turned[1]).T.astype(b16)
            for cc in range(C):
                head_out[b, half, block, cc] = both[cc * part : (cc + 1) * part]
        for p in range(3):
            att_seq(i, p).start()
        lane_at = pl.multiple_of((s * 2 + half) * PAIR, PAIR)
        att[b, :, pl.ds(lane_at, PAIR)] = head_out[b, half, y, c]

    n_block = 256
    r_block = part

    def attention_out():
        @pl.loop(0, streams * 2)
        def _(i):
            for p in range(3):
                att_seq(i, p).wait_recv()

        steps.arrive(piece_names(3, 2))

        @pl.loop(0, width // n_block)
        def _(n):
            at = pl.ds(pl.multiple_of(n * n_block, n_block), n_block)
            w = g_out[:, :, :, :, :, at].reshape(width, n_block)
            got = jnp.dot(att[...].reshape(rows, width), w, preferred_element_type=f32)
            z_one[:, at] = tok[:, :, at].reshape(rows, n_block).astype(f32) + (got + o_rows[3:4, at])

    def rows_of(b):
        return slice(b * part, (b + 1) * part)

    def first_norm(b):
        at = rows_of(b)
        n, inverse = normal_rows(z_one[at])
        n_one[at] = n
        o_r1[at] = jnp.broadcast_to(inverse, (part, 128))
        h = n * o_rows[7:8] + o_rows[4:5]
        z_one[at] = h
        g_h[b, y, c] = h.astype(b16)
        att_t[:, at] = att[b].T

    def hidden_rows(b, away):
        yy = 1 - y if away else y
        steps.arrive([("ux", 0), ("ux", 1)] + ([("hy", b), ("hk1", b)] if away else [("hk0", b)]))
        h = g_h[b, yy].reshape(C * part, width)
        col = pl.ds(pl.multiple_of(yy * C * part, C * part), C * part)
        h_t[b, :, col] = h.T

        @pl.loop(0, hidden // n_block)
        def _(n):
            at = pl.ds(pl.multiple_of(n * n_block, n_block), n_block)
            w = g_up[:, :, :, :, :, at].reshape(width, n_block)
            u = jnp.dot(g_h[b, yy].reshape(C * part, width), w, preferred_element_type=f32) + bias_up[:, at]
            cdf = 0.5 * (1.0 + lax.erf(u * (2.0**-0.5)))
            low = (u * cdf).astype(b16)
            hid[b, yy, :, at] = low
            hid_t[b, at, col] = low.T
            dgelu[b, yy, :, at] = (cdf + u * (jnp.exp(-0.5 * u * u) * ((2.0 * math.pi) ** -0.5))).astype(b16)

    def down_rows(b, away):
        yy = 1 - y if away else y
        steps.arrive([("dx", 0), ("dx", 1)])
        at = rows_of(b)

        @pl.loop(0, width // n_block)
        def _(n):
            col = pl.ds(pl.multiple_of(n * n_block, n_block), n_block)
            w = g_down[:, :, :, col].reshape(hidden, n_block)
            f_send[b, yy, :, col] = jnp.dot(hid[b, yy, pl.ds((1 - c) * part, part)], w, preferred_element_type=f32).astype(b16)
            got = jnp.dot(hid[b, yy, pl.ds(c * part, part)], w, preferred_element_type=f32)
            if away:
                n_two[at, col] = got
            else:
                z_one[at, col] += got + o_rows[5:6, col]

    def core_sum(b):
        steps.arrive([("fc", b)])
        at = rows_of(b)
        f_y_send[b] = (n_two[at] + f_c[b, 1 - y].astype(f32)).astype(b16)

    def second_norm(b):
        steps.arrive([("fy", b)] + piece_names(3, 1))
        at = rows_of(b)
        n, inverse = normal_rows(z_one[at] + f_c[b, y].astype(f32) + f_y[b].astype(f32))
        n_two[at] = n
        o_r2[at] = jnp.broadcast_to(inverse, (part, 128))
        low = (n * o_rows[8:9] + o_rows[6:7]).astype(b16)
        o_nlow_t[:, at] = low.T
        o_res[at] = jnp.dot(low, g_proj[...].reshape(width, wproj.shape[1]), preferred_element_type=f32).astype(b16)

    kept = [(cos4, o_cos), (sin4, o_sin), (tok_t, o_tok_t), (qkv, o_qkv)]
    kept += [
        (g_cols.at[j, :, :, :, :, :, pl.ds(half * PAIR, PAIR)], o_cols.at[half, :, :, :, :, :, pl.ds(j * PAIR, PAIR)])
        for j in range(3)
        for half in range(2)
    ]
    early = len(kept)
    kept += [(g_out, o_out), (att_t, o_att_t), (n_one, o_n1)]
    middle = len(kept)
    kept += [(g_up, o_up), (g_down, o_down), (h_t, o_h_t), (hid_t, o_hid_t), (dgelu, o_dgelu)]
    late = len(kept)
    kept += [(n_two, o_n2), (g_proj, o_proj)]
    copies = [pltpu.make_async_copy(a, b, save.at[i]) for i, (a, b) in enumerate(kept)]

    def keep(first_copy, last_copy):
        for copy in copies[first_copy:last_copy]:
            copy.start()

    work = {
        "tb": all_tables, "bias": whole_rows, "out": attention_out, "ln": first_norm, "up": hidden_rows, "dn": down_rows,
        "f2": core_sum, "ln2": second_norm, "keep": lambda i: keep((0, early, middle, late)[i], (early, middle, late, len(kept))[i]),
    }
    spots = [i for i, name in enumerate(FORWARD_ORDER) if name[0] == "at"]

    def run(first_spot, last_spot):
        for name in FORWARD_ORDER[first_spot:last_spot]:
            if name[0] in work:
                work[name[0]](*name[1:])
            else:
                steps.start(name)

    run(0, spots[0])

    def before(i):
        if i:
            run(spots[i - 1] + 1, spots[i])
        if i % 2 == 0:
            steps.arrive([("wx", j) for j in range(3)] + [("k0", i // 2), ("k1", i // 2)])

    @pl.loop(0, streams * 2)
    def _(i):
        at_index(i, {spot: functools.partial(before, spot) for spot in range(streams * 2)})

        @pl.when(i % 2 == 0)
        def _():
            project(i // 2)

        attend(i)

    run(spots[-1] + 1, len(FORWARD_ORDER))
    for k in range(total):
        for stage in range(4):
            for name in piece_names(stage, k):
                transfer(name).wait_send()
    for j in range(3):
        for p in range(3):
            transfer(("a", j, p)).wait_send()
        for d in range(1, Z):
            transfer(("wz", j, d)).wait_send()
        transfer(("wx", j)).wait_send()
    for p in range(3):
        transfer(("ua", p)).wait_send()
    for kind in "ud":
        for h in range(2):
            for d in range(1, Z):
                transfer((kind + "z", h, d)).wait_send()
            transfer((kind + "x", h)).wait_send()
    for b in range(streams):
        for kind in ("y", "k0", "k1", "hy", "hk0", "hk1", "fc", "fy"):
            transfer((kind, b)).wait_send()

    @pl.loop(0, streams * 2)
    def _(i):
        for p in range(3):
            att_seq(i, p).wait_send()

    for copy in copies:
        copy.wait()


def run_forward(tokens, sizes, wqkv, wout, wup, wdown, wproj, biases, gains, up_bias):
    streams, part, width = tokens.shape
    rows, stream, hidden = streams * part, part * Y * C, wup.shape[1] // (Y * C)
    proj = wproj.shape[1]
    cols = width // (Y * C)
    grid = (Z, X, Y, C)
    shape = jax.ShapeDtypeStruct
    vmem, hbm = pl.BlockSpec(memory_space=pltpu.VMEM), pl.BlockSpec(memory_space=pl.ANY)
    vm = pltpu.VMEM
    outs = [
        ((grid + wout.shape, b16), hbm),
        ((grid + (wup.shape[0], hidden), b16), hbm),
        (((Z, X) + wdown.shape, b16), hbm),
        ((grid + wproj.shape, b16), hbm),
        (((2,) + grid + (wqkv.shape[0], 3 * PAIR), b16), hbm),
        (((16, width), f32), vmem),
        (((streams, width, stream), b16), hbm),
        (((3, streams, 2, stream, PAIR), b16), hbm),
        (((streams * 2, 8, stream), f32), vmem),
        (((width, rows), b16), hbm),
        (((rows, width), f32), hbm),
        (((rows, 128), f32), vmem),
        (((streams, width, stream), b16), hbm),
        (((streams, hidden, stream), b16), hbm),
        (((streams, Y, C * part, hidden), b16), hbm),
        (((rows, width), f32), hbm),
        (((rows, 128), f32), vmem),
        (((width, rows), b16), vmem),
        (((streams, stream, PAIR), f32), hbm),
        (((streams, stream, PAIR), f32), hbm),
        (((rows, proj), b16), vmem),
    ]
    dma = pltpu.SemaphoreType.DMA
    scratch = [
        vm(grid + wout.shape, b16),
        vm(grid + (wup.shape[0], hidden), b16),
        vm((Z, X) + wdown.shape, b16),
        vm(grid + wproj.shape, b16),
        vm(grid + (16, 128), b16),
        vm((3,) + grid + (wqkv.shape[0], cols), b16),
        vm((streams, Y, C, part, width), b16),
        vm((streams, width, stream), b16),
        vm((3, streams, 2, stream, PAIR), b16),
        vm((streams, 2, Y, C, part, PAIR), b16),
        vm((stream, stream), f32),
        vm((streams, part, width), b16),
        vm((width, rows), b16),
        vm((rows, width), f32),
        vm((rows, width), f32),
        vm((streams, Y, C, part, width), b16),
        vm((streams, width, stream), b16),
        vm((streams, Y, C * part, hidden), b16),
        vm((streams, hidden, stream), b16),
        vm((streams, Y, C * part, hidden), b16),
        vm((rows, width), f32),
        vm((1, hidden), f32),
        vm((16, 128), f32),
        vm((streams, stream, PAIR), f32),
        vm((streams, stream, PAIR), f32),
        vm((Y, C, wup.shape[0], hidden), b16),
        vm((streams, Y, part, width), b16), vm((streams, Y, part, width), b16), vm((streams, part, width), b16), vm((streams, part, width), b16),
        dma((3, 6)), dma((3, 6)), dma((3, 3)), dma((3, 3)), dma((3, 3)), dma((3, 3)), dma((3,)), dma((3,)),
        dma((2 * streams,)), dma((2 * streams,)), dma((2 * streams, 2)), dma((2 * streams, 2)), dma((streams * 2, 3)), dma((streams * 2, 3)),
        dma((3,)), dma((3,)), dma((4, 3)), dma((4, 3)), dma((4,)), dma((4,)), dma((streams,)), dma((streams,)), dma((streams,)), dma((streams,)),
        dma((26,)),
    ]
    return pl.pallas_call(
        forward_kernel,
        out_shape=[shape(*o[0]) for o in outs],
        in_specs=[vmem, pl.BlockSpec(memory_space=pltpu.SMEM)] + [vmem] * 8,
        out_specs=[o[1] for o in outs],
        scratch_shapes=scratch,
        compiler_params=pltpu.CompilerParams(collective_id=3, has_side_effects=True, vmem_limit_bytes=63 << 20),
    )(tokens, sizes, wqkv, wout, wup, wdown, wproj, biases, gains, up_bias)


def turned_back(t, cosine, sine, low_half):
    swapped = jnp.where(low_half, pltpu.roll(t, PAIR - HEAD_DIM // 2, 1), pltpu.roll(t, HEAD_DIM // 2, 1))
    return t * cosine - swapped * sine


BACKWARD_ROUTES = ("yxz", "xzy", "yxz")
BACKWARD_ORDER = (
    ("ln2b", 2), ("mk", 1), ("ln2b", 0), ("own", 1), ("ln2b", 1), ("gh", 2, 0), ("gh", 0, 0), ("g1", 0, 0),
    ("add", 1, 0), ("gh", 1, 0), ("g1", 2, 0), ("gk", 2), ("gh", 2, 1), ("g1", 2, 1), ("f2", 2), ("gk", 0),
    ("gh", 0, 1), ("g1", 0, 1), ("add", 1, 1), ("gk", 1), ("w1", 0), ("f2", 0), ("g1", 1, 0), ("gh", 1, 1),
    ("g1", 1, 1), ("ln1b", 2), ("w1", 2), ("fin", 1), ("w1", 3), ("f2", 1), ("w1", 1), ("w2", 0), ("ln1b", 0),
    ("ln1b", 1), ("ga", 1), ("ga", 0), ("ga", 2), ("mk", 0), ("own", 0), ("w2", 2), ("ga", 3), ("at", 0),
    ("at", 1), ("at", 2), ("q1", 0), ("w2", 3), ("at", 3), ("at", 4), ("at", 5), ("q1", 1), ("add", 0, 0),
    ("i1", 0), ("w3", 2), ("w2", 1), ("w3", 0), ("mk", 2), ("i2", 0), ("w4", 0), ("w3", 3), ("own", 2),
    ("i1", 2), ("i2", 2), ("q2", 0), ("i1", 1), ("i2", 1), ("i3", 1), ("w4", 1), ("add", 2, 0), ("w3", 1),
    ("i3", 0), ("i4", 0), ("q2", 1), ("i3", 2), ("i4", 2), ("i4", 1), ("add", 0, 1), ("add", 2, 1), ("q3", 0),
    ("q4", 0), ("q3", 1), ("q4", 1), ("fin", 0), ("fin", 2),
)


def backward_kernel(
    w_out, w_up, w_down, w_proj, w_cols, side_rows, i_tok_t, i_qkv, lse, i_att_t, i_n1, r_one, i_h_t, i_hid_t, i_dgelu, i_n2, r_two, nlow_t,
    cos4, sin4, sizes, cot_f,
    o_in, o_qkv, o_out, o_up, o_down, o_proj, o_side,
    wo, wu, wd, norm, att_t, h_t, hid_t, dgelu, tok_t, qkv, cols_all, sums, sum_up, grad_ffn, grad_branch, grad_att, heads, far,
    turned, send_o, send_p, send_s, cot, w_send, w_x, w_z, u_seq, u_in, apart, g_send, g_c, g_y_send, g_y,
    q_send, q_x, q_z, q_seq, q_in,
    c_send, c_recv, a_send, a_recv, qx_send, qx_recv, qz_send, qz_recv, qs_send, qs_recv, ic_send, ic_recv, iy_send, iy_recv,
    wx_send, wx_recv, wz_send, wz_recv, us_send, us_recv, gy_send, gy_recv, gk_send, gk_recv, gc_send, gc_recv, gf_send, gf_recv,
    load, *pieces,
):
    rows, width = o_in.shape
    streams = qkv.shape[1]
    part, stream = rows // streams, qkv.shape[3]
    hidden = sum_up.shape[1]
    half_width = width // 2
    cols = width // (Y * C)
    block = 512
    z, x, y, c = place()
    s = y * C + c
    seq_peer = [(y, 1 - c), (1 - y, c), (1 - y, 1 - c)]
    others = [(z + d) % Z for d in range(1, Z)]
    nt = (((1,), (1,)), ((), ()))
    grad_u = dgelu

    first_loads = [(i_n2, norm), (w_down, wd), (i_dgelu, dgelu), (w_up, wu), (i_hid_t, hid_t), (i_h_t, h_t), (i_n1, norm), (w_out, wo)]
    first_loads += [(i_att_t, att_t), (i_qkv, qkv), (i_tok_t, tok_t), (w_cols, cols_all)]
    loads = [pltpu.make_async_copy(a, b, load.at[i]) for i, (a, b) in enumerate(first_loads)]
    for i, copy in enumerate(loads):
        if i != 6:
            copy.start()
    loaded = set()

    def need(*which):
        for i in which:
            if i not in loaded:
                loaded.add(i)
                loads[i].wait()

    greet(
        [device(zz, x, y, c) for zz in others]
        + [device(z, 1 - x, y, c)]
        + [device(z, x, yy, cc) for yy, cc in seq_peer]
    )

    outgoing = [send_o, send_p, send_s.at[:, :, :, 1 - c]]
    total = len(outgoing)
    held, landed = pieces[:total], [pieces[total + 3 * k : total + 3 * k + 3] for k in range(total)]
    own_spot = {"z": z, "x": x, "y": y}
    axis_size = {"z": Z, "x": X, "y": Y}

    def to_core(k):
        return send_to(outgoing[k], held[k], c_send.at[k, 8], c_recv.at[k, 8], device(z, x, y, 1 - c))

    def along(k, stage):
        route = BACKWARD_ROUTES[k]
        axis = route[stage]
        if axis == "z":
            peers = [(others[d], device(others[d], x, y, c)) for d in range(Z - 1)]
        else:
            peers = [(1 - x, device(z, 1 - x, y, c))] if axis == "x" else [(1 - y, device(z, x, 1 - y, c))]
        copies = []
        for d, (spot, peer) in enumerate(peers):
            at = {a: own_spot[a] if a in route[:stage] else slice(None) for a in "zxy"} | {axis: spot}
            dst = landed[k][stage].at[d] if axis == "z" else landed[k][stage]
            slot = d if axis == "z" else 3 + stage
            copies.append(send_to(held[k].at[at["z"], at["x"], at["y"]], dst, c_send.at[k, slot], c_recv.at[k, slot], peer))
        return copies

    def begin(k, stage):
        for copy in along(k, stage):
            copy.start()

    def arrived(k, stage):
        for copy in along(k, stage):
            copy.wait_recv()

    def add_landed(k, stage):
        route = BACKWARD_ROUTES[k]
        arrived(k, stage)
        rest = [a for a in "zxy" if a not in route[: stage + 1]]
        count = math.prod(axis_size[a] for a in rest)

        @pl.loop(0, count)
        def _(i):
            at, spot = dict(own_spot), []
            for a in reversed(rest):
                at[a] = i % axis_size[a]
                spot.insert(0, at[a])
                i = i // axis_size[a]
            here = (at["z"], at["x"], at["y"])
            value = held[k][here].astype(f32)
            if route[stage] == "z":
                for d in range(Z - 1):
                    value = value + landed[k][stage][(d, *spot)].astype(f32)
            else:
                value = value + landed[k][stage][tuple(spot)].astype(f32)
            held[k][here] = value.astype(b16)

        begin(k, stage + 1)

    def half_rows(a_t, core, b, at):
        return jnp.dot(a_t[:, :, :, core].reshape(-1, rows), b[:, at], preferred_element_type=f32)

    def make_send(k):
        if k == 0:

            @pl.loop(0, width // block)
            def _(n):
                at = pl.ds(pl.multiple_of(n * block, block), block)
                send_o[:, :, :, :, at] = half_rows(att_t, 1 - c, grad_branch, at).astype(b16).reshape(Z, X, Y, -1, block)

        else:
            send_p[...] = half_rows(nlow_t, 1 - c, cot, slice(None)).astype(b16).reshape(Z, X, Y, -1, cot.shape[1])
        to_core(k).start()

    def own_half(k):
        to_core(k).wait_recv()
        mine = held[k]
        if k == 0:

            @pl.loop(0, width // block)
            def _(n):
                at = pl.ds(pl.multiple_of(n * block, block), block)
                got = half_rows(att_t, c, grad_branch, at).reshape(Z, X, Y, -1, block)
                mine[:, :, :, :, at] = (mine[:, :, :, :, at].astype(f32) + got).astype(b16)

        elif k == 1:
            got = half_rows(nlow_t, c, cot, slice(None)).reshape(Z, X, Y, -1, cot.shape[1])
            mine[...] = (mine[...].astype(f32) + got).astype(b16)
        else:
            mine[...] = (mine[...].astype(f32) + send_s[:, :, :, c].astype(f32)).astype(b16)
        begin(k, 0)

    def finish(k):
        arrived(k, 2)
        value = held[k][z, x, y].astype(f32)
        if BACKWARD_ROUTES[k][2] == "z":
            for d in range(Z - 1):
                value = value + landed[k][2][d].astype(f32)
        else:
            value = value + landed[k][2][...].astype(f32)
        (o_out, o_proj, o_side)[k][...] = value

    def ffn_rows(k, xx, n):
        lanes = pl.ds(pl.multiple_of((k % 2) * half_width + n * 256, 256), 256)
        got = jnp.zeros((Z * 128, 256), f32)
        for b in range(streams):
            left = (hid_t if k < 2 else h_t)[b, :, xx].reshape(Z * 128, stream)
            right = (grad_ffn[b, :, :, :, lanes] if k < 2 else grad_u[b, :, :, lanes]).reshape(stream, 256)
            got = got + jnp.dot(left, right, preferred_element_type=f32)
        return got.reshape(Z, 128, 256)

    def ffn_x(k):
        return send_to(w_send.at[k], w_x.at[k], wx_send.at[k], wx_recv.at[k], device(z, 1 - x, y, c))

    def ffn_z(k, d):
        return send_to(w_x.at[k, others[d]], w_z.at[k, d], wz_send.at[k, d], wz_recv.at[k, d], device(others[d], x, y, c))

    def ffn_seq(h, p):
        yy, cc = seq_peer[p]
        return send_to(u_seq.at[h, yy, cc], u_in.at[h, y, c], us_send.at[h, p], us_recv.at[h, p], device(z, x, yy, cc))

    def ffn_one(k):
        need(4, 5)
        for b in range(streams):
            core_arrived(b, 0)
            core_arrived(b, 1)

        @pl.loop(0, half_width // 256)
        def _(n):
            w_send[k, :, :, pl.ds(pl.multiple_of(n * 256, 256), 256)] = ffn_rows(k, 1 - x, n).astype(b16)

        ffn_x(k).start()

    def ffn_two(k):
        ffn_x(k).wait_recv()

        @pl.loop(0, half_width // 256)
        def _(n):
            at = pl.ds(pl.multiple_of(n * 256, 256), 256)
            w_x[k, :, :, at] = (w_x[k, :, :, at].astype(f32) + ffn_rows(k, x, n)).astype(b16)

        for d in range(Z - 1):
            ffn_z(k, d).start()

    def ffn_three(k):
        value = w_x[k, z].astype(f32)
        for d in range(Z - 1):
            ffn_z(k, d).wait_recv()
        for d in range(Z - 1):
            value = value + w_z[k, d].astype(f32)
        if k < 2:
            o_down[:, k * half_width : (k + 1) * half_width] = value
        else:
            u_seq[k - 2] = value.astype(b16).reshape(Y, C, -1, half_width)
            for p in range(3):
                ffn_seq(k - 2, p).start()
            u_in[k - 2, y, c] = u_seq[k - 2, y, c]

    def ffn_four(h):
        for p in range(3):
            ffn_seq(h, p).wait_recv()
        for owner in range(Y * C):
            for q in range(half_width // 128):
                lane_at = ((h * (half_width // 128) + q) * Y * C + owner) * 128
                o_up[:, lane_at : lane_at + 128] = u_in[h, owner // C, owner % C, :, q * 128 : (q + 1) * 128].astype(f32)

    sums[...] = jnp.zeros_like(sums)
    sum_up[...] = jnp.zeros_like(sum_up)
    cot[...] = cot_f[...].astype(b16)

    def rows_of(b):
        return slice(b * part, (b + 1) * part)

    def norm_back(e, gain_row, n, inverse, spots):
        ge = e * side_rows[gain_row : gain_row + 1]
        mean = jnp.mean(ge, axis=-1, keepdims=True)
        along = jnp.mean(ge * n, axis=-1, keepdims=True)
        grad = inverse * (ge - mean - n * along)
        low = grad.astype(b16)
        for spot, value in zip(spots, (e * n, e, low.astype(f32))):
            sums[spot : spot + 1] += jnp.sum(value, axis=0, keepdims=True)
        return grad, low

    def grad_y(b):
        mine = grad_ffn.at[b, y, c]
        return send_to(mine, mine, gy_send.at[b], gy_recv.at[b], device(z, x, 1 - y, c))

    def grad_core(b, i):
        slab = grad_ffn.at[b, 1 - y if i else y, c]
        return send_to(slab, slab, gk_send.at[b, i], gk_recv.at[b, i], device(z, x, y, 1 - c))

    used = []

    def second_norm_back(b):
        need(0)
        at = rows_of(b)
        e = lax.dot_general(cot[at], w_proj[...], nt, preferred_element_type=f32)
        o_in[at], low = norm_back(e, 8, norm[at], r_two[at, :1], (8, 6, 5))
        grad_ffn[b, y, c] = low
        used.append(b)
        if len(used) == streams:
            loads[6].start()
        grad_y(b).start()
        grad_core(b, 0).start()

    def forward_grad(b):
        grad_y(b).wait_recv()
        grad_core(b, 1).start()

    core_here = set()

    def core_arrived(b, i):
        if (b, i) not in core_here:
            core_here.add((b, i))
            grad_core(b, i).wait_recv()

    def hidden_back(b, away):
        need(1, 2)
        yy = 1 - y if away else y
        core_arrived(b, 1 if away else 0)

        @pl.loop(0, hidden // block)
        def _(n):
            at = pl.ds(pl.multiple_of(n * block, block), block)
            got = lax.dot_general(grad_ffn[b, yy].reshape(C * part, width), wd[at], nt, preferred_element_type=f32)
            low = (got * dgelu[b, yy, :, at].astype(f32)).astype(b16)
            grad_u[b, yy, :, at] = low
            sum_up[:, at] += jnp.sum(low.astype(f32), axis=0, keepdims=True)

    def share_core(b):
        return send_to(g_send.at[b], g_c.at[b], gc_send.at[b], gc_recv.at[b], device(z, x, y, 1 - c))

    def share_y(b):
        return send_to(g_y_send.at[b], g_y.at[b], gf_send.at[b], gf_recv.at[b], device(z, x, 1 - y, c))

    ready = set()

    def inner_back(b, away):
        need(3)
        yy = 1 - y if away else y
        at = rows_of(b)

        @pl.loop(0, width // block)
        def _(n):
            col = pl.ds(pl.multiple_of(n * block, block), block)
            got = lax.dot_general(grad_u[b, yy, pl.ds((1 - c) * part, part)], wu[col], nt, preferred_element_type=f32)
            g_send[b, yy, :, col] = got.astype(b16)
            got = lax.dot_general(grad_u[b, yy, pl.ds(c * part, part)], wu[col], nt, preferred_element_type=f32)
            if away:
                apart[at, col] = got
            else:
                o_in[at, col] += got

        ready.add((b, away))
        if len([r for r in ready if r[0] == b]) == 2:
            share_core(b).start()

    def core_sum(b):
        share_core(b).wait_recv()
        g_y_send[b] = (apart[rows_of(b)] + g_c[b, 1 - y].astype(f32)).astype(b16)
        share_y(b).start()

    def first_norm_back(b):
        need(6)
        at = rows_of(b)
        share_y(b).wait_recv()
        e = o_in[at] + g_c[b, y].astype(f32) + g_y[b].astype(f32)
        o_in[at], grad_branch[at] = norm_back(e, 7, norm[at], r_one[at, :1], (7, 4, 3))

    def att_seq(p):
        yy, cc = seq_peer[p]
        src = grad_att.at[:, :, pl.ds(pl.multiple_of((yy * C + cc) * cols, cols), cols)]
        return send_to(src, heads.at[:, y, c], a_send.at[p], a_recv.at[p], device(z, x, yy, cc))

    def grad_heads(to):
        need(7)
        at = pl.ds(pl.multiple_of(to * cols, cols), cols)
        got = lax.dot_general(grad_branch[...], wo[at], nt, preferred_element_type=f32)
        grad_att[:, :, at] = got.astype(b16).reshape(streams, part, cols)

    def att_back_send(p):
        if p < 3:
            yy, cc = seq_peer[p]
            grad_heads(yy * C + cc)
            att_seq(p).start()
        else:
            grad_heads(s)
            heads[:, y, c] = grad_att[:, :, pl.ds(pl.multiple_of(s * cols, cols), cols)]

    lane = lax.broadcasted_iota(jnp.int32, (1, PAIR), 1)
    low_half = (lane % HEAD_DIM) < HEAD_DIM // 2
    top = lax.broadcasted_iota(jnp.int32, (PAIR, 1), 0) < HEAD_DIM
    masks = [(lane < HEAD_DIM).astype(f32).astype(b16), (lane >= HEAD_DIM).astype(f32).astype(b16)]
    score_scale = HEAD_DIM**-0.5
    q_block = stream // 2

    def attend_back(i):
        half, b = i // streams, i % streams
        far[...] = far_keys(sizes, b, stream)
        queries, keys, values = qkv[0, b, half], qkv[1, b, half], qkv[2, b, half]
        given = heads[b, :, :, :, pl.ds(pl.multiple_of(half * PAIR, PAIR), PAIR)].reshape(stream, PAIR)
        keys_t = keys.T
        grad_k, grad_v = jnp.zeros((stream, PAIR), f32), jnp.zeros((stream, PAIR), f32)
        grad_q = []
        for part_q in range(2):
            at = slice(part_q * q_block, (part_q + 1) * q_block)
            q_t = []
            for head in range(2):
                q = queries[at] * (masks[head] * b16(score_scale))
                g = given[at] * masks[head]
                scores = lax.dot_general(keys, q, nt, preferred_element_type=f32) + far[:, at]
                probs = jnp.exp(scores - lse[b * 2 + half, head : head + 1, at])
                grad_p = lax.dot_general(values, g, nt, preferred_element_type=f32)
                row_dot = jnp.sum(probs * grad_p, axis=0, keepdims=True)
                grad_s = (probs * (grad_p - row_dot)).astype(b16)
                grad_v = grad_v + jnp.dot(probs.astype(b16), g, preferred_element_type=f32)
                grad_k = grad_k + jnp.dot(grad_s, q, preferred_element_type=f32)
                q_t.append(jnp.dot(keys_t, grad_s, preferred_element_type=f32))
            grad_q.append(jnp.where(top, q_t[0], q_t[1]).T * score_scale)
        grad_q = jnp.concatenate(grad_q, axis=0)
        lane_at = pl.multiple_of(s * cols + half * PAIR, PAIR)
        done = []
        for t in (grad_q, grad_k):
            done.append(turned_back(t.astype(b16).astype(f32), cos4[b], sin4[b], low_half).astype(b16))
        done.append(grad_v.astype(b16))
        for j in range(3):
            turned[half, b, :, j * PAIR : (j + 1) * PAIR] = done[j]
            sums[j : j + 1, pl.ds(lane_at, PAIR)] += jnp.sum(done[j].astype(f32), axis=0, keepdims=True)

    def qkv_rows(half, xx):
        got = jnp.zeros((Z * 128, 3 * PAIR), f32)
        for b in range(streams):
            got = got + jnp.dot(tok_t[b, :, xx].reshape(Z * 128, stream), turned[half, b], preferred_element_type=f32)
        return got.reshape(Z, 128, 3 * PAIR)

    def qkv_x(half):
        return send_to(q_send.at[half], q_x.at[half], qx_send.at[half], qx_recv.at[half], device(z, 1 - x, y, c))

    def qkv_z(half, d):
        return send_to(q_x.at[half, others[d]], q_z.at[half, d], qz_send.at[half, d], qz_recv.at[half, d], device(others[d], x, y, c))

    def qkv_seq(half, p):
        yy, cc = seq_peer[p]
        return send_to(q_seq.at[half, yy, cc], q_in.at[half, y, c], qs_send.at[half, p], qs_recv.at[half, p], device(z, x, yy, cc))

    def qkv_one(half):
        q_send[half] = qkv_rows(half, 1 - x).astype(b16)

        qkv_x(half).start()

    def qkv_two(half):
        qkv_x(half).wait_recv()
        q_x[half] = (q_x[half].astype(f32) + qkv_rows(half, x)).astype(b16)

        for d in range(Z - 1):
            qkv_z(half, d).start()

    def qkv_three(half):
        value = q_x[half, z].astype(f32)
        for d in range(Z - 1):
            qkv_z(half, d).wait_recv()
        for d in range(Z - 1):
            value = value + q_z[half, d].astype(f32)
        q_seq[half] = value.reshape(Y, C, -1, 3 * PAIR)
        for p in range(3):
            qkv_seq(half, p).start()
        q_in[half, y, c] = q_seq[half, y, c]

    def qkv_four(half):
        for p in range(3):
            qkv_seq(half, p).wait_recv()
        for owner in range(Y * C):
            for j in range(3):
                lane_at = j * width + owner * cols + half * PAIR
                o_qkv[:, lane_at : lane_at + PAIR] = q_in[half, owner // C, owner % C, :, j * PAIR : (j + 1) * PAIR]

    def in_c(b):
        return send_to(g_send.at[b], g_c.at[b], ic_send.at[b], ic_recv.at[b], device(z, x, y, 1 - c))

    def in_y(b):
        return send_to(g_y_send.at[b], g_y.at[b], iy_send.at[b], iy_recv.at[b], device(z, x, 1 - y, c))

    def input_rows(b, yy, cc):
        at = pl.ds(pl.multiple_of((yy * C + cc) * part, part), part)
        got = lax.dot_general(turned[0, b, at], cols_all[0], nt, preferred_element_type=f32)
        return got + lax.dot_general(turned[1, b, at], cols_all[1], nt, preferred_element_type=f32)

    def input_one(b):
        share_core(b).wait_send()
        for yy in range(Y):
            g_send[b, yy] = input_rows(b, yy, 1 - c).astype(b16)
        in_c(b).start()

    def input_two(b):
        in_c(b).wait_recv()
        share_y(b).wait_send()
        g_y_send[b] = (input_rows(b, 1 - y, c) + g_c[b, 1 - y].astype(f32)).astype(b16)
        in_y(b).start()

    def input_three(b):
        o_in[b * part : (b + 1) * part] += input_rows(b, y, c) + g_c[b, y].astype(f32)

    def input_four(b):
        in_y(b).wait_recv()
        o_in[b * part : (b + 1) * part] += g_y[b].astype(f32)

    def small_sums():
        lanes = lax.broadcasted_iota(jnp.int32, (16, 128), 1)
        spots = lax.broadcasted_iota(jnp.int32, (16, 128), 0)
        share = 128 // (Y * C)
        for zx in range(Z * X):
            tile = sums[:, zx * 128 : (zx + 1) * 128]
            for yc in range(Y * C):
                moved = pltpu.roll(tile, (128 - yc * share) % 128, 1) if yc else tile
                value = jnp.where(lanes < share, moved, 0.0)
                value = jnp.where(spots == 9, sum_up[:, zx * 128 : (zx + 1) * 128] * (s == yc).astype(f32), value)
                send_s[zx // X, zx % X, yc // C, yc % C] = value.astype(b16)
        to_core(2).start()

    work = {
        "ln2b": second_norm_back, "gk": forward_grad, "gh": hidden_back, "g1": inner_back, "f2": core_sum, "ln1b": first_norm_back, "ga": att_back_send,
        "w1": ffn_one, "w2": ffn_two, "w3": ffn_three, "w4": ffn_four,
        "mk": lambda k: make_send(k) if k < 2 else small_sums(), "own": own_half, "add": add_landed, "fin": finish,
        "q1": qkv_one, "q2": qkv_two, "q3": qkv_three, "q4": qkv_four,
        "i1": input_one, "i2": input_two, "i3": input_three, "i4": input_four,
    }
    spots = [i for i, name in enumerate(BACKWARD_ORDER) if name[0] == "at"]

    def run(first_spot, last_spot):
        for name in BACKWARD_ORDER[first_spot:last_spot]:
            if name == ("mk", 0):
                need(8)
            work[name[0]](*name[1:])

    run(0, spots[0])
    need(*range(len(loads)))

    def before(i):
        if i == 0:
            for p in range(3):
                att_seq(p).wait_recv()
        else:
            run(spots[i - 1] + 1, spots[i])

    @pl.loop(0, streams * 2)
    def _(i):
        at_index(i, {spot: functools.partial(before, spot) for spot in range(streams * 2)})
        attend_back(i)

    run(spots[-1] + 1, len(BACKWARD_ORDER))

    for k in range(total):
        to_core(k).wait_send()
        for stage in range(3):
            for copy in along(k, stage):
                copy.wait_send()
    for k in range(4):
        ffn_x(k).wait_send()
        for d in range(Z - 1):
            ffn_z(k, d).wait_send()
    for p in range(3):
        att_seq(p).wait_send()
        for half in range(2):
            qkv_seq(half, p).wait_send()
            ffn_seq(half, p).wait_send()
    for half in range(2):
        qkv_x(half).wait_send()
        for d in range(Z - 1):
            qkv_z(half, d).wait_send()
    for b in range(streams):
        for copy in (in_c(b), in_y(b), grad_y(b), grad_core(b, 0), grad_core(b, 1)):
            copy.wait_send()


def run_backward(kept, sizes, cot):
    (
        w_out, w_up, w_down, w_proj, w_cols, side_rows, tok_t, qkv, lse, att_t, n_one, r_one, h_t, hid_t, dgelu, n_two, r_two, nlow_t, cos4, sin4,
    ) = kept
    rows, width = n_one.shape
    streams, _, stream = tok_t.shape
    hidden = dgelu.shape[-1]
    ff = hidden * Y * C
    proj = w_proj.shape[-1]
    cols, half_width = width // (Y * C), width // 2
    grid = (Z, X, Y, C)
    part = rows // streams
    vm, dma = pltpu.VMEM, pltpu.SemaphoreType.DMA
    vmem, hbm = pl.BlockSpec(memory_space=pltpu.VMEM), pl.BlockSpec(memory_space=pl.ANY)
    owner = width // OWNERS
    tails = [(owner, width), (owner, proj), (16, 128)]
    split_rows = (streams, Z, X, width // (Z * X), stream)
    inputs = [
        (w_out.reshape(width, width), hbm), (w_up.reshape(width, hidden), hbm), (w_down.reshape(hidden, width), hbm),
        (w_proj.reshape(width, proj), vmem), (w_cols.reshape(2, width, 3 * PAIR), hbm), (side_rows, vmem), (tok_t.reshape(split_rows), hbm), (qkv, hbm),
        (lse, vmem), (att_t.reshape(grid + (owner, rows)), hbm), (n_one, hbm), (r_one, vmem), (h_t.reshape(split_rows), hbm),
        (hid_t.reshape(split_rows), hbm), (dgelu, hbm), (n_two, hbm), (r_two, vmem), (nlow_t.reshape(grid + (owner, rows)), vmem),
        (cos4, vmem), (sin4, vmem), (sizes, pl.BlockSpec(memory_space=pltpu.SMEM)), (cot, vmem),
    ]
    scratch = [
        vm((width, width), b16), vm((width, hidden), b16), vm((hidden, width), b16), vm((rows, width), f32),
        vm(grid + (owner, rows), b16), vm(split_rows, b16), vm(split_rows, b16), vm(dgelu.shape, b16), vm(split_rows, b16),
        vm(qkv.shape, b16), vm((2, width, 3 * PAIR), b16), vm((16, width), f32), vm((1, hidden), f32),
        vm((streams, Y, C, part, width), b16), vm((rows, width), b16), vm((streams, part, width), b16),
        vm((streams, Y, C, part, cols), b16), vm((stream, stream), f32), vm((2, streams, stream, 3 * PAIR), b16),
        vm((Z, X, Y) + tails[0], b16), vm((Z, X, Y) + tails[1], b16), vm(grid + tails[2], b16), vm(cot.shape, b16),
        vm((4, Z, 128, half_width), b16), vm((4, Z, 128, half_width), b16), vm((4, Z - 1, 128, half_width), b16),
        vm((2, Y, C, owner, half_width), b16), vm((2, Y, C, owner, half_width), b16), vm((rows, width), f32),
        vm((streams, Y, part, width), b16), vm((streams, Y, part, width), b16), vm((streams, part, width), b16), vm((streams, part, width), b16),
        vm((2, Z, 128, 3 * PAIR), b16), vm((2, Z, 128, 3 * PAIR), b16), vm((2, Z - 1, 128, 3 * PAIR), b16),
        vm((2, Y, C, 32, 3 * PAIR), f32), vm((2, Y, C, 32, 3 * PAIR), f32),
        dma((3, 9)), dma((3, 9)), dma((3,)), dma((3,)), dma((2,)), dma((2,)), dma((2, 3)), dma((2, 3)), dma((2, 3)), dma((2, 3)),
        dma((streams,)), dma((streams,)), dma((streams,)), dma((streams,)),
        dma((4,)), dma((4,)), dma((4, 3)), dma((4, 3)), dma((2, 3)), dma((2, 3)), dma((streams,)), dma((streams,)), dma((streams, 2)), dma((streams, 2)),
        dma((streams,)), dma((streams,)), dma((streams,)), dma((streams,)),
        dma((12,)),
    ]
    size = {"z": Z, "x": X, "y": Y}
    scratch += [vm((Z, X, Y) + tail, b16) for tail in tails]
    for route, tail in zip(BACKWARD_ROUTES, tails):
        for stage in range(3):
            rest = tuple(size[a] for a in "zxy" if a not in route[: stage + 1])
            scratch.append(vm(((Z - 1,) if route[stage] == "z" else ()) + rest + tail, b16))
    outs = [(rows, width), (owner, 3 * width), (owner, width), (owner, ff), (ff // OWNERS, width), (owner, proj), (16, 128)]
    return pl.pallas_call(
        backward_kernel,
        out_shape=[jax.ShapeDtypeStruct(o, f32) for o in outs],
        in_specs=[spec for _, spec in inputs],
        out_specs=[vmem] * len(outs),
        scratch_shapes=scratch,
        compiler_params=pltpu.CompilerParams(collective_id=4, has_side_effects=True, vmem_limit_bytes=63 << 20),
    )(*[a for a, _ in inputs])


def layer_norm(field, gain_row, shift_row):
    average = jnp.mean(field, axis=-1, keepdims=True)
    centred = field - average
    variance = jnp.mean(centred * centred, axis=-1, keepdims=True)
    return centred * lax.rsqrt(variance + epsilon) * gain_row + shift_row


def doc_layout(doc_sizes, places):
    doc_ends = jnp.cumsum(doc_sizes)
    passed = places[:, None] >= doc_ends[None, :]
    segment = jnp.sum(passed.astype(jnp.int32), axis=1)
    starts = jnp.sum(jnp.where(passed, doc_sizes[None, :], 0), axis=1)
    return (segment, places - starts)


def rope_tables(position, half_dim):
    steps_f = jnp.arange(half_dim, dtype=jnp.float32)
    inverse = jnp.exp(steps_f * (-math.log(rope_base) / half_dim))
    angle = position.astype(jnp.float32)[:, None] * inverse[None, :]
    return (jnp.cos(angle), jnp.sin(angle))


def rotate(field, cosine, sine_tab, head_count):
    length = field.shape[0]
    halves = field.reshape(length, head_count, 2, -1)
    first_half = halves[:, :, 0]
    second_half = halves[:, :, 1]
    cos_b = cosine[:, None, :]
    sin_b = sine_tab[:, None, :]
    turned = jnp.stack(
        [first_half * cos_b - second_half * sin_b, second_half * cos_b + first_half * sin_b], axis=2
    )
    return turned.reshape(length, -1)


def gelu_exact(field):
    return jax.nn.gelu(field, approximate=False)


def scores_of(query_blk, seg_blk, keys_all, stream_seg, score_scale):
    raw_scores = (
        jnp.einsum("qhd,khd->hqk", query_blk, keys_all, preferred_element_type=jnp.float32)
        * score_scale
    )
    same_doc = (seg_blk[:, None] == stream_seg[None, :])[None]
    return jnp.where(same_doc, raw_scores, neg_fill)


def per_device_any(
    tokens,
    doc_lengths,
    qkv_weight,
    out_weight,
    up_weight,
    down_weight,
    proj_weight,
    biases,
    gains,
    up_bias,
    cotangent,
):
    stream_count = tokens.shape[0]
    seg_rows = tokens.shape[1]
    model_width = tokens.shape[2]
    seq_parts = lax.axis_size("seq")
    stream = seg_rows * seq_parts
    head_count = model_width // HEAD_DIM
    local_heads = head_count // seq_parts
    flat_width = local_heads * HEAD_DIM
    score_scale = HEAD_DIM ** (-0.5)
    tok_flat = tokens.reshape(stream_count * seg_rows, model_width)
    gathered = (
        lax.all_gather(qkv_weight, ("rows", "seq"), axis=0, tiled=True),
        lax.all_gather(out_weight, ("rows", "seq"), axis=0, tiled=True),
        lax.all_gather(up_weight, ("rows", "seq"), axis=0, tiled=True),
        lax.all_gather(down_weight, ("rows", "seq"), axis=0, tiled=True),
        lax.all_gather(proj_weight, ("rows", "seq"), axis=0, tiled=True),
        lax.all_gather(biases, ("rows", "seq"), axis=1, tiled=True),
        lax.all_gather(gains, ("rows", "seq"), axis=1, tiled=True),
        lax.all_gather(up_bias, ("rows", "seq"), axis=0, tiled=True),
    )
    w_qkv, w_out, w_up, w_down, w_proj = (
        gathered[0],
        gathered[1],
        gathered[2],
        gathered[3],
        gathered[4],
    )
    bias_rows = gathered[5].astype(jnp.float32)
    gain_rows = gathered[6].astype(jnp.float32)
    bias_up = gathered[7].astype(jnp.float32)
    token_places = lax.axis_index("seq") * seg_rows + jnp.arange(seg_rows, dtype=jnp.int32)
    layout_rows = jax.vmap(doc_layout, in_axes=(0, None))
    token_seg, position = layout_rows(doc_lengths, token_places)
    cosine, sine_tab = rope_tables(position.reshape(-1), HEAD_DIM // 2)
    projected = jnp.dot(tok_flat, w_qkv, preferred_element_type=jnp.float32) + bias_rows[
        0:3
    ].reshape(-1)
    queries = (
        rotate(projected[:, :model_width], cosine, sine_tab, head_count)
        .astype(jnp.bfloat16)
        .reshape(stream_count, seg_rows, model_width)
    )
    keys_tok = (
        rotate(projected[:, model_width : 2 * model_width], cosine, sine_tab, head_count)
        .astype(jnp.bfloat16)
        .reshape(stream_count, seg_rows, model_width)
    )
    values_tok = (
        projected[:, 2 * model_width :]
        .astype(jnp.bfloat16)
        .reshape(stream_count, seg_rows, model_width)
    )
    queries_h, keys_h, values_h = (
        lax.all_to_all(queries, "seq", split_axis=2, concat_axis=1, tiled=True),
        lax.all_to_all(keys_tok, "seq", split_axis=2, concat_axis=1, tiled=True),
        lax.all_to_all(values_tok, "seq", split_axis=2, concat_axis=1, tiled=True),
    )
    stream_seg, stream_pos = layout_rows(doc_lengths, jnp.arange(stream, dtype=jnp.int32))
    block_rows = math.gcd(stream, 512)
    block_count = stream // block_rows

    def forward_stream(element):
        query_s, key_s, value_s, seg_s = element
        query_blocks = query_s.reshape(block_count, block_rows, local_heads, HEAD_DIM)
        keys_all = key_s.reshape(stream, local_heads, HEAD_DIM)
        values_all = value_s.reshape(stream, local_heads, HEAD_DIM)
        seg_blocks = seg_s.reshape(block_count, block_rows)

        def forward_block(inner):
            query_blk, seg_blk = inner
            scores = scores_of(query_blk, seg_blk, keys_all, seg_s, score_scale)
            row_max = jnp.max(scores, axis=-1, keepdims=True)
            row_total = jnp.sum(jnp.exp(scores - row_max), axis=-1, keepdims=True)
            log_total = row_max + jnp.log(row_total)
            probs_low = jnp.exp(scores - log_total).astype(jnp.bfloat16)
            attn_blk = jnp.einsum(
                "hqk,khd->qhd", probs_low, values_all, preferred_element_type=jnp.float32
            )
            return (attn_blk.astype(jnp.bfloat16), log_total[:, :, 0])

        attn_blocks, log_blocks = lax.map(forward_block, (query_blocks, seg_blocks))
        return (attn_blocks.reshape(stream, flat_width), log_blocks)

    attn_heads, log_totals = lax.map(forward_stream, (queries_h, keys_h, values_h, stream_seg))
    attended = lax.all_to_all(attn_heads, "seq", split_axis=1, concat_axis=2, tiled=True).reshape(
        stream_count * seg_rows, model_width
    )
    branch = jnp.dot(attended, w_out, preferred_element_type=jnp.float32) + bias_rows[3]
    h_one, norm_one = jax.vjp(
        layer_norm, tok_flat.astype(jnp.float32) + branch, gain_rows[0], bias_rows[4]
    )
    h_low = h_one.astype(jnp.bfloat16)
    u_pre = jnp.dot(h_low, w_up, preferred_element_type=jnp.float32) + bias_up
    hidden_f, gelu_back = jax.vjp(gelu_exact, u_pre)
    hidden = hidden_f.astype(jnp.bfloat16)
    ffn_out = jnp.dot(hidden, w_down, preferred_element_type=jnp.float32) + bias_rows[5]
    normed, norm_two = jax.vjp(layer_norm, h_one + ffn_out, gain_rows[1], bias_rows[6])
    normed_low = normed.astype(jnp.bfloat16)
    result = jnp.dot(normed_low, w_proj, preferred_element_type=jnp.float32).astype(jnp.bfloat16)
    w_qkv, w_out, w_up, w_down, w_proj = (
        lax.all_gather(qkv_weight, ("rows", "seq"), axis=0, tiled=True),
        lax.all_gather(out_weight, ("rows", "seq"), axis=0, tiled=True),
        lax.all_gather(up_weight, ("rows", "seq"), axis=0, tiled=True),
        lax.all_gather(down_weight, ("rows", "seq"), axis=0, tiled=True),
        lax.all_gather(proj_weight, ("rows", "seq"), axis=0, tiled=True),
    )
    cot_low = cotangent.reshape(stream_count * seg_rows, -1).astype(jnp.bfloat16)
    proj_part = jnp.dot(normed_low.T, cot_low, preferred_element_type=jnp.float32)
    grad_normed = jnp.dot(cot_low, w_proj.T, preferred_element_type=jnp.float32)
    grad_z2, grad_g2, grad_b2 = norm_two(grad_normed)
    grad_ffn = grad_z2.astype(jnp.bfloat16)
    grad_c2 = jnp.sum(grad_ffn, axis=0, dtype=jnp.float32)
    down_part = jnp.dot(hidden.T, grad_ffn, preferred_element_type=jnp.float32)
    grad_hidden = jnp.dot(grad_ffn, w_down.T, preferred_element_type=jnp.float32)
    grad_u = gelu_back(grad_hidden)[0].astype(jnp.bfloat16)
    grad_c1 = jnp.sum(grad_u, axis=0, dtype=jnp.float32)
    up_part = jnp.dot(h_low.T, grad_u, preferred_element_type=jnp.float32)
    ffn_sums = (up_part, down_part, proj_part, grad_c1)
    grad_h1 = grad_z2 + jnp.dot(grad_u, w_up.T, preferred_element_type=jnp.float32)
    grad_z1, grad_g1, grad_b1 = norm_one(grad_h1)
    grad_branch = grad_z1.astype(jnp.bfloat16)
    grad_bo = jnp.sum(grad_branch, axis=0, dtype=jnp.float32)
    out_part = jnp.dot(attended.T, grad_branch, preferred_element_type=jnp.float32)
    grad_attn = jnp.dot(grad_branch, w_out.T, preferred_element_type=jnp.float32).astype(
        jnp.bfloat16
    )
    grad_heads = lax.all_to_all(
        grad_attn.reshape(stream_count, seg_rows, model_width),
        "seq",
        split_axis=2,
        concat_axis=1,
        tiled=True,
    )

    def backward_stream(element):
        query_s, key_s, value_s, seg_s, log_s, grad_s = element
        query_blocks = query_s.reshape(block_count, block_rows, local_heads, HEAD_DIM)
        keys_all = key_s.reshape(stream, local_heads, HEAD_DIM)
        values_all = value_s.reshape(stream, local_heads, HEAD_DIM)
        seg_blocks = seg_s.reshape(block_count, block_rows)
        grad_blocks = grad_s.reshape(block_count, block_rows, local_heads, HEAD_DIM)

        def backward_block(carried, inner):
            grad_keys, grad_values = carried
            query_blk, seg_blk, log_total, grad_blk = inner
            probs_f = jnp.exp(
                scores_of(query_blk, seg_blk, keys_all, seg_s, score_scale) - log_total[:, :, None]
            )
            grad_values = grad_values + jnp.einsum(
                "hqk,qhd->khd",
                probs_f.astype(jnp.bfloat16),
                grad_blk,
                preferred_element_type=jnp.float32,
            )
            grad_probs = jnp.einsum(
                "qhd,khd->hqk", grad_blk, values_all, preferred_element_type=jnp.float32
            )
            row_dot = jnp.sum(probs_f * grad_probs, axis=-1, keepdims=True)
            grad_scores = (probs_f * (grad_probs - row_dot) * score_scale).astype(jnp.bfloat16)
            grad_query = jnp.einsum(
                "hqk,khd->qhd", grad_scores, keys_all, preferred_element_type=jnp.float32
            )
            grad_keys = grad_keys + jnp.einsum(
                "hqk,qhd->khd", grad_scores, query_blk, preferred_element_type=jnp.float32
            )
            return ((grad_keys, grad_values), grad_query.astype(jnp.bfloat16))

        zero_acc = jnp.zeros((stream, local_heads, HEAD_DIM), jnp.float32)
        (grad_keys, grad_values), grad_queries = lax.scan(
            backward_block, (zero_acc, zero_acc), (query_blocks, seg_blocks, log_s, grad_blocks)
        )
        return (
            grad_queries.reshape(stream, flat_width),
            grad_keys.astype(jnp.bfloat16).reshape(stream, flat_width),
            grad_values.astype(jnp.bfloat16).reshape(stream, flat_width),
        )

    head_q, head_k, head_v = lax.map(
        backward_stream, (queries_h, keys_h, values_h, stream_seg, log_totals, grad_heads)
    )
    back_q, back_k, back_v = (
        lax.all_to_all(head_q, "seq", split_axis=1, concat_axis=2, tiled=True),
        lax.all_to_all(head_k, "seq", split_axis=1, concat_axis=2, tiled=True),
        lax.all_to_all(head_v, "seq", split_axis=1, concat_axis=2, tiled=True),
    )
    flat_rows = stream_count * seg_rows
    turned_q = rotate(
        back_q.reshape(flat_rows, model_width).astype(jnp.float32), cosine, -sine_tab, head_count
    )
    turned_k = rotate(
        back_k.reshape(flat_rows, model_width).astype(jnp.float32), cosine, -sine_tab, head_count
    )
    grad_project = jnp.concatenate(
        [turned_q, turned_k, back_v.reshape(flat_rows, model_width).astype(jnp.float32)], axis=1
    ).astype(jnp.bfloat16)
    grad_bqkv = jnp.sum(grad_project, axis=0, dtype=jnp.float32).reshape(3, model_width)
    qkv_part = jnp.dot(tok_flat.T, grad_project, preferred_element_type=jnp.float32)
    input_grad = grad_z1 + jnp.dot(grad_project, w_qkv.T, preferred_element_type=jnp.float32)
    bias_part = jnp.concatenate(
        [grad_bqkv, jnp.stack([grad_bo, grad_b1, grad_c2, grad_b2])], axis=0
    )
    gain_part = jnp.stack([grad_g1, grad_g2])
    qkv_sum, out_sum, up_sum, down_sum, proj_sum, bias_sum, gain_sum, c1_sum = (
        lax.psum_scatter(qkv_part, ("rows", "seq"), scatter_dimension=0, tiled=True),
        lax.psum_scatter(out_part, ("rows", "seq"), scatter_dimension=0, tiled=True),
        lax.psum_scatter(ffn_sums[0], ("rows", "seq"), scatter_dimension=0, tiled=True),
        lax.psum_scatter(ffn_sums[1], ("rows", "seq"), scatter_dimension=0, tiled=True),
        lax.psum_scatter(ffn_sums[2], ("rows", "seq"), scatter_dimension=0, tiled=True),
        lax.psum_scatter(bias_part, ("rows", "seq"), scatter_dimension=1, tiled=True),
        lax.psum_scatter(gain_part, ("rows", "seq"), scatter_dimension=1, tiled=True),
        lax.psum_scatter(ffn_sums[3], ("rows", "seq"), scatter_dimension=0, tiled=True),
    )
    output = result.reshape(stream_count, seg_rows, -1)
    return (
        output,
        input_grad.reshape(stream_count, seg_rows, model_width),
        qkv_sum,
        out_sum,
        up_sum,
        down_sum,
        proj_sum,
        bias_sum,
        gain_sum,
        c1_sum,
    )


def direct_links():
    return lax.axis_size("rows") == Z * X and lax.axis_size("seq") == Y * C


def copy_out(count, *refs):
    for src, dst in zip(refs[:count], refs[count + 1 :]):
        dst[...] = src[...]
    side, (o_bias, o_gain, o_up) = refs[count], refs[-3:]
    lanes = o_bias.shape[1]
    o_bias[...] = side[:7, :lanes]
    o_gain[...] = side[7:9, :lanes]
    o_up[...] = side[9:10]


def per_device_direct(
    tokens, doc_lengths, qkv_weight, out_weight, up_weight, down_weight, proj_weight, biases, gains, up_bias, cotangent
):
    streams, part, width = tokens.shape
    *kept, result = run_forward(
        tokens, doc_lengths, qkv_weight, out_weight, up_weight, down_weight, proj_weight, biases, gains, up_bias.reshape(1, -1)
    )
    *big, side_sum = run_backward(kept, doc_lengths, cotangent.reshape(streams * part, -1))
    lanes = biases.shape[1]
    shape = jax.ShapeDtypeStruct
    vmem = pl.BlockSpec(memory_space=pltpu.VMEM)
    input_grad, qkv, out, up, down, proj, bias_sum, gain_sum, up_sum = pl.pallas_call(
        functools.partial(copy_out, len(big)),
        out_shape=[shape(a.shape, f32) for a in big] + [shape((7, lanes), f32), shape((2, lanes), f32), shape((1, 128), f32)],
        in_specs=[vmem] * (len(big) + 1),
        out_specs=[vmem] * (len(big) + 3),
    )(*big, side_sum)
    return (
        result.reshape(streams, part, -1),
        input_grad.reshape(streams, part, width),
        qkv,
        out,
        up,
        down,
        proj,
        bias_sum,
        gain_sum,
        up_sum.reshape(-1),
    )


def per_device(*args):
    return per_device_direct(*args) if direct_links() else per_device_any(*args)


def solution(mesh):
    in_specs = (
        P("rows", "seq", None),
        P("rows", None),
        P(("rows", "seq"), None),
        P(("rows", "seq"), None),
        P(("rows", "seq"), None),
        P(("rows", "seq"), None),
        P(("rows", "seq"), None),
        P(None, ("rows", "seq")),
        P(None, ("rows", "seq")),
        P(("rows", "seq")),
        P("rows", "seq", None),
    )
    out_specs = (
        P("rows", "seq", None),
        P("rows", "seq", None),
        P(("rows", "seq"), None),
        P(("rows", "seq"), None),
        P(("rows", "seq"), None),
        P(("rows", "seq"), None),
        P(("rows", "seq"), None),
        P(None, ("rows", "seq")),
        P(None, ("rows", "seq")),
        P(("rows", "seq")),
    )
    return jax.shard_map(
        per_device, mesh=mesh, in_specs=in_specs, out_specs=out_specs, check_vma=False
    )
```

```python
import functools
import math

import jax
import jax.numpy as jnp
from jax import lax
from jax.experimental import pallas as pl
from jax.experimental.pallas import tpu as pltpu
from jax.sharding import PartitionSpec as P

epsilon = 1e-05
rope_base = 10000.0
neg_fill = -1e30

HEAD_DIM = 64
PAIR = 2 * HEAD_DIM
MESH = pl.DeviceIdType.MESH
Z, X, Y, C = 4, 2, 2, 2
OWNERS = Z * X * Y * C
f32, b16 = jnp.float32, jnp.bfloat16
FAR = -1e30


def place():
    r, s = lax.axis_index("rows"), lax.axis_index("seq")
    return r // X, r % X, s // C, s % C


def device(z, x, y, c):
    return (z * X + x, y * C + c)


def greet(peers):
    barrier = pltpu.get_barrier_semaphore()
    for peer in peers:
        pl.semaphore_signal(barrier, inc=1, device_id=peer, device_id_type=MESH)
    pl.semaphore_wait(barrier, len(peers))


def send_to(src, dst, send, recv, peer):
    return pltpu.make_async_remote_copy(
        src_ref=src, dst_ref=dst, send_sem=send, recv_sem=recv, device_id=peer, device_id_type=MESH
    )


def normal_rows(field):
    average = jnp.mean(field, axis=-1, keepdims=True)
    centred = field - average
    inverse = lax.rsqrt(jnp.mean(centred * centred, axis=-1, keepdims=True) + epsilon)
    return centred * inverse, inverse


def doc_marks(sizes, b, places):
    segment, start, end = jnp.zeros_like(places), jnp.zeros_like(places), jnp.int32(0)
    for d in range(sizes.shape[1]):
        end = end + sizes[b, d]
        passed = places >= end
        segment = segment + jnp.where(passed, 1, 0)
        start = start + jnp.where(passed, sizes[b, d], 0)
    return segment, places - start


def far_keys(sizes, b, stream):
    down, _ = doc_marks(sizes, b, lax.broadcasted_iota(jnp.int32, (stream, 1), 0))
    across, _ = doc_marks(sizes, b, lax.broadcasted_iota(jnp.int32, (1, stream), 1))
    return jnp.where(down == across, 0.0, FAR)


class Steps:
    def __init__(self, copies, needs):
        self.copies, self.needs, self.seen = copies, needs, set()

    def arrive(self, names):
        for name in names:
            if name not in self.seen:
                self.seen.add(name)
                self.copies(name).wait_recv()

    def start(self, name):
        self.arrive(self.needs(name))
        self.copies(name).start()

    def run(self, names):
        for name in names:
            self.start(name)


def at_index(index, plan):
    for spot, call in plan.items():

        @pl.when(index == spot)
        def _(call=call):
            call()


FORWARD_ROUTES = ("xzy", "xzy", "zxy")
FORWARD_ORDER = (
    (0, 2, 2), ("a", 0, 1), ("a", 0, 2), (0, 2, 3), ("tb",), ("a", 1, 1), (0, 0), ("a", 1, 2), (0, 2, 1),
    ("a", 0, 0), ("wz", 0, 1), ("a", 2, 1), ("wz", 0, 3), (0, 1), ("wz", 0, 2), ("a", 2, 0), ("a", 2, 2),
    ("wz", 2, 3), (1, 2), ("y", 2), ("a", 1, 0), ("wz", 1, 2), ("ua", 1), ("wz", 1, 3), ("wx", 0), (1, 0, 3),
    (1, 0, 2), (1, 0, 1), ("wz", 1, 1), ("wz", 2, 2), ("ua", 2), ("k0", 2), ("y", 0), ("k0", 0), ("wz", 2, 1),
    ("ua", 0), ("uz", 0, 3), ("k0", 1), ("wx", 1), ("uz", 0, 2), ("uz", 0, 1), (2, 0), ("y", 1), ("k1", 2),
    (2, 2), ("uz", 1, 3), ("k1", 0), ("wx", 2), ("uz", 1, 2), ("uz", 1, 1), (3, 0), ("bias",), ("dz", 1, 1),
    ("dz", 1, 3), ("dz", 0, 3), ("dz", 0, 1), ("ux", 0), ("k1", 1), ("at", 0), ("at", 1), ("at", 2),
    ("dz", 0, 2), ("dz", 1, 2), ("ux", 1), ("at", 3), ("at", 4), ("at", 5), ("keep", 0), ("dz", 2, 3),
    (1, 1, 2), (1, 1, 1), (3, 2), ("dz", 2, 2), ("dx", 0), ("dz", 2, 1), ("dz", 3, 1), ("dz", 3, 3), ("out",),
    ("ln", 0), ("hy", 0), ("ln", 2), ("hk0", 2), ("ln", 1), ("keep", 1), ("hk0", 1), ("hy", 1), ("dx", 1),
    ("hk0", 0), ("dz", 3, 2), ("up", 2, 0), ("up", 0, 0), ("up", 1, 0), ("dx", 2), ("hk1", 0), ("up", 0, 1),
    (1, 1, 3), ("dx", 3), ("hk1", 1), ("up", 1, 1), ("hy", 2), (2, 1), ("dn", 0, 0), ("dn", 0, 1), ("fc", 0),
    ("f2", 0), ("fy", 0), ("dn", 1, 0), ("dn", 1, 1), ("fc", 1), ("hk1", 2), ("dn", 2, 0), (3, 1), ("f2", 1),
    ("fy", 1), ("up", 2, 1), ("dn", 2, 1), ("keep", 2), ("fc", 2), ("f2", 2), ("fy", 2), ("ln2", 0),
    ("ln2", 1), ("ln2", 2), ("keep", 3),
)


def forward_kernel(
    tok, sizes, wqkv, wout, wup, wdown, wproj, biases, gains, up_bias,
    o_out, o_up, o_down, o_proj, o_cols, o_rows, o_tok_t, o_qkv, o_lse, o_att_t, o_n1, o_r1, o_h_t, o_hid_t, o_dgelu,
    o_n2, o_r2, o_nlow_t, o_cos, o_sin, o_res,
    g_out, g_up, g_down, g_proj, g_side, g_cols, g_tok, tok_t, qkv, head_out, far, att, att_t, z_one, n_one, g_h, h_t,
    hid, hid_t, dgelu, n_two, bias_up, mix, cos4, sin4, up_mix, f_send, f_c, f_y_send, f_y,
    c_send, c_recv, a_send, a_recv, wz_send, wz_recv, wx_send, wx_recv, y_send, y_recv, k_send, k_recv, t_send, t_recv,
    ua_send, ua_recv, uz_send, uz_recv, ux_send, ux_recv, fc_send, fc_recv, fy_send, fy_recv, save,
):
    streams, part, width = tok.shape
    rows, stream = streams * part, part * Y * C
    z, x, y, c = place()
    s = y * C + c
    seq_peer = [(y, 1 - c), (1 - y, c), (1 - y, 1 - c)]
    others = [(z + d) % Z for d in range(1, Z)]
    half_width = width // 2
    hidden = g_up.shape[-1]
    cols = wqkv.shape[1] // (3 * Y * C)

    targets = [g_side, g_proj, g_out]
    total = len(targets)
    axis_peer = {"x": device(z, 1 - x, y, c), "y": device(z, x, 1 - y, c)}

    def piece(name):
        stage, k = name[0], name[1]
        route, held = FORWARD_ROUTES[k], targets[k]
        every = slice(None)
        along = {"x": x, "y": y, "z": z}
        spot = {axis: every if axis in route[:stage] else along[axis] for axis in "zxy"}
        if stage == 3:
            slab, slot, peer = held.at[:, :, :, c], 5, device(z, x, y, 1 - c)
        else:
            slab = held.at[spot["z"], spot["x"], spot["y"], c]
            if route[stage] == "z":
                slot, peer = name[2] - 1, device(others[name[2] - 1], x, y, c)
            else:
                slot, peer = 3 + "xy".index(route[stage]), axis_peer[route[stage]]
        return send_to(slab, slab, c_send.at[k, slot], c_recv.at[k, slot], peer)

    def piece_names(stage, k):
        if stage < 3 and FORWARD_ROUTES[k][stage] == "z":
            return [(stage, k, d) for d in range(1, Z)]
        return [(stage, k)]

    def transfer(name):
        kind = name[0]
        if not isinstance(kind, str):
            return piece(name)
        if kind == "a":
            j, p = name[1:]
            yy, cc = seq_peer[p]
            src = wqkv.at[:, pl.ds(pl.multiple_of(j * width + (yy * C + cc) * cols, 128), cols)]
            return send_to(src, g_cols.at[j, z, x, y, c], a_send.at[j, p], a_recv.at[j, p], device(z, x, yy, cc))
        if kind == "wz":
            j, d = name[1:]
            slab = g_cols.at[j, z, x]
            return send_to(slab, slab, wz_send.at[j, d - 1], wz_recv.at[j, d - 1], device(others[d - 1], x, y, c))
        if kind == "wx":
            j = name[1]
            slab = g_cols.at[j, :, x]
            return send_to(slab, slab, wx_send.at[j], wx_recv.at[j], device(z, 1 - x, y, c))
        if kind == "ua":
            p = name[1]
            yy, cc = seq_peer[p]
            return send_to(up_mix.at[yy, cc], g_up.at[z, x, y, c], ua_send.at[p], ua_recv.at[p], device(z, x, yy, cc))
        if kind in ("uz", "dz", "ux", "dx"):
            wide = half_width if kind[0] == "u" else half_width // 2
            row, lanes = name[1] + (2 if kind[0] == "d" else 0), pl.ds(name[1] * wide, wide)
            xs = (z, x) if kind[1] == "z" else (slice(None), x)
            slab = g_up.at[*xs, :, :, :, lanes] if kind[0] == "u" else g_down.at[*xs, :, lanes]
            if kind[1] == "z":
                d = name[2]
                return send_to(slab, slab, uz_send.at[row, d - 1], uz_recv.at[row, d - 1], device(others[d - 1], x, y, c))
            return send_to(slab, slab, ux_send.at[row], ux_recv.at[row], device(z, 1 - x, y, c))
        b = name[1]
        if kind == "fc":
            return send_to(f_send.at[b], f_c.at[b], fc_send.at[b], fc_recv.at[b], device(z, x, y, 1 - c))
        if kind == "fy":
            return send_to(f_y_send.at[b], f_y.at[b], fy_send.at[b], fy_recv.at[b], device(z, x, 1 - y, c))
        if kind[0] == "h":
            mine = g_h.at[b, y, c]
            if kind == "hy":
                return send_to(mine, mine, y_send.at[streams + b], y_recv.at[streams + b], device(z, x, 1 - y, c))
            slab = mine if kind == "hk0" else g_h.at[b, 1 - y, c]
            i = int(kind[2])
            return send_to(slab, slab, k_send.at[streams + b, i], k_recv.at[streams + b, i], device(z, x, y, 1 - c))
        if kind == "y":
            return send_to(tok.at[b], g_tok.at[b, y, c], y_send.at[b], y_recv.at[b], device(z, x, 1 - y, c))
        if kind == "k0":
            return send_to(tok.at[b], g_tok.at[b, y, c], k_send.at[b, 0], k_recv.at[b, 0], device(z, x, y, 1 - c))
        slab = g_tok.at[b, 1 - y, c]
        return send_to(slab, slab, k_send.at[b, 1], k_recv.at[b, 1], device(z, x, y, 1 - c))

    def needs(name):
        kind = name[0]
        if not isinstance(kind, str):
            return piece_names(kind - 1, name[1]) if kind else []
        if kind == "wz":
            return [("a", name[1], p) for p in range(3)]
        if kind == "wx":
            return [("wz", name[1], d) for d in range(1, Z)]
        if kind in ("uz", "ux"):
            return [("ua", p) for p in range(3)] if kind == "uz" else [("uz", name[1], d) for d in range(1, Z)]
        if kind == "dx":
            return [("dz", name[1], d) for d in range(1, Z)]
        return {"k1": [("y", name[1])], "hk1": [("hy", name[1])]}.get(kind, [])

    steps = Steps(transfer, needs)

    def att_seq(i, p):
        b, half = i // 2, i % 2
        yy, cc = seq_peer[p]
        lane = pl.multiple_of((s * 2 + half) * PAIR, PAIR)
        dst = att.at[b, :, pl.ds(lane, PAIR)]
        return send_to(head_out.at[b, half, yy, cc], dst, t_send.at[i, p], t_recv.at[i, p], device(z, x, yy, cc))

    mix[...] = jnp.zeros_like(mix)
    lanes_own = biases.shape[1]
    mix[0:7, 0:lanes_own] = biases[...].astype(f32)
    mix[7:9, 0:lanes_own] = gains[...].astype(f32)
    mix[9:10] = up_bias[...].astype(f32)
    g_side[z, x, y, c] = mix[...].astype(b16)
    g_proj[z, x, y, c] = wproj[...]
    g_out[z, x, y, c] = wout[...]
    for yc in range(Y * C):
        for zx in range(Z * X):
            lane_at = (zx * Y * C + yc) * 128
            up_mix[yc // C, yc % C, :, zx * 128 : (zx + 1) * 128] = wup[:, lane_at : lane_at + 128]
    g_up[z, x, y, c] = up_mix[y, c]
    g_down[z, x] = wdown[...]
    for j in range(3):
        g_cols[j, z, x, y, c] = wqkv[:, pl.ds(pl.multiple_of(j * width + s * cols, 128), cols)]
    for b in range(streams):
        g_tok[b, y, c] = tok[b]
    greet(
        [device(zz, x, y, c) for zz in others]
        + [device(z, 1 - x, y, c)]
        + [device(z, x, yy, cc) for yy, cc in seq_peer]
    )

    lane = lax.broadcasted_iota(jnp.int32, (1, PAIR), 1)
    low_half = (lane % HEAD_DIM) < HEAD_DIM // 2
    inverse_f = jnp.exp((lane % (HEAD_DIM // 2)).astype(f32) * (-math.log(rope_base) / (HEAD_DIM // 2)))

    def tables(b):
        _, position = doc_marks(sizes, b, lax.broadcasted_iota(jnp.int32, (stream, PAIR), 0))
        angle = position.astype(f32) * inverse_f
        cos4[b] = jnp.cos(angle)
        sin4[b] = jnp.sin(angle) * jnp.where(low_half, -1.0, 1.0)

    def all_tables():
        pl.loop(0, streams)(tables)

    def whole_rows():
        steps.arrive(piece_names(3, 0))
        lanes = lax.broadcasted_iota(jnp.int32, (16, 128), 1)
        share = 128 // (Y * C)
        for zx in range(Z * X):
            tile = jnp.zeros((16, 128), f32)
            for yc in range(Y * C):
                block = g_side[zx // X, zx % X, yc // C, yc % C].astype(f32)
                tile = tile + pltpu.roll(jnp.where(lanes < share, block, 0.0), yc * share, 1)
            o_rows[:, pl.ds(zx * 128, 128)] = tile
            bias_up[:, pl.ds(zx * 128, 128)] = g_side[zx // X, zx % X, y, c].astype(f32)[9:10]

    def project(b):
        rows_b = g_tok[b].reshape(stream, width)
        tok_t[b] = rows_b.T
        for j in range(3):
            bias_row = o_rows[pl.ds(j, 1), pl.ds(pl.multiple_of(s * cols, 128), cols)]
            got = jnp.dot(rows_b, g_cols[j].reshape(width, cols), preferred_element_type=f32) + bias_row
            for half in range(2):
                t = got[:, half * PAIR : (half + 1) * PAIR]
                if j < 2:
                    swapped = jnp.where(
                        low_half, pltpu.roll(t, PAIR - HEAD_DIM // 2, 1), pltpu.roll(t, HEAD_DIM // 2, 1)
                    )
                    t = t * cos4[b] + swapped * sin4[b]
                qkv[j, b, half] = t.astype(b16)
        far[...] = far_keys(sizes, b, stream)

    q_block = stream // 2
    top = lax.broadcasted_iota(jnp.int32, (PAIR, 1), 0) < HEAD_DIM
    score_scale = HEAD_DIM**-0.5
    masks = [jnp.where(lane < HEAD_DIM, score_scale, 0.0).astype(b16), jnp.where(lane < HEAD_DIM, 0.0, score_scale).astype(b16)]

    def attend(i):
        b, half = i // 2, i % 2
        queries, keys = qkv[0, b, half], qkv[1, b, half]
        values_t = qkv[2, b, half].T
        for block in range(2):
            at = slice(block * q_block, (block + 1) * q_block)
            turned = []
            for head in range(2):
                q = queries[at] * masks[head]
                scores = lax.dot_general(keys, q, (((1,), (1,)), ((), ())), preferred_element_type=f32)
                scores = scores + far[:, pl.ds(block * q_block, q_block)]
                most = jnp.max(scores, axis=0, keepdims=True)
                e = jnp.exp(scores - most)
                mass = jnp.sum(e, axis=0, keepdims=True)
                o_lse[i, pl.ds(head, 1), pl.ds(block * q_block, q_block)] = most + jnp.log(mass)
                probs = (e * (1.0 / mass)).astype(b16)
                turned.append(jnp.dot(values_t, probs, preferred_element_type=f32))
            both = jnp.where(top, turned[0], turned[1]).T.astype(b16)
            for cc in range(C):
                head_out[b, half, block, cc] = both[cc * part : (cc + 1) * part]
        for p in range(3):
            att_seq(i, p).start()
        lane_at = pl.multiple_of((s * 2 + half) * PAIR, PAIR)
        att[b, :, pl.ds(lane_at, PAIR)] = head_out[b, half, y, c]

    n_block = 256
    r_block = part

    def attention_out():
        @pl.loop(0, streams * 2)
        def _(i):
            for p in range(3):
                att_seq(i, p).wait_recv()

        steps.arrive(piece_names(3, 2))

        @pl.loop(0, width // n_block)
        def _(n):
            at = pl.ds(pl.multiple_of(n * n_block, n_block), n_block)
            w = g_out[:, :, :, :, :, at].reshape(width, n_block)
            got = jnp.dot(att[...].reshape(rows, width), w, preferred_element_type=f32)
            z_one[:, at] = tok[:, :, at].reshape(rows, n_block).astype(f32) + (got + o_rows[3:4, at])

    def rows_of(b):
        return slice(b * part, (b + 1) * part)

    def first_norm(b):
        at = rows_of(b)
        n, inverse = normal_rows(z_one[at])
        n_one[at] = n
        o_r1[at] = jnp.broadcast_to(inverse, (part, 128))
        h = n * o_rows[7:8] + o_rows[4:5]
        z_one[at] = h
        g_h[b, y, c] = h.astype(b16)
        att_t[:, at] = att[b].T

    def hidden_rows(b, away):
        yy = 1 - y if away else y
        steps.arrive([("ux", 0), ("ux", 1)] + ([("hy", b), ("hk1", b)] if away else [("hk0", b)]))
        h = g_h[b, yy].reshape(C * part, width)
        col = pl.ds(pl.multiple_of(yy * C * part, C * part), C * part)
        h_t[b, :, col] = h.T

        @pl.loop(0, hidden // n_block)
        def _(n):
            at = pl.ds(pl.multiple_of(n * n_block, n_block), n_block)
            w = g_up[:, :, :, :, :, at].reshape(width, n_block)
            u = jnp.dot(g_h[b, yy].reshape(C * part, width), w, preferred_element_type=f32) + bias_up[:, at]
            cdf = 0.5 * (1.0 + lax.erf(u * (2.0**-0.5)))
            low = (u * cdf).astype(b16)
            hid[b, yy, :, at] = low
            hid_t[b, at, col] = low.T
            dgelu[b, yy, :, at] = (cdf + u * (jnp.exp(-0.5 * u * u) * ((2.0 * math.pi) ** -0.5))).astype(b16)

    def down_rows(b, away):
        yy = 1 - y if away else y
        steps.arrive([("dx", h) for h in range(4)])
        at = rows_of(b)

        @pl.loop(0, width // n_block)
        def _(n):
            col = pl.ds(pl.multiple_of(n * n_block, n_block), n_block)
            w = g_down[:, :, :, col].reshape(hidden, n_block)
            f_send[b, yy, :, col] = jnp.dot(hid[b, yy, pl.ds((1 - c) * part, part)], w, preferred_element_type=f32).astype(b16)
            got = jnp.dot(hid[b, yy, pl.ds(c * part, part)], w, preferred_element_type=f32)
            if away:
                n_two[at, col] = got
            else:
                z_one[at, col] += got + o_rows[5:6, col]

    def core_sum(b):
        steps.arrive([("fc", b)])
        at = rows_of(b)
        f_y_send[b] = (n_two[at] + f_c[b, 1 - y].astype(f32)).astype(b16)

    def second_norm(b):
        steps.arrive([("fy", b)] + piece_names(3, 1))
        at = rows_of(b)
        n, inverse = normal_rows(z_one[at] + f_c[b, y].astype(f32) + f_y[b].astype(f32))
        n_two[at] = n
        o_r2[at] = jnp.broadcast_to(inverse, (part, 128))
        low = (n * o_rows[8:9] + o_rows[6:7]).astype(b16)
        o_nlow_t[:, at] = low.T
        o_res[at] = jnp.dot(low, g_proj[...].reshape(width, wproj.shape[1]), preferred_element_type=f32).astype(b16)

    kept = [(cos4, o_cos), (sin4, o_sin), (tok_t, o_tok_t), (qkv, o_qkv)]
    kept += [
        (g_cols.at[j, :, :, :, :, :, pl.ds(half * PAIR, PAIR)], o_cols.at[half, :, :, :, :, :, pl.ds(j * PAIR, PAIR)])
        for j in range(3)
        for half in range(2)
    ]
    early = len(kept)
    kept += [(g_out, o_out), (att_t, o_att_t), (n_one, o_n1)]
    middle = len(kept)
    kept += [(g_up, o_up), (g_down, o_down), (h_t, o_h_t), (hid_t, o_hid_t), (dgelu, o_dgelu)]
    late = len(kept)
    kept += [(n_two, o_n2), (g_proj, o_proj)]
    copies = [pltpu.make_async_copy(a, b, save.at[i]) for i, (a, b) in enumerate(kept)]

    def keep(first_copy, last_copy):
        for copy in copies[first_copy:last_copy]:
            copy.start()

    work = {
        "tb": all_tables, "bias": whole_rows, "out": attention_out, "ln": first_norm, "up": hidden_rows, "dn": down_rows,
        "f2": core_sum, "ln2": second_norm, "keep": lambda i: keep((0, early, middle, late)[i], (early, middle, late, len(kept))[i]),
    }
    spots = [i for i, name in enumerate(FORWARD_ORDER) if name[0] == "at"]

    def run(first_spot, last_spot):
        for name in FORWARD_ORDER[first_spot:last_spot]:
            if name[0] in work:
                work[name[0]](*name[1:])
            else:
                steps.start(name)

    run(0, spots[0])

    def before(i):
        if i:
            run(spots[i - 1] + 1, spots[i])
        if i % 2 == 0:
            steps.arrive([("wx", j) for j in range(3)] + [("k0", i // 2), ("k1", i // 2)])

    @pl.loop(0, streams * 2)
    def _(i):
        at_index(i, {spot: functools.partial(before, spot) for spot in range(streams * 2)})

        @pl.when(i % 2 == 0)
        def _():
            project(i // 2)

        attend(i)

    run(spots[-1] + 1, len(FORWARD_ORDER))
    for k in range(total):
        for stage in range(4):
            for name in piece_names(stage, k):
                transfer(name).wait_send()
    for j in range(3):
        for p in range(3):
            transfer(("a", j, p)).wait_send()
        for d in range(1, Z):
            transfer(("wz", j, d)).wait_send()
        transfer(("wx", j)).wait_send()
    for p in range(3):
        transfer(("ua", p)).wait_send()
    for kind in "ud":
        for h in range(2 if kind == "u" else 4):
            for d in range(1, Z):
                transfer((kind + "z", h, d)).wait_send()
            transfer((kind + "x", h)).wait_send()
    for b in range(streams):
        for kind in ("y", "k0", "k1", "hy", "hk0", "hk1", "fc", "fy"):
            transfer((kind, b)).wait_send()

    @pl.loop(0, streams * 2)
    def _(i):
        for p in range(3):
            att_seq(i, p).wait_send()

    for copy in copies:
        copy.wait()


def run_forward(tokens, sizes, wqkv, wout, wup, wdown, wproj, biases, gains, up_bias):
    streams, part, width = tokens.shape
    rows, stream, hidden = streams * part, part * Y * C, wup.shape[1] // (Y * C)
    proj = wproj.shape[1]
    cols = width // (Y * C)
    grid = (Z, X, Y, C)
    shape = jax.ShapeDtypeStruct
    vmem, hbm = pl.BlockSpec(memory_space=pltpu.VMEM), pl.BlockSpec(memory_space=pl.ANY)
    vm = pltpu.VMEM
    outs = [
        ((grid + wout.shape, b16), hbm),
        ((grid + (wup.shape[0], hidden), b16), hbm),
        (((Z, X) + wdown.shape, b16), hbm),
        ((grid + wproj.shape, b16), hbm),
        (((2,) + grid + (wqkv.shape[0], 3 * PAIR), b16), hbm),
        (((16, width), f32), vmem),
        (((streams, width, stream), b16), hbm),
        (((3, streams, 2, stream, PAIR), b16), hbm),
        (((streams * 2, 8, stream), f32), vmem),
        (((width, rows), b16), hbm),
        (((rows, width), f32), hbm),
        (((rows, 128), f32), vmem),
        (((streams, width, stream), b16), hbm),
        (((streams, hidden, stream), b16), hbm),
        (((streams, Y, C * part, hidden), b16), hbm),
        (((rows, width), f32), hbm),
        (((rows, 128), f32), vmem),
        (((width, rows), b16), vmem),
        (((streams, stream, PAIR), f32), hbm),
        (((streams, stream, PAIR), f32), hbm),
        (((rows, proj), b16), vmem),
    ]
    dma = pltpu.SemaphoreType.DMA
    scratch = [
        vm(grid + wout.shape, b16),
        vm(grid + (wup.shape[0], hidden), b16),
        vm((Z, X) + wdown.shape, b16),
        vm(grid + wproj.shape, b16),
        vm(grid + (16, 128), b16),
        vm((3,) + grid + (wqkv.shape[0], cols), b16),
        vm((streams, Y, C, part, width), b16),
        vm((streams, width, stream), b16),
        vm((3, streams, 2, stream, PAIR), b16),
        vm((streams, 2, Y, C, part, PAIR), b16),
        vm((stream, stream), f32),
        vm((streams, part, width), b16),
        vm((width, rows), b16),
        vm((rows, width), f32),
        vm((rows, width), f32),
        vm((streams, Y, C, part, width), b16),
        vm((streams, width, stream), b16),
        vm((streams, Y, C * part, hidden), b16),
        vm((streams, hidden, stream), b16),
        vm((streams, Y, C * part, hidden), b16),
        vm((rows, width), f32),
        vm((1, hidden), f32),
        vm((16, 128), f32),
        vm((streams, stream, PAIR), f32),
        vm((streams, stream, PAIR), f32),
        vm((Y, C, wup.shape[0], hidden), b16),
        vm((streams, Y, part, width), b16), vm((streams, Y, part, width), b16), vm((streams, part, width), b16), vm((streams, part, width), b16),
        dma((3, 6)), dma((3, 6)), dma((3, 3)), dma((3, 3)), dma((3, 3)), dma((3, 3)), dma((3,)), dma((3,)),
        dma((2 * streams,)), dma((2 * streams,)), dma((2 * streams, 2)), dma((2 * streams, 2)), dma((streams * 2, 3)), dma((streams * 2, 3)),
        dma((3,)), dma((3,)), dma((6, 3)), dma((6, 3)), dma((6,)), dma((6,)), dma((streams,)), dma((streams,)), dma((streams,)), dma((streams,)),
        dma((26,)),
    ]
    return pl.pallas_call(
        forward_kernel,
        out_shape=[shape(*o[0]) for o in outs],
        in_specs=[vmem, pl.BlockSpec(memory_space=pltpu.SMEM)] + [vmem] * 8,
        out_specs=[o[1] for o in outs],
        scratch_shapes=scratch,
        compiler_params=pltpu.CompilerParams(collective_id=3, has_side_effects=True, vmem_limit_bytes=63 << 20),
    )(tokens, sizes, wqkv, wout, wup, wdown, wproj, biases, gains, up_bias)


def turned_back(t, cosine, sine, low_half):
    swapped = jnp.where(low_half, pltpu.roll(t, PAIR - HEAD_DIM // 2, 1), pltpu.roll(t, HEAD_DIM // 2, 1))
    return t * cosine - swapped * sine


BACKWARD_ROUTES = ("yxz", "xzy", "yxz")
BACKWARD_ORDER = (
    ("ln2b", 2), ("mk", 1), ("ln2b", 0), ("own", 1), ("ln2b", 1), ("gh", 2, 0), ("gh", 0, 0), ("g1", 0, 0),
    ("add", 1, 0), ("gh", 1, 0), ("g1", 2, 0), ("gk", 2), ("gh", 2, 1), ("g1", 2, 1), ("f2", 2), ("gk", 0),
    ("gh", 0, 1), ("g1", 0, 1), ("add", 1, 1), ("gk", 1), ("w1", 0), ("f2", 0), ("g1", 1, 0), ("gh", 1, 1),
    ("g1", 1, 1), ("ln1b", 2), ("w1", 2), ("fin", 1), ("w1", 3), ("f2", 1), ("w1", 1), ("w2", 0), ("ln1b", 0),
    ("ln1b", 1), ("ga", 1), ("ga", 0), ("ga", 2), ("mk", 0), ("own", 0), ("w2", 2), ("ga", 3), ("at", 0),
    ("at", 1), ("at", 2), ("q1", 0), ("w2", 3), ("at", 3), ("at", 4), ("at", 5), ("q1", 1), ("add", 0, 0),
    ("i1", 0), ("w3", 2), ("w2", 1), ("w3", 0), ("mk", 2), ("i2", 0), ("w4", 0), ("w3", 3), ("own", 2),
    ("i1", 2), ("i2", 2), ("q2", 0), ("i1", 1), ("i2", 1), ("i3", 1), ("w4", 1), ("add", 2, 0), ("w3", 1),
    ("i3", 0), ("i4", 0), ("q2", 1), ("i3", 2), ("i4", 2), ("i4", 1), ("add", 0, 1), ("add", 2, 1), ("q3", 0),
    ("q4", 0), ("q3", 1), ("q4", 1), ("fin", 0), ("fin", 2),
)


def backward_kernel(
    w_out, w_up, w_down, w_proj, w_cols, side_rows, i_tok_t, i_qkv, lse, i_att_t, i_n1, r_one, i_h_t, i_hid_t, i_dgelu, i_n2, r_two, nlow_t,
    cos4, sin4, sizes, cot_f,
    o_in, o_qkv, o_out, o_up, o_down, o_proj, o_side,
    wo, wu, wd, norm, att_t, h_t, hid_t, dgelu, tok_t, qkv, cols_all, sums, sum_up, grad_ffn, grad_branch, grad_att, heads, far,
    turned, send_o, send_p, send_s, cot, w_send, w_x, w_z, u_seq, u_in, apart, g_send, g_c, g_y_send, g_y,
    q_send, q_x, q_z, q_seq, q_in,
    c_send, c_recv, a_send, a_recv, qx_send, qx_recv, qz_send, qz_recv, qs_send, qs_recv, ic_send, ic_recv, iy_send, iy_recv,
    wx_send, wx_recv, wz_send, wz_recv, us_send, us_recv, gy_send, gy_recv, gk_send, gk_recv, gc_send, gc_recv, gf_send, gf_recv,
    load, *pieces,
):
    rows, width = o_in.shape
    streams = qkv.shape[1]
    part, stream = rows // streams, qkv.shape[3]
    hidden = sum_up.shape[1]
    half_width = width // 2
    cols = width // (Y * C)
    block = 512
    z, x, y, c = place()
    s = y * C + c
    seq_peer = [(y, 1 - c), (1 - y, c), (1 - y, 1 - c)]
    others = [(z + d) % Z for d in range(1, Z)]
    nt = (((1,), (1,)), ((), ()))
    grad_u = dgelu

    first_loads = [(i_n2, norm), (w_down, wd), (i_dgelu, dgelu), (w_up, wu), (i_hid_t, hid_t), (i_h_t, h_t), (i_n1, norm), (w_out, wo)]
    first_loads += [(i_att_t, att_t), (i_qkv, qkv), (i_tok_t, tok_t), (w_cols, cols_all)]
    loads = [pltpu.make_async_copy(a, b, load.at[i]) for i, (a, b) in enumerate(first_loads)]
    for i, copy in enumerate(loads):
        if i != 6:
            copy.start()
    loaded = set()

    def need(*which):
        for i in which:
            if i not in loaded:
                loaded.add(i)
                loads[i].wait()

    greet(
        [device(zz, x, y, c) for zz in others]
        + [device(z, 1 - x, y, c)]
        + [device(z, x, yy, cc) for yy, cc in seq_peer]
    )

    outgoing = [send_o, send_p, send_s.at[:, :, :, 1 - c]]
    total = len(outgoing)
    held, landed = pieces[:total], [pieces[total + 3 * k : total + 3 * k + 3] for k in range(total)]
    own_spot = {"z": z, "x": x, "y": y}
    axis_size = {"z": Z, "x": X, "y": Y}

    def to_core(k):
        return send_to(outgoing[k], held[k], c_send.at[k, 8], c_recv.at[k, 8], device(z, x, y, 1 - c))

    def along(k, stage):
        route = BACKWARD_ROUTES[k]
        axis = route[stage]
        if axis == "z":
            peers = [(others[d], device(others[d], x, y, c)) for d in range(Z - 1)]
        else:
            peers = [(1 - x, device(z, 1 - x, y, c))] if axis == "x" else [(1 - y, device(z, x, 1 - y, c))]
        copies = []
        for d, (spot, peer) in enumerate(peers):
            at = {a: own_spot[a] if a in route[:stage] else slice(None) for a in "zxy"} | {axis: spot}
            dst = landed[k][stage].at[d] if axis == "z" else landed[k][stage]
            slot = d if axis == "z" else 3 + stage
            copies.append(send_to(held[k].at[at["z"], at["x"], at["y"]], dst, c_send.at[k, slot], c_recv.at[k, slot], peer))
        return copies

    def begin(k, stage):
        for copy in along(k, stage):
            copy.start()

    def arrived(k, stage):
        for copy in along(k, stage):
            copy.wait_recv()

    def add_landed(k, stage):
        route = BACKWARD_ROUTES[k]
        arrived(k, stage)
        rest = [a for a in "zxy" if a not in route[: stage + 1]]
        count = math.prod(axis_size[a] for a in rest)

        @pl.loop(0, count)
        def _(i):
            at, spot = dict(own_spot), []
            for a in reversed(rest):
                at[a] = i % axis_size[a]
                spot.insert(0, at[a])
                i = i // axis_size[a]
            here = (at["z"], at["x"], at["y"])
            value = held[k][here].astype(f32)
            if route[stage] == "z":
                for d in range(Z - 1):
                    value = value + landed[k][stage][(d, *spot)].astype(f32)
            else:
                value = value + landed[k][stage][tuple(spot)].astype(f32)
            held[k][here] = value.astype(b16)

        begin(k, stage + 1)

    def half_rows(a_t, core, b, at):
        return jnp.dot(a_t[:, :, :, core].reshape(-1, rows), b[:, at], preferred_element_type=f32)

    def make_send(k):
        if k == 0:

            @pl.loop(0, width // block)
            def _(n):
                at = pl.ds(pl.multiple_of(n * block, block), block)
                send_o[:, :, :, :, at] = half_rows(att_t, 1 - c, grad_branch, at).astype(b16).reshape(Z, X, Y, -1, block)

        else:
            send_p[...] = half_rows(nlow_t, 1 - c, cot, slice(None)).astype(b16).reshape(Z, X, Y, -1, cot.shape[1])
        to_core(k).start()

    def own_half(k):
        to_core(k).wait_recv()
        mine = held[k]
        if k == 0:

            @pl.loop(0, width // block)
            def _(n):
                at = pl.ds(pl.multiple_of(n * block, block), block)
                got = half_rows(att_t, c, grad_branch, at).reshape(Z, X, Y, -1, block)
                mine[:, :, :, :, at] = (mine[:, :, :, :, at].astype(f32) + got).astype(b16)

        elif k == 1:
            got = half_rows(nlow_t, c, cot, slice(None)).reshape(Z, X, Y, -1, cot.shape[1])
            mine[...] = (mine[...].astype(f32) + got).astype(b16)
        else:
            mine[...] = (mine[...].astype(f32) + send_s[:, :, :, c].astype(f32)).astype(b16)
        begin(k, 0)

    def finish(k):
        arrived(k, 2)
        value = held[k][z, x, y].astype(f32)
        if BACKWARD_ROUTES[k][2] == "z":
            for d in range(Z - 1):
                value = value + landed[k][2][d].astype(f32)
        else:
            value = value + landed[k][2][...].astype(f32)
        (o_out, o_proj, o_side)[k][...] = value

    def ffn_rows(k, xx, n):
        lanes = pl.ds(pl.multiple_of((k % 2) * half_width + n * 256, 256), 256)
        got = jnp.zeros((Z * 128, 256), f32)
        for b in range(streams):
            left = (hid_t if k < 2 else h_t)[b, :, xx].reshape(Z * 128, stream)
            right = (grad_ffn[b, :, :, :, lanes] if k < 2 else grad_u[b, :, :, lanes]).reshape(stream, 256)
            got = got + jnp.dot(left, right, preferred_element_type=f32)
        return got.reshape(Z, 128, 256)

    def ffn_x(k):
        return send_to(w_send.at[k], w_x.at[k], wx_send.at[k], wx_recv.at[k], device(z, 1 - x, y, c))

    def ffn_z(k, d):
        return send_to(w_x.at[k, others[d]], w_z.at[k, d], wz_send.at[k, d], wz_recv.at[k, d], device(others[d], x, y, c))

    def ffn_seq(h, p):
        yy, cc = seq_peer[p]
        return send_to(u_seq.at[h, yy, cc], u_in.at[h, y, c], us_send.at[h, p], us_recv.at[h, p], device(z, x, yy, cc))

    def ffn_one(k):
        need(4, 5)
        for b in range(streams):
            core_arrived(b, 0)
            core_arrived(b, 1)

        @pl.loop(0, half_width // 256)
        def _(n):
            w_send[k, :, :, pl.ds(pl.multiple_of(n * 256, 256), 256)] = ffn_rows(k, 1 - x, n).astype(b16)

        ffn_x(k).start()

    def ffn_two(k):
        ffn_x(k).wait_recv()

        @pl.loop(0, half_width // 256)
        def _(n):
            at = pl.ds(pl.multiple_of(n * 256, 256), 256)
            w_x[k, :, :, at] = (w_x[k, :, :, at].astype(f32) + ffn_rows(k, x, n)).astype(b16)

        for d in range(Z - 1):
            ffn_z(k, d).start()

    def ffn_three(k):
        value = w_x[k, z].astype(f32)
        for d in range(Z - 1):
            ffn_z(k, d).wait_recv()
        for d in range(Z - 1):
            value = value + w_z[k, d].astype(f32)
        if k < 2:
            o_down[:, k * half_width : (k + 1) * half_width] = value
        else:
            u_seq[k - 2] = value.astype(b16).reshape(Y, C, -1, half_width)
            for p in range(3):
                ffn_seq(k - 2, p).start()
            u_in[k - 2, y, c] = u_seq[k - 2, y, c]

    def ffn_four(h):
        for p in range(3):
            ffn_seq(h, p).wait_recv()
        for owner in range(Y * C):
            for q in range(half_width // 128):
                lane_at = ((h * (half_width // 128) + q) * Y * C + owner) * 128
                o_up[:, lane_at : lane_at + 128] = u_in[h, owner // C, owner % C, :, q * 128 : (q + 1) * 128].astype(f32)

    sums[...] = jnp.zeros_like(sums)
    sum_up[...] = jnp.zeros_like(sum_up)
    cot[...] = cot_f[...].astype(b16)

    def rows_of(b):
        return slice(b * part, (b + 1) * part)

    def norm_back(e, gain_row, n, inverse, spots):
        ge = e * side_rows[gain_row : gain_row + 1]
        mean = jnp.mean(ge, axis=-1, keepdims=True)
        along = jnp.mean(ge * n, axis=-1, keepdims=True)
        grad = inverse * (ge - mean - n * along)
        low = grad.astype(b16)
        for spot, value in zip(spots, (e * n, e, low.astype(f32))):
            sums[spot : spot + 1] += jnp.sum(value, axis=0, keepdims=True)
        return grad, low

    def grad_y(b):
        mine = grad_ffn.at[b, y, c]
        return send_to(mine, mine, gy_send.at[b], gy_recv.at[b], device(z, x, 1 - y, c))

    def grad_core(b, i):
        slab = grad_ffn.at[b, 1 - y if i else y, c]
        return send_to(slab, slab, gk_send.at[b, i], gk_recv.at[b, i], device(z, x, y, 1 - c))

    used = []

    def second_norm_back(b):
        need(0)
        at = rows_of(b)
        e = lax.dot_general(cot[at], w_proj[...], nt, preferred_element_type=f32)
        o_in[at], low = norm_back(e, 8, norm[at], r_two[at, :1], (8, 6, 5))
        grad_ffn[b, y, c] = low
        used.append(b)
        if len(used) == streams:
            loads[6].start()
        grad_y(b).start()
        grad_core(b, 0).start()

    def forward_grad(b):
        grad_y(b).wait_recv()
        grad_core(b, 1).start()

    core_here = set()

    def core_arrived(b, i):
        if (b, i) not in core_here:
            core_here.add((b, i))
            grad_core(b, i).wait_recv()

    def hidden_back(b, away):
        need(1, 2)
        yy = 1 - y if away else y
        core_arrived(b, 1 if away else 0)

        @pl.loop(0, hidden // block)
        def _(n):
            at = pl.ds(pl.multiple_of(n * block, block), block)
            got = lax.dot_general(grad_ffn[b, yy].reshape(C * part, width), wd[at], nt, preferred_element_type=f32)
            low = (got * dgelu[b, yy, :, at].astype(f32)).astype(b16)
            grad_u[b, yy, :, at] = low
            sum_up[:, at] += jnp.sum(low.astype(f32), axis=0, keepdims=True)

    def share_core(b):
        return send_to(g_send.at[b], g_c.at[b], gc_send.at[b], gc_recv.at[b], device(z, x, y, 1 - c))

    def share_y(b):
        return send_to(g_y_send.at[b], g_y.at[b], gf_send.at[b], gf_recv.at[b], device(z, x, 1 - y, c))

    ready = set()

    def inner_back(b, away):
        need(3)
        yy = 1 - y if away else y
        at = rows_of(b)

        @pl.loop(0, width // block)
        def _(n):
            col = pl.ds(pl.multiple_of(n * block, block), block)
            got = lax.dot_general(grad_u[b, yy, pl.ds((1 - c) * part, part)], wu[col], nt, preferred_element_type=f32)
            g_send[b, yy, :, col] = got.astype(b16)
            got = lax.dot_general(grad_u[b, yy, pl.ds(c * part, part)], wu[col], nt, preferred_element_type=f32)
            if away:
                apart[at, col] = got
            else:
                o_in[at, col] += got

        ready.add((b, away))
        if len([r for r in ready if r[0] == b]) == 2:
            share_core(b).start()

    def core_sum(b):
        share_core(b).wait_recv()
        g_y_send[b] = (apart[rows_of(b)] + g_c[b, 1 - y].astype(f32)).astype(b16)
        share_y(b).start()

    def first_norm_back(b):
        need(6)
        at = rows_of(b)
        share_y(b).wait_recv()
        e = o_in[at] + g_c[b, y].astype(f32) + g_y[b].astype(f32)
        o_in[at], grad_branch[at] = norm_back(e, 7, norm[at], r_one[at, :1], (7, 4, 3))

    def att_seq(p):
        yy, cc = seq_peer[p]
        src = grad_att.at[:, :, pl.ds(pl.multiple_of((yy * C + cc) * cols, cols), cols)]
        return send_to(src, heads.at[:, y, c], a_send.at[p], a_recv.at[p], device(z, x, yy, cc))

    def grad_heads(to):
        need(7)
        at = pl.ds(pl.multiple_of(to * cols, cols), cols)
        got = lax.dot_general(grad_branch[...], wo[at], nt, preferred_element_type=f32)
        grad_att[:, :, at] = got.astype(b16).reshape(streams, part, cols)

    def att_back_send(p):
        if p < 3:
            yy, cc = seq_peer[p]
            grad_heads(yy * C + cc)
            att_seq(p).start()
        else:
            grad_heads(s)
            heads[:, y, c] = grad_att[:, :, pl.ds(pl.multiple_of(s * cols, cols), cols)]

    lane = lax.broadcasted_iota(jnp.int32, (1, PAIR), 1)
    low_half = (lane % HEAD_DIM) < HEAD_DIM // 2
    top = lax.broadcasted_iota(jnp.int32, (PAIR, 1), 0) < HEAD_DIM
    masks = [(lane < HEAD_DIM).astype(f32).astype(b16), (lane >= HEAD_DIM).astype(f32).astype(b16)]
    score_scale = HEAD_DIM**-0.5
    q_block = stream // 2

    def attend_back(i):
        half, b = i // streams, i % streams
        far[...] = far_keys(sizes, b, stream)
        queries, keys, values = qkv[0, b, half], qkv[1, b, half], qkv[2, b, half]
        given = heads[b, :, :, :, pl.ds(pl.multiple_of(half * PAIR, PAIR), PAIR)].reshape(stream, PAIR)
        keys_t = keys.T
        grad_k, grad_v = jnp.zeros((stream, PAIR), f32), jnp.zeros((stream, PAIR), f32)
        grad_q = []
        for part_q in range(2):
            at = slice(part_q * q_block, (part_q + 1) * q_block)
            q_t = []
            for head in range(2):
                q = queries[at] * (masks[head] * b16(score_scale))
                g = given[at] * masks[head]
                scores = lax.dot_general(keys, q, nt, preferred_element_type=f32) + far[:, at]
                probs = jnp.exp(scores - lse[b * 2 + half, head : head + 1, at])
                grad_p = lax.dot_general(values, g, nt, preferred_element_type=f32)
                row_dot = jnp.sum(probs * grad_p, axis=0, keepdims=True)
                grad_s = (probs * (grad_p - row_dot)).astype(b16)
                grad_v = grad_v + jnp.dot(probs.astype(b16), g, preferred_element_type=f32)
                grad_k = grad_k + jnp.dot(grad_s, q, preferred_element_type=f32)
                q_t.append(jnp.dot(keys_t, grad_s, preferred_element_type=f32))
            grad_q.append(jnp.where(top, q_t[0], q_t[1]).T * score_scale)
        grad_q = jnp.concatenate(grad_q, axis=0)
        lane_at = pl.multiple_of(s * cols + half * PAIR, PAIR)
        done = []
        for t in (grad_q, grad_k):
            done.append(turned_back(t.astype(b16).astype(f32), cos4[b], sin4[b], low_half).astype(b16))
        done.append(grad_v.astype(b16))
        for j in range(3):
            turned[half, b, :, j * PAIR : (j + 1) * PAIR] = done[j]
            sums[j : j + 1, pl.ds(lane_at, PAIR)] += jnp.sum(done[j].astype(f32), axis=0, keepdims=True)

    def qkv_rows(half, xx):
        got = jnp.zeros((Z * 128, 3 * PAIR), f32)
        for b in range(streams):
            got = got + jnp.dot(tok_t[b, :, xx].reshape(Z * 128, stream), turned[half, b], preferred_element_type=f32)
        return got.reshape(Z, 128, 3 * PAIR)

    def qkv_x(half):
        return send_to(q_send.at[half], q_x.at[half], qx_send.at[half], qx_recv.at[half], device(z, 1 - x, y, c))

    def qkv_z(half, d):
        return send_to(q_x.at[half, others[d]], q_z.at[half, d], qz_send.at[half, d], qz_recv.at[half, d], device(others[d], x, y, c))

    def qkv_seq(half, p):
        yy, cc = seq_peer[p]
        return send_to(q_seq.at[half, yy, cc], q_in.at[half, y, c], qs_send.at[half, p], qs_recv.at[half, p], device(z, x, yy, cc))

    def qkv_one(half):
        q_send[half] = qkv_rows(half, 1 - x).astype(b16)

        qkv_x(half).start()

    def qkv_two(half):
        qkv_x(half).wait_recv()
        q_x[half] = (q_x[half].astype(f32) + qkv_rows(half, x)).astype(b16)

        for d in range(Z - 1):
            qkv_z(half, d).start()

    def qkv_three(half):
        value = q_x[half, z].astype(f32)
        for d in range(Z - 1):
            qkv_z(half, d).wait_recv()
        for d in range(Z - 1):
            value = value + q_z[half, d].astype(f32)
        q_seq[half] = value.reshape(Y, C, -1, 3 * PAIR)
        for p in range(3):
            qkv_seq(half, p).start()
        q_in[half, y, c] = q_seq[half, y, c]

    def qkv_four(half):
        for p in range(3):
            qkv_seq(half, p).wait_recv()
        for owner in range(Y * C):
            for j in range(3):
                lane_at = j * width + owner * cols + half * PAIR
                o_qkv[:, lane_at : lane_at + PAIR] = q_in[half, owner // C, owner % C, :, j * PAIR : (j + 1) * PAIR]

    def in_c(b):
        return send_to(g_send.at[b], g_c.at[b], ic_send.at[b], ic_recv.at[b], device(z, x, y, 1 - c))

    def in_y(b):
        return send_to(g_y_send.at[b], g_y.at[b], iy_send.at[b], iy_recv.at[b], device(z, x, 1 - y, c))

    def input_rows(b, yy, cc):
        at = pl.ds(pl.multiple_of((yy * C + cc) * part, part), part)
        got = lax.dot_general(turned[0, b, at], cols_all[0], nt, preferred_element_type=f32)
        return got + lax.dot_general(turned[1, b, at], cols_all[1], nt, preferred_element_type=f32)

    def input_one(b):
        share_core(b).wait_send()
        for yy in range(Y):
            g_send[b, yy] = input_rows(b, yy, 1 - c).astype(b16)
        in_c(b).start()

    def input_two(b):
        in_c(b).wait_recv()
        share_y(b).wait_send()
        g_y_send[b] = (input_rows(b, 1 - y, c) + g_c[b, 1 - y].astype(f32)).astype(b16)
        in_y(b).start()

    def input_three(b):
        o_in[b * part : (b + 1) * part] += input_rows(b, y, c) + g_c[b, y].astype(f32)

    def input_four(b):
        in_y(b).wait_recv()
        o_in[b * part : (b + 1) * part] += g_y[b].astype(f32)

    def small_sums():
        lanes = lax.broadcasted_iota(jnp.int32, (16, 128), 1)
        spots = lax.broadcasted_iota(jnp.int32, (16, 128), 0)
        share = 128 // (Y * C)
        for zx in range(Z * X):
            tile = sums[:, zx * 128 : (zx + 1) * 128]
            for yc in range(Y * C):
                moved = pltpu.roll(tile, (128 - yc * share) % 128, 1) if yc else tile
                value = jnp.where(lanes < share, moved, 0.0)
                value = jnp.where(spots == 9, sum_up[:, zx * 128 : (zx + 1) * 128] * (s == yc).astype(f32), value)
                send_s[zx // X, zx % X, yc // C, yc % C] = value.astype(b16)
        to_core(2).start()

    work = {
        "ln2b": second_norm_back, "gk": forward_grad, "gh": hidden_back, "g1": inner_back, "f2": core_sum, "ln1b": first_norm_back, "ga": att_back_send,
        "w1": ffn_one, "w2": ffn_two, "w3": ffn_three, "w4": ffn_four,
        "mk": lambda k: make_send(k) if k < 2 else small_sums(), "own": own_half, "add": add_landed, "fin": finish,
        "q1": qkv_one, "q2": qkv_two, "q3": qkv_three, "q4": qkv_four,
        "i1": input_one, "i2": input_two, "i3": input_three, "i4": input_four,
    }
    spots = [i for i, name in enumerate(BACKWARD_ORDER) if name[0] == "at"]

    def run(first_spot, last_spot):
        for name in BACKWARD_ORDER[first_spot:last_spot]:
            if name == ("mk", 0):
                need(8)
            work[name[0]](*name[1:])

    run(0, spots[0])
    need(*range(len(loads)))

    def before(i):
        if i == 0:
            for p in range(3):
                att_seq(p).wait_recv()
        else:
            run(spots[i - 1] + 1, spots[i])

    @pl.loop(0, streams * 2)
    def _(i):
        at_index(i, {spot: functools.partial(before, spot) for spot in range(streams * 2)})
        attend_back(i)

    run(spots[-1] + 1, len(BACKWARD_ORDER))

    for k in range(total):
        to_core(k).wait_send()
        for stage in range(3):
            for copy in along(k, stage):
                copy.wait_send()
    for k in range(4):
        ffn_x(k).wait_send()
        for d in range(Z - 1):
            ffn_z(k, d).wait_send()
    for p in range(3):
        att_seq(p).wait_send()
        for half in range(2):
            qkv_seq(half, p).wait_send()
            ffn_seq(half, p).wait_send()
    for half in range(2):
        qkv_x(half).wait_send()
        for d in range(Z - 1):
            qkv_z(half, d).wait_send()
    for b in range(streams):
        for copy in (in_c(b), in_y(b), grad_y(b), grad_core(b, 0), grad_core(b, 1)):
            copy.wait_send()


def run_backward(kept, sizes, cot):
    (
        w_out, w_up, w_down, w_proj, w_cols, side_rows, tok_t, qkv, lse, att_t, n_one, r_one, h_t, hid_t, dgelu, n_two, r_two, nlow_t, cos4, sin4,
    ) = kept
    rows, width = n_one.shape
    streams, _, stream = tok_t.shape
    hidden = dgelu.shape[-1]
    ff = hidden * Y * C
    proj = w_proj.shape[-1]
    cols, half_width = width // (Y * C), width // 2
    grid = (Z, X, Y, C)
    part = rows // streams
    vm, dma = pltpu.VMEM, pltpu.SemaphoreType.DMA
    vmem, hbm = pl.BlockSpec(memory_space=pltpu.VMEM), pl.BlockSpec(memory_space=pl.ANY)
    owner = width // OWNERS
    tails = [(owner, width), (owner, proj), (16, 128)]
    split_rows = (streams, Z, X, width // (Z * X), stream)
    inputs = [
        (w_out.reshape(width, width), hbm), (w_up.reshape(width, hidden), hbm), (w_down.reshape(hidden, width), hbm),
        (w_proj.reshape(width, proj), vmem), (w_cols.reshape(2, width, 3 * PAIR), hbm), (side_rows, vmem), (tok_t.reshape(split_rows), hbm), (qkv, hbm),
        (lse, vmem), (att_t.reshape(grid + (owner, rows)), hbm), (n_one, hbm), (r_one, vmem), (h_t.reshape(split_rows), hbm),
        (hid_t.reshape(split_rows), hbm), (dgelu, hbm), (n_two, hbm), (r_two, vmem), (nlow_t.reshape(grid + (owner, rows)), vmem),
        (cos4, vmem), (sin4, vmem), (sizes, pl.BlockSpec(memory_space=pltpu.SMEM)), (cot, vmem),
    ]
    scratch = [
        vm((width, width), b16), vm((width, hidden), b16), vm((hidden, width), b16), vm((rows, width), f32),
        vm(grid + (owner, rows), b16), vm(split_rows, b16), vm(split_rows, b16), vm(dgelu.shape, b16), vm(split_rows, b16),
        vm(qkv.shape, b16), vm((2, width, 3 * PAIR), b16), vm((16, width), f32), vm((1, hidden), f32),
        vm((streams, Y, C, part, width), b16), vm((rows, width), b16), vm((streams, part, width), b16),
        vm((streams, Y, C, part, cols), b16), vm((stream, stream), f32), vm((2, streams, stream, 3 * PAIR), b16),
        vm((Z, X, Y) + tails[0], b16), vm((Z, X, Y) + tails[1], b16), vm(grid + tails[2], b16), vm(cot.shape, b16),
        vm((4, Z, 128, half_width), b16), vm((4, Z, 128, half_width), b16), vm((4, Z - 1, 128, half_width), b16),
        vm((2, Y, C, owner, half_width), b16), vm((2, Y, C, owner, half_width), b16), vm((rows, width), f32),
        vm((streams, Y, part, width), b16), vm((streams, Y, part, width), b16), vm((streams, part, width), b16), vm((streams, part, width), b16),
        vm((2, Z, 128, 3 * PAIR), b16), vm((2, Z, 128, 3 * PAIR), b16), vm((2, Z - 1, 128, 3 * PAIR), b16),
        vm((2, Y, C, 32, 3 * PAIR), f32), vm((2, Y, C, 32, 3 * PAIR), f32),
        dma((3, 9)), dma((3, 9)), dma((3,)), dma((3,)), dma((2,)), dma((2,)), dma((2, 3)), dma((2, 3)), dma((2, 3)), dma((2, 3)),
        dma((streams,)), dma((streams,)), dma((streams,)), dma((streams,)),
        dma((4,)), dma((4,)), dma((4, 3)), dma((4, 3)), dma((2, 3)), dma((2, 3)), dma((streams,)), dma((streams,)), dma((streams, 2)), dma((streams, 2)),
        dma((streams,)), dma((streams,)), dma((streams,)), dma((streams,)),
        dma((12,)),
    ]
    size = {"z": Z, "x": X, "y": Y}
    scratch += [vm((Z, X, Y) + tail, b16) for tail in tails]
    for route, tail in zip(BACKWARD_ROUTES, tails):
        for stage in range(3):
            rest = tuple(size[a] for a in "zxy" if a not in route[: stage + 1])
            scratch.append(vm(((Z - 1,) if route[stage] == "z" else ()) + rest + tail, b16))
    outs = [(rows, width), (owner, 3 * width), (owner, width), (owner, ff), (ff // OWNERS, width), (owner, proj), (16, 128)]
    return pl.pallas_call(
        backward_kernel,
        out_shape=[jax.ShapeDtypeStruct(o, f32) for o in outs],
        in_specs=[spec for _, spec in inputs],
        out_specs=[vmem] * len(outs),
        scratch_shapes=scratch,
        compiler_params=pltpu.CompilerParams(collective_id=4, has_side_effects=True, vmem_limit_bytes=63 << 20),
    )(*[a for a, _ in inputs])


def layer_norm(field, gain_row, shift_row):
    average = jnp.mean(field, axis=-1, keepdims=True)
    centred = field - average
    variance = jnp.mean(centred * centred, axis=-1, keepdims=True)
    return centred * lax.rsqrt(variance + epsilon) * gain_row + shift_row


def doc_layout(doc_sizes, places):
    doc_ends = jnp.cumsum(doc_sizes)
    passed = places[:, None] >= doc_ends[None, :]
    segment = jnp.sum(passed.astype(jnp.int32), axis=1)
    starts = jnp.sum(jnp.where(passed, doc_sizes[None, :], 0), axis=1)
    return (segment, places - starts)


def rope_tables(position, half_dim):
    steps_f = jnp.arange(half_dim, dtype=jnp.float32)
    inverse = jnp.exp(steps_f * (-math.log(rope_base) / half_dim))
    angle = position.astype(jnp.float32)[:, None] * inverse[None, :]
    return (jnp.cos(angle), jnp.sin(angle))


def rotate(field, cosine, sine_tab, head_count):
    length = field.shape[0]
    halves = field.reshape(length, head_count, 2, -1)
    first_half = halves[:, :, 0]
    second_half = halves[:, :, 1]
    cos_b = cosine[:, None, :]
    sin_b = sine_tab[:, None, :]
    turned = jnp.stack(
        [first_half * cos_b - second_half * sin_b, second_half * cos_b + first_half * sin_b], axis=2
    )
    return turned.reshape(length, -1)


def gelu_exact(field):
    return jax.nn.gelu(field, approximate=False)


def scores_of(query_blk, seg_blk, keys_all, stream_seg, score_scale):
    raw_scores = (
        jnp.einsum("qhd,khd->hqk", query_blk, keys_all, preferred_element_type=jnp.float32)
        * score_scale
    )
    same_doc = (seg_blk[:, None] == stream_seg[None, :])[None]
    return jnp.where(same_doc, raw_scores, neg_fill)


def per_device_any(
    tokens,
    doc_lengths,
    qkv_weight,
    out_weight,
    up_weight,
    down_weight,
    proj_weight,
    biases,
    gains,
    up_bias,
    cotangent,
):
    stream_count = tokens.shape[0]
    seg_rows = tokens.shape[1]
    model_width = tokens.shape[2]
    seq_parts = lax.axis_size("seq")
    stream = seg_rows * seq_parts
    head_count = model_width // HEAD_DIM
    local_heads = head_count // seq_parts
    flat_width = local_heads * HEAD_DIM
    score_scale = HEAD_DIM ** (-0.5)
    tok_flat = tokens.reshape(stream_count * seg_rows, model_width)
    gathered = (
        lax.all_gather(qkv_weight, ("rows", "seq"), axis=0, tiled=True),
        lax.all_gather(out_weight, ("rows", "seq"), axis=0, tiled=True),
        lax.all_gather(up_weight, ("rows", "seq"), axis=0, tiled=True),
        lax.all_gather(down_weight, ("rows", "seq"), axis=0, tiled=True),
        lax.all_gather(proj_weight, ("rows", "seq"), axis=0, tiled=True),
        lax.all_gather(biases, ("rows", "seq"), axis=1, tiled=True),
        lax.all_gather(gains, ("rows", "seq"), axis=1, tiled=True),
        lax.all_gather(up_bias, ("rows", "seq"), axis=0, tiled=True),
    )
    w_qkv, w_out, w_up, w_down, w_proj = (
        gathered[0],
        gathered[1],
        gathered[2],
        gathered[3],
        gathered[4],
    )
    bias_rows = gathered[5].astype(jnp.float32)
    gain_rows = gathered[6].astype(jnp.float32)
    bias_up = gathered[7].astype(jnp.float32)
    token_places = lax.axis_index("seq") * seg_rows + jnp.arange(seg_rows, dtype=jnp.int32)
    layout_rows = jax.vmap(doc_layout, in_axes=(0, None))
    token_seg, position = layout_rows(doc_lengths, token_places)
    cosine, sine_tab = rope_tables(position.reshape(-1), HEAD_DIM // 2)
    projected = jnp.dot(tok_flat, w_qkv, preferred_element_type=jnp.float32) + bias_rows[
        0:3
    ].reshape(-1)
    queries = (
        rotate(projected[:, :model_width], cosine, sine_tab, head_count)
        .astype(jnp.bfloat16)
        .reshape(stream_count, seg_rows, model_width)
    )
    keys_tok = (
        rotate(projected[:, model_width : 2 * model_width], cosine, sine_tab, head_count)
        .astype(jnp.bfloat16)
        .reshape(stream_count, seg_rows, model_width)
    )
    values_tok = (
        projected[:, 2 * model_width :]
        .astype(jnp.bfloat16)
        .reshape(stream_count, seg_rows, model_width)
    )
    queries_h, keys_h, values_h = (
        lax.all_to_all(queries, "seq", split_axis=2, concat_axis=1, tiled=True),
        lax.all_to_all(keys_tok, "seq", split_axis=2, concat_axis=1, tiled=True),
        lax.all_to_all(values_tok, "seq", split_axis=2, concat_axis=1, tiled=True),
    )
    stream_seg, stream_pos = layout_rows(doc_lengths, jnp.arange(stream, dtype=jnp.int32))
    block_rows = math.gcd(stream, 512)
    block_count = stream // block_rows

    def forward_stream(element):
        query_s, key_s, value_s, seg_s = element
        query_blocks = query_s.reshape(block_count, block_rows, local_heads, HEAD_DIM)
        keys_all = key_s.reshape(stream, local_heads, HEAD_DIM)
        values_all = value_s.reshape(stream, local_heads, HEAD_DIM)
        seg_blocks = seg_s.reshape(block_count, block_rows)

        def forward_block(inner):
            query_blk, seg_blk = inner
            scores = scores_of(query_blk, seg_blk, keys_all, seg_s, score_scale)
            row_max = jnp.max(scores, axis=-1, keepdims=True)
            row_total = jnp.sum(jnp.exp(scores - row_max), axis=-1, keepdims=True)
            log_total = row_max + jnp.log(row_total)
            probs_low = jnp.exp(scores - log_total).astype(jnp.bfloat16)
            attn_blk = jnp.einsum(
                "hqk,khd->qhd", probs_low, values_all, preferred_element_type=jnp.float32
            )
            return (attn_blk.astype(jnp.bfloat16), log_total[:, :, 0])

        attn_blocks, log_blocks = lax.map(forward_block, (query_blocks, seg_blocks))
        return (attn_blocks.reshape(stream, flat_width), log_blocks)

    attn_heads, log_totals = lax.map(forward_stream, (queries_h, keys_h, values_h, stream_seg))
    attended = lax.all_to_all(attn_heads, "seq", split_axis=1, concat_axis=2, tiled=True).reshape(
        stream_count * seg_rows, model_width
    )
    branch = jnp.dot(attended, w_out, preferred_element_type=jnp.float32) + bias_rows[3]
    h_one, norm_one = jax.vjp(
        layer_norm, tok_flat.astype(jnp.float32) + branch, gain_rows[0], bias_rows[4]
    )
    h_low = h_one.astype(jnp.bfloat16)
    u_pre = jnp.dot(h_low, w_up, preferred_element_type=jnp.float32) + bias_up
    hidden_f, gelu_back = jax.vjp(gelu_exact, u_pre)
    hidden = hidden_f.astype(jnp.bfloat16)
    ffn_out = jnp.dot(hidden, w_down, preferred_element_type=jnp.float32) + bias_rows[5]
    normed, norm_two = jax.vjp(layer_norm, h_one + ffn_out, gain_rows[1], bias_rows[6])
    normed_low = normed.astype(jnp.bfloat16)
    result = jnp.dot(normed_low, w_proj, preferred_element_type=jnp.float32).astype(jnp.bfloat16)
    w_qkv, w_out, w_up, w_down, w_proj = (
        lax.all_gather(qkv_weight, ("rows", "seq"), axis=0, tiled=True),
        lax.all_gather(out_weight, ("rows", "seq"), axis=0, tiled=True),
        lax.all_gather(up_weight, ("rows", "seq"), axis=0, tiled=True),
        lax.all_gather(down_weight, ("rows", "seq"), axis=0, tiled=True),
        lax.all_gather(proj_weight, ("rows", "seq"), axis=0, tiled=True),
    )
    cot_low = cotangent.reshape(stream_count * seg_rows, -1).astype(jnp.bfloat16)
    proj_part = jnp.dot(normed_low.T, cot_low, preferred_element_type=jnp.float32)
    grad_normed = jnp.dot(cot_low, w_proj.T, preferred_element_type=jnp.float32)
    grad_z2, grad_g2, grad_b2 = norm_two(grad_normed)
    grad_ffn = grad_z2.astype(jnp.bfloat16)
    grad_c2 = jnp.sum(grad_ffn, axis=0, dtype=jnp.float32)
    down_part = jnp.dot(hidden.T, grad_ffn, preferred_element_type=jnp.float32)
    grad_hidden = jnp.dot(grad_ffn, w_down.T, preferred_element_type=jnp.float32)
    grad_u = gelu_back(grad_hidden)[0].astype(jnp.bfloat16)
    grad_c1 = jnp.sum(grad_u, axis=0, dtype=jnp.float32)
    up_part = jnp.dot(h_low.T, grad_u, preferred_element_type=jnp.float32)
    ffn_sums = (up_part, down_part, proj_part, grad_c1)
    grad_h1 = grad_z2 + jnp.dot(grad_u, w_up.T, preferred_element_type=jnp.float32)
    grad_z1, grad_g1, grad_b1 = norm_one(grad_h1)
    grad_branch = grad_z1.astype(jnp.bfloat16)
    grad_bo = jnp.sum(grad_branch, axis=0, dtype=jnp.float32)
    out_part = jnp.dot(attended.T, grad_branch, preferred_element_type=jnp.float32)
    grad_attn = jnp.dot(grad_branch, w_out.T, preferred_element_type=jnp.float32).astype(
        jnp.bfloat16
    )
    grad_heads = lax.all_to_all(
        grad_attn.reshape(stream_count, seg_rows, model_width),
        "seq",
        split_axis=2,
        concat_axis=1,
        tiled=True,
    )

    def backward_stream(element):
        query_s, key_s, value_s, seg_s, log_s, grad_s = element
        query_blocks = query_s.reshape(block_count, block_rows, local_heads, HEAD_DIM)
        keys_all = key_s.reshape(stream, local_heads, HEAD_DIM)
        values_all = value_s.reshape(stream, local_heads, HEAD_DIM)
        seg_blocks = seg_s.reshape(block_count, block_rows)
        grad_blocks = grad_s.reshape(block_count, block_rows, local_heads, HEAD_DIM)

        def backward_block(carried, inner):
            grad_keys, grad_values = carried
            query_blk, seg_blk, log_total, grad_blk = inner
            probs_f = jnp.exp(
                scores_of(query_blk, seg_blk, keys_all, seg_s, score_scale) - log_total[:, :, None]
            )
            grad_values = grad_values + jnp.einsum(
                "hqk,qhd->khd",
                probs_f.astype(jnp.bfloat16),
                grad_blk,
                preferred_element_type=jnp.float32,
            )
            grad_probs = jnp.einsum(
                "qhd,khd->hqk", grad_blk, values_all, preferred_element_type=jnp.float32
            )
            row_dot = jnp.sum(probs_f * grad_probs, axis=-1, keepdims=True)
            grad_scores = (probs_f * (grad_probs - row_dot) * score_scale).astype(jnp.bfloat16)
            grad_query = jnp.einsum(
                "hqk,khd->qhd", grad_scores, keys_all, preferred_element_type=jnp.float32
            )
            grad_keys = grad_keys + jnp.einsum(
                "hqk,qhd->khd", grad_scores, query_blk, preferred_element_type=jnp.float32
            )
            return ((grad_keys, grad_values), grad_query.astype(jnp.bfloat16))

        zero_acc = jnp.zeros((stream, local_heads, HEAD_DIM), jnp.float32)
        (grad_keys, grad_values), grad_queries = lax.scan(
            backward_block, (zero_acc, zero_acc), (query_blocks, seg_blocks, log_s, grad_blocks)
        )
        return (
            grad_queries.reshape(stream, flat_width),
            grad_keys.astype(jnp.bfloat16).reshape(stream, flat_width),
            grad_values.astype(jnp.bfloat16).reshape(stream, flat_width),
        )

    head_q, head_k, head_v = lax.map(
        backward_stream, (queries_h, keys_h, values_h, stream_seg, log_totals, grad_heads)
    )
    back_q, back_k, back_v = (
        lax.all_to_all(head_q, "seq", split_axis=1, concat_axis=2, tiled=True),
        lax.all_to_all(head_k, "seq", split_axis=1, concat_axis=2, tiled=True),
        lax.all_to_all(head_v, "seq", split_axis=1, concat_axis=2, tiled=True),
    )
    flat_rows = stream_count * seg_rows
    turned_q = rotate(
        back_q.reshape(flat_rows, model_width).astype(jnp.float32), cosine, -sine_tab, head_count
    )
    turned_k = rotate(
        back_k.reshape(flat_rows, model_width).astype(jnp.float32), cosine, -sine_tab, head_count
    )
    grad_project = jnp.concatenate(
        [turned_q, turned_k, back_v.reshape(flat_rows, model_width).astype(jnp.float32)], axis=1
    ).astype(jnp.bfloat16)
    grad_bqkv = jnp.sum(grad_project, axis=0, dtype=jnp.float32).reshape(3, model_width)
    qkv_part = jnp.dot(tok_flat.T, grad_project, preferred_element_type=jnp.float32)
    input_grad = grad_z1 + jnp.dot(grad_project, w_qkv.T, preferred_element_type=jnp.float32)
    bias_part = jnp.concatenate(
        [grad_bqkv, jnp.stack([grad_bo, grad_b1, grad_c2, grad_b2])], axis=0
    )
    gain_part = jnp.stack([grad_g1, grad_g2])
    qkv_sum, out_sum, up_sum, down_sum, proj_sum, bias_sum, gain_sum, c1_sum = (
        lax.psum_scatter(qkv_part, ("rows", "seq"), scatter_dimension=0, tiled=True),
        lax.psum_scatter(out_part, ("rows", "seq"), scatter_dimension=0, tiled=True),
        lax.psum_scatter(ffn_sums[0], ("rows", "seq"), scatter_dimension=0, tiled=True),
        lax.psum_scatter(ffn_sums[1], ("rows", "seq"), scatter_dimension=0, tiled=True),
        lax.psum_scatter(ffn_sums[2], ("rows", "seq"), scatter_dimension=0, tiled=True),
        lax.psum_scatter(bias_part, ("rows", "seq"), scatter_dimension=1, tiled=True),
        lax.psum_scatter(gain_part, ("rows", "seq"), scatter_dimension=1, tiled=True),
        lax.psum_scatter(ffn_sums[3], ("rows", "seq"), scatter_dimension=0, tiled=True),
    )
    output = result.reshape(stream_count, seg_rows, -1)
    return (
        output,
        input_grad.reshape(stream_count, seg_rows, model_width),
        qkv_sum,
        out_sum,
        up_sum,
        down_sum,
        proj_sum,
        bias_sum,
        gain_sum,
        c1_sum,
    )


def direct_links():
    return lax.axis_size("rows") == Z * X and lax.axis_size("seq") == Y * C


def copy_out(count, *refs):
    for src, dst in zip(refs[:count], refs[count + 1 :]):
        dst[...] = src[...]
    side, (o_bias, o_gain, o_up) = refs[count], refs[-3:]
    lanes = o_bias.shape[1]
    o_bias[...] = side[:7, :lanes]
    o_gain[...] = side[7:9, :lanes]
    o_up[...] = side[9:10]


def per_device_direct(
    tokens, doc_lengths, qkv_weight, out_weight, up_weight, down_weight, proj_weight, biases, gains, up_bias, cotangent
):
    streams, part, width = tokens.shape
    *kept, result = run_forward(
        tokens, doc_lengths, qkv_weight, out_weight, up_weight, down_weight, proj_weight, biases, gains, up_bias.reshape(1, -1)
    )
    *big, side_sum = run_backward(kept, doc_lengths, cotangent.reshape(streams * part, -1))
    lanes = biases.shape[1]
    shape = jax.ShapeDtypeStruct
    vmem = pl.BlockSpec(memory_space=pltpu.VMEM)
    input_grad, qkv, out, up, down, proj, bias_sum, gain_sum, up_sum = pl.pallas_call(
        functools.partial(copy_out, len(big)),
        out_shape=[shape(a.shape, f32) for a in big] + [shape((7, lanes), f32), shape((2, lanes), f32), shape((1, 128), f32)],
        in_specs=[vmem] * (len(big) + 1),
        out_specs=[vmem] * (len(big) + 3),
    )(*big, side_sum)
    return (
        result.reshape(streams, part, -1),
        input_grad.reshape(streams, part, width),
        qkv,
        out,
        up,
        down,
        proj,
        bias_sum,
        gain_sum,
        up_sum.reshape(-1),
    )


def per_device(*args):
    return per_device_direct(*args) if direct_links() else per_device_any(*args)


def solution(mesh):
    in_specs = (
        P("rows", "seq", None),
        P("rows", None),
        P(("rows", "seq"), None),
        P(("rows", "seq"), None),
        P(("rows", "seq"), None),
        P(("rows", "seq"), None),
        P(("rows", "seq"), None),
        P(None, ("rows", "seq")),
        P(None, ("rows", "seq")),
        P(("rows", "seq")),
        P("rows", "seq", None),
    )
    out_specs = (
        P("rows", "seq", None),
        P("rows", "seq", None),
        P(("rows", "seq"), None),
        P(("rows", "seq"), None),
        P(("rows", "seq"), None),
        P(("rows", "seq"), None),
        P(("rows", "seq"), None),
        P(None, ("rows", "seq")),
        P(None, ("rows", "seq")),
        P(("rows", "seq")),
    )
    return jax.shard_map(
        per_device, mesh=mesh, in_specs=in_specs, out_specs=out_specs, check_vma=False
    )
```
